32 devices in a mesh: dp: 16 (over z, x, core), mp: 2 (over y).
Axes of the slice: x: 2, y: 2, z: 4, core: 2. Of those that a mesh axis runs over, the one named last changes fastest.
Arguments:
- captions: bfloat16 [2048, 16, 768], P('dp'), may hold values from -6 to 6
- image_cache: bfloat16 [2048, 768], P('dp'), may hold values from -6 to 6
- send_order: int32 [16, 128], P('dp'), may hold values from 0 to 127, each once within a row
- arrive_order: int32 [16, 128], P('dp'), may hold values from 0 to 127, each once within a row
- counts: int32 [16, 2], replicated, may hold values from 4 to 64, as said below
- keep_mask: int32 [2048], replicated, may hold values 0 or 1
- end_pos: int32 [2048], P('dp'), may hold values from 4 to 15
- w_qkv: bfloat16 [768, 3, 768], P('dp', None, 'mp'), may hold values from -0.21875 to 0.21875
- w_out: bfloat16 [768, 768], P('dp', 'mp'), may hold values from -0.625 to 0.625
- w_up: bfloat16 [768, 3072], P('dp', 'mp'), may hold values from -0.21875 to 0.21875
- w_down: bfloat16 [768, 3072], P('dp', 'mp'), may hold values from -0.15625 to 0.15625
- w_proj: bfloat16 [768, 768], P('dp'), may hold values from -0.21875 to 0.21875
- ln1_gain: float32 [768], P('dp'), may hold values from 0.5 to 1.5
- ln2_gain: float32 [768], P('dp'), may hold values from 0.5 to 1.5
Outputs:
- loss: float32 [], replicated
- grad_captions: float32 [2048, 16, 768], P('dp')
- grad_qkv: float32 [768, 3, 768], P('dp', None, 'mp')
- grad_out: float32 [768, 768], P('dp', 'mp')
- grad_up: float32 [768, 3072], P('dp', 'mp')
- grad_down: float32 [768, 3072], P('dp', 'mp')
- grad_proj: float32 [768, 768], P('dp')
- grad_ln1: float32 [768], P('dp')
- grad_ln2: float32 [768], P('dp')
The draws below stay inside these ranges and needn't reach their ends.
Inputs may be any that keep to these rules, and one draw needn't show every extreme that they name: `send_order`: each row is a permutation; entry (d, p * 8 * 8 + k) names the local cache row that index d of dp hands to index p as its k-th (8 = 1 there, so k = 0). `arrive_order`: each row is a permutation; entry (d, j) = p * 8 * 8 + k names the k-th embedding handed to index d by index p (8 = 1 there, so k = 0). `counts`: every entry is either 64 // 16 or 64; index 0 of dp fills 64 // 16 slots and the last index fills all 64 in every micro-batch.
All inputs are finite; a program needn't handle non-finite values.
Results may differ from the reference program's by a relative error of at most 0.035.
Values may be sent and summed in bfloat16 or wider, within the bound.
No kernel may reach another device: no remote copies, remote signals or barrier semaphores. Data moves between devices by JAX's collectives and lax.ppermute only.
A program may use at most 256 MiB of HBM per device.

```python
import math
import jax
import jax.numpy as jnp
from jax import lax

D = 768
HEADS = 12
HEAD = 64
FF = 3072
L = 16
MICRO = 2
CAP_DEV = 64
ROWS_DEV = 128
CAPTIONS = 2048
BATCH = 1024
PER_PEER = 8
N_DP = 16
N_MP = 2


def draw_counts(key, part):
    least = CAP_DEV // 16
    rank = jnp.arange(N_DP, dtype=jnp.int32)[:, None]
    coins = jax.random.randint(key, (N_DP, MICRO), 0, N_DP - 1)
    values = jnp.where(coins < rank, CAP_DEV, least)
    values = jnp.where(rank == 0, least, values)
    values = jnp.where(rank == N_DP - 1, CAP_DEV, values)
    return values.astype(jnp.int32)


def with_ends(array, rng, low, largest):
    extent = array.shape
    place = [jax.random.randint(jax.random.fold_in(rng, axis), (), 0, extent[axis]) for axis in range(len(extent))]
    array = array.at[tuple(place)].set(low)
    longest = extent.index(max(extent))
    place[longest] = (place[longest] + 1) % extent[longest]
    return array.at[tuple(place)].set(largest)


def level_of(stream_key, extent, pieces, low, top_value):
    loudness = 1.0
    for position, blocks in pieces:
        steps = jax.random.uniform(jax.random.fold_in(jax.random.fold_in(stream_key, 6), position), (blocks,), jnp.float32, low / len(pieces), top_value / len(pieces))
        loudness = loudness * jnp.repeat(jnp.exp(steps), extent[position] // blocks).reshape((-1,) + (1,) * (len(extent) - 1 - position))
    return loudness


def centred(own_key, extent, width, reach, pieces=(), kind=jnp.bfloat16):
    loudness = level_of(own_key, extent, pieces, -0.22, 0.18) if pieces else 1.0
    drawn = jax.random.normal(own_key, extent, jnp.float32) * width * loudness
    return jnp.minimum(jnp.maximum(drawn, -reach), reach).astype(kind)


def setup_inputs(seed: int = 0) -> dict:
    key_of = jax.random.split(jax.random.key(seed), 15)
    captions = centred(key_of[0], (CAPTIONS, L, D), 1.0, 6.0, ((0, 16),))
    image_cache = centred(key_of[1], (CAPTIONS, D), 1.0, 6.0, ((0, 16),))
    send_order = jax.vmap(lambda own: jax.random.permutation(own, ROWS_DEV))(jax.random.split(key_of[2], N_DP)).reshape((N_DP, ROWS_DEV)).astype(jnp.int32)
    arrive_order = jax.vmap(lambda own: jax.random.permutation(own, ROWS_DEV))(jax.random.split(key_of[3], N_DP)).reshape((N_DP, ROWS_DEV)).astype(jnp.int32)
    counts = draw_counts(jax.random.fold_in(key_of[14], 71), 0)
    keep_mask = with_ends((jax.random.randint(key_of[5], (CAPTIONS,), 0, 16) < 15).astype(jnp.int32), jax.random.fold_in(key_of[5], 1), 0, 1)
    end_pos = with_ends(jax.random.randint(key_of[6], (CAPTIONS,), L // 4, L), jax.random.fold_in(key_of[6], 1), L // 4, L - 1).astype(jnp.int32)
    w_qkv = centred(key_of[7], (D, 3, D), D ** -0.5, 0.21875, ((0, 16), (2, 2)))
    w_out = centred(key_of[8], (D, D), (D // 8) ** -0.5, 0.625, ((0, 16), (1, 2)))
    w_up = centred(key_of[9], (D, FF), D ** -0.5, 0.21875, ((0, 16), (1, 2)))
    w_down = centred(key_of[10], (D, FF), (FF // 2) ** -0.5, 0.15625, ((0, 16), (1, 2)))
    w_proj = centred(key_of[11], (D, D), D ** -0.5, 0.21875, ((0, 16),))
    ln1_gain = jnp.clip(1.0 + 0.1 * jax.random.normal(key_of[12], (D,), jnp.float32), 0.5, 1.5)
    ln2_gain = jnp.clip(1.0 + 0.1 * jax.random.normal(key_of[13], (D,), jnp.float32), 0.5, 1.5)
    return {"captions": captions, "image_cache": image_cache, "send_order": send_order, "arrive_order": arrive_order, "counts": counts, "keep_mask": keep_mask, "end_pos": end_pos, "w_qkv": w_qkv, "w_out": w_out, "w_up": w_up, "w_down": w_down, "w_proj": w_proj, "ln1_gain": ln1_gain, "ln2_gain": ln2_gain}


@jax.custom_vjp
def low(v):
    return lax.optimization_barrier(v.astype(jnp.bfloat16)).astype(jnp.float32)

@jax.custom_vjp
def low_back(v):
    return v

def low_keep(v):
    return (low(v), None)

def low_pass(kept, grad):
    return (grad,)

def back_keep(v):
    return (v, None)

def back_low(kept, grad):
    return (low(grad),)
low.defvjp(low_keep, low_pass)
low_back.defvjp(back_keep, back_low)
logit_scale = 40.0
highest = lax.Precision.HIGHEST

def high_dot(left_side, right_side):
    return jnp.dot(left_side, right_side, precision=highest)

def norm_rows(inputs, gain_row):
    center = inputs - lax.optimization_barrier(jnp.mean(inputs, -1, keepdims=True))
    variance = lax.optimization_barrier(jnp.mean(center * center, -1, keepdims=True))
    return center * lax.rsqrt(variance + 1e-05) * gain_row

def encode(block_in, finish, params):
    w_mix, w_back, w_raise, w_lower, w_embed, gain_first, gain_second = params
    count = block_in.shape[0]
    tokens = count * L
    stream = block_in.reshape(tokens, D)
    head_width = D // N_MP
    hidden_width = FF // N_MP
    head_count = HEADS // N_MP
    score_scale = 1.0 / math.sqrt(HEAD)
    causal = jnp.arange(L)[:, None] >= jnp.arange(L)[None, :]
    normed_first = low(norm_rows(stream, gain_first))
    attention = jnp.zeros((tokens, D), jnp.float32)
    for group_index in range(N_MP):
        columns = slice(group_index * head_width, (group_index + 1) * head_width)
        mixed_heads = jnp.einsum('rd,dte->rte', normed_first, w_mix[:, :, columns], precision=highest)
        mixed_heads = low_back(low(mixed_heads))
        queries = mixed_heads[:, 0].reshape(count, L, head_count, HEAD)
        key_rows = mixed_heads[:, 1].reshape(count, L, head_count, HEAD)
        value_rows = mixed_heads[:, 2].reshape(count, L, head_count, HEAD)
        scores = jnp.einsum('cqhd,ckhd->chqk', queries, key_rows, precision=highest) * score_scale
        scores = low_back(jnp.where(causal, scores, -1e+30))
        probs = jax.nn.softmax(scores, axis=-1)
        attended = jnp.einsum('chqk,ckhd->cqhd', low(probs), value_rows, precision=highest)
        attended = low_back(low(attended.reshape(tokens, head_width)))
        attention = attention + low(high_dot(attended, w_back[:, columns].T))
    middle = stream + low_back(attention)
    normed_second = low(norm_rows(middle, gain_second))
    feed = jnp.zeros((tokens, D), jnp.float32)
    for group_index in range(N_MP):
        columns = slice(group_index * hidden_width, (group_index + 1) * hidden_width)
        raised = low_back(high_dot(normed_second, w_raise[:, columns]))
        active = low(jax.nn.gelu(raised, approximate=False))
        feed = feed + low(high_dot(active, w_lower[:, columns].T))
    output_rows = middle + low_back(feed)
    picker = (jnp.arange(L)[None, :] == finish[:, None]).astype(jnp.float32)
    pooled = low(lax.optimization_barrier(jnp.sum(output_rows.reshape(count, L, D) * picker[:, :, None], axis=1)))
    embedding = low_back(high_dot(pooled, w_embed))
    unit_text = embedding * lax.rsqrt(lax.optimization_barrier(jnp.sum(embedding * embedding, -1, keepdims=True)) + 1e-06)
    return low(unit_text)

def micro_objective(params, batch_in, batch_end, batch_pics, batch_valid, block_size):
    blocks = BATCH // block_size

    def one_block(items):
        return encode(items[0], items[1], params)
    texts = lax.map(jax.checkpoint(one_block), (batch_in.reshape(blocks, block_size, L, D), batch_end.reshape(blocks, block_size)))
    texts = texts.reshape(BATCH, D)
    sims = low_back(logit_scale * high_dot(texts, batch_pics.T))
    allowed = batch_valid[:, None] & batch_valid[None, :]
    masked = jnp.where(allowed, sims, -1e+30)
    row_lse = jax.scipy.special.logsumexp(masked, axis=1)
    col_lse = jax.scipy.special.logsumexp(masked, axis=0)
    diagonal = jnp.diagonal(sims)
    return 0.5 * jnp.sum(jnp.where(batch_valid, row_lse - diagonal, 0.0)) + 0.5 * jnp.sum(jnp.where(batch_valid, col_lse - diagonal, 0.0))

def reference(captions, image_cache, send_order, arrive_order, counts, keep_mask, end_pos, w_qkv, w_out, w_up, w_down, w_proj, ln1_gain, ln2_gain):
    params = tuple((weight.astype(jnp.float32) for weight in (w_qkv, w_out, w_up, w_down, w_proj, ln1_gain, ln2_gain)))
    device_ids = jnp.arange(N_DP, dtype=jnp.int32)[:, None]
    source = (arrive_order // PER_PEER).astype(jnp.int32)
    column = (device_ids * PER_PEER + arrive_order % PER_PEER).astype(jnp.int32)
    cache_row = (source * ROWS_DEV + send_order[source, column]).astype(jnp.int32)
    pictures = image_cache.astype(jnp.float32)[cache_row.reshape(-1)]
    pictures = low(pictures * lax.rsqrt(lax.optimization_barrier(jnp.sum(pictures * pictures, -1, keepdims=True)) + 1e-06))
    pictures = pictures.reshape(N_DP, ROWS_DEV, D)
    inputs = captions.astype(jnp.float32).reshape(N_DP, ROWS_DEV, L, D)
    finish = end_pos.reshape(N_DP, ROWS_DEV)
    keep_rows = keep_mask.reshape(N_DP, ROWS_DEV) == 1
    block_size = math.gcd(BATCH, max(1, 4096 // L))
    totals = tuple((jnp.zeros_like(weight) for weight in params))
    objective_sum = jnp.zeros((), jnp.float32)
    valid_count = jnp.zeros((), jnp.float32)
    input_grads = []
    for micro_index in range(MICRO):
        first_row = micro_index * CAP_DEV
        batch_in = inputs[:, first_row:first_row + CAP_DEV].reshape(BATCH, L, D)
        batch_end = finish[:, first_row:first_row + CAP_DEV].reshape(BATCH)
        batch_pics = pictures[:, first_row:first_row + CAP_DEV].reshape(BATCH, D)
        batch_valid = (jnp.arange(CAP_DEV)[None, :] < counts[:, micro_index][:, None]) & keep_rows[:, first_row:first_row + CAP_DEV]
        batch_valid = batch_valid.reshape(BATCH)

        def objective(weights, rows_in):
            return micro_objective(weights, rows_in, batch_end, batch_pics, batch_valid, block_size)
        value_now, pull = jax.vjp(objective, params, batch_in)
        d_params, d_inputs = pull(jnp.ones_like(value_now))
        totals = jax.tree.map(jnp.add, totals, d_params)
        objective_sum = objective_sum + value_now
        valid_count = valid_count + jnp.sum(batch_valid.astype(jnp.float32))
        input_grads.append(d_inputs.reshape(N_DP, CAP_DEV, L, D))
    grad_captions = jnp.stack(input_grads, axis=1).reshape(CAPTIONS, L, D)
    loss = objective_sum / valid_count
    return (loss, grad_captions, totals[0], totals[1], totals[2], totals[3], totals[4], totals[5], totals[6])
```

```python
import math

import jax
import jax.numpy as jnp
from jax import lax
from jax.sharding import PartitionSpec as P

HEAD = 64
MICRO = 2
CAP_DEV = 64
LOGIT_SCALE = 40.0
SCORE_SCALE = 1.0 / math.sqrt(HEAD)

low = jnp.bfloat16
full = jnp.float32


def mm(a, b):
    return lax.dot_general(a, b, (((1,), (0,)), ((), ())), preferred_element_type=full)


def mm_nt(a, b):
    return lax.dot_general(a, b, (((1,), (1,)), ((), ())), preferred_element_type=full)


def mm_tn(a, b):
    return lax.dot_general(a, b, (((0,), (0,)), ((), ())), preferred_element_type=full)


def pick(flag, when_zero, when_one):
    return jnp.where(flag == 0, when_zero, when_one)


class Plane:
    def __init__(self):
        self.count = lax.axis_size("dp")
        self.index = lax.axis_index("dp")
        self.core = self.index % 2
        self.side = (self.index // 2) % 2
        self.depth = self.index // 4
        self.fast = self.count == 16

    def swap_core(self, x):
        return lax.ppermute(x, "dp", [(i, i ^ 1) for i in range(self.count)])

    def swap_side(self, x):
        return lax.ppermute(x, "dp", [(i, i ^ 2) for i in range(self.count)])

    def shift_depth(self, x, step):
        return lax.ppermute(
            x, "dp", [(i, (i + 4 * step) % self.count) for i in range(self.count)]
        )

    def gather(self, zero_half, one_half):
        if not self.fast:
            zero_all = lax.all_gather(zero_half, "dp", axis=0, tiled=True)
            one_all = lax.all_gather(one_half, "dp", axis=0, tiled=True)
            return pick(self.core, zero_all, one_all), pick(self.core, one_all, zero_all)
        rows, width = zero_half.shape
        mine = pick(self.core, zero_half, one_half)
        arrived = self.swap_core(pick(self.core, one_half, zero_half))
        block = pick(
            self.core,
            jnp.concatenate([mine, arrived], 0),
            jnp.concatenate([arrived, mine], 0),
        )
        whole = jnp.zeros((rows * self.count, width), zero_half.dtype)
        here = block
        for step in range(4):
            place = ((self.depth - step) % 4) * 2
            across = self.swap_side(here)
            whole = lax.dynamic_update_slice(whole, here, ((place + self.side) * 2 * rows, 0))
            whole = lax.dynamic_update_slice(
                whole, across, ((place + 1 - self.side) * 2 * rows, 0)
            )
            if step < 3:
                here = self.shift_depth(here, 1)
        return whole, self.swap_core(whole)

    def scatter(self, own_half, other_half):
        own_half = own_half.astype(low)
        other_half = other_half.astype(low)
        if not self.fast:
            halves = (pick(self.core, own_half, other_half), pick(self.core, other_half, own_half))
            return jnp.concatenate(
                [
                    lax.psum_scatter(half, "dp", scatter_dimension=0, tiled=True)
                    for half in halves
                ],
                axis=1,
            ).astype(full)
        rows = own_half.shape[0] // self.count
        width = own_half.shape[1]
        pair = own_half.astype(full) + self.swap_core(other_half).astype(full)
        pair = pair.astype(low).reshape(4, 2, 2 * rows, width)
        keep = lax.dynamic_index_in_dim(pair, self.side, 1, False)
        send = lax.dynamic_index_in_dim(pair, 1 - self.side, 1, False)
        quad = (keep.astype(full) + self.swap_side(send).astype(full)).astype(low)
        total = lax.dynamic_index_in_dim(quad, self.depth, 0, False).astype(full)
        for step in range(1, 4):
            send = lax.dynamic_index_in_dim(quad, (self.depth + step) % 4, 0, False)
            total = total + self.shift_depth(send, step).astype(full)
        total = total.reshape(2, rows, width)
        mine = lax.dynamic_index_in_dim(total, self.core, 0, False)
        arrived = self.swap_core(lax.dynamic_index_in_dim(total, 1 - self.core, 0, False))
        return pick(
            self.core,
            jnp.concatenate([mine, arrived], 1),
            jnp.concatenate([arrived, mine], 1),
        )

    def total(self, x):
        if not self.fast:
            return lax.psum(x, "dp")
        x = x + self.swap_core(x)
        x = x + self.swap_side(x)
        return x + sum(self.shift_depth(x, step) for step in range(1, 4))


def swap_group(x):
    return lax.ppermute(x, "mp", [(0, 1), (1, 0)])


def norm_rows(inputs):
    center = inputs - jnp.mean(inputs, -1, keepdims=True)
    scale = lax.rsqrt(jnp.mean(center * center, -1, keepdims=True) + 1e-05)
    return center * scale, scale


def norm_back(inner, unit, scale):
    return scale * (
        inner
        - jnp.mean(inner, -1, keepdims=True)
        - unit * jnp.mean(inner * unit, -1, keepdims=True)
    )


def gelu_parts(raised):
    cumulative = 0.5 * (1.0 + lax.erf(raised * 0.7071067811865476))
    slope = cumulative + raised * jnp.exp(-0.5 * raised * raised) * 0.3989422804014327
    return raised * cumulative, slope


def local(
    captions,
    image_cache,
    send_order,
    arrive_order,
    counts,
    keep_mask,
    end_pos,
    w_qkv,
    w_out,
    w_up,
    w_down,
    w_proj,
    ln1_gain,
    ln2_gain,
):
    plane = Plane()
    core = plane.core
    group = lax.axis_index("mp")
    spread = plane.count
    rows_dev, length, width = captions.shape
    rows = w_out.shape[0]
    per_peer = rows_dev // spread
    heads_half = w_qkv.shape[2] // HEAD // 2
    half_width = heads_half * HEAD

    mix = (w_qkv.astype(full) * ln1_gain[:, None, None]).astype(low)
    raise_low = (w_up.astype(full) * ln2_gain[:, None]).astype(low)

    def mix_half(half):
        part = mix[:, :, half * half_width : (half + 1) * half_width]
        return jnp.concatenate([part[:, 1], part[:, 2], part[:, 0]], axis=1)

    def columns(w, half):
        wide = w.shape[1] // 2
        return w[:, half * wide : (half + 1) * wide]

    proj_here = lax.dynamic_slice_in_dim(w_proj, group * (width // 2), width // 2, 1)
    mixes = plane.gather(mix_half(0), mix_half(1))
    second = plane.gather(
        *[jnp.concatenate([columns(raise_low, h), columns(w_out, h)], 1) for h in range(2)]
    )
    third = plane.gather(
        *[jnp.concatenate([columns(w_down, h), columns(proj_here, h)], 1) for h in range(2)]
    )
    hidden = w_up.shape[1] // 2
    ups = [w[:, :hidden] for w in second]
    backs = [w[:, hidden:] for w in second]
    lowers = [w[:, :hidden] for w in third]
    embed_half = jnp.concatenate(
        [
            pick(core, third[0][:, hidden:], third[1][:, hidden:]),
            pick(core, third[1][:, hidden:], third[0][:, hidden:]),
        ],
        1,
    )
    embed_far_own = swap_group(third[0][:, hidden:])
    embed_far_other = plane.swap_core(embed_far_own)
    embed_far = jnp.concatenate(
        [
            pick(core, embed_far_own, embed_far_other),
            pick(core, embed_far_other, embed_far_own),
        ],
        1,
    )
    w_embed = jnp.concatenate(
        [pick(group, embed_half, embed_far), pick(group, embed_far, embed_half)], 1
    )
    far_own = swap_group(mixes[0])
    far_mixes = (far_own, plane.swap_core(far_own))

    cached = image_cache.astype(full)
    cached = (cached * lax.rsqrt(jnp.sum(cached * cached, -1, keepdims=True) + 1e-06)).astype(low)
    places = jnp.arange(rows_dev, dtype=jnp.int32)
    hand_out = (send_order[0][:, None] == places[None, :]).astype(low)
    outgoing = mm(hand_out, cached).astype(low).reshape(spread, per_peer, width)
    incoming = lax.all_to_all(outgoing, "dp", split_axis=0, concat_axis=0, tiled=True)
    own_arrive = lax.dynamic_slice_in_dim(arrive_order[0], group * CAP_DEV, CAP_DEV, 0)
    take_in = (own_arrive[:, None] == places[None, :]).astype(low)
    pictures = mm(take_in, incoming.reshape(rows_dev, width)).astype(low)
    picture_halves = plane.gather(pictures[:, : width // 2], pictures[:, width // 2 :])
    pictures_all = jnp.concatenate(
        [pick(core, *picture_halves), pick(core, picture_halves[1], picture_halves[0])], 1
    )

    stream = captions.astype(full)
    unit_first, scale_first = norm_rows(stream)
    unit_low = unit_first.astype(low)
    picker = jnp.arange(length, dtype=jnp.int32)[None, :] == end_pos[:, None]
    at_end = picker[:, :, None].astype(full)
    stream_end = jnp.sum(stream * at_end, 1)
    unit_end = jnp.sum(unit_low.astype(full) * at_end, 1).astype(low)
    unit_rows = unit_low.reshape(rows_dev * length, width)
    allowed_keys = jnp.arange(length, dtype=jnp.int32)[None, :, None] <= end_pos[:, None, None]
    block_ones = (
        jnp.arange(half_width, dtype=jnp.int32)[:, None] // HEAD
        == jnp.arange(heads_half, dtype=jnp.int32)[None, :]
    )

    def head_sum(products):
        flat = products.reshape(rows_dev * length, half_width)
        out = lax.dot_general(
            flat,
            block_ones.astype(full),
            (((1,), (0,)), ((), ())),
            precision=lax.Precision.HIGHEST,
            preferred_element_type=full,
        )
        return out.reshape(rows_dev, length, heads_half)

    def head_spread(small):
        flat = small.reshape(rows_dev * length, heads_half)
        return mm_nt(flat, block_ones.astype(low)).reshape(rows_dev, length, half_width)

    kept = []
    attention_part = 0.0
    for half in range(2):
        w_mix = mixes[half]
        mixed = mm(unit_rows, w_mix[:, : 2 * half_width]).astype(low)
        mixed = mixed.reshape(rows_dev, length, 2 * half_width)
        keys = mixed[:, :, :half_width]
        values = mixed[:, :, half_width:]
        queries = mm(unit_end, w_mix[:, 2 * half_width :]).astype(low)
        scores = head_sum(keys.astype(full) * queries.astype(full)[:, None, :]) * SCORE_SCALE
        scores = jnp.where(allowed_keys, scores, -1e30)
        weight = jnp.exp(scores - jnp.max(scores, 1, keepdims=True))
        probs = weight / jnp.sum(weight, 1, keepdims=True)
        probs_low = probs.astype(low)
        attended = jnp.sum(head_spread(probs_low) * values.astype(full), 1).astype(low)
        attention_part = attention_part + mm_nt(attended, backs[half])
        kept.append((keys, values, queries, probs, probs_low, attended))

    attention_low = attention_part.astype(low)
    attention = attention_low.astype(full) + swap_group(attention_low).astype(full)
    middle = stream_end + attention
    unit_second, scale_second = norm_rows(middle)
    second_low = unit_second.astype(low)
    lowered = 0.0
    raised_kept = []
    for half in range(2):
        raised = mm(second_low, ups[half])
        active, slope = gelu_parts(raised)
        active = active.astype(low)
        raised_kept.append((active, slope))
        lowered = lowered + mm_nt(active, lowers[half])
    lowered_low = lowered.astype(low)

    def own_rows(x):
        return lax.dynamic_slice_in_dim(x, group * CAP_DEV, CAP_DEV, 0)

    def far_rows(x):
        return lax.dynamic_slice_in_dim(x, (1 - group) * CAP_DEV, CAP_DEV, 0)

    def both_rows(own):
        far = swap_group(own)
        return pick(
            group, jnp.concatenate([own, far], 0), jnp.concatenate([far, own], 0)
        )

    feed = own_rows(lowered_low).astype(full) + swap_group(far_rows(lowered_low)).astype(full)
    pooled = (own_rows(middle) + feed).astype(low)
    embedding = mm(pooled, w_embed)
    inverse = lax.rsqrt(jnp.sum(embedding * embedding, -1, keepdims=True) + 1e-06)
    unit_text = embedding * inverse
    text_low = unit_text.astype(low)

    keep_rows = keep_mask.reshape(spread, MICRO, CAP_DEV) == 1
    filled = jnp.arange(CAP_DEV, dtype=jnp.int32)[None, None, :] < counts[:, :, None]
    valid = keep_rows & filled
    total_valid = jnp.sum(valid.astype(full))
    batch_valid = lax.dynamic_index_in_dim(valid, group, 1, False)
    own_valid = lax.dynamic_index_in_dim(batch_valid, plane.index, 0, False)
    batch_valid = batch_valid.reshape(-1)
    sims = LOGIT_SCALE * mm_nt(text_low, pictures_all)
    allowed = own_valid[:, None] & batch_valid[None, :]
    weight = jnp.where(allowed, jnp.exp(sims), 0.0)
    row_sum = jnp.sum(weight, 1)
    slot = plane.index * CAP_DEV + jnp.arange(CAP_DEV, dtype=jnp.int32)
    target = (
        jnp.arange(spread * CAP_DEV, dtype=jnp.int32)[None, :] == slot[:, None]
    ) & own_valid[:, None]
    row_safe = jnp.where(own_valid, row_sum, 1.0)
    row_part = 0.5 * jnp.sum(jnp.log(row_safe)) - jnp.sum(jnp.where(target, sims, 0.0))
    col_part = jnp.sum(weight, 0)
    packed = jnp.concatenate([col_part, jnp.full((128,), 1.0 / 128, full) * row_part])
    packed = plane.total(packed.reshape(-1, 128)).reshape(-1)
    col_sum = packed[: spread * CAP_DEV]
    col_safe = jnp.where(batch_valid, col_sum, 1.0)
    objective = jnp.sum(packed[spread * CAP_DEV :]) + 0.5 * jnp.sum(jnp.log(col_safe))
    objective = jnp.full((8, 128), objective)
    loss = (objective + swap_group(objective))[0, 0] / total_valid
    d_sims = (
        weight * (0.5 / row_safe[:, None] + 0.5 / col_safe[None, :]) - target.astype(full)
    ).astype(low)
    d_unit = LOGIT_SCALE * mm(d_sims, pictures_all)
    d_embed = (
        (d_unit - unit_text * jnp.sum(unit_text * d_unit, -1, keepdims=True)) * inverse
    ).astype(low)

    pooled_all = both_rows(pooled)
    d_embed_all = both_rows(d_embed)
    d_embed_here = lax.dynamic_slice_in_dim(d_embed_all, group * (width // 2), width // 2, 1)
    g_embed = [
        mm_tn(
            pooled_all,
            lax.dynamic_slice_in_dim(d_embed_here, side * (width // 4), width // 4, 1),
        ).astype(low)
        for side in (core, 1 - core)
    ]
    d_pooled = mm_nt(d_embed_all, w_embed)
    d_out_low = d_pooled.astype(low)
    g_lower = []
    g_raise = []
    d_second = 0.0
    for half in range(2):
        active, slope = raised_kept[half]
        g_lower.append(mm_tn(d_out_low, active).astype(low))
        d_raised = (mm(d_out_low, lowers[half]) * slope).astype(low)
        g_raise.append(mm_tn(second_low, d_raised).astype(low))
        d_second = d_second + mm_nt(d_raised, ups[half])
    lower_sum = plane.scatter(
        *[jnp.concatenate([g_lower[half], g_embed[half]], 1) for half in range(2)]
    )
    raise_sum = plane.scatter(*g_raise)
    d_second_low = d_second.astype(low)
    inner = d_second_low.astype(full) + swap_group(d_second_low).astype(full)
    d_middle = d_pooled + norm_back(inner, unit_second, scale_second)
    d_middle_low = d_middle.astype(low)
    g_mix = []
    sends = []
    pairs = []
    for half in range(2):
        keys, values, queries, probs, probs_low, attended = kept[half]
        g_back = mm_tn(d_middle_low, attended).astype(low)
        d_attended = mm(d_middle_low, backs[half]).astype(low)
        d_probs = head_sum(values.astype(full) * d_attended.astype(full)[:, None, :])
        d_scores = probs * (d_probs - jnp.sum(probs * d_probs, 1, keepdims=True))
        d_scores = (d_scores * SCORE_SCALE).astype(low)
        score_wide = head_spread(d_scores)
        d_queries = jnp.sum(score_wide * keys.astype(full), 1).astype(low)
        d_keys = (score_wide * queries.astype(full)[:, None, :]).astype(low)
        d_values = (head_spread(probs_low) * d_attended.astype(full)[:, None, :]).astype(low)
        d_mixed = jnp.concatenate([d_keys, d_values], 2).reshape(rows_dev * length, -1)
        pairs.append((d_mixed, d_queries))
        g_mix.append(
            jnp.concatenate(
                [
                    mm_tn(unit_rows, d_mixed).astype(low),
                    mm_tn(unit_end, d_queries).astype(low),
                    g_back,
                ],
                1,
            )
        )
        sends.append(
            jnp.concatenate(
                [
                    queries,
                    d_attended,
                    d_queries,
                    probs_low.reshape(rows_dev, -1),
                    d_scores.reshape(rows_dev, -1),
                ],
                1,
            )
        )
    mix_sum = plane.scatter(*g_mix)
    arrived = swap_group(jnp.concatenate(sends, 1))
    far_width = arrived.shape[1] // 2
    small = length * heads_half
    for half in range(2):
        part = arrived[:, half * far_width : (half + 1) * far_width]
        queries = part[:, :half_width]
        d_attended = part[:, half_width : 2 * half_width]
        d_queries = part[:, 2 * half_width : 3 * half_width]
        probs_low = part[:, 3 * half_width : 3 * half_width + small]
        d_scores = part[:, 3 * half_width + small :]
        probs_low = probs_low.reshape(rows_dev, length, heads_half)
        d_scores = d_scores.reshape(rows_dev, length, heads_half)
        d_keys = (head_spread(d_scores) * queries.astype(full)[:, None, :]).astype(low)
        d_values = (head_spread(probs_low) * d_attended.astype(full)[:, None, :]).astype(low)
        d_mixed = jnp.concatenate([d_keys, d_values], 2).reshape(rows_dev * length, -1)
        pairs.append((d_mixed, d_queries))
    inner = 0.0
    inner_end = 0.0
    for (d_mixed, d_queries), w_mix in zip(pairs, (*mixes, *far_mixes)):
        inner = inner + mm_nt(d_mixed, w_mix[:, : 2 * half_width])
        inner_end = inner_end + mm_nt(d_queries, w_mix[:, 2 * half_width :])
    inner = inner.reshape(rows_dev, length, width) + at_end * inner_end[:, None, :]
    grad_captions = at_end * d_middle[:, None, :] + norm_back(inner, unit_first, scale_first)

    down_cols = lower_sum.reshape(rows, 2, hidden + width // 4)
    grad_down = down_cols[:, :, :hidden].reshape(rows, 2 * hidden)
    proj_own = down_cols[:, :, hidden:].reshape(rows, width // 2)
    proj_far = swap_group(proj_own)
    grad_proj = pick(
        group,
        jnp.concatenate([proj_own, proj_far], 1),
        jnp.concatenate([proj_far, proj_own], 1),
    )
    mix_cols = mix_sum.reshape(rows, 2, 4, half_width)
    grad_out = mix_cols[:, :, 3].reshape(rows, 2 * half_width)
    unit_mix = mix_cols[:, :, jnp.array([2, 0, 1])].transpose(0, 2, 1, 3)
    unit_mix = unit_mix.reshape(rows, 3, 2 * half_width)
    grad_qkv = unit_mix * ln1_gain[:, None, None]
    grad_up = raise_sum * ln2_gain[:, None]
    gains = jnp.stack(
        [
            jnp.sum(unit_mix * w_qkv.astype(full), (1, 2)),
            jnp.sum(raise_sum * w_up.astype(full), 1),
        ]
    )
    gains = gains + swap_group(gains)
    return (
        loss,
        grad_captions,
        grad_qkv,
        grad_out,
        grad_up,
        grad_down,
        grad_proj,
        gains[0],
        gains[1],
    )


def solution(mesh):
    return jax.shard_map(
        local,
        mesh=mesh,
        in_specs=(
            P("dp", None, None),
            P("dp", None),
            P("dp", None),
            P("dp", None),
            P(),
            P(),
            P("dp"),
            P("dp", None, "mp"),
            P("dp", "mp"),
            P("dp", "mp"),
            P("dp", "mp"),
            P("dp", None),
            P("dp"),
            P("dp"),
        ),
        out_specs=(
            P(),
            P("dp", None, None),
            P("dp", None, "mp"),
            P("dp", "mp"),
            P("dp", "mp"),
            P("dp", "mp"),
            P("dp", None),
            P("dp"),
            P("dp"),
        ),
        check_vma=False,
    )
```

```python
import math

import jax
import jax.numpy as jnp
from jax import lax
from jax.sharding import PartitionSpec as P

HEAD = 64
MICRO = 2
CAP_DEV = 64
LOGIT_SCALE = 40.0
SCORE_SCALE = 1.0 / math.sqrt(HEAD)

low = jnp.bfloat16
full = jnp.float32


def mm(a, b):
    return lax.dot_general(a, b, (((1,), (0,)), ((), ())), preferred_element_type=full)


def mm_nt(a, b):
    return lax.dot_general(a, b, (((1,), (1,)), ((), ())), preferred_element_type=full)


def mm_tn(a, b):
    return lax.dot_general(a, b, (((0,), (0,)), ((), ())), preferred_element_type=full)


def pick(flag, when_zero, when_one):
    return jnp.where(flag == 0, when_zero, when_one)


class Plane:
    def __init__(self):
        self.count = lax.axis_size("dp")
        self.index = lax.axis_index("dp")
        self.core = self.index % 2
        self.side = (self.index // 2) % 2
        self.depth = self.index // 4
        self.fast = self.count == 16

    def swap_core(self, x):
        return lax.ppermute(x, "dp", [(i, i ^ 1) for i in range(self.count)])

    def swap_side(self, x):
        return lax.ppermute(x, "dp", [(i, i ^ 2) for i in range(self.count)])

    def shift_depth(self, x, step):
        return lax.ppermute(
            x, "dp", [(i, (i + 4 * step) % self.count) for i in range(self.count)]
        )

    def gather(self, zero_half, one_half):
        if not self.fast:
            zero_all = lax.all_gather(zero_half, "dp", axis=0, tiled=True)
            one_all = lax.all_gather(one_half, "dp", axis=0, tiled=True)
            return pick(self.core, zero_all, one_all), pick(self.core, one_all, zero_all)
        rows, width = zero_half.shape
        mine = pick(self.core, zero_half, one_half)
        arrived = self.swap_core(pick(self.core, one_half, zero_half))
        block = pick(
            self.core,
            jnp.concatenate([mine, arrived], 0),
            jnp.concatenate([arrived, mine], 0),
        )
        whole = jnp.zeros((self.count // 2, 2 * rows, width), zero_half.dtype)
        here = block
        for step in range(4):
            place = ((self.depth - step) % 4) * 2
            across = self.swap_side(here)
            whole = lax.dynamic_update_slice(whole, here[None], (place + self.side, 0, 0))
            whole = lax.dynamic_update_slice(
                whole, across[None], (place + 1 - self.side, 0, 0)
            )
            if step < 3:
                here = self.shift_depth(here, 1)
        whole = whole.reshape(rows * self.count, width)
        return whole, self.swap_core(whole)

    def scatter(self, own_half, other_half):
        own_half = own_half.astype(low)
        other_half = other_half.astype(low)
        if not self.fast:
            halves = (pick(self.core, own_half, other_half), pick(self.core, other_half, own_half))
            return jnp.concatenate(
                [
                    lax.psum_scatter(half, "dp", scatter_dimension=0, tiled=True)
                    for half in halves
                ],
                axis=1,
            ).astype(full)
        rows = own_half.shape[0] // self.count
        width = own_half.shape[1]
        pair = own_half.astype(full) + self.swap_core(other_half).astype(full)
        pair = pair.astype(low).reshape(4, 2, 2 * rows, width)
        keep = lax.dynamic_index_in_dim(pair, self.side, 1, False)
        send = lax.dynamic_index_in_dim(pair, 1 - self.side, 1, False)
        quad = (keep.astype(full) + self.swap_side(send).astype(full)).astype(low)
        total = lax.dynamic_index_in_dim(quad, self.depth, 0, False).astype(full)
        for step in range(1, 4):
            send = lax.dynamic_index_in_dim(quad, (self.depth + step) % 4, 0, False)
            total = total + self.shift_depth(send, step).astype(full)
        total = total.reshape(2, rows, width)
        mine = lax.dynamic_index_in_dim(total, self.core, 0, False)
        arrived = self.swap_core(lax.dynamic_index_in_dim(total, 1 - self.core, 0, False))
        return pick(
            self.core,
            jnp.concatenate([mine, arrived], 1),
            jnp.concatenate([arrived, mine], 1),
        )

    def total(self, x):
        if not self.fast:
            return lax.psum(x, "dp")
        x = x + self.swap_core(x)
        x = x + self.swap_side(x)
        return x + sum(self.shift_depth(x, step) for step in range(1, 4))


def swap_group(x):
    return lax.ppermute(x, "mp", [(0, 1), (1, 0)])


def norm_rows(inputs):
    center = inputs - jnp.mean(inputs, -1, keepdims=True)
    scale = lax.rsqrt(jnp.mean(center * center, -1, keepdims=True) + 1e-05)
    return center * scale, scale


def norm_back(inner, unit, scale):
    return scale * (
        inner
        - jnp.mean(inner, -1, keepdims=True)
        - unit * jnp.mean(inner * unit, -1, keepdims=True)
    )


def gelu_parts(raised):
    cumulative = 0.5 * (1.0 + lax.erf(raised * 0.7071067811865476))
    slope = cumulative + raised * jnp.exp(-0.5 * raised * raised) * 0.3989422804014327
    return raised * cumulative, slope


def local(
    captions,
    image_cache,
    send_order,
    arrive_order,
    counts,
    keep_mask,
    end_pos,
    w_qkv,
    w_out,
    w_up,
    w_down,
    w_proj,
    ln1_gain,
    ln2_gain,
):
    plane = Plane()
    core = plane.core
    group = lax.axis_index("mp")
    spread = plane.count
    rows_dev, length, width = captions.shape
    rows = w_out.shape[0]
    per_peer = rows_dev // spread
    heads_half = w_qkv.shape[2] // HEAD // 2
    half_width = heads_half * HEAD

    mix = (w_qkv.astype(full) * ln1_gain[:, None, None]).astype(low)
    raise_low = (w_up.astype(full) * ln2_gain[:, None]).astype(low)

    def mix_half(half):
        part = mix[:, :, half * half_width : (half + 1) * half_width]
        return jnp.concatenate([part[:, 1], part[:, 2], part[:, 0]], axis=1)

    def columns(w, half):
        wide = w.shape[1] // 2
        return w[:, half * wide : (half + 1) * wide]

    proj_here = lax.dynamic_slice_in_dim(w_proj, group * (width // 2), width // 2, 1)
    mixes = plane.gather(mix_half(0), mix_half(1))
    second = plane.gather(
        *[jnp.concatenate([columns(raise_low, h), columns(w_out, h)], 1) for h in range(2)]
    )
    third = plane.gather(
        *[jnp.concatenate([columns(w_down, h), columns(proj_here, h)], 1) for h in range(2)]
    )
    hidden = w_up.shape[1] // 2
    ups = [w[:, :hidden] for w in second]
    backs = [w[:, hidden:] for w in second]
    lowers = [w[:, :hidden] for w in third]
    embed_half = jnp.concatenate(
        [
            pick(core, third[0][:, hidden:], third[1][:, hidden:]),
            pick(core, third[1][:, hidden:], third[0][:, hidden:]),
        ],
        1,
    )
    embed_far_own = swap_group(third[0][:, hidden:])
    embed_far_other = plane.swap_core(embed_far_own)
    embed_far = jnp.concatenate(
        [
            pick(core, embed_far_own, embed_far_other),
            pick(core, embed_far_other, embed_far_own),
        ],
        1,
    )
    w_embed = jnp.concatenate(
        [pick(group, embed_half, embed_far), pick(group, embed_far, embed_half)], 1
    )
    far_own = swap_group(mixes[0])
    far_mixes = (far_own, plane.swap_core(far_own))

    cached = image_cache.astype(full)
    cached = (cached * lax.rsqrt(jnp.sum(cached * cached, -1, keepdims=True) + 1e-06)).astype(low)
    places = jnp.arange(rows_dev, dtype=jnp.int32)
    hand_out = (send_order[0][:, None] == places[None, :]).astype(low)
    outgoing = mm(hand_out, cached).astype(low).reshape(spread, per_peer, width)
    incoming = lax.all_to_all(outgoing, "dp", split_axis=0, concat_axis=0, tiled=True)
    own_arrive = lax.dynamic_slice_in_dim(arrive_order[0], group * CAP_DEV, CAP_DEV, 0)
    take_in = (own_arrive[:, None] == places[None, :]).astype(low)
    pictures = mm(take_in, incoming.reshape(rows_dev, width)).astype(low)
    picture_halves = plane.gather(pictures[:, : width // 2], pictures[:, width // 2 :])
    pictures_all = jnp.concatenate(
        [pick(core, *picture_halves), pick(core, picture_halves[1], picture_halves[0])], 1
    )

    stream = captions.astype(full)
    unit_first, scale_first = norm_rows(stream)
    unit_low = unit_first.astype(low)
    picker = jnp.arange(length, dtype=jnp.int32)[None, :] == end_pos[:, None]
    at_end = picker[:, :, None].astype(full)
    stream_end = jnp.sum(stream * at_end, 1)
    unit_end = jnp.sum(unit_low.astype(full) * at_end, 1).astype(low)
    unit_rows = unit_low.reshape(rows_dev * length, width)
    allowed_keys = jnp.arange(length, dtype=jnp.int32)[None, :, None] <= end_pos[:, None, None]
    block_ones = (
        jnp.arange(half_width, dtype=jnp.int32)[:, None] // HEAD
        == jnp.arange(heads_half, dtype=jnp.int32)[None, :]
    )

    def head_sum(products):
        flat = products.reshape(rows_dev * length, half_width)
        out = lax.dot_general(
            flat,
            block_ones.astype(full),
            (((1,), (0,)), ((), ())),
            precision=lax.Precision.HIGHEST,
            preferred_element_type=full,
        )
        return out.reshape(rows_dev, length, heads_half)

    def head_spread(small):
        flat = small.reshape(rows_dev * length, heads_half)
        return mm_nt(flat, block_ones.astype(low)).reshape(rows_dev, length, half_width)

    kept = []
    attention_part = 0.0
    for half in range(2):
        w_mix = mixes[half]
        mixed = mm(unit_rows, w_mix[:, : 2 * half_width]).astype(low)
        mixed = mixed.reshape(rows_dev, length, 2 * half_width)
        keys = mixed[:, :, :half_width]
        values = mixed[:, :, half_width:]
        queries = mm(unit_end, w_mix[:, 2 * half_width :]).astype(low)
        scores = head_sum(keys.astype(full) * queries.astype(full)[:, None, :]) * SCORE_SCALE
        scores = jnp.where(allowed_keys, scores, -1e30)
        weight = jnp.exp(scores - jnp.max(scores, 1, keepdims=True))
        probs = weight / jnp.sum(weight, 1, keepdims=True)
        probs_low = probs.astype(low)
        attended = jnp.sum(head_spread(probs_low) * values.astype(full), 1).astype(low)
        attention_part = attention_part + mm_nt(attended, backs[half])
        kept.append((keys, values, queries, probs, probs_low, attended))

    attention_low = attention_part.astype(low)
    attention = attention_low.astype(full) + swap_group(attention_low).astype(full)
    middle = stream_end + attention
    unit_second, scale_second = norm_rows(middle)
    second_low = unit_second.astype(low)
    lowered = 0.0
    raised_kept = []
    for half in range(2):
        raised = mm(second_low, ups[half])
        active, slope = gelu_parts(raised)
        active = active.astype(low)
        raised_kept.append((active, slope))
        lowered = lowered + mm_nt(active, lowers[half])
    lowered_low = lowered.astype(low)

    def own_rows(x):
        return lax.dynamic_slice_in_dim(x, group * CAP_DEV, CAP_DEV, 0)

    def far_rows(x):
        return lax.dynamic_slice_in_dim(x, (1 - group) * CAP_DEV, CAP_DEV, 0)

    def both_rows(own):
        far = swap_group(own)
        return pick(
            group, jnp.concatenate([own, far], 0), jnp.concatenate([far, own], 0)
        )

    feed = own_rows(lowered_low).astype(full) + swap_group(far_rows(lowered_low)).astype(full)
    pooled = (own_rows(middle) + feed).astype(low)
    embedding = mm(pooled, w_embed)
    inverse = lax.rsqrt(jnp.sum(embedding * embedding, -1, keepdims=True) + 1e-06)
    unit_text = embedding * inverse
    text_low = unit_text.astype(low)

    keep_rows = keep_mask.reshape(spread, MICRO, CAP_DEV) == 1
    filled = jnp.arange(CAP_DEV, dtype=jnp.int32)[None, None, :] < counts[:, :, None]
    valid = keep_rows & filled
    total_valid = jnp.sum(valid.astype(full))
    batch_valid = lax.dynamic_index_in_dim(valid, group, 1, False)
    own_valid = lax.dynamic_index_in_dim(batch_valid, plane.index, 0, False)
    batch_valid = batch_valid.reshape(-1)
    sims = LOGIT_SCALE * mm_nt(text_low, pictures_all)
    allowed = own_valid[:, None] & batch_valid[None, :]
    weight = jnp.where(allowed, jnp.exp(sims), 0.0)
    row_sum = jnp.sum(weight, 1)
    slot = plane.index * CAP_DEV + jnp.arange(CAP_DEV, dtype=jnp.int32)
    target = (
        jnp.arange(spread * CAP_DEV, dtype=jnp.int32)[None, :] == slot[:, None]
    ) & own_valid[:, None]
    row_safe = jnp.where(own_valid, row_sum, 1.0)
    row_part = 0.5 * jnp.sum(jnp.log(row_safe)) - jnp.sum(jnp.where(target, sims, 0.0))
    col_part = jnp.sum(weight, 0)
    packed = jnp.concatenate([col_part, jnp.full((128,), 1.0 / 128, full) * row_part])
    packed = plane.total(packed.reshape(-1, 128)).reshape(-1)
    col_sum = packed[: spread * CAP_DEV]
    col_safe = jnp.where(batch_valid, col_sum, 1.0)
    objective = jnp.sum(packed[spread * CAP_DEV :]) + 0.5 * jnp.sum(jnp.log(col_safe))
    objective = jnp.full((8, 128), objective)
    loss = (objective + swap_group(objective))[0, 0] / total_valid
    d_sims = (
        weight * (0.5 / row_safe[:, None] + 0.5 / col_safe[None, :]) - target.astype(full)
    ).astype(low)
    d_unit = LOGIT_SCALE * mm(d_sims, pictures_all)
    d_embed = (
        (d_unit - unit_text * jnp.sum(unit_text * d_unit, -1, keepdims=True)) * inverse
    ).astype(low)

    pooled_all = both_rows(pooled)
    d_embed_all = both_rows(d_embed)
    d_embed_here = lax.dynamic_slice_in_dim(d_embed_all, group * (width // 2), width // 2, 1)
    g_embed = [
        mm_tn(
            pooled_all,
            lax.dynamic_slice_in_dim(d_embed_here, side * (width // 4), width // 4, 1),
        ).astype(low)
        for side in (core, 1 - core)
    ]
    d_pooled = mm_nt(d_embed_all, w_embed)
    d_out_low = d_pooled.astype(low)
    g_lower = []
    g_raise = []
    d_second = 0.0
    for half in range(2):
        active, slope = raised_kept[half]
        g_lower.append(mm_tn(d_out_low, active).astype(low))
        d_raised = (mm(d_out_low, lowers[half]) * slope).astype(low)
        g_raise.append(mm_tn(second_low, d_raised).astype(low))
        d_second = d_second + mm_nt(d_raised, ups[half])
    lower_sum = plane.scatter(
        *[jnp.concatenate([g_lower[half], g_embed[half]], 1) for half in range(2)]
    )
    raise_sum = plane.scatter(*g_raise)
    d_second_low = d_second.astype(low)
    inner = d_second_low.astype(full) + swap_group(d_second_low).astype(full)
    d_middle = d_pooled + norm_back(inner, unit_second, scale_second)
    d_middle_low = d_middle.astype(low)
    g_mix = []
    sends = []
    pairs = []
    for half in range(2):
        keys, values, queries, probs, probs_low, attended = kept[half]
        g_back = mm_tn(d_middle_low, attended).astype(low)
        d_attended = mm(d_middle_low, backs[half]).astype(low)
        d_probs = head_sum(values.astype(full) * d_attended.astype(full)[:, None, :])
        d_scores = probs * (d_probs - jnp.sum(probs * d_probs, 1, keepdims=True))
        d_scores = (d_scores * SCORE_SCALE).astype(low)
        score_wide = head_spread(d_scores)
        d_queries = jnp.sum(score_wide * keys.astype(full), 1).astype(low)
        d_keys = (score_wide * queries.astype(full)[:, None, :]).astype(low)
        d_values = (head_spread(probs_low) * d_attended.astype(full)[:, None, :]).astype(low)
        d_mixed = jnp.concatenate([d_keys, d_values], 2).reshape(rows_dev * length, -1)
        pairs.append((d_mixed, d_queries))
        g_mix.append(
            jnp.concatenate(
                [
                    mm_tn(unit_rows, d_mixed).astype(low),
                    mm_tn(unit_end, d_queries).astype(low),
                    g_back,
                ],
                1,
            )
        )
        sends.append(
            jnp.concatenate(
                [
                    queries,
                    d_attended,
                    d_queries,
                    probs_low.reshape(rows_dev, -1),
                    d_scores.reshape(rows_dev, -1),
                ],
                1,
            )
        )
    mix_sum = plane.scatter(*g_mix)
    arrived = swap_group(jnp.concatenate(sends, 1))
    far_width = arrived.shape[1] // 2
    small = length * heads_half
    for half in range(2):
        part = arrived[:, half * far_width : (half + 1) * far_width]
        queries = part[:, :half_width]
        d_attended = part[:, half_width : 2 * half_width]
        d_queries = part[:, 2 * half_width : 3 * half_width]
        probs_low = part[:, 3 * half_width : 3 * half_width + small]
        d_scores = part[:, 3 * half_width + small :]
        probs_low = probs_low.reshape(rows_dev, length, heads_half)
        d_scores = d_scores.reshape(rows_dev, length, heads_half)
        d_keys = (head_spread(d_scores) * queries.astype(full)[:, None, :]).astype(low)
        d_values = (head_spread(probs_low) * d_attended.astype(full)[:, None, :]).astype(low)
        d_mixed = jnp.concatenate([d_keys, d_values], 2).reshape(rows_dev * length, -1)
        pairs.append((d_mixed, d_queries))
    inner = 0.0
    inner_end = 0.0
    for (d_mixed, d_queries), w_mix in zip(pairs, (*mixes, *far_mixes)):
        inner = inner + mm_nt(d_mixed, w_mix[:, : 2 * half_width])
        inner_end = inner_end + mm_nt(d_queries, w_mix[:, 2 * half_width :])
    inner = inner.reshape(rows_dev, length, width) + at_end * inner_end[:, None, :]
    grad_captions = at_end * d_middle[:, None, :] + norm_back(inner, unit_first, scale_first)

    down_cols = lower_sum.reshape(rows, 2, hidden + width // 4)
    grad_down = down_cols[:, :, :hidden].reshape(rows, 2 * hidden)
    proj_own = down_cols[:, :, hidden:].reshape(rows, width // 2)
    proj_far = swap_group(proj_own)
    grad_proj = pick(
        group,
        jnp.concatenate([proj_own, proj_far], 1),
        jnp.concatenate([proj_far, proj_own], 1),
    )
    mix_cols = mix_sum.reshape(rows, 2, 4, half_width)
    grad_out = mix_cols[:, :, 3].reshape(rows, 2 * half_width)
    unit_mix = mix_cols[:, :, jnp.array([2, 0, 1])].transpose(0, 2, 1, 3)
    unit_mix = unit_mix.reshape(rows, 3, 2 * half_width)
    grad_qkv = unit_mix * ln1_gain[:, None, None]
    grad_up = raise_sum * ln2_gain[:, None]
    gains = jnp.stack(
        [
            jnp.sum(unit_mix * w_qkv.astype(full), (1, 2)),
            jnp.sum(raise_sum * w_up.astype(full), 1),
        ]
    )
    gains = gains + swap_group(gains)
    return (
        loss,
        grad_captions,
        grad_qkv,
        grad_out,
        grad_up,
        grad_down,
        grad_proj,
        gains[0],
        gains[1],
    )


def solution(mesh):
    return jax.shard_map(
        local,
        mesh=mesh,
        in_specs=(
            P("dp", None, None),
            P("dp", None),
            P("dp", None),
            P("dp", None),
            P(),
            P(),
            P("dp"),
            P("dp", None, "mp"),
            P("dp", "mp"),
            P("dp", "mp"),
            P("dp", "mp"),
            P("dp", None),
            P("dp"),
            P("dp"),
        ),
        out_specs=(
            P(),
            P("dp", None, None),
            P("dp", None, "mp"),
            P("dp", "mp"),
            P("dp", "mp"),
            P("dp", "mp"),
            P("dp", None),
            P("dp"),
            P("dp"),
        ),
        check_vma=False,
    )
```

```python
import math

import jax
import jax.numpy as jnp
from jax import lax
from jax.experimental import pallas as pl
from jax.experimental.pallas import tpu as pltpu
from jax.sharding import PartitionSpec as P

HEAD = 64
MICRO = 2
CAP_DEV = 64
LOGIT_SCALE = 40.0
SCORE_SCALE = 1.0 / math.sqrt(HEAD)
LENGTH = 16
WIDTH = 768
HEADS_HERE = 6
COLS = HEADS_HERE * HEAD
BLOCK = 16
TOKENS = BLOCK * LENGTH
STACK = HEADS_HERE * BLOCK

low = jnp.bfloat16
full = jnp.float32


def mm(a, b):
    return lax.dot_general(a, b, (((1,), (0,)), ((), ())), preferred_element_type=full)


def mm_nt(a, b):
    return lax.dot_general(a, b, (((1,), (1,)), ((), ())), preferred_element_type=full)


def mm_tn(a, b):
    return lax.dot_general(a, b, (((0,), (0,)), ((), ())), preferred_element_type=full)


def pick(flag, when_zero, when_one):
    return jnp.where(flag == 0, when_zero, when_one)


class Plane:
    def __init__(self):
        self.count = lax.axis_size("dp")
        self.index = lax.axis_index("dp")
        self.core = self.index % 2
        self.side = (self.index // 2) % 2
        self.depth = self.index // 4
        self.fast = self.count == 16

    def swap_core(self, x):
        return lax.ppermute(x, "dp", [(i, i ^ 1) for i in range(self.count)])

    def swap_side(self, x):
        return lax.ppermute(x, "dp", [(i, i ^ 2) for i in range(self.count)])

    def shift_depth(self, x, step):
        return lax.ppermute(
            x, "dp", [(i, (i + 4 * step) % self.count) for i in range(self.count)]
        )

    def gather(self, mine, send, after=None):
        if not self.fast:
            zero_all = lax.all_gather(pick(self.core, mine, send), "dp", axis=0, tiled=True)
            one_all = lax.all_gather(pick(self.core, send, mine), "dp", axis=0, tiled=True)
            return pick(self.core, zero_all, one_all)
        rows, width = mine.shape
        arrived = self.swap_core(send)
        block = jnp.zeros((2, rows, width), mine.dtype)
        block = lax.dynamic_update_slice(block, mine[None], (self.core, 0, 0))
        block = lax.dynamic_update_slice(block, arrived[None], (1 - self.core, 0, 0))
        block = block.reshape(2 * rows, width)
        if after is not None:
            block, _ = lax.optimization_barrier((block, after))
        up = self.shift_depth(block, 1)
        down = self.shift_depth(block, -1)
        far = self.shift_depth(up, 1)
        self.last = up
        whole = jnp.zeros((self.count // 2, 2 * rows, width), mine.dtype)
        for step, here in ((0, block), (1, up), (-1, down), (2, far)):
            place = ((self.depth - step) % 4) * 2
            across = self.swap_side(here)
            whole = lax.dynamic_update_slice(whole, here[None], (place + self.side, 0, 0))
            whole = lax.dynamic_update_slice(
                whole, across[None], (place + 1 - self.side, 0, 0)
            )
        return whole.reshape(rows * self.count, width)

    def scatter(self, keep, send=None):
        if not self.fast:
            if send is None:
                send = jnp.zeros_like(keep)
            halves = (pick(self.core, keep, send), pick(self.core, send, keep))
            return [
                lax.psum_scatter(half, "dp", scatter_dimension=0, tiled=True).astype(full)
                for half in halves
            ]
        rows = keep.shape[0] // self.count
        width = keep.shape[1]
        pair = keep
        if send is not None:
            pair = (keep.astype(full) + self.swap_core(send).astype(full)).astype(low)
        pair = pair.reshape(4, 2, 2 * rows, width)
        stay = lax.dynamic_index_in_dim(pair, self.side, 1, False)
        leave = lax.dynamic_index_in_dim(pair, 1 - self.side, 1, False)
        quad_sum = (stay.astype(full) + self.swap_side(leave).astype(full)).astype(low)
        total = lax.dynamic_index_in_dim(quad_sum, self.depth, 0, False).astype(full)
        for step in range(1, 4):
            leave = lax.dynamic_index_in_dim(quad_sum, (self.depth + step) % 4, 0, False)
            total = total + self.shift_depth(leave, step).astype(full)
        total = total.reshape(2, rows, width)
        mine = lax.dynamic_index_in_dim(total, self.core, 0, False)
        arrived = self.swap_core(lax.dynamic_index_in_dim(total, 1 - self.core, 0, False))
        return pick(self.core, mine, arrived), pick(self.core, arrived, mine)

    def total(self, x):
        if not self.fast:
            return lax.psum(x, "dp")
        x = (x + self.swap_core(x)) + (self.swap_side(x) + self.swap_both(x))
        return x + sum(self.shift_depth(x, step) for step in range(1, 4))

    def swap_both(self, x):
        return lax.ppermute(x, "dp", [(i, i ^ 3) for i in range(self.count)])


def swap_near(x, flip):
    size = 2 * lax.axis_size("dp")
    return lax.ppermute(x, ("dp", "mp"), [(i, i ^ flip) for i in range(size)])


def swap_group(x):
    return swap_near(x, 1)


def roll_rows(x):
    half = x.shape[0] // 2
    return jnp.concatenate([x[half:], x[:half]], 0)


def norm_rows(inputs):
    center = inputs - jnp.mean(inputs, -1, keepdims=True)
    scale = lax.rsqrt(jnp.mean(center * center, -1, keepdims=True) + 1e-05)
    return center * scale, scale


def norm_back(inner, unit, scale):
    return scale * (
        inner
        - jnp.mean(inner, -1, keepdims=True)
        - unit * jnp.mean(inner * unit, -1, keepdims=True)
    )


def gelu_parts(raised):
    cumulative = 0.5 * (1.0 + lax.erf(raised * 0.7071067811865476))
    slope = cumulative + raised * jnp.exp(-0.5 * raised * raised) * 0.3989422804014327
    return raised * cumulative, slope


def whole_block(shape):
    return pl.BlockSpec(shape, lambda *_: (0,) * len(shape))


def shapes(*items):
    return [jax.ShapeDtypeStruct(shape, kind) for shape, kind in items]


def pack_body(core_ref, mix_ref, back_ref, raise_ref, lower_ref, embed_ref, g1_ref, g2_ref, *outs):
    first = core_ref[0] == 0
    g1 = g1_ref[...]
    g2 = g2_ref[...]

    def part(index):
        return (mix_ref[:, index, :].astype(full) * g1).astype(low)

    def put(index, columns, zero, one):
        outs[index][:, columns] = jnp.where(first, zero, one)
        outs[index + 1][:, columns] = jnp.where(first, one, zero)

    put(0, slice(0, COLS), part(1), part(2))
    put(0, slice(COLS, 2 * COLS), part(0), back_ref[...])
    hidden = raise_ref.shape[1] // 2
    raised = (raise_ref[...].astype(full) * g2).astype(low)
    put(2, slice(0, hidden), raised[:, :hidden], raised[:, hidden:])
    put(2, slice(hidden, 2 * hidden), lower_ref[:, :hidden], lower_ref[:, hidden:])
    put(4, slice(0, COLS), embed_ref[:, :COLS], embed_ref[:, COLS:])


def pack(core, w_qkv, w_out, w_up, w_down, w_proj, g1, g2):
    rows, hidden = w_up.shape
    vmem = pl.BlockSpec(memory_space=pltpu.VMEM)
    return pl.pallas_call(
        pack_body,
        out_shape=shapes(
            *[((rows, 2 * COLS), low)] * 2, *[((rows, hidden), low)] * 2, *[((rows, COLS), low)] * 2
        ),
        in_specs=[pl.BlockSpec(memory_space=pltpu.SMEM)] + [vmem] * 7,
        out_specs=[vmem] * 6,
        name="pack",
    )(core, w_qkv, w_out, w_up, w_down, w_proj, g1, g2)


def end_picks(ends, copies):
    ends = jnp.concatenate([ends] * copies, 0)
    shape = (copies * BLOCK, TOKENS)
    row = lax.broadcasted_iota(jnp.int32, shape, 0) & (BLOCK - 1)
    return lax.broadcasted_iota(jnp.int32, shape, 1) == row * LENGTH + ends


def norm_body(group_ref, x_ref, ends_ref, unit_ref, scale_ref, unit_end_ref, stream_end_ref):
    x = x_ref[...]
    stream = x.astype(full)
    center = stream - jnp.sum(stream, -1, keepdims=True) * (1.0 / WIDTH)
    scale = lax.rsqrt(jnp.sum(center * center, -1, keepdims=True) * (1.0 / WIDTH) + 1e-05)
    unit = (center * scale).astype(low)
    unit_ref[...] = unit
    scale_ref[...] = jnp.broadcast_to(scale, scale_ref.shape)
    picks = end_picks(ends_ref[...], 1).astype(low)
    unit_end_ref[...] = mm(picks, unit).astype(low)
    stream_end_ref[...] = mm(picks, x).astype(low)


def norm_first(group, x, ends):
    steps = ends.shape[0] // BLOCK
    return pl.pallas_call(
        norm_body,
        out_shape=shapes(
            (x.shape, low), ((x.shape[0], 128), full), *[((ends.shape[0], WIDTH), low)] * 2
        ),
        grid_spec=pltpu.PrefetchScalarGridSpec(
            num_scalar_prefetch=1,
            grid=(steps,),
            in_specs=[
                pl.BlockSpec((TOKENS, WIDTH), lambda i, g: ((i + g[0] * (steps // 2)) % steps, 0)),
                pl.BlockSpec((BLOCK, 1), lambda i, g: (i, 0)),
            ],
            out_specs=[
                pl.BlockSpec((TOKENS, WIDTH), lambda i, g: (i, 0)),
                pl.BlockSpec((TOKENS, 128), lambda i, g: (i, 0)),
                pl.BlockSpec((BLOCK, WIDTH), lambda i, g: (i, 0)),
                pl.BlockSpec((BLOCK, WIDTH), lambda i, g: (i, 0)),
            ],
        ),
        name="norm_first",
    )(group, x, ends)


def head_mask(head):
    return lax.broadcasted_iota(jnp.int32, (BLOCK, COLS), 1) // HEAD == head


def head_stack(x):
    zero = jnp.zeros_like(x)
    return jnp.concatenate([jnp.where(head_mask(h), x, zero) for h in range(HEADS_HERE)], 0)


def head_fold(x):
    out = jnp.zeros((BLOCK, COLS), full)
    for h in range(HEADS_HERE):
        out = jnp.where(head_mask(h), x[h * BLOCK : (h + 1) * BLOCK], out)
    return out


def stack_grid():
    row = lax.broadcasted_iota(jnp.int32, (STACK, TOKENS), 0) & (BLOCK - 1)
    token = lax.broadcasted_iota(jnp.int32, (STACK, TOKENS), 1)
    return row, token


def step_rows(i):
    return pl.ds(pl.multiple_of(i * BLOCK, BLOCK), BLOCK)


def attend_body(
    unit_ref, unit_end_ref, ends_ref, kq_ref, vo_ref, k_ref, v_ref, p_ref, q_ref, att_ref, out_ref
):
    i = pl.program_id(0)

    @pl.when(i == 0)
    def _():
        q_ref[...] = mm(unit_end_ref[...], kq_ref[:, COLS:]).astype(low)

    unit = unit_ref[...]
    keys = mm(unit, kq_ref[:, :COLS]).astype(low)
    values = mm(unit, vo_ref[:, :COLS]).astype(low)
    k_ref[...] = keys
    v_ref[...] = values
    scores = mm_nt(head_stack(q_ref[step_rows(i), :]), keys) * SCORE_SCALE
    row, token = stack_grid()
    ends = jnp.concatenate([ends_ref[...]] * HEADS_HERE, 0)
    allowed = (token >= row * LENGTH) & (token <= row * LENGTH + ends)
    scores = jnp.where(allowed, scores, -1e30)
    weight = jnp.exp(scores - jnp.max(scores, 1, keepdims=True))
    probs = weight / jnp.sum(weight, 1, keepdims=True)
    p_ref[...] = probs
    att_ref[step_rows(i), :] = head_fold(mm(probs.astype(low), values)).astype(low)

    @pl.when(i == pl.num_programs(0) - 1)
    def _():
        out_ref[...] = mm_nt(att_ref[...], vo_ref[:, COLS:]).astype(low)


def attend(unit, unit_end, ends, kq, vo):
    count = ends.shape[0]
    steps = count // BLOCK
    return pl.pallas_call(
        attend_body,
        grid=(steps,),
        out_shape=shapes(
            *[((count * LENGTH, COLS), low)] * 2,
            ((steps * STACK, TOKENS), full),
            *[((count, COLS), low)] * 2,
            ((count, WIDTH), low),
        ),
        in_specs=[
            pl.BlockSpec((TOKENS, WIDTH), lambda i: (i, 0)),
            whole_block((count, WIDTH)),
            pl.BlockSpec((BLOCK, 1), lambda i: (i, 0)),
            whole_block(kq.shape),
            whole_block(vo.shape),
        ],
        out_specs=[
            pl.BlockSpec((TOKENS, COLS), lambda i: (i, 0)),
            pl.BlockSpec((TOKENS, COLS), lambda i: (i, 0)),
            pl.BlockSpec((STACK, TOKENS), lambda i: (i, 0)),
            whole_block((count, COLS)),
            whole_block((count, COLS)),
            whole_block((count, WIDTH)),
        ],
        name="attend",
    )(unit, unit_end, ends, kq, vo)


def attend_back_body(
    core_ref, d_mid_ref, unit_ref, unit_end_ref, vo_ref, k_ref, v_ref, p_ref, q_ref, att_ref,
    keep_ref, send_ref, dk_ref, dv_ref, small_ref, probs_ref,
    sum_ref, d_att_ref, dq_ref,
):
    i = pl.program_id(0)

    @pl.when(i == 0)
    def _():
        sum_ref[...] = jnp.zeros_like(sum_ref)
        d_att_ref[...] = mm(d_mid_ref[...], vo_ref[:, COLS:]).astype(low)

    values = v_ref[...]
    probs = p_ref[...]
    probs_low = probs.astype(low)
    queries = head_stack(q_ref[step_rows(i), :])
    d_att = head_stack(d_att_ref[step_rows(i), :])
    d_probs = mm_nt(d_att, values)
    d_scores = probs * (d_probs - jnp.sum(probs * d_probs, 1, keepdims=True))
    d_scores = (d_scores * SCORE_SCALE).astype(low)
    dq_ref[step_rows(i), :] = head_fold(mm(d_scores, k_ref[...])).astype(low)
    d_keys = mm_tn(d_scores, queries).astype(low)
    d_values = mm_tn(probs_low, d_att).astype(low)
    dk_ref[...] = d_keys
    dv_ref[...] = d_values
    spot = lax.broadcasted_iota(jnp.int32, (TOKENS, 128), 0) & (LENGTH - 1)
    lane = lax.broadcasted_iota(jnp.int32, (TOKENS, 128), 1)
    squeeze = (spot == lane).astype(low)
    squeeze_far = (spot + LENGTH == lane).astype(low)
    probs_ref[...] = (mm(probs_low, squeeze) + mm(d_scores, squeeze_far)).astype(low)
    sum_ref[...] += mm_tn(unit_ref[...], jnp.concatenate([d_keys, d_values], 1))

    @pl.when(i == pl.num_programs(0) - 1)
    def _():
        first = core_ref[0] == 0
        d_queries = dq_ref[...]
        small_ref[:, :COLS] = q_ref[...]
        small_ref[:, COLS : 2 * COLS] = d_att_ref[...]
        small_ref[:, 2 * COLS :] = d_queries
        g_key = sum_ref[:, :COLS].astype(low)
        g_value = sum_ref[:, COLS:].astype(low)
        g_query = mm_tn(unit_end_ref[...], d_queries).astype(low)
        g_back = mm_tn(d_mid_ref[...], att_ref[...]).astype(low)
        keep_ref[:, :COLS] = jnp.where(first, g_key, g_value)
        send_ref[:, :COLS] = jnp.where(first, g_value, g_key)
        keep_ref[:, COLS:] = jnp.where(first, g_query, g_back)
        send_ref[:, COLS:] = jnp.where(first, g_back, g_query)


def attend_back(core, d_mid, unit, unit_end, vo, keys, values, probs, queries, attended):
    count = d_mid.shape[0]
    steps = count // BLOCK
    return pl.pallas_call(
        attend_back_body,
        grid=(steps,),
        out_shape=shapes(
            *[((WIDTH, 2 * COLS), low)] * 2,
            *[((count * LENGTH, COLS), low)] * 2,
            ((count, 3 * COLS), low),
            ((steps * STACK, 128), low),
        ),
        in_specs=[
            pl.BlockSpec(memory_space=pltpu.SMEM),
            whole_block((count, WIDTH)),
            pl.BlockSpec((TOKENS, WIDTH), lambda i: (i, 0)),
            whole_block((count, WIDTH)),
            whole_block(vo.shape),
            pl.BlockSpec((TOKENS, COLS), lambda i: (i, 0)),
            pl.BlockSpec((TOKENS, COLS), lambda i: (i, 0)),
            pl.BlockSpec((STACK, TOKENS), lambda i: (i, 0)),
            whole_block((count, COLS)),
            whole_block((count, COLS)),
        ],
        out_specs=[
            whole_block((WIDTH, 2 * COLS)),
            whole_block((WIDTH, 2 * COLS)),
            pl.BlockSpec((TOKENS, COLS), lambda i: (i, 0)),
            pl.BlockSpec((TOKENS, COLS), lambda i: (i, 0)),
            whole_block((count, 3 * COLS)),
            pl.BlockSpec((STACK, 128), lambda i: (i, 0)),
        ],
        scratch_shapes=[
            pltpu.VMEM((WIDTH, 2 * COLS), full),
            pltpu.VMEM((count, COLS), low),
            pltpu.VMEM((count, COLS), low),
        ],
        name="attend_back",
    )(core, d_mid, unit, unit_end, vo, keys, values, probs, queries, attended)


def place_rows(picks, rows):
    high = rows.astype(low)
    rest = (rows - high.astype(full)).astype(low)
    return mm_tn(picks, jnp.concatenate([high, rest], 0))


def captions_body(
    group_ref, ends_ref, unit_ref, scale_ref, d_mid_ref, dk_ref, dv_ref, small_ref,
    small_far_ref, probs_far_ref, kq_ref, vo_ref, kq_far_ref, vo_far_ref, out_ref, inner_end_ref,
):
    i = pl.program_id(0)
    count = small_ref.shape[0]
    half = count // 2

    @pl.when(i == 0)
    def _():
        far = mm_nt(small_far_ref[:, 2 * COLS :], kq_far_ref[:, COLS:])
        own = mm_nt(small_ref[:, 2 * COLS :], kq_ref[:, COLS:])
        inner_end_ref[:half] = own[:half] + far[half:]
        inner_end_ref[half:] = own[half:] + far[:half]

    steps = pl.num_programs(0)
    far_rows = step_rows((i + steps // 2) % steps)
    row, token = stack_grid()
    own_caption = token // LENGTH == row
    lane = lax.broadcasted_iota(jnp.int32, (128, TOKENS), 0)
    spot = lax.broadcasted_iota(jnp.int32, (128, TOKENS), 1) & (LENGTH - 1)
    pair = probs_far_ref[...]
    probs = jnp.where(own_caption, mm(pair, (spot == lane).astype(low)), 0.0).astype(low)
    d_scores = jnp.where(
        own_caption, mm(pair, (spot + LENGTH == lane).astype(low)), 0.0
    ).astype(low)
    d_keys = mm_tn(d_scores, head_stack(small_far_ref[far_rows, :COLS])).astype(low)
    d_values = mm_tn(probs, head_stack(small_far_ref[far_rows, COLS : 2 * COLS])).astype(low)
    inner = mm_nt(dk_ref[...], kq_ref[:, :COLS]) + mm_nt(dv_ref[...], vo_ref[:, :COLS])
    inner += mm_nt(d_keys, kq_far_ref[:, :COLS]) + mm_nt(d_values, vo_far_ref[:, :COLS])
    picks = end_picks(ends_ref[...], 2).astype(low)
    inner += place_rows(picks, inner_end_ref[step_rows(i), :])
    unit = unit_ref[...].astype(full)
    flat = jnp.sum(inner, -1, keepdims=True) * (1.0 / WIDTH)
    tilt = jnp.sum(inner * unit, -1, keepdims=True) * (1.0 / WIDTH)
    out_ref[...] = place_rows(picks, d_mid_ref[...]) + scale_ref[:, :1] * (
        inner - flat - unit * tilt
    )


def captions_back(
    group, ends, unit, scale, d_mid, d_keys, d_values, small, small_far, probs_far, kq, vo,
    kq_far, vo_far,
):
    count = ends.shape[0]
    steps = count // BLOCK
    return pl.pallas_call(
        captions_body,
        out_shape=jax.ShapeDtypeStruct(unit.shape, full),
        grid_spec=pltpu.PrefetchScalarGridSpec(
            num_scalar_prefetch=1,
            grid=(steps,),
            in_specs=[
                pl.BlockSpec((BLOCK, 1), lambda i, g: (i, 0)),
                pl.BlockSpec((TOKENS, WIDTH), lambda i, g: (i, 0)),
                pl.BlockSpec((TOKENS, 128), lambda i, g: (i, 0)),
                pl.BlockSpec((BLOCK, WIDTH), lambda i, g: (i, 0)),
                pl.BlockSpec((TOKENS, COLS), lambda i, g: (i, 0)),
                pl.BlockSpec((TOKENS, COLS), lambda i, g: (i, 0)),
                whole_block(small.shape),
                whole_block(small.shape),
                pl.BlockSpec((STACK, 128), lambda i, g: ((i + steps // 2) % steps, 0)),
            ]
            + [whole_block(kq.shape)] * 4,
            out_specs=pl.BlockSpec(
                (TOKENS, WIDTH), lambda i, g: ((i + g[0] * (steps // 2)) % steps, 0)
            ),
            scratch_shapes=[pltpu.VMEM((count, WIDTH), full)],
        ),
        name="captions_back",
    )(
        group, ends, unit, scale, d_mid, d_keys, d_values, small, small_far, probs_far, kq, vo,
        kq_far, vo_far,
    )


def local(
    captions,
    image_cache,
    send_order,
    arrive_order,
    counts,
    keep_mask,
    end_pos,
    w_qkv,
    w_out,
    w_up,
    w_down,
    w_proj,
    ln1_gain,
    ln2_gain,
):
    plane = Plane()
    core = plane.core
    group = lax.axis_index("mp")
    spread = plane.count
    rows_dev, length, width = captions.shape
    rows = w_out.shape[0]
    per_peer = rows_dev // spread
    hidden = w_up.shape[1] // 2
    quarter = width // 4
    core_flag = core.reshape(1).astype(jnp.int32)
    group_flag = group.reshape(1).astype(jnp.int32)

    packed = pack(
        core_flag, w_qkv, w_out, w_up, w_down, w_proj, ln1_gain[:, None], ln2_gain[:, None]
    )
    mix_own = plane.gather(packed[0], packed[1])
    mix_other = plane.swap_core(mix_own)
    feeds = plane.gather(packed[2], packed[3], plane.last if plane.fast else None)

    cached = image_cache.astype(full)
    cached = (cached * lax.rsqrt(jnp.sum(cached * cached, -1, keepdims=True) + 1e-06)).astype(low)
    places = jnp.arange(rows_dev, dtype=jnp.int32)
    hand_out = (send_order[0][:, None] == places[None, :]).astype(low)
    outgoing = mm(hand_out, cached).astype(low).reshape(spread, per_peer, width)
    incoming = lax.all_to_all(outgoing, "dp", split_axis=0, concat_axis=0, tiled=True)
    own_arrive = lax.dynamic_slice_in_dim(arrive_order[0], group * CAP_DEV, CAP_DEV, 0)
    take_in = (own_arrive[:, None] == places[None, :]).astype(low)
    pictures = mm(take_in, incoming.reshape(rows_dev, width)).astype(low)
    wide = width // 2
    picture_mine = pick(core, pictures[:, :wide], pictures[:, wide:])
    picture_send = pick(core, pictures[:, wide:], pictures[:, :wide])
    main = rows if plane.fast else CAP_DEV
    spare = CAP_DEV - main
    if plane.fast:

        def join(embed, half):
            parts = [half[main:, i * 128 : (i + 1) * 128] for i in range(wide // 128)]
            return jnp.concatenate([embed, half[:main], jnp.concatenate(parts, 0)], 1)

        third = plane.gather(
            join(packed[4], picture_mine), join(packed[5], picture_send), plane.last
        )
        third_other = plane.swap_core(third)

        def images(x):
            extra = x[:, 2 * wide :].reshape(spread, wide // 128, spare, 128)
            extra = extra.transpose(0, 2, 1, 3).reshape(spread * spare, wide)
            return jnp.concatenate([x[:, wide : 2 * wide], extra], 0)

        image_halves = images(third), images(third_other)
        embed_halves = third[:, :wide], third_other[:, :wide]
    else:
        image_half = plane.gather(picture_mine, picture_send)
        image_halves = image_half, plane.swap_core(image_half)
        embed_half = plane.gather(packed[4], packed[5])
        embed_halves = embed_half, plane.swap_core(embed_half)

    def sides(pair):
        return jnp.concatenate([pick(core, *pair), pick(core, pair[1], pair[0])], 1)

    pictures_all = sides(image_halves)
    w_embed = sides(embed_halves)
    kq = pick(core, mix_own, mix_other)
    vo = pick(core, mix_other, mix_own)
    far_own = swap_group(mix_own)
    far_other = plane.swap_core(far_own)
    kq_far = pick(core, far_own, far_other)
    vo_far = pick(core, far_other, far_own)

    flipped = jnp.concatenate([end_pos, end_pos], 0)
    ends = lax.dynamic_slice_in_dim(flipped, group * CAP_DEV, rows_dev, 0)[:, None]
    unit, scale, unit_end, stream_end = norm_first(
        group_flag, captions.reshape(rows_dev * length, width), ends
    )
    keys, values, probs, queries, attended, attention = attend(unit, unit_end, ends, kq, vo)

    stream_near = swap_near(stream_end, 2)
    from_group, from_core, from_both = [swap_near(attention, flip) for flip in (1, 2, 3)]
    attention = jnp.concatenate([attention, from_core], 0).astype(full)
    attention = attention + jnp.concatenate(
        [roll_rows(from_group), roll_rows(from_both)], 0
    ).astype(full)
    middle = jnp.concatenate([stream_end, stream_near], 0).astype(full) + attention
    unit_second, scale_second = norm_rows(middle)
    second_low = unit_second.astype(low)
    w_raise = feeds[:, :hidden]
    w_lower = feeds[:, hidden:]
    active, slope = gelu_parts(mm(second_low, w_raise))
    active = active.astype(low)
    lowered = mm_nt(active, w_lower).astype(low)
    feed = lowered[:CAP_DEV].astype(full)
    for flip in (1, 2, 3):
        part = swap_near(lowered[flip * CAP_DEV : (flip + 1) * CAP_DEV], flip)
        feed = feed + part.astype(full)
    pooled = (middle[:CAP_DEV] + feed).astype(low)
    embedding = mm(pooled, w_embed)
    inverse = lax.rsqrt(jnp.sum(embedding * embedding, -1, keepdims=True) + 1e-06)
    unit_text = embedding * inverse
    text_low = unit_text.astype(low)

    keep_rows = keep_mask.reshape(spread, MICRO, CAP_DEV) == 1
    filled = jnp.arange(CAP_DEV, dtype=jnp.int32)[None, None, :] < counts[:, :, None]
    valid = keep_rows & filled
    total_valid = jnp.sum(valid.astype(full))
    batch_valid = lax.dynamic_index_in_dim(valid, group, 1, False)
    own_valid = lax.dynamic_index_in_dim(batch_valid, plane.index, 0, False)
    batch_valid = jnp.concatenate(
        [batch_valid[:, :main].reshape(-1), batch_valid[:, main:].reshape(-1)]
    )
    sims = LOGIT_SCALE * mm_nt(text_low, pictures_all)
    allowed = own_valid[:, None] & batch_valid[None, :]
    weight = jnp.where(allowed, jnp.exp(sims), 0.0)
    row_sum = jnp.sum(weight, 1)
    place = jnp.arange(CAP_DEV, dtype=jnp.int32)
    slot = jnp.where(
        place < main,
        plane.index * main + place,
        spread * main + plane.index * spare + place - main,
    )
    target = (
        jnp.arange(spread * CAP_DEV, dtype=jnp.int32)[None, :] == slot[:, None]
    ) & own_valid[:, None]
    row_safe = jnp.where(own_valid, row_sum, 1.0)
    row_part = 0.5 * jnp.sum(jnp.log(row_safe)) - jnp.sum(jnp.where(target, sims, 0.0))
    col_part = jnp.sum(weight, 0)
    totals = jnp.concatenate([col_part, jnp.full((128,), 1.0 / 128, full) * row_part])
    totals = plane.total(totals.reshape(-1, 128)).reshape(-1)
    col_sum = totals[: spread * CAP_DEV]
    col_safe = jnp.where(batch_valid, col_sum, 1.0)
    objective = jnp.sum(totals[spread * CAP_DEV :]) + 0.5 * jnp.sum(jnp.log(col_safe))
    objective = jnp.full((8, 128), objective)
    loss = (objective + swap_group(objective))[0, 0] / total_valid
    d_sims = (
        weight * (0.5 / row_safe[:, None] + 0.5 / col_safe[None, :]) - target.astype(full)
    ).astype(low)
    d_unit = LOGIT_SCALE * mm(d_sims, pictures_all)
    d_embed = (
        (d_unit - unit_text * jnp.sum(unit_text * d_unit, -1, keepdims=True)) * inverse
    ).astype(low)

    pooled_all = jnp.concatenate([pooled] + [swap_near(pooled, flip) for flip in (1, 2, 3)], 0)
    d_embed_all = jnp.concatenate([d_embed] + [swap_near(d_embed, flip) for flip in (1, 2, 3)], 0)
    d_pooled = mm_nt(d_embed_all, w_embed)
    d_out_low = d_pooled.astype(low)
    g_lower = mm_tn(d_out_low, active).astype(low)
    d_raised = (mm(d_out_low, w_lower) * slope).astype(low)
    g_raise = mm_tn(second_low, d_raised).astype(low)
    d_second = mm_nt(d_raised, w_raise).astype(low)
    d_embed_half = pick(group, d_embed_all[:, :wide], d_embed_all[:, wide:])
    d_embed_here = pick(core, d_embed_half[:, :quarter], d_embed_half[:, quarter:])
    g_embed = mm_tn(pooled_all, d_embed_here).astype(low)
    lower_sum = plane.scatter(jnp.concatenate([g_lower, g_embed], 1))
    raise_sum = plane.scatter(g_raise)
    inner = d_second[:rows_dev].astype(full)
    inner = inner + roll_rows(swap_near(d_second[:rows_dev], 1)).astype(full)
    inner = inner + swap_near(d_second[rows_dev:], 2).astype(full)
    inner = inner + roll_rows(swap_near(d_second[rows_dev:], 3)).astype(full)
    d_middle = d_pooled[:rows_dev] + norm_back(
        inner, unit_second[:rows_dev], scale_second[:rows_dev]
    )

    g_keep, g_send, d_keys, d_values, small, small_probs = attend_back(
        core_flag, d_middle.astype(low), unit, unit_end, vo, keys, values, probs, queries, attended
    )
    mix_sum = plane.scatter(g_keep, g_send)
    small_far = swap_group(small)
    probs_far = swap_group(small_probs)
    grad_captions = captions_back(
        group_flag, ends, unit, scale, d_middle, d_keys, d_values, small, small_far, probs_far,
        kq, vo, kq_far, vo_far,
    ).reshape(rows_dev, length, width)

    grad_down = jnp.concatenate([part[:, :hidden] for part in lower_sum], 1)
    proj_own = jnp.concatenate([part[:, hidden:] for part in lower_sum], 1)
    proj_far = swap_group(proj_own)
    grad_proj = pick(
        group,
        jnp.concatenate([proj_own, proj_far], 1),
        jnp.concatenate([proj_far, proj_own], 1),
    )
    grad_out = mix_sum[1][:, COLS:]
    unit_mix = jnp.stack([mix_sum[0][:, COLS:], mix_sum[0][:, :COLS], mix_sum[1][:, :COLS]], 1)
    grad_qkv = unit_mix * ln1_gain[:, None, None]
    raised_sum = jnp.concatenate(raise_sum, 1)
    grad_up = raised_sum * ln2_gain[:, None]
    gains = jnp.stack(
        [
            jnp.sum(unit_mix * w_qkv.astype(full), (1, 2)),
            jnp.sum(raised_sum * w_up.astype(full), 1),
        ]
    )
    gains = gains + swap_group(gains)
    return (
        loss,
        grad_captions,
        grad_qkv,
        grad_out,
        grad_up,
        grad_down,
        grad_proj,
        gains[0],
        gains[1],
    )


def solution(mesh):
    return jax.shard_map(
        local,
        mesh=mesh,
        in_specs=(
            P("dp", None, None),
            P("dp", None),
            P("dp", None),
            P("dp", None),
            P(),
            P(),
            P("dp"),
            P("dp", None, "mp"),
            P("dp", "mp"),
            P("dp", "mp"),
            P("dp", "mp"),
            P("dp", None),
            P("dp"),
            P("dp"),
        ),
        out_specs=(
            P(),
            P("dp", None, None),
            P("dp", None, "mp"),
            P("dp", "mp"),
            P("dp", "mp"),
            P("dp", "mp"),
            P("dp", None),
            P("dp"),
            P("dp"),
        ),
        check_vma=False,
    )
```

```python
import math

import jax
import jax.numpy as jnp
from jax import lax
from jax.experimental import pallas as pl
from jax.experimental.pallas import tpu as pltpu
from jax.sharding import PartitionSpec as P

HEAD = 64
MICRO = 2
CAP_DEV = 64
LOGIT_SCALE = 40.0
SCORE_SCALE = 1.0 / math.sqrt(HEAD)
LENGTH = 16
WIDTH = 768
HEADS_HERE = 6
COLS = HEADS_HERE * HEAD
BLOCK = 16
TOKENS = BLOCK * LENGTH
STACK = HEADS_HERE * BLOCK

low = jnp.bfloat16
full = jnp.float32


def mm(a, b):
    return lax.dot_general(a, b, (((1,), (0,)), ((), ())), preferred_element_type=full)


def mm_nt(a, b):
    return lax.dot_general(a, b, (((1,), (1,)), ((), ())), preferred_element_type=full)


def mm_tn(a, b):
    return lax.dot_general(a, b, (((0,), (0,)), ((), ())), preferred_element_type=full)


def pick(flag, when_zero, when_one):
    return jnp.where(flag == 0, when_zero, when_one)


class Plane:
    def __init__(self):
        self.count = lax.axis_size("dp")
        self.index = lax.axis_index("dp")
        self.core = self.index % 2
        self.side = (self.index // 2) % 2
        self.depth = self.index // 4
        self.fast = self.count == 16

    def swap_core(self, x):
        return lax.ppermute(x, "dp", [(i, i ^ 1) for i in range(self.count)])

    def swap_side(self, x):
        return lax.ppermute(x, "dp", [(i, i ^ 2) for i in range(self.count)])

    def shift_depth(self, x, step):
        return lax.ppermute(
            x, "dp", [(i, (i + 4 * step) % self.count) for i in range(self.count)]
        )

    def gather(self, mine, send, ring_after=(), last_after=None):
        if not self.fast:
            zero_all = lax.all_gather(pick(self.core, mine, send), "dp", axis=0, tiled=True)
            one_all = lax.all_gather(pick(self.core, send, mine), "dp", axis=0, tiled=True)
            self.near = self.far = mine
            return pick(self.core, zero_all, one_all)
        rows, width = mine.shape
        arrived = self.swap_core(send)
        block = jnp.zeros((2, rows, width), mine.dtype)
        block = lax.dynamic_update_slice(block, mine[None], (self.core, 0, 0))
        block = lax.dynamic_update_slice(block, arrived[None], (1 - self.core, 0, 0))
        block = block.reshape(2 * rows, width)
        if ring_after:
            block = after(block, *ring_after)
        up = self.shift_depth(block, 1)
        down = self.shift_depth(block, -1)
        far = self.shift_depth(up, 1)
        self.near = up
        self.far = far
        if last_after is not None:
            far = after(far, last_after(self))
        whole = jnp.zeros((self.count // 2, 2 * rows, width), mine.dtype)
        for step, here in ((0, block), (1, up), (-1, down), (2, far)):
            place = ((self.depth - step) % 4) * 2
            across = self.swap_side(here)
            whole = lax.dynamic_update_slice(whole, here[None], (place + self.side, 0, 0))
            whole = lax.dynamic_update_slice(
                whole, across[None], (place + 1 - self.side, 0, 0)
            )
        return whole.reshape(rows * self.count, width)

    def scatter_side(self, keep, send=None):
        if not self.fast:
            return keep, send
        rows = keep.shape[0] // self.count
        width = keep.shape[1]
        pair = keep
        if send is not None:
            pair = (keep.astype(full) + self.swap_core(send).astype(full)).astype(low)
        self.pair = pair
        pair = pair.reshape(4, 2, 2 * rows, width)
        stay = lax.dynamic_index_in_dim(pair, self.side, 1, False)
        leave = lax.dynamic_index_in_dim(pair, 1 - self.side, 1, False)
        return (stay.astype(full) + self.swap_side(leave).astype(full)).astype(low)

    def scatter_depth(self, quad_sum):
        if not self.fast:
            keep, send = quad_sum
            if send is None:
                send = jnp.zeros_like(keep)
            halves = (pick(self.core, keep, send), pick(self.core, send, keep))
            return [
                lax.psum_scatter(half, "dp", scatter_dimension=0, tiled=True).astype(full)
                for half in halves
            ]
        total = lax.dynamic_index_in_dim(quad_sum, self.depth, 0, False).astype(full)
        for step in range(1, 4):
            leave = lax.dynamic_index_in_dim(quad_sum, (self.depth + step) % 4, 0, False)
            total = total + self.shift_depth(leave, step).astype(full)
        return total

    def scatter_core(self, total):
        if not self.fast:
            return total
        rows, width = total.shape[0] // 2, total.shape[1]
        total = total.reshape(2, rows, width)
        mine = lax.dynamic_index_in_dim(total, self.core, 0, False)
        arrived = self.swap_core(lax.dynamic_index_in_dim(total, 1 - self.core, 0, False))
        return pick(self.core, mine, arrived), pick(self.core, arrived, mine)

    def total(self, x):
        if not self.fast:
            return lax.psum(x, "dp")
        x = (x + self.swap_core(x)) + (self.swap_side(x) + self.swap_both(x))
        return x + sum(self.shift_depth(x, step) for step in range(1, 4))

    def swap_both(self, x):
        return lax.ppermute(x, "dp", [(i, i ^ 3) for i in range(self.count)])


def swap_near(x, flip):
    size = 2 * lax.axis_size("dp")
    return lax.ppermute(x, ("dp", "mp"), [(i, i ^ flip) for i in range(size)])


def swap_group(x):
    return swap_near(x, 1)


def after(x, *others):
    return lax.optimization_barrier((x, *others))[0]


def roll_rows(x):
    half = x.shape[0] // 2
    return jnp.concatenate([x[half:], x[:half]], 0)


def norm_rows(inputs):
    center = inputs - jnp.mean(inputs, -1, keepdims=True)
    scale = lax.rsqrt(jnp.mean(center * center, -1, keepdims=True) + 1e-05)
    return center * scale, scale


def norm_back(inner, unit, scale):
    return scale * (
        inner
        - jnp.mean(inner, -1, keepdims=True)
        - unit * jnp.mean(inner * unit, -1, keepdims=True)
    )


def gelu_parts(raised):
    cumulative = 0.5 * (1.0 + lax.erf(raised * 0.7071067811865476))
    slope = cumulative + raised * jnp.exp(-0.5 * raised * raised) * 0.3989422804014327
    return raised * cumulative, slope


def whole_block(shape):
    return pl.BlockSpec(shape, lambda *_: (0,) * len(shape))


def shapes(*items):
    return [jax.ShapeDtypeStruct(shape, kind) for shape, kind in items]


def pack_body(core_ref, mix_ref, back_ref, raise_ref, lower_ref, embed_ref, g1_ref, g2_ref, *outs):
    first = core_ref[0] == 0
    rows = back_ref.shape[0]
    spot = lax.broadcasted_iota(jnp.int32, (rows, rows), 0)
    diagonal = spot == lax.broadcasted_iota(jnp.int32, (rows, rows), 1)
    g1, g2 = [
        jnp.sum(jnp.where(diagonal, ref[...], 0.0), 1, keepdims=True) for ref in (g1_ref, g2_ref)
    ]

    def part(index):
        return (mix_ref[index].astype(full) * g1).astype(low)

    def put(index, columns, zero, one):
        outs[index][:, columns] = jnp.where(first, zero, one)
        outs[index + 1][:, columns] = jnp.where(first, one, zero)

    put(0, slice(0, COLS), part(1), part(2))
    put(0, slice(COLS, 2 * COLS), part(0), back_ref[...])
    hidden = raise_ref.shape[1] // 2
    raised = (raise_ref[...].astype(full) * g2).astype(low)
    put(2, slice(0, hidden), raised[:, :hidden], raised[:, hidden:])
    put(2, slice(hidden, 2 * hidden), lower_ref[:, :hidden], lower_ref[:, hidden:])
    put(4, slice(0, COLS), embed_ref[:, :COLS], embed_ref[:, COLS:])


def pack(core, w_qkv, w_out, w_up, w_down, w_proj, g1, g2):
    rows, hidden = w_up.shape
    vmem = pl.BlockSpec(memory_space=pltpu.VMEM)
    return pl.pallas_call(
        pack_body,
        out_shape=shapes(
            *[((rows, 2 * COLS), low)] * 2, *[((rows, hidden), low)] * 2, *[((rows, COLS), low)] * 2
        ),
        in_specs=[pl.BlockSpec(memory_space=pltpu.SMEM)] + [vmem] * 7,
        out_specs=[vmem] * 6,
        name="pack",
    )(core, w_qkv, w_out, w_up, w_down, w_proj, g1, g2)


def end_picks(ends, copies):
    ends = jnp.concatenate([ends] * copies, 0)
    shape = (copies * BLOCK, TOKENS)
    row = lax.broadcasted_iota(jnp.int32, shape, 0) & (BLOCK - 1)
    return lax.broadcasted_iota(jnp.int32, shape, 1) == row * LENGTH + ends


def norm_body(group_ref, x_ref, ends_ref, unit_ref, scale_ref, unit_end_ref, stream_end_ref):
    x = x_ref[...]
    stream = x.astype(full)
    center = stream - jnp.sum(stream, -1, keepdims=True) * (1.0 / WIDTH)
    scale = lax.rsqrt(jnp.sum(center * center, -1, keepdims=True) * (1.0 / WIDTH) + 1e-05)
    unit = (center * scale).astype(low)
    unit_ref[...] = unit
    scale_ref[...] = jnp.broadcast_to(scale, scale_ref.shape)
    picks = end_picks(ends_ref[...], 1).astype(low)
    unit_end_ref[...] = mm(picks, unit).astype(low)
    stream_end_ref[...] = mm(picks, x).astype(low)


def norm_first(group, x, ends):
    steps = ends.shape[0] // BLOCK
    return pl.pallas_call(
        norm_body,
        out_shape=shapes(
            (x.shape, low), ((x.shape[0], 128), full), *[((ends.shape[0], WIDTH), low)] * 2
        ),
        grid_spec=pltpu.PrefetchScalarGridSpec(
            num_scalar_prefetch=1,
            grid=(steps,),
            in_specs=[
                pl.BlockSpec((TOKENS, WIDTH), lambda i, g: ((i + g[0] * (steps // 2)) % steps, 0)),
                pl.BlockSpec((BLOCK, 1), lambda i, g: (i, 0)),
            ],
            out_specs=[
                pl.BlockSpec((TOKENS, WIDTH), lambda i, g: (i, 0)),
                pl.BlockSpec((TOKENS, 128), lambda i, g: (i, 0)),
                pl.BlockSpec((BLOCK, WIDTH), lambda i, g: (i, 0)),
                pl.BlockSpec((BLOCK, WIDTH), lambda i, g: (i, 0)),
            ],
        ),
        name="norm_first",
    )(group, x, ends)


def head_mask(head):
    return lax.broadcasted_iota(jnp.int32, (BLOCK, COLS), 1) // HEAD == head


def head_stack(x):
    zero = jnp.zeros_like(x)
    return jnp.concatenate([jnp.where(head_mask(h), x, zero) for h in range(HEADS_HERE)], 0)


def head_fold(x):
    out = jnp.zeros((BLOCK, COLS), full)
    for h in range(HEADS_HERE):
        out = jnp.where(head_mask(h), x[h * BLOCK : (h + 1) * BLOCK], out)
    return out


def stack_grid():
    row = lax.broadcasted_iota(jnp.int32, (STACK, TOKENS), 0) & (BLOCK - 1)
    token = lax.broadcasted_iota(jnp.int32, (STACK, TOKENS), 1)
    return row, token


def step_rows(i):
    return pl.ds(pl.multiple_of(i * BLOCK, BLOCK), BLOCK)


def attend_body(
    unit_ref, unit_end_ref, ends_ref, kq_ref, vo_ref, k_ref, v_ref, p_ref, q_ref, att_ref, out_ref
):
    i = pl.program_id(0)

    @pl.when(i == 0)
    def _():
        q_ref[...] = mm(unit_end_ref[...], kq_ref[:, COLS:]).astype(low)

    unit = unit_ref[...]
    keys = mm(unit, kq_ref[:, :COLS]).astype(low)
    values = mm(unit, vo_ref[:, :COLS]).astype(low)
    k_ref[...] = keys
    v_ref[...] = values
    scores = mm_nt(head_stack(q_ref[step_rows(i), :]), keys) * SCORE_SCALE
    row, token = stack_grid()
    ends = jnp.concatenate([ends_ref[...]] * HEADS_HERE, 0)
    allowed = (token >= row * LENGTH) & (token <= row * LENGTH + ends)
    scores = jnp.where(allowed, scores, -1e30)
    weight = jnp.exp(scores - jnp.max(scores, 1, keepdims=True))
    probs = weight / jnp.sum(weight, 1, keepdims=True)
    p_ref[...] = probs
    att_ref[step_rows(i), :] = head_fold(mm(probs.astype(low), values)).astype(low)

    @pl.when(i == pl.num_programs(0) - 1)
    def _():
        out_ref[...] = mm_nt(att_ref[...], vo_ref[:, COLS:]).astype(low)


def attend(unit, unit_end, ends, kq, vo):
    count = ends.shape[0]
    steps = count // BLOCK
    return pl.pallas_call(
        attend_body,
        grid=(steps,),
        out_shape=shapes(
            *[((count * LENGTH, COLS), low)] * 2,
            ((steps * STACK, TOKENS), full),
            *[((count, COLS), low)] * 2,
            ((count, WIDTH), low),
        ),
        in_specs=[
            pl.BlockSpec((TOKENS, WIDTH), lambda i: (i, 0)),
            whole_block((count, WIDTH)),
            pl.BlockSpec((BLOCK, 1), lambda i: (i, 0)),
            whole_block(kq.shape),
            whole_block(vo.shape),
        ],
        out_specs=[
            pl.BlockSpec((TOKENS, COLS), lambda i: (i, 0)),
            pl.BlockSpec((TOKENS, COLS), lambda i: (i, 0)),
            pl.BlockSpec((STACK, TOKENS), lambda i: (i, 0)),
            whole_block((count, COLS)),
            whole_block((count, COLS)),
            whole_block((count, WIDTH)),
        ],
        name="attend",
    )(unit, unit_end, ends, kq, vo)


def lane_group():
    return lax.broadcasted_iota(jnp.int32, (BLOCK, 128), 1) // (2 * LENGTH)


def attend_back_body(
    core_ref, d_mid_ref, d_att_ref, unit_ref, unit_end_ref, k_ref, v_ref, p_ref, q_ref, att_ref,
    keep_ref, send_ref, dk_ref, dv_ref, dq_ref, probs_ref, sum_ref,
):
    i = pl.program_id(0)

    @pl.when(i == 0)
    def _():
        sum_ref[...] = jnp.zeros_like(sum_ref)

    values = v_ref[...]
    probs = p_ref[...]
    probs_low = probs.astype(low)
    queries = head_stack(q_ref[step_rows(i), :])
    d_att = head_stack(d_att_ref[step_rows(i), :])
    d_probs = mm_nt(d_att, values)
    d_scores = probs * (d_probs - jnp.sum(probs * d_probs, 1, keepdims=True))
    d_scores = (d_scores * SCORE_SCALE).astype(low)
    dq_ref[step_rows(i), :] = head_fold(mm(d_scores, k_ref[...])).astype(low)
    d_keys = mm_tn(d_scores, queries).astype(low)
    d_values = mm_tn(probs_low, d_att).astype(low)
    dk_ref[...] = d_keys
    dv_ref[...] = d_values
    spot = lax.broadcasted_iota(jnp.int32, (TOKENS, 128), 0) & (LENGTH - 1)
    lane = lax.broadcasted_iota(jnp.int32, (TOKENS, 128), 1) & (2 * LENGTH - 1)
    squeezed = mm(probs_low, (spot == lane).astype(low))
    squeezed += mm(d_scores, (spot + LENGTH == lane).astype(low))
    for first in (0, 4):
        out = jnp.zeros((BLOCK, 128), full)
        for h in range(first, min(first + 4, HEADS_HERE)):
            out = jnp.where(lane_group() == h - first, squeezed[h * BLOCK : (h + 1) * BLOCK], out)
        probs_ref[first * 4 : first * 4 + BLOCK] = out.astype(low)
    sum_ref[...] += mm_tn(unit_ref[...], jnp.concatenate([d_keys, d_values], 1))

    @pl.when(i == pl.num_programs(0) - 1)
    def _():
        first = core_ref[0] == 0
        d_queries = dq_ref[...]
        g_key = sum_ref[:, :COLS].astype(low)
        g_value = sum_ref[:, COLS:].astype(low)
        g_query = mm_tn(unit_end_ref[...], d_queries).astype(low)
        g_back = mm_tn(d_mid_ref[...], att_ref[...]).astype(low)
        keep_ref[:, :COLS] = jnp.where(first, g_key, g_value)
        send_ref[:, :COLS] = jnp.where(first, g_value, g_key)
        keep_ref[:, COLS:] = jnp.where(first, g_query, g_back)
        send_ref[:, COLS:] = jnp.where(first, g_back, g_query)


def attend_back(core, d_mid, d_att, unit, unit_end, keys, values, probs, queries, attended):
    count = d_mid.shape[0]
    steps = count // BLOCK
    return pl.pallas_call(
        attend_back_body,
        grid=(steps,),
        out_shape=shapes(
            *[((WIDTH, 2 * COLS), low)] * 2,
            *[((count * LENGTH, COLS), low)] * 2,
            ((count, COLS), low),
            ((steps * 2 * BLOCK, 128), low),
        ),
        in_specs=[
            pl.BlockSpec(memory_space=pltpu.SMEM),
            whole_block((count, WIDTH)),
            whole_block((count, COLS)),
            pl.BlockSpec((TOKENS, WIDTH), lambda i: (i, 0)),
            whole_block((count, WIDTH)),
            pl.BlockSpec((TOKENS, COLS), lambda i: (i, 0)),
            pl.BlockSpec((TOKENS, COLS), lambda i: (i, 0)),
            pl.BlockSpec((STACK, TOKENS), lambda i: (i, 0)),
            whole_block((count, COLS)),
            whole_block((count, COLS)),
        ],
        out_specs=[
            whole_block((WIDTH, 2 * COLS)),
            whole_block((WIDTH, 2 * COLS)),
            pl.BlockSpec((TOKENS, COLS), lambda i: (i, 0)),
            pl.BlockSpec((TOKENS, COLS), lambda i: (i, 0)),
            whole_block((count, COLS)),
            pl.BlockSpec((2 * BLOCK, 128), lambda i: (i, 0)),
        ],
        scratch_shapes=[pltpu.VMEM((WIDTH, 2 * COLS), full)],
        name="attend_back",
    )(core, d_mid, d_att, unit, unit_end, keys, values, probs, queries, attended)


def place_rows(picks, rows):
    high = rows.astype(low)
    rest = (rows - high.astype(full)).astype(low)
    return mm_tn(picks, jnp.concatenate([high, rest], 0))


def captions_body(
    group_ref, ends_ref, unit_ref, scale_ref, d_mid_ref, dk_ref, dv_ref, dq_ref,
    q_far_ref, d_att_far_ref, dq_far_ref, probs_far_ref, kq_ref, vo_ref, kq_far_ref, vo_far_ref,
    *refs,
):
    out_ref, inner_end_ref = refs[-2:]
    i = pl.program_id(0)

    @pl.when(i == 0)
    def _():
        inner_end_ref[...] = mm_nt(dq_ref[...], kq_ref[:, COLS:]) + mm_nt(
            dq_far_ref[...], kq_far_ref[:, COLS:]
        )

    row, token = stack_grid()
    own_caption = token // LENGTH == row
    lane = lax.broadcasted_iota(jnp.int32, (128, TOKENS), 0) & (2 * LENGTH - 1)
    spot = lax.broadcasted_iota(jnp.int32, (128, TOKENS), 1) & (LENGTH - 1)
    packed = probs_far_ref[...]
    zero = jnp.zeros((BLOCK, 128), low)
    pair = jnp.concatenate(
        [
            jnp.where(lane_group() == h % 4, packed[h // 4 * BLOCK : (h // 4 + 1) * BLOCK], zero)
            for h in range(HEADS_HERE)
        ],
        0,
    )
    probs = jnp.where(own_caption, mm(pair, (spot == lane).astype(low)), 0.0).astype(low)
    d_scores = jnp.where(
        own_caption, mm(pair, (spot + LENGTH == lane).astype(low)), 0.0
    ).astype(low)
    d_keys = mm_tn(d_scores, head_stack(q_far_ref[step_rows(i), :])).astype(low)
    d_values = mm_tn(probs, head_stack(d_att_far_ref[step_rows(i), :])).astype(low)
    inner = mm_nt(dk_ref[...], kq_ref[:, :COLS]) + mm_nt(dv_ref[...], vo_ref[:, :COLS])
    inner += mm_nt(d_keys, kq_far_ref[:, :COLS]) + mm_nt(d_values, vo_far_ref[:, :COLS])
    picks = end_picks(ends_ref[...], 2).astype(low)
    inner += place_rows(picks, inner_end_ref[step_rows(i), :])
    unit = unit_ref[...].astype(full)
    flat = jnp.sum(inner, -1, keepdims=True) * (1.0 / WIDTH)
    tilt = jnp.sum(inner * unit, -1, keepdims=True) * (1.0 / WIDTH)
    out_ref[...] = place_rows(picks, d_mid_ref[...]) + scale_ref[:, :1] * (
        inner - flat - unit * tilt
    )


def captions_back(
    part, group, ends, unit, scale, d_mid, d_keys, d_values, dq, q_far, d_att_far, dq_far,
    probs_far, kq, vo, kq_far, vo_far, done=None,
):
    count = ends.shape[0]
    steps = count // BLOCK
    half = steps // 2
    start = part * half
    far = (1 - part) * half
    own_half = pl.BlockSpec((count // 2, COLS), lambda i, g: (part, 0))
    far_half = pl.BlockSpec((count // 2, COLS), lambda i, g: (1 - part, 0))
    operands = [
        group, ends, unit, scale, d_mid, d_keys, d_values, dq, q_far, d_att_far, dq_far,
        probs_far, kq, vo, kq_far, vo_far,
    ]
    in_specs = [
        pl.BlockSpec((BLOCK, 1), lambda i, g: (i + start, 0)),
        pl.BlockSpec((TOKENS, WIDTH), lambda i, g: (i + start, 0)),
        pl.BlockSpec((TOKENS, 128), lambda i, g: (i + start, 0)),
        pl.BlockSpec((BLOCK, WIDTH), lambda i, g: (i + start, 0)),
        pl.BlockSpec((TOKENS, COLS), lambda i, g: (i + start, 0)),
        pl.BlockSpec((TOKENS, COLS), lambda i, g: (i + start, 0)),
        own_half,
        far_half,
        far_half,
        far_half,
        pl.BlockSpec((2 * BLOCK, 128), lambda i, g: (i + far, 0)),
    ] + [whole_block(kq.shape)] * 4
    aliases = {}
    if done is not None:
        aliases = {len(operands): 0}
        operands.append(done)
        in_specs.append(pl.BlockSpec(memory_space=pl.ANY))
    return pl.pallas_call(
        captions_body,
        out_shape=jax.ShapeDtypeStruct(unit.shape, full),
        grid_spec=pltpu.PrefetchScalarGridSpec(
            num_scalar_prefetch=1,
            grid=(half,),
            in_specs=in_specs,
            out_specs=pl.BlockSpec(
                (TOKENS, WIDTH), lambda i, g: ((i + start + g[0] * half) % steps, 0)
            ),
            scratch_shapes=[pltpu.VMEM((count // 2, WIDTH), full)],
        ),
        input_output_aliases=aliases,
        name="captions_back",
    )(*operands)


def local(
    captions,
    image_cache,
    send_order,
    arrive_order,
    counts,
    keep_mask,
    end_pos,
    w_qkv,
    w_out,
    w_up,
    w_down,
    w_proj,
    ln1_gain,
    ln2_gain,
):
    plane = Plane()
    core = plane.core
    group = lax.axis_index("mp")
    spread = plane.count
    rows_dev, length, width = captions.shape
    rows = w_out.shape[0]
    per_peer = rows_dev // spread
    hidden = w_up.shape[1] // 2
    quarter = width // 4
    core_flag = core.reshape(1).astype(jnp.int32)
    group_flag = group.reshape(1).astype(jnp.int32)

    packed = pack(
        core_flag,
        w_qkv.transpose(1, 0, 2),
        w_out,
        w_up,
        w_down,
        w_proj,
        ln1_gain[None],
        ln2_gain[None],
    )
    mix_own = plane.gather(packed[0], packed[1])
    mix_near, mix_last = plane.near, plane.far
    mix_other = plane.swap_core(mix_own)
    kq = pick(core, mix_own, mix_other)
    vo = pick(core, mix_other, mix_own)
    far_own = swap_group(mix_own)
    far_other = plane.swap_core(far_own)
    kq_far = pick(core, far_own, far_other)
    vo_far = pick(core, far_other, far_own)

    flipped = jnp.concatenate([end_pos, end_pos], 0)
    ends = lax.dynamic_slice_in_dim(flipped, group * CAP_DEV, rows_dev, 0)[:, None]
    unit, scale, unit_end, stream_end = norm_first(
        group_flag, after(captions, mix_near).reshape(rows_dev * length, width), ends
    )
    keys, values, probs, queries, attended, attention = attend(unit, unit_end, ends, kq, vo)
    feeds = plane.gather(packed[2], packed[3], (mix_last,), lambda _: attention)

    cached = image_cache.astype(full)
    cached = (cached * lax.rsqrt(jnp.sum(cached * cached, -1, keepdims=True) + 1e-06)).astype(low)
    places = jnp.arange(rows_dev, dtype=jnp.int32)
    hand_out = (send_order[0][:, None] == places[None, :]).astype(low)
    outgoing = mm(hand_out, cached).astype(low).reshape(spread, per_peer, width)
    outgoing = after(outgoing, mix_near)
    incoming = lax.all_to_all(outgoing, "dp", split_axis=0, concat_axis=0, tiled=True)
    own_arrive = lax.dynamic_slice_in_dim(arrive_order[0], group * CAP_DEV, CAP_DEV, 0)
    take_in = (own_arrive[:, None] == places[None, :]).astype(low)
    pictures = mm(take_in, incoming.reshape(rows_dev, width)).astype(low)
    wide = width // 2
    picture_mine = pick(core, pictures[:, :wide], pictures[:, wide:])
    picture_send = pick(core, pictures[:, wide:], pictures[:, :wide])
    main = rows if plane.fast else CAP_DEV
    spare = CAP_DEV - main
    if plane.fast:

        def join(embed, half):
            parts = [half[main:, i * 128 : (i + 1) * 128] for i in range(wide // 128)]
            return jnp.concatenate([embed, half[:main], jnp.concatenate(parts, 0)], 1)

        third = plane.gather(
            join(packed[4], picture_mine), join(packed[5], picture_send), (plane.far, attention)
        )
        third_other = plane.swap_core(third)

        def images(x):
            extra = x[:, 2 * wide :].reshape(spread, wide // 128, spare, 128)
            extra = extra.transpose(0, 2, 1, 3).reshape(spread * spare, wide)
            return jnp.concatenate([x[:, wide : 2 * wide], extra], 0)

        image_halves = images(third), images(third_other)
        embed_halves = third[:, :wide], third_other[:, :wide]
    else:
        image_half = plane.gather(picture_mine, picture_send)
        image_halves = image_half, plane.swap_core(image_half)
        embed_half = plane.gather(packed[4], packed[5])
        embed_halves = embed_half, plane.swap_core(embed_half)

    def sides(pair):
        return jnp.concatenate([pick(core, *pair), pick(core, pair[1], pair[0])], 1)

    pictures_all = sides(image_halves)
    w_embed = sides(embed_halves)

    stream_near = swap_near(stream_end, 2)
    from_group, from_core, from_both = [swap_near(attention, flip) for flip in (1, 2, 3)]
    attention = jnp.concatenate([attention, from_core], 0).astype(full)
    attention = attention + jnp.concatenate(
        [roll_rows(from_group), roll_rows(from_both)], 0
    ).astype(full)
    middle = jnp.concatenate([stream_end, stream_near], 0).astype(full) + attention
    unit_second, scale_second = norm_rows(middle)
    second_low = unit_second.astype(low)
    feeds = after(feeds, far_own)
    queries_far = swap_group(queries)
    w_raise = feeds[:, :hidden]
    w_lower = feeds[:, hidden:]
    active, slope = gelu_parts(mm(second_low, w_raise))
    active = active.astype(low)
    lowered = mm_nt(active, w_lower).astype(low)
    feed = lowered[:CAP_DEV].astype(full)
    for flip in (1, 2, 3):
        part = swap_near(lowered[flip * CAP_DEV : (flip + 1) * CAP_DEV], flip)
        feed = feed + part.astype(full)
    pooled = (middle[:CAP_DEV] + feed).astype(low)
    embedding = mm(pooled, w_embed)
    inverse = lax.rsqrt(jnp.sum(embedding * embedding, -1, keepdims=True) + 1e-06)
    unit_text = embedding * inverse
    text_low = unit_text.astype(low)

    keep_rows = keep_mask.reshape(spread, MICRO, CAP_DEV) == 1
    filled = jnp.arange(CAP_DEV, dtype=jnp.int32)[None, None, :] < counts[:, :, None]
    valid = keep_rows & filled
    total_valid = jnp.sum(valid.astype(full))
    batch_valid = lax.dynamic_index_in_dim(valid, group, 1, False)
    own_valid = lax.dynamic_index_in_dim(batch_valid, plane.index, 0, False)
    batch_valid = jnp.concatenate(
        [batch_valid[:, :main].reshape(-1), batch_valid[:, main:].reshape(-1)]
    )
    sims = LOGIT_SCALE * mm_nt(text_low, pictures_all)
    allowed = own_valid[:, None] & batch_valid[None, :]
    weight = jnp.where(allowed, jnp.exp(sims), 0.0)
    row_sum = jnp.sum(weight, 1)
    place = jnp.arange(CAP_DEV, dtype=jnp.int32)
    slot = jnp.where(
        place < main,
        plane.index * main + place,
        spread * main + plane.index * spare + place - main,
    )
    target = (
        jnp.arange(spread * CAP_DEV, dtype=jnp.int32)[None, :] == slot[:, None]
    ) & own_valid[:, None]
    row_safe = jnp.where(own_valid, row_sum, 1.0)
    row_part = 0.5 * jnp.sum(jnp.log(row_safe)) - jnp.sum(jnp.where(target, sims, 0.0))
    col_part = jnp.sum(weight, 0)
    totals = jnp.concatenate([col_part, jnp.full((128,), 1.0 / 128, full) * row_part])
    totals = plane.total(totals.reshape(-1, 128)).reshape(-1)
    col_sum = totals[: spread * CAP_DEV]
    col_safe = jnp.where(batch_valid, col_sum, 1.0)
    objective = jnp.sum(totals[spread * CAP_DEV :]) + 0.5 * jnp.sum(jnp.log(col_safe))
    objective = jnp.full((8, 128), objective)
    loss = (objective + swap_group(objective))[0, 0] / total_valid
    d_sims = (
        weight * (0.5 / row_safe[:, None] + 0.5 / col_safe[None, :]) - target.astype(full)
    ).astype(low)
    d_unit = LOGIT_SCALE * mm(d_sims, pictures_all)
    d_embed = (
        (d_unit - unit_text * jnp.sum(unit_text * d_unit, -1, keepdims=True)) * inverse
    ).astype(low)

    pooled_all = jnp.concatenate([pooled] + [swap_near(pooled, flip) for flip in (1, 2, 3)], 0)
    d_embed_all = jnp.concatenate([d_embed] + [swap_near(d_embed, flip) for flip in (1, 2, 3)], 0)
    d_pooled = mm_nt(d_embed_all, w_embed)
    d_out_low = d_pooled.astype(low)
    g_lower = mm_tn(d_out_low, active).astype(low)
    d_raised = (mm(d_out_low, w_lower) * slope).astype(low)
    g_raise = mm_tn(second_low, d_raised).astype(low)
    d_second = mm_nt(d_raised, w_raise).astype(low)
    d_embed_half = pick(group, d_embed_all[:, :wide], d_embed_all[:, wide:])
    d_embed_here = pick(core, d_embed_half[:, :quarter], d_embed_half[:, quarter:])
    g_embed = mm_tn(pooled_all, d_embed_here).astype(low)
    lower_quad = plane.scatter_side(jnp.concatenate([g_lower, g_embed], 1))
    raise_quad = plane.scatter_side(g_raise)
    inner = d_second[:rows_dev].astype(full)
    inner = inner + roll_rows(swap_near(d_second[:rows_dev], 1)).astype(full)
    inner = inner + swap_near(d_second[rows_dev:], 2).astype(full)
    inner = inner + roll_rows(swap_near(d_second[rows_dev:], 3)).astype(full)
    d_middle = d_pooled[:rows_dev] + norm_back(
        inner, unit_second[:rows_dev], scale_second[:rows_dev]
    )

    d_middle_low = d_middle.astype(low)
    d_attended = mm(d_middle_low, vo[:, COLS:]).astype(low)
    d_attended_far = swap_group(d_attended)
    g_keep, g_send, d_keys, d_values, d_queries, small_probs = attend_back(
        core_flag, d_middle_low, d_attended, unit, unit_end, keys, values, probs, queries, attended
    )
    d_queries_far = swap_group(d_queries)
    probs_far = swap_group(small_probs)
    mix_quad = plane.scatter_side(g_keep, g_send)
    lower_sum = plane.scatter_core(plane.scatter_depth(lower_quad))
    raise_sum = plane.scatter_core(plane.scatter_depth(raise_quad))
    operands = (
        unit, scale, d_middle, d_keys, d_values, d_queries, queries_far, d_attended_far,
        d_queries_far, probs_far, kq, vo, kq_far, vo_far,
    )
    first_ends = after(ends, lower_quad, plane.pair) if plane.fast else ends
    first_half = captions_back(0, group_flag, first_ends, *operands)
    second_ends = after(ends, mix_quad) if plane.fast else ends
    grad_captions = captions_back(1, group_flag, second_ends, *operands, done=first_half)
    mix_total = plane.scatter_depth(mix_quad)
    if plane.fast:
        mix_total, grad_captions = lax.optimization_barrier((mix_total, grad_captions))
    mix_sum = plane.scatter_core(mix_total)
    grad_captions = grad_captions.reshape(rows_dev, length, width)

    grad_down = jnp.concatenate([part[:, :hidden] for part in lower_sum], 1)
    proj_own = jnp.concatenate([part[:, hidden:] for part in lower_sum], 1)
    proj_far = swap_group(proj_own)
    grad_proj = pick(
        group,
        jnp.concatenate([proj_own, proj_far], 1),
        jnp.concatenate([proj_far, proj_own], 1),
    )
    grad_out = mix_sum[1][:, COLS:]
    unit_mix = jnp.stack([mix_sum[0][:, COLS:], mix_sum[0][:, :COLS], mix_sum[1][:, :COLS]], 1)
    grad_qkv = unit_mix * ln1_gain[:, None, None]
    raised_sum = jnp.concatenate(raise_sum, 1)
    grad_up = raised_sum * ln2_gain[:, None]
    gains = jnp.stack(
        [
            jnp.sum(unit_mix * w_qkv.astype(full), (1, 2)),
            jnp.sum(raised_sum * w_up.astype(full), 1),
        ]
    )
    gains = gains + swap_group(gains)
    return (
        loss,
        grad_captions,
        grad_qkv,
        grad_out,
        grad_up,
        grad_down,
        grad_proj,
        gains[0],
        gains[1],
    )


def solution(mesh):
    return jax.shard_map(
        local,
        mesh=mesh,
        in_specs=(
            P("dp", None, None),
            P("dp", None),
            P("dp", None),
            P("dp", None),
            P(),
            P(),
            P("dp"),
            P("dp", None, "mp"),
            P("dp", "mp"),
            P("dp", "mp"),
            P("dp", "mp"),
            P("dp", None),
            P("dp"),
            P("dp"),
        ),
        out_specs=(
            P(),
            P("dp", None, None),
            P("dp", None, "mp"),
            P("dp", "mp"),
            P("dp", "mp"),
            P("dp", "mp"),
            P("dp", None),
            P("dp"),
            P("dp"),
        ),
        check_vma=False,
    )
```

```python
import functools
import math

import jax
import jax.numpy as jnp
from jax import lax
from jax.experimental import pallas as pl
from jax.experimental.pallas import tpu as pltpu
from jax.sharding import PartitionSpec as P

HEAD = 64
MICRO = 2
CAP_DEV = 64
LOGIT_SCALE = 40.0
SCORE_SCALE = 1.0 / math.sqrt(HEAD)
LENGTH = 16
WIDTH = 768
HEADS_HERE = 6
COLS = HEADS_HERE * HEAD
BLOCK = 16
TOKENS = BLOCK * LENGTH
STACK = HEADS_HERE * BLOCK

low = jnp.bfloat16
full = jnp.float32


def mm(a, b):
    return lax.dot_general(a, b, (((1,), (0,)), ((), ())), preferred_element_type=full)


def mm_nt(a, b):
    return lax.dot_general(a, b, (((1,), (1,)), ((), ())), preferred_element_type=full)


def mm_tn(a, b):
    return lax.dot_general(a, b, (((0,), (0,)), ((), ())), preferred_element_type=full)


def pick(flag, when_zero, when_one):
    return jnp.where(flag == 0, when_zero, when_one)


class Plane:
    def __init__(self):
        self.count = lax.axis_size("dp")
        self.index = lax.axis_index("dp")
        self.core = self.index % 2
        self.side = (self.index // 2) % 2
        self.depth = self.index // 4
        self.fast = self.count == 16

    def swap_core(self, x):
        return lax.ppermute(x, "dp", [(i, i ^ 1) for i in range(self.count)])

    def swap_side(self, x):
        return lax.ppermute(x, "dp", [(i, i ^ 2) for i in range(self.count)])

    def shift_depth(self, x, step):
        return lax.ppermute(
            x, "dp", [(i, (i + 4 * step) % self.count) for i in range(self.count)]
        )

    def join_cores(self, mine, send):
        rows, width = mine.shape
        self.arrived = self.swap_core(send)
        block = jnp.zeros((2, rows, width), mine.dtype)
        block = lax.dynamic_update_slice(block, mine[None], (self.core, 0, 0))
        block = lax.dynamic_update_slice(block, self.arrived[None], (1 - self.core, 0, 0))
        return block.reshape(2 * rows, width)

    def spread_blocks(self, blocks, cuts):
        rows = blocks[0][1].shape[0]
        wholes = [
            jnp.zeros((self.count // 2, rows, end - start), low)
            for start, end in zip(cuts, cuts[1:])
        ]
        for step, here in blocks:
            place = ((self.depth - step) % 4) * 2
            across = self.swap_side(here)
            for block, spot in ((here, place + self.side), (across, place + 1 - self.side)):
                for i, (start, end) in enumerate(zip(cuts, cuts[1:])):
                    wholes[i] = lax.dynamic_update_slice(
                        wholes[i], block[None, :, start:end], (spot, 0, 0)
                    )
        return [whole.reshape(rows * self.count // 2, -1) for whole in wholes]

    def gather_plain(self, mine, send):
        zero_all = lax.all_gather(pick(self.core, mine, send), "dp", axis=0, tiled=True)
        one_all = lax.all_gather(pick(self.core, send, mine), "dp", axis=0, tiled=True)
        return pick(self.core, zero_all, one_all)

    def scatter_side(self, keep, send=None, before=None):
        if not self.fast:
            return keep, send
        rows = keep.shape[0] // self.count
        width = keep.shape[1]
        pair = keep
        if send is not None:
            pair = (keep.astype(full) + self.swap_core(send).astype(full)).astype(low)
        self.pair = pair
        pair = pair.reshape(4, 2, 2 * rows, width)
        stay = lax.dynamic_index_in_dim(pair, self.side, 1, False)
        leave = lax.dynamic_index_in_dim(pair, 1 - self.side, 1, False)
        arrived = self.swap_side(leave)
        if before is not None:
            arrived = after(arrived, before(self))
        return (stay.astype(full) + arrived.astype(full)).astype(low)

    def scatter_depth(self, quad_sum):
        if not self.fast:
            keep, send = quad_sum
            if send is None:
                send = jnp.zeros_like(keep)
            halves = (pick(self.core, keep, send), pick(self.core, send, keep))
            return [
                lax.psum_scatter(half, "dp", scatter_dimension=0, tiled=True).astype(full)
                for half in halves
            ]
        total = lax.dynamic_index_in_dim(quad_sum, self.depth, 0, False).astype(full)
        for step in range(1, 4):
            leave = lax.dynamic_index_in_dim(quad_sum, (self.depth + step) % 4, 0, False)
            total = total + self.shift_depth(leave, step).astype(full)
        return total

    def scatter_core(self, total):
        if not self.fast:
            return total
        rows, width = total.shape[0] // 2, total.shape[1]
        total = total.reshape(2, rows, width)
        mine = lax.dynamic_index_in_dim(total, self.core, 0, False)
        arrived = self.swap_core(lax.dynamic_index_in_dim(total, 1 - self.core, 0, False))
        return pick(self.core, mine, arrived), pick(self.core, arrived, mine)

    def total(self, x):
        if not self.fast:
            return lax.psum(x, "dp")
        x = (x + self.swap_core(x)) + (self.swap_side(x) + self.swap_both(x))
        return x + sum(self.shift_depth(x, step) for step in range(1, 4))

    def swap_both(self, x):
        return lax.ppermute(x, "dp", [(i, i ^ 3) for i in range(self.count)])


def swap_near(x, flip):
    size = 2 * lax.axis_size("dp")
    return lax.ppermute(x, ("dp", "mp"), [(i, i ^ flip) for i in range(size)])


def swap_group(x):
    return swap_near(x, 1)


def after(x, *others):
    return lax.optimization_barrier((x, *others))[0]


def roll_rows(x):
    half = x.shape[0] // 2
    return jnp.concatenate([x[half:], x[:half]], 0)


def norm_rows(inputs):
    center = inputs - jnp.mean(inputs, -1, keepdims=True)
    scale = lax.rsqrt(jnp.mean(center * center, -1, keepdims=True) + 1e-05)
    return center * scale, scale


def norm_back(inner, unit, scale):
    return scale * (
        inner
        - jnp.mean(inner, -1, keepdims=True)
        - unit * jnp.mean(inner * unit, -1, keepdims=True)
    )


def gelu_parts(raised):
    cumulative = 0.5 * (1.0 + lax.erf(raised * 0.7071067811865476))
    slope = cumulative + raised * jnp.exp(-0.5 * raised * raised) * 0.3989422804014327
    return raised * cumulative, slope


def whole_block(shape):
    return pl.BlockSpec(shape, lambda *_: (0,) * len(shape))


def shapes(*items):
    return [jax.ShapeDtypeStruct(shape, kind) for shape, kind in items]


def pack_body(core_ref, mix_ref, back_ref, raise_ref, lower_ref, embed_ref, g1_ref, g2_ref, *outs):
    first = core_ref[0] == 0
    rows = back_ref.shape[0]
    spot = lax.broadcasted_iota(jnp.int32, (rows, rows), 0)
    diagonal = spot == lax.broadcasted_iota(jnp.int32, (rows, rows), 1)
    g1, g2 = [
        jnp.sum(jnp.where(diagonal, ref[...], 0.0), 1, keepdims=True) for ref in (g1_ref, g2_ref)
    ]

    def part(index):
        return (mix_ref[index].astype(full) * g1).astype(low)

    def put(index, columns, zero, one):
        outs[index][:, columns] = jnp.where(first, zero, one)
        outs[index + 1][:, columns] = jnp.where(first, one, zero)

    put(0, slice(0, COLS), part(1), part(0))
    put(0, slice(COLS, 2 * COLS), part(2), back_ref[...])
    hidden = raise_ref.shape[1] // 2
    raised = (raise_ref[...].astype(full) * g2).astype(low)
    put(2, slice(0, hidden), raised[:, :hidden], raised[:, hidden:])
    put(2, slice(hidden, 2 * hidden), lower_ref[:, :hidden], lower_ref[:, hidden:])
    put(4, slice(0, COLS), embed_ref[:, :COLS], embed_ref[:, COLS:])


def pack(core, w_qkv, w_out, w_up, w_down, w_proj, g1, g2):
    rows, hidden = w_up.shape
    vmem = pl.BlockSpec(memory_space=pltpu.VMEM)
    return pl.pallas_call(
        pack_body,
        out_shape=shapes(
            *[((rows, 2 * COLS), low)] * 2, *[((rows, hidden), low)] * 2, *[((rows, COLS), low)] * 2
        ),
        in_specs=[pl.BlockSpec(memory_space=pltpu.SMEM)] + [vmem] * 7,
        out_specs=[vmem] * 6,
        name="pack",
    )(core, w_qkv, w_out, w_up, w_down, w_proj, g1, g2)


def end_picks(ends, copies):
    ends = jnp.concatenate([ends] * copies, 0)
    shape = (copies * BLOCK, TOKENS)
    row = lax.broadcasted_iota(jnp.int32, shape, 0) & (BLOCK - 1)
    return lax.broadcasted_iota(jnp.int32, shape, 1) == row * LENGTH + ends


def norm_body(group_ref, x_ref, ends_ref, unit_ref, scale_ref, unit_end_ref, stream_end_ref):
    x = x_ref[...]
    stream = x.astype(full)
    center = stream - jnp.sum(stream, -1, keepdims=True) * (1.0 / WIDTH)
    scale = lax.rsqrt(jnp.sum(center * center, -1, keepdims=True) * (1.0 / WIDTH) + 1e-05)
    unit = (center * scale).astype(low)
    unit_ref[...] = unit
    scale_ref[...] = jnp.broadcast_to(scale, scale_ref.shape)
    picks = end_picks(ends_ref[...], 1).astype(low)
    unit_end_ref[...] = mm(picks, unit).astype(low)
    stream_end_ref[...] = mm(picks, x).astype(low)


def norm_first(group, x, ends):
    steps = ends.shape[0] // BLOCK
    return pl.pallas_call(
        norm_body,
        out_shape=shapes(
            (x.shape, low), ((x.shape[0], 128), full), *[((ends.shape[0], WIDTH), low)] * 2
        ),
        grid_spec=pltpu.PrefetchScalarGridSpec(
            num_scalar_prefetch=1,
            grid=(steps,),
            in_specs=[
                pl.BlockSpec((TOKENS, WIDTH), lambda i, g: ((i + g[0] * (steps // 2)) % steps, 0)),
                pl.BlockSpec((BLOCK, 1), lambda i, g: (i, 0)),
            ],
            out_specs=[
                pl.BlockSpec((TOKENS, WIDTH), lambda i, g: (i, 0)),
                pl.BlockSpec((TOKENS, 128), lambda i, g: (i, 0)),
                pl.BlockSpec((BLOCK, WIDTH), lambda i, g: (i, 0)),
                pl.BlockSpec((BLOCK, WIDTH), lambda i, g: (i, 0)),
            ],
        ),
        name="norm_first",
    )(group, x, ends)


def head_mask(head):
    return lax.broadcasted_iota(jnp.int32, (BLOCK, COLS), 1) // HEAD == head


def head_stack(x):
    zero = jnp.zeros_like(x)
    return jnp.concatenate([jnp.where(head_mask(h), x, zero) for h in range(HEADS_HERE)], 0)


def head_fold(x):
    out = jnp.zeros((BLOCK, COLS), full)
    for h in range(HEADS_HERE):
        out = jnp.where(head_mask(h), x[h * BLOCK : (h + 1) * BLOCK], out)
    return out


def stack_grid():
    row = lax.broadcasted_iota(jnp.int32, (STACK, TOKENS), 0) & (BLOCK - 1)
    token = lax.broadcasted_iota(jnp.int32, (STACK, TOKENS), 1)
    return row, token


def step_rows(i):
    return pl.ds(pl.multiple_of(i * BLOCK, BLOCK), BLOCK)


def attend_body(
    unit_ref, unit_end_ref, ends_ref, kv_ref, qo_ref, mixed_ref, p_ref, q_ref, att_ref, out_ref
):
    i = pl.program_id(0)

    @pl.when(i == 0)
    def _():
        q_ref[...] = mm(unit_end_ref[...], qo_ref[:, :COLS]).astype(low)

    mixed = mm(unit_ref[...], kv_ref[...]).astype(low)
    mixed_ref[...] = mixed
    scores = mm_nt(head_stack(q_ref[step_rows(i), :]), mixed[:, :COLS]) * SCORE_SCALE
    row, token = stack_grid()
    ends = jnp.concatenate([ends_ref[...]] * HEADS_HERE, 0)
    allowed = (token >= row * LENGTH) & (token <= row * LENGTH + ends)
    scores = jnp.where(allowed, scores, -1e30)
    weight = jnp.exp(scores - jnp.max(scores, 1, keepdims=True))
    probs = weight / jnp.sum(weight, 1, keepdims=True)
    p_ref[...] = probs
    att_ref[step_rows(i), :] = head_fold(mm(probs.astype(low), mixed[:, COLS:])).astype(low)

    @pl.when(i == pl.num_programs(0) - 1)
    def _():
        out_ref[...] = mm_nt(att_ref[...], qo_ref[:, COLS:]).astype(low)


def attend(unit, unit_end, ends, kv, qo):
    count = ends.shape[0]
    steps = count // BLOCK
    return pl.pallas_call(
        attend_body,
        grid=(steps,),
        out_shape=shapes(
            ((count * LENGTH, 2 * COLS), low),
            ((steps * STACK, TOKENS), full),
            *[((count, COLS), low)] * 2,
            ((count, WIDTH), low),
        ),
        in_specs=[
            pl.BlockSpec((TOKENS, WIDTH), lambda i: (i, 0)),
            whole_block((count, WIDTH)),
            pl.BlockSpec((BLOCK, 1), lambda i: (i, 0)),
            whole_block(kv.shape),
            whole_block(qo.shape),
        ],
        out_specs=[
            pl.BlockSpec((TOKENS, 2 * COLS), lambda i: (i, 0)),
            pl.BlockSpec((STACK, TOKENS), lambda i: (i, 0)),
            whole_block((count, COLS)),
            whole_block((count, COLS)),
            whole_block((count, WIDTH)),
        ],
        name="attend",
    )(unit, unit_end, ends, kv, qo)


def lane_group():
    return lax.broadcasted_iota(jnp.int32, (BLOCK, 128), 1) // (2 * LENGTH)


def attend_back_body(
    core_ref, d_mid_ref, d_att_ref, unit_ref, unit_end_ref, mixed_ref, p_ref, q_ref, att_ref,
    keep_ref, send_ref, d_mixed_ref, dq_ref, small_ref, sum_ref,
):
    i = pl.program_id(0)
    count = dq_ref.shape[0]

    @pl.when(i == 0)
    def _():
        sum_ref[...] = jnp.zeros_like(sum_ref)

    probs = p_ref[...]
    probs_low = probs.astype(low)
    queries = head_stack(q_ref[step_rows(i), :])
    d_att = head_stack(d_att_ref[step_rows(i), :])
    d_probs = mm_nt(d_att, mixed_ref[:, COLS:])
    d_scores = probs * (d_probs - jnp.sum(probs * d_probs, 1, keepdims=True))
    d_scores = (d_scores * SCORE_SCALE).astype(low)
    dq_ref[step_rows(i), :] = head_fold(mm(d_scores, mixed_ref[:, :COLS])).astype(low)
    d_mixed = jnp.concatenate(
        [mm_tn(d_scores, queries).astype(low), mm_tn(probs_low, d_att).astype(low)], 1
    )
    d_mixed_ref[...] = d_mixed
    spot = lax.broadcasted_iota(jnp.int32, (TOKENS, 128), 0) & (LENGTH - 1)
    lane = lax.broadcasted_iota(jnp.int32, (TOKENS, 128), 1) & (2 * LENGTH - 1)
    squeezed = mm(probs_low, (spot == lane).astype(low))
    squeezed += mm(d_scores, (spot + LENGTH == lane).astype(low))
    for first in (0, 4):
        out = jnp.zeros((BLOCK, 128), full)
        for h in range(first, min(first + 4, HEADS_HERE)):
            out = jnp.where(lane_group() == h - first, squeezed[h * BLOCK : (h + 1) * BLOCK], out)
        place = pl.multiple_of((2 * i + first // 4) * BLOCK, BLOCK)
        small_ref[pl.ds(3 * count + place, BLOCK), :] = out.astype(low)
    sum_ref[...] += mm_tn(unit_ref[...], d_mixed)

    @pl.when(i == pl.num_programs(0) - 1)
    def _():
        first = core_ref[0] == 0
        d_queries = dq_ref[...]
        for piece in range(3):
            small_ref[piece * count : (piece + 1) * count] = d_queries[
                :, piece * 128 : (piece + 1) * 128
            ]
        g_mix = sum_ref[...].astype(low)
        g_query = mm_tn(unit_end_ref[...], d_queries).astype(low)
        g_back = mm_tn(d_mid_ref[...], att_ref[...]).astype(low)
        g_rest = jnp.concatenate([g_query, g_back], 1)
        keep_ref[...] = jnp.where(first, g_mix, g_rest)
        send_ref[...] = jnp.where(first, g_rest, g_mix)


def attend_back(core, d_mid, d_att, unit, unit_end, mixed, probs, queries, attended):
    count = d_mid.shape[0]
    steps = count // BLOCK
    return pl.pallas_call(
        attend_back_body,
        grid=(steps,),
        out_shape=shapes(
            *[((WIDTH, 2 * COLS), low)] * 2,
            ((count * LENGTH, 2 * COLS), low),
            ((count, COLS), low),
            ((3 * count + steps * 2 * BLOCK, 128), low),
        ),
        in_specs=[
            pl.BlockSpec(memory_space=pltpu.SMEM),
            whole_block((count, WIDTH)),
            whole_block((count, COLS)),
            pl.BlockSpec((TOKENS, WIDTH), lambda i: (i, 0)),
            whole_block((count, WIDTH)),
            pl.BlockSpec((TOKENS, 2 * COLS), lambda i: (i, 0)),
            pl.BlockSpec((STACK, TOKENS), lambda i: (i, 0)),
            whole_block((count, COLS)),
            whole_block((count, COLS)),
        ],
        out_specs=[
            whole_block((WIDTH, 2 * COLS)),
            whole_block((WIDTH, 2 * COLS)),
            pl.BlockSpec((TOKENS, 2 * COLS), lambda i: (i, 0)),
            whole_block((count, COLS)),
            whole_block((3 * count + steps * 2 * BLOCK, 128)),
        ],
        scratch_shapes=[pltpu.VMEM((WIDTH, 2 * COLS), full)],
        name="attend_back",
    )(core, d_mid, d_att, unit, unit_end, mixed, probs, queries, attended)


def place_rows(picks, rows):
    high = rows.astype(low)
    rest = (rows - high.astype(full)).astype(low)
    return mm_tn(picks, jnp.concatenate([high, rest], 0))


def captions_body(
    part, group_ref, ends_ref, unit_ref, scale_ref, d_mid_ref, d_mixed_ref, dq_ref,
    q_far_ref, d_att_far_ref, small_far_ref, kv_ref, qo_ref, kv_far_ref, qo_far_ref, *refs,
):
    out_ref, inner_end_ref = refs[-2:]
    i = pl.program_id(0)
    half = dq_ref.shape[0]
    far_start = (1 - part) * half

    @pl.when(i == 0)
    def _():
        dq_far = jnp.concatenate(
            [
                small_far_ref[piece * 2 * half + far_start : piece * 2 * half + far_start + half]
                for piece in range(3)
            ],
            1,
        )
        inner_end_ref[...] = mm_nt(dq_ref[...], qo_ref[:, :COLS]) + mm_nt(
            dq_far, qo_far_ref[:, :COLS]
        )

    row, token = stack_grid()
    own_caption = token // LENGTH == row
    lane = lax.broadcasted_iota(jnp.int32, (128, TOKENS), 0) & (2 * LENGTH - 1)
    spot = lax.broadcasted_iota(jnp.int32, (128, TOKENS), 1) & (LENGTH - 1)
    zero = jnp.zeros((BLOCK, 128), low)
    place = pl.multiple_of(6 * half + 2 * far_start + 2 * BLOCK * i, 2 * BLOCK)
    packed = small_far_ref[pl.ds(place, 2 * BLOCK), :]
    pair = jnp.concatenate(
        [
            jnp.where(lane_group() == h % 4, packed[h // 4 * BLOCK : (h // 4 + 1) * BLOCK], zero)
            for h in range(HEADS_HERE)
        ],
        0,
    )
    probs = jnp.where(own_caption, mm(pair, (spot == lane).astype(low)), 0.0).astype(low)
    d_scores = jnp.where(
        own_caption, mm(pair, (spot + LENGTH == lane).astype(low)), 0.0
    ).astype(low)
    d_mixed = jnp.concatenate(
        [
            mm_tn(d_scores, head_stack(q_far_ref[step_rows(i), :])).astype(low),
            mm_tn(probs, head_stack(d_att_far_ref[step_rows(i), :])).astype(low),
        ],
        1,
    )
    inner = mm_nt(d_mixed_ref[...], kv_ref[...]) + mm_nt(d_mixed, kv_far_ref[...])
    picks = end_picks(ends_ref[...], 2).astype(low)
    inner += place_rows(picks, inner_end_ref[step_rows(i), :])
    unit = unit_ref[...].astype(full)
    flat = jnp.sum(inner, -1, keepdims=True) * (1.0 / WIDTH)
    tilt = jnp.sum(inner * unit, -1, keepdims=True) * (1.0 / WIDTH)
    out_ref[...] = place_rows(picks, d_mid_ref[...]) + scale_ref[:, :1] * (
        inner - flat - unit * tilt
    )


def captions_back(
    part, group, ends, unit, scale, d_mid, d_mixed, dq, q_far, d_att_far, small_far, kv, qo,
    kv_far, qo_far, done=None,
):
    count = ends.shape[0]
    steps = count // BLOCK
    half = steps // 2
    start = part * half
    own_half = pl.BlockSpec((count // 2, COLS), lambda i, g: (part, 0))
    far_half = pl.BlockSpec((count // 2, COLS), lambda i, g: (1 - part, 0))
    operands = [
        group, ends, unit, scale, d_mid, d_mixed, dq, q_far, d_att_far, small_far, kv, qo,
        kv_far, qo_far,
    ]
    in_specs = [
        pl.BlockSpec((BLOCK, 1), lambda i, g: (i + start, 0)),
        pl.BlockSpec((TOKENS, WIDTH), lambda i, g: (i + start, 0)),
        pl.BlockSpec((TOKENS, 128), lambda i, g: (i + start, 0)),
        pl.BlockSpec((BLOCK, WIDTH), lambda i, g: (i + start, 0)),
        pl.BlockSpec((TOKENS, 2 * COLS), lambda i, g: (i + start, 0)),
        own_half,
        far_half,
        far_half,
        whole_block(small_far.shape),
    ] + [whole_block(kv.shape)] * 4
    aliases = {}
    if done is not None:
        aliases = {len(operands): 0}
        operands.append(done)
        in_specs.append(pl.BlockSpec(memory_space=pl.ANY))
    return pl.pallas_call(
        functools.partial(captions_body, part),
        out_shape=jax.ShapeDtypeStruct(unit.shape, full),
        grid_spec=pltpu.PrefetchScalarGridSpec(
            num_scalar_prefetch=1,
            grid=(half,),
            in_specs=in_specs,
            out_specs=pl.BlockSpec(
                (TOKENS, WIDTH), lambda i, g: ((i + start + g[0] * half) % steps, 0)
            ),
            scratch_shapes=[pltpu.VMEM((count // 2, WIDTH), full)],
        ),
        input_output_aliases=aliases,
        name="captions_back",
    )(*operands)


def local(
    captions,
    image_cache,
    send_order,
    arrive_order,
    counts,
    keep_mask,
    end_pos,
    w_qkv,
    w_out,
    w_up,
    w_down,
    w_proj,
    ln1_gain,
    ln2_gain,
):
    plane = Plane()
    core = plane.core
    group = lax.axis_index("mp")
    spread = plane.count
    rows_dev, length, width = captions.shape
    rows = w_out.shape[0]
    per_peer = rows_dev // spread
    hidden = w_up.shape[1] // 2
    quarter = width // 4
    core_flag = core.reshape(1).astype(jnp.int32)
    group_flag = group.reshape(1).astype(jnp.int32)

    packed = pack(
        core_flag,
        w_qkv.transpose(1, 0, 2),
        w_out,
        w_up,
        w_down,
        w_proj,
        ln1_gain[None],
        ln2_gain[None],
    )
    flipped = jnp.concatenate([end_pos, end_pos], 0)
    ends = lax.dynamic_slice_in_dim(flipped, group * CAP_DEV, rows_dev, 0)[:, None]
    wide = width // 2

    def pictures_of_batch(outgoing):
        incoming = lax.all_to_all(outgoing, "dp", split_axis=0, concat_axis=0, tiled=True)
        own_arrive = lax.dynamic_slice_in_dim(arrive_order[0], group * CAP_DEV, CAP_DEV, 0)
        take_in = (own_arrive[:, None] == places[None, :]).astype(low)
        pictures = mm(take_in, incoming.reshape(rows_dev, width)).astype(low)
        mine = pick(core, pictures[:, :wide], pictures[:, wide:])
        send = pick(core, pictures[:, wide:], pictures[:, :wide])
        return mine, send

    cached = image_cache.astype(full)
    cached = (cached * lax.rsqrt(jnp.sum(cached * cached, -1, keepdims=True) + 1e-06)).astype(low)
    places = jnp.arange(rows_dev, dtype=jnp.int32)
    hand_out = (send_order[0][:, None] == places[None, :]).astype(low)
    outgoing = mm(hand_out, cached).astype(low).reshape(spread, per_peer, width)

    def first_parts(stream):
        return norm_first(group_flag, stream.reshape(rows_dev * length, width), ends)

    def attention_of(kv, qo, parts):
        return attend(parts[0], parts[2], ends, kv, qo)

    main = rows if plane.fast else CAP_DEV
    spare = CAP_DEV - main
    if plane.fast:

        def join(feed, embed, half):
            parts = [half[main:, i * 128 : (i + 1) * 128] for i in range(wide // 128)]
            return jnp.concatenate([feed, embed, half[:main], jnp.concatenate(parts, 0)], 1)

        block = plane.join_cores(packed[0], packed[1])
        pictures = pictures_of_batch(after(outgoing, plane.arrived))
        up = plane.shift_depth(block, 1)
        down = plane.shift_depth(block, -1)
        up = after(up, pictures[0])
        far = plane.shift_depth(up, 1)
        parts = first_parts(after(captions, up))
        far = after(far, parts[0])
        (mix_own,) = plane.spread_blocks(
            ((0, block), (1, up), (-1, down), (2, far)), (0, 2 * COLS)
        )
        mix_other = plane.swap_core(mix_own)
        far_own = swap_group(mix_own)

        block = plane.join_cores(
            join(packed[2], packed[4], pictures[0]), join(packed[3], packed[5], pictures[1])
        )
        block = after(block, far)
        one = plane.shift_depth(block, 1)
        two = plane.shift_depth(one, 1)
        kv = pick(core, mix_own, mix_other)
        qo = pick(core, mix_other, mix_own)
        attending = attention_of(kv, after(qo, one), parts)
        two = after(two, attending[-1])
        three = plane.shift_depth(two, 1)
        cut = 2 * hidden
        feeds, third = plane.spread_blocks(
            ((0, block), (1, one), (2, two), (3, three)), (0, cut, cut + 2 * wide + 128)
        )
        third_other = plane.swap_core(third)

        def images(x):
            extra = x[:, 2 * wide :].reshape(spread, wide // 128, spare, 128)
            extra = extra.transpose(0, 2, 1, 3).reshape(spread * spare, wide)
            return jnp.concatenate([x[:, wide : 2 * wide], extra], 0)

        image_halves = images(third), images(third_other)
        embed_halves = third[:, :wide], third_other[:, :wide]
    else:
        pictures = pictures_of_batch(outgoing)
        parts = first_parts(captions)
        mix_own = plane.gather_plain(packed[0], packed[1])
        mix_other = plane.swap_core(mix_own)
        far_own = swap_group(mix_own)
        kv = pick(core, mix_own, mix_other)
        qo = pick(core, mix_other, mix_own)
        attending = attention_of(kv, qo, parts)
        feeds = plane.gather_plain(packed[2], packed[3])
        image_half = plane.gather_plain(*pictures)
        image_halves = image_half, plane.swap_core(image_half)
        embed_half = plane.gather_plain(packed[4], packed[5])
        embed_halves = embed_half, plane.swap_core(embed_half)
    unit, scale, unit_end, stream_end = parts
    mixed, probs, queries, attended, attention = attending
    far_other = plane.swap_core(far_own)
    kv_far = pick(core, far_own, far_other)
    qo_far = pick(core, far_other, far_own)

    def sides(pair):
        return jnp.concatenate([pick(core, *pair), pick(core, pair[1], pair[0])], 1)

    pictures_all = sides(image_halves)
    w_embed = sides(embed_halves)

    stream_near = swap_near(stream_end, 2)
    from_group, from_core, from_both = [swap_near(attention, flip) for flip in (1, 2, 3)]
    attention = jnp.concatenate([attention, from_core], 0).astype(full)
    attention = attention + jnp.concatenate(
        [roll_rows(from_group), roll_rows(from_both)], 0
    ).astype(full)
    middle = jnp.concatenate([stream_end, stream_near], 0).astype(full) + attention
    unit_second, scale_second = norm_rows(middle)
    second_low = unit_second.astype(low)
    feeds = after(feeds, far_own)
    w_raise = feeds[:, :hidden]
    w_lower = feeds[:, hidden:]
    active, slope = gelu_parts(mm(second_low, w_raise))
    active = active.astype(low)
    lowered = mm_nt(active, w_lower).astype(low)
    feed = lowered[:CAP_DEV].astype(full)
    for flip in (1, 2, 3):
        part = swap_near(lowered[flip * CAP_DEV : (flip + 1) * CAP_DEV], flip)
        feed = feed + part.astype(full)
    pooled = (middle[:CAP_DEV] + feed).astype(low)
    embedding = mm(pooled, w_embed)
    inverse = lax.rsqrt(jnp.sum(embedding * embedding, -1, keepdims=True) + 1e-06)
    unit_text = embedding * inverse
    text_low = unit_text.astype(low)

    keep_rows = keep_mask.reshape(spread, MICRO, CAP_DEV) == 1
    filled = jnp.arange(CAP_DEV, dtype=jnp.int32)[None, None, :] < counts[:, :, None]
    valid = keep_rows & filled
    total_valid = jnp.sum(valid.astype(full))
    batch_valid = lax.dynamic_index_in_dim(valid, group, 1, False)
    own_valid = lax.dynamic_index_in_dim(batch_valid, plane.index, 0, False)
    batch_valid = jnp.concatenate(
        [batch_valid[:, :main].reshape(-1), batch_valid[:, main:].reshape(-1)]
    )
    sims = LOGIT_SCALE * mm_nt(text_low, pictures_all)
    allowed = own_valid[:, None] & batch_valid[None, :]
    weight = jnp.where(allowed, jnp.exp(sims), 0.0)
    row_sum = jnp.sum(weight, 1)
    place = jnp.arange(CAP_DEV, dtype=jnp.int32)
    slot = jnp.where(
        place < main,
        plane.index * main + place,
        spread * main + plane.index * spare + place - main,
    )
    target = (
        jnp.arange(spread * CAP_DEV, dtype=jnp.int32)[None, :] == slot[:, None]
    ) & own_valid[:, None]
    row_safe = jnp.where(own_valid, row_sum, 1.0)
    row_part = 0.5 * jnp.sum(jnp.log(row_safe)) - jnp.sum(jnp.where(target, sims, 0.0))
    col_part = jnp.sum(weight, 0)
    totals = jnp.concatenate([col_part, jnp.full((128,), 1.0 / 128, full) * row_part])
    totals = plane.total(totals.reshape(-1, 128)).reshape(-1)
    col_sum = totals[: spread * CAP_DEV]
    col_safe = jnp.where(batch_valid, col_sum, 1.0)
    objective = jnp.sum(totals[spread * CAP_DEV :]) + 0.5 * jnp.sum(jnp.log(col_safe))
    objective = jnp.full((8, 128), objective)
    loss = (objective + swap_group(objective))[0, 0] / total_valid
    d_sims = (
        weight * (0.5 / row_safe[:, None] + 0.5 / col_safe[None, :]) - target.astype(full)
    ).astype(low)
    d_unit = LOGIT_SCALE * mm(d_sims, pictures_all)
    d_embed = (
        (d_unit - unit_text * jnp.sum(unit_text * d_unit, -1, keepdims=True)) * inverse
    ).astype(low)

    pooled_all = jnp.concatenate([pooled] + [swap_near(pooled, flip) for flip in (1, 2, 3)], 0)
    d_embed_all = jnp.concatenate([d_embed] + [swap_near(d_embed, flip) for flip in (1, 2, 3)], 0)
    d_pooled = mm_nt(d_embed_all, w_embed)
    d_out_low = d_pooled.astype(low)
    g_lower = mm_tn(d_out_low, active).astype(low)
    d_raised = (mm(d_out_low, w_lower) * slope).astype(low)
    g_raise = mm_tn(second_low, d_raised).astype(low)
    d_second = mm_nt(d_raised, w_raise).astype(low)
    d_embed_half = pick(group, d_embed_all[:, :wide], d_embed_all[:, wide:])
    d_embed_here = pick(core, d_embed_half[:, :quarter], d_embed_half[:, quarter:])
    g_embed = mm_tn(pooled_all, d_embed_here).astype(low)
    lower_quad = plane.scatter_side(jnp.concatenate([g_lower, g_embed], 1))
    raise_quad = plane.scatter_side(g_raise)
    queries_far = swap_group(queries)
    inner = d_second[:rows_dev].astype(full)
    inner = inner + roll_rows(swap_near(d_second[:rows_dev], 1)).astype(full)
    inner = inner + swap_near(d_second[rows_dev:], 2).astype(full)
    inner = inner + roll_rows(swap_near(d_second[rows_dev:], 3)).astype(full)
    d_middle = d_pooled[:rows_dev] + norm_back(
        inner, unit_second[:rows_dev], scale_second[:rows_dev]
    )

    d_middle_low = d_middle.astype(low)
    d_attended = mm(d_middle_low, qo[:, COLS:]).astype(low)
    d_attended_far = swap_group(d_attended)
    back_start = after(d_middle_low, lower_quad) if plane.fast else d_middle_low
    g_keep, g_send, d_mixed, d_queries, small = attend_back(
        core_flag, back_start, d_attended, unit, unit_end, mixed, probs, queries, attended
    )
    small_far = swap_group(small)
    operands = (
        unit, scale, d_middle, d_mixed, d_queries, queries_far, d_attended_far, small_far, kv, qo,
        kv_far, qo_far,
    )
    halves = []

    def first_half(plane):
        first_ends = after(ends, raise_quad, plane.pair)
        halves.append(captions_back(0, group_flag, first_ends, *operands))
        return halves[0]

    mix_quad = plane.scatter_side(g_keep, g_send, first_half)
    if not plane.fast:
        halves.append(captions_back(0, group_flag, ends, *operands))
    lower_sum = plane.scatter_core(plane.scatter_depth(lower_quad))
    raise_sum = plane.scatter_core(plane.scatter_depth(raise_quad))
    second_ends = after(ends, mix_quad) if plane.fast else ends
    grad_captions = captions_back(1, group_flag, second_ends, *operands, done=halves[0])
    mix_total = plane.scatter_depth(mix_quad)
    if plane.fast:
        mix_total, grad_captions = lax.optimization_barrier((mix_total, grad_captions))
    mix_sum = plane.scatter_core(mix_total)
    grad_captions = grad_captions.reshape(rows_dev, length, width)

    grad_down = jnp.concatenate([part[:, :hidden] for part in lower_sum], 1)
    proj_own = jnp.concatenate([part[:, hidden:] for part in lower_sum], 1)
    proj_far = swap_group(proj_own)
    grad_proj = pick(
        group,
        jnp.concatenate([proj_own, proj_far], 1),
        jnp.concatenate([proj_far, proj_own], 1),
    )
    grad_out = mix_sum[1][:, COLS:]
    unit_mix = jnp.stack([mix_sum[1][:, :COLS], mix_sum[0][:, :COLS], mix_sum[0][:, COLS:]], 1)
    grad_qkv = unit_mix * ln1_gain[:, None, None]
    raised_sum = jnp.concatenate(raise_sum, 1)
    grad_up = raised_sum * ln2_gain[:, None]
    gains = jnp.stack(
        [
            jnp.sum(unit_mix * w_qkv.astype(full), (1, 2)),
            jnp.sum(raised_sum * w_up.astype(full), 1),
        ]
    )
    gains = gains + swap_group(gains)
    return (
        loss,
        grad_captions,
        grad_qkv,
        grad_out,
        grad_up,
        grad_down,
        grad_proj,
        gains[0],
        gains[1],
    )


def solution(mesh):
    return jax.shard_map(
        local,
        mesh=mesh,
        in_specs=(
            P("dp", None, None),
            P("dp", None),
            P("dp", None),
            P("dp", None),
            P(),
            P(),
            P("dp"),
            P("dp", None, "mp"),
            P("dp", "mp"),
            P("dp", "mp"),
            P("dp", "mp"),
            P("dp", None),
            P("dp"),
            P("dp"),
        ),
        out_specs=(
            P(),
            P("dp", None, None),
            P("dp", None, "mp"),
            P("dp", "mp"),
            P("dp", "mp"),
            P("dp", "mp"),
            P("dp", None),
            P("dp"),
            P("dp"),
        ),
        check_vma=False,
    )
```

```python
import functools
import math

import jax
import jax.numpy as jnp
from jax import lax
from jax.experimental import pallas as pl
from jax.experimental.pallas import tpu as pltpu
from jax.sharding import PartitionSpec as P

HEAD = 64
MICRO = 2
CAP_DEV = 64
LOGIT_SCALE = 40.0
SCORE_SCALE = 1.0 / math.sqrt(HEAD)
LENGTH = 16
WIDTH = 768
HEADS_HERE = 6
COLS = HEADS_HERE * HEAD
BLOCK = 16
TOKENS = BLOCK * LENGTH
STACK = HEADS_HERE * BLOCK

low = jnp.bfloat16
full = jnp.float32


def mm(a, b):
    return lax.dot_general(a, b, (((1,), (0,)), ((), ())), preferred_element_type=full)


def mm_nt(a, b):
    return lax.dot_general(a, b, (((1,), (1,)), ((), ())), preferred_element_type=full)


def mm_tn(a, b):
    return lax.dot_general(a, b, (((0,), (0,)), ((), ())), preferred_element_type=full)


def pick(flag, when_zero, when_one):
    return jnp.where(flag == 0, when_zero, when_one)


class Plane:
    def __init__(self):
        self.count = lax.axis_size("dp")
        self.index = lax.axis_index("dp")
        self.core = self.index % 2
        self.side = (self.index // 2) % 2
        self.depth = self.index // 4
        self.fast = self.count == 16

    def swap_core(self, x):
        return lax.ppermute(x, "dp", [(i, i ^ 1) for i in range(self.count)])

    def swap_side(self, x):
        return lax.ppermute(x, "dp", [(i, i ^ 2) for i in range(self.count)])

    def shift_depth(self, x, step):
        return lax.ppermute(
            x, "dp", [(i, (i + 4 * step) % self.count) for i in range(self.count)]
        )

    def join_cores(self, mine, arrived):
        rows, width = mine.shape
        block = jnp.zeros((2, rows, width), mine.dtype)
        block = lax.dynamic_update_slice(block, mine[None], (self.core, 0, 0))
        block = lax.dynamic_update_slice(block, arrived[None], (1 - self.core, 0, 0))
        return block.reshape(2 * rows, width)

    def place(self, wholes, cuts, step, here, across):
        spot = ((self.depth - step) % 4) * 2
        for block, at in ((here, spot + self.side), (across, spot + 1 - self.side)):
            wholes = [
                lax.dynamic_update_slice(whole, block[None, :, start:end], (at, 0, 0))
                for whole, start, end in zip(wholes, cuts, cuts[1:])
            ]
        return wholes

    def empty(self, rows, cuts):
        return [
            jnp.zeros((self.count // 2, rows, end - start), low)
            for start, end in zip(cuts, cuts[1:])
        ]

    def gather_plain(self, mine, send):
        zero_all = lax.all_gather(pick(self.core, mine, send), "dp", axis=0, tiled=True)
        one_all = lax.all_gather(pick(self.core, send, mine), "dp", axis=0, tiled=True)
        return pick(self.core, zero_all, one_all)

    def halve(self, x, axis, bit):
        spot = (self.index // bit) % 2
        stay = lax.dynamic_index_in_dim(x, spot, axis, False)
        leave = lax.dynamic_index_in_dim(x, 1 - spot, axis, False)
        return stay, lax.ppermute(leave, "dp", [(i, i ^ bit) for i in range(self.count)])

    def scatter_plain(self, keep, send=None):
        if send is None:
            send = jnp.zeros_like(keep)
        halves = (pick(self.core, keep, send), pick(self.core, send, keep))
        return [
            lax.psum_scatter(half, "dp", scatter_dimension=0, tiled=True).astype(full)
            for half in halves
        ]

    def scatter_core(self, total):
        rows, width = total.shape[0] // 2, total.shape[1]
        total = total.reshape(2, rows, width)
        mine = lax.dynamic_index_in_dim(total, self.core, 0, False)
        arrived = self.swap_core(lax.dynamic_index_in_dim(total, 1 - self.core, 0, False))
        return pick(self.core, mine, arrived), pick(self.core, arrived, mine)

    def total(self, x):
        if not self.fast:
            return lax.psum(x, "dp")
        x = (x + self.swap_core(x)) + (self.swap_side(x) + self.swap_both(x))
        return x + sum(self.shift_depth(x, step) for step in range(1, 4))

    def swap_both(self, x):
        return lax.ppermute(x, "dp", [(i, i ^ 3) for i in range(self.count)])


def swap_near(x, flip):
    size = 2 * lax.axis_size("dp")
    return lax.ppermute(x, ("dp", "mp"), [(i, i ^ flip) for i in range(size)])


def swap_group(x):
    return swap_near(x, 1)


def after(x, *others):
    return lax.optimization_barrier((x, *others))[0]


def joint(*values):
    return lax.optimization_barrier(values)


def add_low(pair):
    return (pair[0].astype(full) + pair[1].astype(full)).astype(low)


def roll_rows(x):
    half = x.shape[0] // 2
    return jnp.concatenate([x[half:], x[:half]], 0)


def norm_rows(inputs):
    center = inputs - jnp.mean(inputs, -1, keepdims=True)
    scale = lax.rsqrt(jnp.mean(center * center, -1, keepdims=True) + 1e-05)
    return center * scale, scale


def norm_back(inner, unit, scale):
    return scale * (
        inner
        - jnp.mean(inner, -1, keepdims=True)
        - unit * jnp.mean(inner * unit, -1, keepdims=True)
    )


def gelu_parts(raised):
    cumulative = 0.5 * (1.0 + lax.erf(raised * 0.7071067811865476))
    slope = cumulative + raised * jnp.exp(-0.5 * raised * raised) * 0.3989422804014327
    return raised * cumulative, slope


def whole_block(shape):
    return pl.BlockSpec(shape, lambda *_: (0,) * len(shape))


def shapes(*items):
    return [jax.ShapeDtypeStruct(shape, kind) for shape, kind in items]


def pack_body(core_ref, mix_ref, back_ref, raise_ref, lower_ref, embed_ref, g1_ref, g2_ref, *outs):
    first = core_ref[0] == 0
    rows = back_ref.shape[0]
    spot = lax.broadcasted_iota(jnp.int32, (rows, rows), 0)
    diagonal = spot == lax.broadcasted_iota(jnp.int32, (rows, rows), 1)
    g1, g2 = [
        jnp.sum(jnp.where(diagonal, ref[...], 0.0), 1, keepdims=True) for ref in (g1_ref, g2_ref)
    ]

    def part(index):
        return (mix_ref[index].astype(full) * g1).astype(low)

    def put(index, columns, zero, one):
        outs[index][:, columns] = jnp.where(first, zero, one)
        outs[index + 1][:, columns] = jnp.where(first, one, zero)

    put(0, slice(0, COLS), part(1), part(0))
    put(0, slice(COLS, 2 * COLS), part(2), back_ref[...])
    hidden = raise_ref.shape[1] // 2
    raised = (raise_ref[...].astype(full) * g2).astype(low)
    put(2, slice(0, hidden), raised[:, :hidden], raised[:, hidden:])
    put(2, slice(hidden, 2 * hidden), lower_ref[:, :hidden], lower_ref[:, hidden:])
    put(4, slice(0, COLS), embed_ref[:, :COLS], embed_ref[:, COLS:])


def pack(core, w_qkv, w_out, w_up, w_down, w_proj, g1, g2):
    rows, hidden = w_up.shape
    vmem = pl.BlockSpec(memory_space=pltpu.VMEM)
    return pl.pallas_call(
        pack_body,
        out_shape=shapes(
            *[((rows, 2 * COLS), low)] * 2, *[((rows, hidden), low)] * 2, *[((rows, COLS), low)] * 2
        ),
        in_specs=[pl.BlockSpec(memory_space=pltpu.SMEM)] + [vmem] * 7,
        out_specs=[vmem] * 6,
        name="pack",
    )(core, w_qkv, w_out, w_up, w_down, w_proj, g1, g2)


def end_picks(ends, copies):
    ends = jnp.concatenate([ends] * copies, 0)
    shape = (copies * BLOCK, TOKENS)
    row = lax.broadcasted_iota(jnp.int32, shape, 0) & (BLOCK - 1)
    return lax.broadcasted_iota(jnp.int32, shape, 1) == row * LENGTH + ends


def norm_body(group_ref, x_ref, ends_ref, unit_ref, scale_ref, unit_end_ref, stream_end_ref):
    x = x_ref[...]
    stream = x.astype(full)
    center = stream - jnp.sum(stream, -1, keepdims=True) * (1.0 / WIDTH)
    scale = lax.rsqrt(jnp.sum(center * center, -1, keepdims=True) * (1.0 / WIDTH) + 1e-05)
    unit = (center * scale).astype(low)
    unit_ref[...] = unit
    scale_ref[...] = jnp.broadcast_to(scale, scale_ref.shape)
    picks = end_picks(ends_ref[...], 1).astype(low)
    unit_end_ref[...] = mm(picks, unit).astype(low)
    stream_end_ref[...] = mm(picks, x).astype(low)


def norm_first(group, x, ends):
    steps = ends.shape[0] // BLOCK
    return pl.pallas_call(
        norm_body,
        out_shape=shapes(
            (x.shape, low), ((x.shape[0], 128), full), *[((ends.shape[0], WIDTH), low)] * 2
        ),
        grid_spec=pltpu.PrefetchScalarGridSpec(
            num_scalar_prefetch=1,
            grid=(steps,),
            in_specs=[
                pl.BlockSpec((TOKENS, WIDTH), lambda i, g: ((i + g[0] * (steps // 2)) % steps, 0)),
                pl.BlockSpec((BLOCK, 1), lambda i, g: (i, 0)),
            ],
            out_specs=[
                pl.BlockSpec((TOKENS, WIDTH), lambda i, g: (i, 0)),
                pl.BlockSpec((TOKENS, 128), lambda i, g: (i, 0)),
                pl.BlockSpec((BLOCK, WIDTH), lambda i, g: (i, 0)),
                pl.BlockSpec((BLOCK, WIDTH), lambda i, g: (i, 0)),
            ],
        ),
        name="norm_first",
    )(group, x, ends)


def head_mask(head):
    return lax.broadcasted_iota(jnp.int32, (BLOCK, COLS), 1) // HEAD == head


def head_stack(x):
    zero = jnp.zeros_like(x)
    return jnp.concatenate([jnp.where(head_mask(h), x, zero) for h in range(HEADS_HERE)], 0)


def head_fold(x):
    out = jnp.zeros((BLOCK, COLS), full)
    for h in range(HEADS_HERE):
        out = jnp.where(head_mask(h), x[h * BLOCK : (h + 1) * BLOCK], out)
    return out


def stack_grid():
    row = lax.broadcasted_iota(jnp.int32, (STACK, TOKENS), 0) & (BLOCK - 1)
    token = lax.broadcasted_iota(jnp.int32, (STACK, TOKENS), 1)
    return row, token


def step_rows(i):
    return pl.ds(pl.multiple_of(i * BLOCK, BLOCK), BLOCK)


def attend_body(
    unit_ref, unit_end_ref, ends_ref, kv_ref, qo_ref, mixed_ref, p_ref, q_ref, att_ref, out_ref
):
    i = pl.program_id(0)

    @pl.when(i == 0)
    def _():
        q_ref[...] = mm(unit_end_ref[...], qo_ref[:, :COLS]).astype(low)

    mixed = mm(unit_ref[...], kv_ref[...]).astype(low)
    mixed_ref[...] = mixed
    scores = mm_nt(head_stack(q_ref[step_rows(i), :]), mixed[:, :COLS]) * SCORE_SCALE
    row, token = stack_grid()
    ends = jnp.concatenate([ends_ref[...]] * HEADS_HERE, 0)
    allowed = (token >= row * LENGTH) & (token <= row * LENGTH + ends)
    scores = jnp.where(allowed, scores, -1e30)
    weight = jnp.exp(scores - jnp.max(scores, 1, keepdims=True))
    probs = weight / jnp.sum(weight, 1, keepdims=True)
    p_ref[...] = probs
    att_ref[step_rows(i), :] = head_fold(mm(probs.astype(low), mixed[:, COLS:])).astype(low)

    @pl.when(i == pl.num_programs(0) - 1)
    def _():
        out_ref[...] = mm_nt(att_ref[...], qo_ref[:, COLS:]).astype(low)


def attend(unit, unit_end, ends, kv, qo):
    count = ends.shape[0]
    steps = count // BLOCK
    return pl.pallas_call(
        attend_body,
        grid=(steps,),
        out_shape=shapes(
            ((count * LENGTH, 2 * COLS), low),
            ((steps * STACK, TOKENS), full),
            *[((count, COLS), low)] * 2,
            ((count, WIDTH), low),
        ),
        in_specs=[
            pl.BlockSpec((TOKENS, WIDTH), lambda i: (i, 0)),
            whole_block((count, WIDTH)),
            pl.BlockSpec((BLOCK, 1), lambda i: (i, 0)),
            whole_block(kv.shape),
            whole_block(qo.shape),
        ],
        out_specs=[
            pl.BlockSpec((TOKENS, 2 * COLS), lambda i: (i, 0)),
            pl.BlockSpec((STACK, TOKENS), lambda i: (i, 0)),
            whole_block((count, COLS)),
            whole_block((count, COLS)),
            whole_block((count, WIDTH)),
        ],
        name="attend",
    )(unit, unit_end, ends, kv, qo)


def lane_group():
    return lax.broadcasted_iota(jnp.int32, (BLOCK, 128), 1) // (2 * LENGTH)


def attend_back_body(
    core_ref, d_mid_ref, d_att_ref, unit_ref, unit_end_ref, mixed_ref, p_ref, q_ref, att_ref,
    keep_ref, send_ref, d_mixed_ref, dq_ref, small_ref, sum_ref,
):
    i = pl.program_id(0)
    count = dq_ref.shape[0]

    @pl.when(i == 0)
    def _():
        sum_ref[...] = jnp.zeros_like(sum_ref)

    probs = p_ref[...]
    probs_low = probs.astype(low)
    queries = head_stack(q_ref[step_rows(i), :])
    d_att = head_stack(d_att_ref[step_rows(i), :])
    d_probs = mm_nt(d_att, mixed_ref[:, COLS:])
    d_scores = probs * (d_probs - jnp.sum(probs * d_probs, 1, keepdims=True))
    d_scores = (d_scores * SCORE_SCALE).astype(low)
    dq_ref[step_rows(i), :] = head_fold(mm(d_scores, mixed_ref[:, :COLS])).astype(low)
    d_mixed = jnp.concatenate(
        [mm_tn(d_scores, queries).astype(low), mm_tn(probs_low, d_att).astype(low)], 1
    )
    d_mixed_ref[...] = d_mixed
    spot = lax.broadcasted_iota(jnp.int32, (TOKENS, 128), 0) & (LENGTH - 1)
    lane = lax.broadcasted_iota(jnp.int32, (TOKENS, 128), 1) & (2 * LENGTH - 1)
    squeezed = mm(probs_low, (spot == lane).astype(low))
    squeezed += mm(d_scores, (spot + LENGTH == lane).astype(low))
    for first in (0, 4):
        out = jnp.zeros((BLOCK, 128), full)
        for h in range(first, min(first + 4, HEADS_HERE)):
            out = jnp.where(lane_group() == h - first, squeezed[h * BLOCK : (h + 1) * BLOCK], out)
        place = pl.multiple_of((2 * i + first // 4) * BLOCK, BLOCK)
        small_ref[pl.ds(3 * count + place, BLOCK), :] = out.astype(low)
    sum_ref[...] += mm_tn(unit_ref[...], d_mixed)

    @pl.when(i == pl.num_programs(0) - 1)
    def _():
        first = core_ref[0] == 0
        d_queries = dq_ref[...]
        for piece in range(3):
            small_ref[piece * count : (piece + 1) * count] = d_queries[
                :, piece * 128 : (piece + 1) * 128
            ]
        g_mix = sum_ref[...].astype(low)
        g_query = mm_tn(unit_end_ref[...], d_queries).astype(low)
        g_back = mm_tn(d_mid_ref[...], att_ref[...]).astype(low)
        g_rest = jnp.concatenate([g_query, g_back], 1)
        keep_ref[...] = jnp.where(first, g_mix, g_rest)
        send_ref[...] = jnp.where(first, g_rest, g_mix)


def attend_back(core, d_mid, d_att, unit, unit_end, mixed, probs, queries, attended):
    count = d_mid.shape[0]
    steps = count // BLOCK
    return pl.pallas_call(
        attend_back_body,
        grid=(steps,),
        out_shape=shapes(
            *[((WIDTH, 2 * COLS), low)] * 2,
            ((count * LENGTH, 2 * COLS), low),
            ((count, COLS), low),
            ((3 * count + steps * 2 * BLOCK, 128), low),
        ),
        in_specs=[
            pl.BlockSpec(memory_space=pltpu.SMEM),
            whole_block((count, WIDTH)),
            whole_block((count, COLS)),
            pl.BlockSpec((TOKENS, WIDTH), lambda i: (i, 0)),
            whole_block((count, WIDTH)),
            pl.BlockSpec((TOKENS, 2 * COLS), lambda i: (i, 0)),
            pl.BlockSpec((STACK, TOKENS), lambda i: (i, 0)),
            whole_block((count, COLS)),
            whole_block((count, COLS)),
        ],
        out_specs=[
            whole_block((WIDTH, 2 * COLS)),
            whole_block((WIDTH, 2 * COLS)),
            pl.BlockSpec((TOKENS, 2 * COLS), lambda i: (i, 0)),
            whole_block((count, COLS)),
            whole_block((3 * count + steps * 2 * BLOCK, 128)),
        ],
        scratch_shapes=[pltpu.VMEM((WIDTH, 2 * COLS), full)],
        name="attend_back",
    )(core, d_mid, d_att, unit, unit_end, mixed, probs, queries, attended)


def lower_back_body(flag_ref, d_out_ref, active_ref, both_ref, out_ref):
    hidden = active_ref.shape[1]
    quarter = WIDTH // 4
    out_ref[:, :hidden] = mm_tn(d_out_ref[...], active_ref[...]).astype(low)
    here = both_ref[:, :quarter]
    for index in range(1, 4):
        part = both_ref[:, index * quarter : (index + 1) * quarter]
        here = jnp.where(flag_ref[0] == index, part, here)
    out_ref[:, hidden:] = mm_tn(both_ref[:, WIDTH:], here).astype(low)


def lower_back(flag, d_out, active, both):
    vmem = pl.BlockSpec(memory_space=pltpu.VMEM)
    return pl.pallas_call(
        lower_back_body,
        out_shape=jax.ShapeDtypeStruct((WIDTH, active.shape[1] + WIDTH // 4), low),
        in_specs=[pl.BlockSpec(memory_space=pltpu.SMEM)] + [vmem] * 3,
        out_specs=vmem,
        name="lower_back",
    )(flag, d_out, active, both)


def place_rows(picks, rows):
    high = rows.astype(low)
    rest = (rows - high.astype(full)).astype(low)
    return mm_tn(picks, jnp.concatenate([high, rest], 0))


def captions_body(
    part, group_ref, ends_ref, unit_ref, scale_ref, d_mid_ref, d_mixed_ref, dq_ref,
    q_far_ref, d_att_far_ref, small_far_ref, kv_ref, qo_ref, kv_far_ref, qo_far_ref, *refs,
):
    out_ref, inner_end_ref = refs[-2:]
    i = pl.program_id(0)
    half = dq_ref.shape[0]
    far_start = (1 - part) * half

    @pl.when(i == 0)
    def _():
        dq_far = jnp.concatenate(
            [
                small_far_ref[piece * 2 * half + far_start : piece * 2 * half + far_start + half]
                for piece in range(3)
            ],
            1,
        )
        inner_end_ref[...] = mm_nt(dq_ref[...], qo_ref[:, :COLS]) + mm_nt(
            dq_far, qo_far_ref[:, :COLS]
        )

    row, token = stack_grid()
    own_caption = token // LENGTH == row
    lane = lax.broadcasted_iota(jnp.int32, (128, TOKENS), 0) & (2 * LENGTH - 1)
    spot = lax.broadcasted_iota(jnp.int32, (128, TOKENS), 1) & (LENGTH - 1)
    zero = jnp.zeros((BLOCK, 128), low)
    place = pl.multiple_of(6 * half + 2 * far_start + 2 * BLOCK * i, 2 * BLOCK)
    packed = small_far_ref[pl.ds(place, 2 * BLOCK), :]
    pair = jnp.concatenate(
        [
            jnp.where(lane_group() == h % 4, packed[h // 4 * BLOCK : (h // 4 + 1) * BLOCK], zero)
            for h in range(HEADS_HERE)
        ],
        0,
    )
    probs = jnp.where(own_caption, mm(pair, (spot == lane).astype(low)), 0.0).astype(low)
    d_scores = jnp.where(
        own_caption, mm(pair, (spot + LENGTH == lane).astype(low)), 0.0
    ).astype(low)
    d_mixed = jnp.concatenate(
        [
            mm_tn(d_scores, head_stack(q_far_ref[step_rows(i), :])).astype(low),
            mm_tn(probs, head_stack(d_att_far_ref[step_rows(i), :])).astype(low),
        ],
        1,
    )
    inner = mm_nt(d_mixed_ref[...], kv_ref[...]) + mm_nt(d_mixed, kv_far_ref[...])
    picks = end_picks(ends_ref[...], 2).astype(low)
    inner += place_rows(picks, inner_end_ref[step_rows(i), :])
    unit = unit_ref[...].astype(full)
    flat = jnp.sum(inner, -1, keepdims=True) * (1.0 / WIDTH)
    tilt = jnp.sum(inner * unit, -1, keepdims=True) * (1.0 / WIDTH)
    out_ref[...] = place_rows(picks, d_mid_ref[...]) + scale_ref[:, :1] * (
        inner - flat - unit * tilt
    )


def captions_back(
    part, group, ends, unit, scale, d_mid, d_mixed, dq, q_far, d_att_far, small_far, kv, qo,
    kv_far, qo_far, done=None,
):
    count = ends.shape[0]
    steps = count // BLOCK
    half = steps // 2
    start = part * half
    own_half = pl.BlockSpec((count // 2, COLS), lambda i, g: (part, 0))
    far_half = pl.BlockSpec((count // 2, COLS), lambda i, g: (1 - part, 0))
    operands = [
        group, ends, unit, scale, d_mid, d_mixed, dq, q_far, d_att_far, small_far, kv, qo,
        kv_far, qo_far,
    ]
    in_specs = [
        pl.BlockSpec((BLOCK, 1), lambda i, g: (i + start, 0)),
        pl.BlockSpec((TOKENS, WIDTH), lambda i, g: (i + start, 0)),
        pl.BlockSpec((TOKENS, 128), lambda i, g: (i + start, 0)),
        pl.BlockSpec((BLOCK, WIDTH), lambda i, g: (i + start, 0)),
        pl.BlockSpec((TOKENS, 2 * COLS), lambda i, g: (i + start, 0)),
        own_half,
        far_half,
        far_half,
        whole_block(small_far.shape),
    ] + [whole_block(kv.shape)] * 4
    aliases = {}
    if done is not None:
        aliases = {len(operands): 0}
        operands.append(done)
        in_specs.append(pl.BlockSpec(memory_space=pl.ANY))
    return pl.pallas_call(
        functools.partial(captions_body, part),
        out_shape=jax.ShapeDtypeStruct(unit.shape, full),
        grid_spec=pltpu.PrefetchScalarGridSpec(
            num_scalar_prefetch=1,
            grid=(half,),
            in_specs=in_specs,
            out_specs=pl.BlockSpec(
                (TOKENS, WIDTH), lambda i, g: ((i + start + g[0] * half) % steps, 0)
            ),
            scratch_shapes=[pltpu.VMEM((count // 2, WIDTH), full)],
        ),
        input_output_aliases=aliases,
        name="captions_back",
    )(*operands)


def local(
    captions,
    image_cache,
    send_order,
    arrive_order,
    counts,
    keep_mask,
    end_pos,
    w_qkv,
    w_out,
    w_up,
    w_down,
    w_proj,
    ln1_gain,
    ln2_gain,
):
    plane = Plane()
    core = plane.core
    group = lax.axis_index("mp")
    spread = plane.count
    rows_dev, length, width = captions.shape
    rows = w_out.shape[0]
    per_peer = rows_dev // spread
    hidden = w_up.shape[1] // 2
    core_flag = core.reshape(1).astype(jnp.int32)
    group_flag = group.reshape(1).astype(jnp.int32)

    packed = pack(
        core_flag,
        w_qkv.transpose(1, 0, 2),
        w_out,
        w_up,
        w_down,
        w_proj,
        ln1_gain[None],
        ln2_gain[None],
    )
    flipped = jnp.concatenate([end_pos, end_pos], 0)
    ends = lax.dynamic_slice_in_dim(flipped, group * CAP_DEV, rows_dev, 0)[:, None]
    wide = width // 2

    def pictures_of_batch(incoming):
        own_arrive = lax.dynamic_slice_in_dim(arrive_order[0], group * CAP_DEV, CAP_DEV, 0)
        take_in = (own_arrive[:, None] == places[None, :]).astype(low)
        pictures = mm(take_in, incoming.reshape(rows_dev, width)).astype(low)
        mine = pick(core, pictures[:, :wide], pictures[:, wide:])
        send = pick(core, pictures[:, wide:], pictures[:, :wide])
        return mine, send

    cached = image_cache.astype(full)
    cached = (cached * lax.rsqrt(jnp.sum(cached * cached, -1, keepdims=True) + 1e-06)).astype(low)
    places = jnp.arange(rows_dev, dtype=jnp.int32)
    hand_out = (send_order[0][:, None] == places[None, :]).astype(low)
    outgoing = mm(hand_out, cached).astype(low).reshape(spread, per_peer, width)

    def deal(outgoing):
        return lax.all_to_all(outgoing, "dp", split_axis=0, concat_axis=0, tiled=True)

    def first_parts(stream):
        return norm_first(group_flag, stream.reshape(rows_dev * length, width), ends)

    def attention_of(kv, qo, parts):
        return attend(parts[0], parts[2], ends, kv, qo)

    main = rows if plane.fast else CAP_DEV
    spare = CAP_DEV - main
    if plane.fast:

        def join(feed, embed, half):
            parts = [half[main:, i * 128 : (i + 1) * 128] for i in range(wide // 128)]
            return jnp.concatenate([feed, embed, half[:main], jnp.concatenate(parts, 0)], 1)

        mix_cuts = (0, 2 * COLS)
        cuts = (0, 2 * hidden, 2 * hidden + 2 * wide + 128)
        arrived = plane.swap_core(packed[1])
        arrived, outgoing = joint(arrived, outgoing)
        block = plane.join_cores(packed[0], arrived)
        incoming = deal(outgoing)
        up = plane.shift_depth(block, 1)
        down = plane.shift_depth(block, -1)
        across = plane.swap_side(block)
        up, down, across, block = joint(up, down, across, block)

        mixes = plane.place(plane.empty(2 * rows, mix_cuts), mix_cuts, 0, block, across)
        far = plane.shift_depth(up, 1)
        across_up = plane.swap_side(up)
        across_down = plane.swap_side(down)
        parts = first_parts(after(captions, up))
        far, across_up, across_down, incoming, *parts = joint(
            far, across_up, across_down, incoming, *parts
        )

        across = plane.swap_side(far)
        pictures = pictures_of_batch(incoming)
        mine = join(packed[2], packed[4], pictures[0])
        arrived = plane.swap_core(join(packed[3], packed[5], pictures[1]))
        stream_near = swap_near(parts[3], 2)
        mixes = plane.place(mixes, mix_cuts, 1, up, across_up)
        mixes = plane.place(mixes, mix_cuts, -1, down, across_down)
        across, arrived, stream_near, mixes = joint(across, arrived, stream_near, mixes)

        block = plane.join_cores(mine, arrived)
        one = plane.shift_depth(block, 1)
        across_block = plane.swap_side(block)
        mixes = plane.place(mixes, mix_cuts, 2, far, across)
        mix_own = mixes[0].reshape(width, 2 * COLS)
        mix_other = plane.swap_core(mix_own)
        far_own = swap_group(mix_own)
        kv = pick(core, mix_own, mix_other)
        qo = pick(core, mix_other, mix_own)
        one, kv, qo = joint(one, kv, qo)

        two = plane.shift_depth(one, 1)
        across_one = plane.swap_side(one)
        attending = attention_of(kv, qo, parts)
        two, across_block, across_one, *attending = joint(
            two, across_block, across_one, *attending
        )

        three = plane.shift_depth(two, 1)
        across_two = plane.swap_side(two)
        wholes = plane.place(plane.empty(2 * rows, cuts), cuts, 0, block, across_block)
        wholes = plane.place(wholes, cuts, 1, one, across_one)
        attention = after(attending[-1], far_own)
        near = [swap_near(attention, flip) for flip in (1, 2, 3)]
        three, across_two, *near = joint(three, across_two, *near)

        across = plane.swap_side(three)
        queries_far = swap_group(attending[2])
        far_other = plane.swap_core(far_own)
        kv_far = pick(core, far_own, far_other)
        qo_far = pick(core, far_other, far_own)
        wholes = plane.place(wholes, cuts, 2, two, across_two)
        across, queries_far, kv_far, qo_far, wholes = joint(
            across, queries_far, kv_far, qo_far, wholes
        )
        wholes = plane.place(wholes, cuts, 3, three, across)
        feeds, third = [whole.reshape(width, -1) for whole in wholes]
        third_other = plane.swap_core(third)

        def images(x):
            extra = x[:, 2 * wide :].reshape(spread, wide // 128, spare, 128)
            extra = extra.transpose(0, 2, 1, 3).reshape(spread * spare, wide)
            return jnp.concatenate([x[:, wide : 2 * wide], extra], 0)

        image_halves = images(third), images(third_other)
        embed_halves = third[:, :wide], third_other[:, :wide]
    else:
        pictures = pictures_of_batch(deal(outgoing))
        parts = first_parts(captions)
        mix_own = plane.gather_plain(packed[0], packed[1])
        mix_other = plane.swap_core(mix_own)
        far_own = swap_group(mix_own)
        kv = pick(core, mix_own, mix_other)
        qo = pick(core, mix_other, mix_own)
        attending = attention_of(kv, qo, parts)
        feeds = plane.gather_plain(packed[2], packed[3])
        image_half = plane.gather_plain(*pictures)
        image_halves = image_half, plane.swap_core(image_half)
        embed_half = plane.gather_plain(packed[4], packed[5])
        embed_halves = embed_half, plane.swap_core(embed_half)
        far_other = plane.swap_core(far_own)
        kv_far = pick(core, far_own, far_other)
        qo_far = pick(core, far_other, far_own)
        stream_near = swap_near(parts[3], 2)
        attention = attending[-1]
        near = [swap_near(attention, flip) for flip in (1, 2, 3)]
        queries_far = swap_group(attending[2])
    unit, scale, unit_end, stream_end = parts
    mixed, probs, queries, attended, _ = attending

    def sides(pair):
        return jnp.concatenate([pick(core, *pair), pick(core, pair[1], pair[0])], 1)

    pictures_all = sides(image_halves)
    w_embed = sides(embed_halves)

    from_group, from_core, from_both = near
    attention = jnp.concatenate([attention, from_core], 0).astype(full)
    attention = attention + jnp.concatenate(
        [roll_rows(from_group), roll_rows(from_both)], 0
    ).astype(full)
    middle = jnp.concatenate([stream_end, stream_near], 0).astype(full) + attention
    unit_second, scale_second = norm_rows(middle)
    second_low = unit_second.astype(low)
    w_raise = feeds[:, :hidden]
    w_lower = feeds[:, hidden:]
    active, slope = gelu_parts(mm(second_low, w_raise))
    active = active.astype(low)
    lowered = mm_nt(active, w_lower).astype(low)
    feed = lowered[:CAP_DEV].astype(full)
    for flip in (1, 2, 3):
        part = swap_near(lowered[flip * CAP_DEV : (flip + 1) * CAP_DEV], flip)
        feed = feed + part.astype(full)
    pooled = (middle[:CAP_DEV] + feed).astype(low)
    embedding = mm(pooled, w_embed)
    inverse = lax.rsqrt(jnp.sum(embedding * embedding, -1, keepdims=True) + 1e-06)
    unit_text = embedding * inverse
    text_low = unit_text.astype(low)

    keep_rows = keep_mask.reshape(spread, MICRO, CAP_DEV) == 1
    filled = jnp.arange(CAP_DEV, dtype=jnp.int32)[None, None, :] < counts[:, :, None]
    valid = keep_rows & filled
    total_valid = jnp.sum(valid.astype(full))
    batch_valid = lax.dynamic_index_in_dim(valid, group, 1, False)
    own_valid = lax.dynamic_index_in_dim(batch_valid, plane.index, 0, False)
    batch_valid = jnp.concatenate(
        [batch_valid[:, :main].reshape(-1), batch_valid[:, main:].reshape(-1)]
    )
    sims = LOGIT_SCALE * mm_nt(text_low, pictures_all)
    allowed = own_valid[:, None] & batch_valid[None, :]
    weight = jnp.where(allowed, jnp.exp(sims), 0.0)
    row_sum = jnp.sum(weight, 1)
    place = jnp.arange(CAP_DEV, dtype=jnp.int32)
    slot = jnp.where(
        place < main,
        plane.index * main + place,
        spread * main + plane.index * spare + place - main,
    )
    target = (
        jnp.arange(spread * CAP_DEV, dtype=jnp.int32)[None, :] == slot[:, None]
    ) & own_valid[:, None]
    row_safe = jnp.where(own_valid, row_sum, 1.0)
    row_part = 0.5 * jnp.sum(jnp.log(row_safe)) - jnp.sum(jnp.where(target, sims, 0.0))
    col_part = jnp.sum(weight, 0)
    totals = jnp.concatenate([col_part, jnp.full((128,), 1.0 / 128, full) * row_part])
    totals = plane.total(totals.reshape(-1, 128)).reshape(-1)
    col_sum = totals[: spread * CAP_DEV]
    col_safe = jnp.where(batch_valid, col_sum, 1.0)
    objective = jnp.sum(totals[spread * CAP_DEV :]) + 0.5 * jnp.sum(jnp.log(col_safe))
    d_sims = (
        weight * (0.5 / row_safe[:, None] + 0.5 / col_safe[None, :]) - target.astype(full)
    ).astype(low)
    d_unit = LOGIT_SCALE * mm(d_sims, pictures_all)
    d_embed = (
        (d_unit - unit_text * jnp.sum(unit_text * d_unit, -1, keepdims=True)) * inverse
    ).astype(low)

    both = jnp.concatenate([d_embed, pooled], 1)
    both = jnp.concatenate([both] + [swap_near(both, flip) for flip in (1, 2, 3)], 0)
    d_embed_all = both[:, :width]
    d_pooled = mm_nt(d_embed_all, w_embed)
    d_out_low = d_pooled.astype(low)
    d_raised = (mm(d_out_low, w_lower) * slope).astype(low)
    d_second = mm_nt(d_raised, w_raise).astype(low)
    g_raise = mm_tn(second_low, d_raised).astype(low)
    d_out_late = after(d_out_low, g_raise, d_second)
    g_lower = lower_back(2 * group_flag + core_flag, d_out_late, active, both)
    if plane.fast:
        raise_stay, raise_in = plane.halve(g_raise.reshape(2, 2, 2, 2 * rows, -1), 1, 4)
        lower_stay, lower_in = plane.halve(g_lower.reshape(2, 2, 2, 2 * rows, -1), 2, 2)
    inner = d_second[:rows_dev].astype(full)
    inner = inner + roll_rows(swap_near(d_second[:rows_dev], 1)).astype(full)
    inner = inner + swap_near(d_second[rows_dev:], 2).astype(full)
    inner = inner + roll_rows(swap_near(d_second[rows_dev:], 3)).astype(full)
    d_middle = d_pooled[:rows_dev] + norm_back(
        inner, unit_second[:rows_dev], scale_second[:rows_dev]
    )

    d_middle_low = d_middle.astype(low)
    d_attended = mm(d_middle_low, qo[:, COLS:]).astype(low)
    d_attended_far = swap_group(d_attended)
    g_keep, g_send, d_mixed, d_queries, small = attend_back(
        core_flag, d_middle_low, d_attended, unit, unit_end, mixed, probs, queries, attended
    )

    def captions_part(part, d_queries_here, done=None):
        return captions_back(
            part, group_flag, ends, unit, scale, d_middle, d_mixed, d_queries_here, queries_far,
            d_attended_far, small_far, kv, qo, kv_far, qo_far, done=done,
        )

    if plane.fast:
        raise_stay, raise_in, lower_stay, lower_in, small, d_queries, g_send = joint(
            raise_stay, raise_in, lower_stay, lower_in, small, d_queries, g_send
        )
        small_far = swap_group(small)
        mix_in = plane.swap_core(g_send)
        raise_side = plane.halve(add_low((raise_stay, raise_in)), 1, 2)
        lower_depth = plane.halve(add_low((lower_stay, lower_in)), 1, 4)
        mix_pair = add_low((g_keep, mix_in)).reshape(2, 2, 2, 2 * rows, 2 * COLS)
        mix_side = plane.halve(mix_pair, 2, 2)
        first_half = captions_part(0, after(d_queries, mix_side[0]))
        raise_side, lower_depth, mix_side, first_half = joint(
            raise_side, lower_depth, mix_side, first_half
        )
        mix_depth = plane.halve(add_low(mix_side), 1, 4)
        raise_last = plane.halve(add_low(raise_side), 0, 8)
        lower_last = plane.halve(add_low(lower_depth), 0, 8)
        starts = after(d_queries, mix_depth[0], raise_last[0], lower_last[0])
        grad_captions = captions_part(1, starts, first_half)
        mix_depth, raise_last, lower_last, grad_captions = joint(
            mix_depth, raise_last, lower_last, grad_captions
        )
        mix_last = plane.halve(add_low(mix_depth), 0, 8)
        raise_sum, lower_sum, mix_sum = [
            plane.scatter_core(pair[0].astype(full) + pair[1].astype(full))
            for pair in (raise_last, lower_last, mix_last)
        ]
    else:
        small_far = swap_group(small)
        grad_captions = captions_part(1, d_queries, captions_part(0, d_queries))
        raise_sum = plane.scatter_plain(g_raise)
        lower_sum = plane.scatter_plain(g_lower)
        mix_sum = plane.scatter_plain(g_keep, g_send)
    grad_captions = grad_captions.reshape(rows_dev, length, width)

    grad_down = jnp.concatenate([part[:, :hidden] for part in lower_sum], 1)
    proj_own = jnp.concatenate([part[:, hidden:] for part in lower_sum], 1)
    proj_far = swap_group(proj_own)
    grad_proj = pick(
        group,
        jnp.concatenate([proj_own, proj_far], 1),
        jnp.concatenate([proj_far, proj_own], 1),
    )
    grad_out = mix_sum[1][:, COLS:]
    unit_mix = jnp.stack([mix_sum[1][:, :COLS], mix_sum[0][:, :COLS], mix_sum[0][:, COLS:]], 1)
    grad_qkv = unit_mix * ln1_gain[:, None, None]
    raised_sum = jnp.concatenate(raise_sum, 1)
    grad_up = raised_sum * ln2_gain[:, None]
    gains = jnp.stack(
        [
            jnp.sum(unit_mix * w_qkv.astype(full), (1, 2)),
            jnp.sum(raised_sum * w_up.astype(full), 1),
            jnp.broadcast_to(objective, (rows,)),
        ]
    )
    gains = gains + swap_group(gains)
    loss = gains[2, 0] / total_valid
    return (
        loss,
        grad_captions,
        grad_qkv,
        grad_out,
        grad_up,
        grad_down,
        grad_proj,
        gains[0],
        gains[1],
    )


def solution(mesh):
    return jax.shard_map(
        local,
        mesh=mesh,
        in_specs=(
            P("dp", None, None),
            P("dp", None),
            P("dp", None),
            P("dp", None),
            P(),
            P(),
            P("dp"),
            P("dp", None, "mp"),
            P("dp", "mp"),
            P("dp", "mp"),
            P("dp", "mp"),
            P("dp", None),
            P("dp"),
            P("dp"),
        ),
        out_specs=(
            P(),
            P("dp", None, None),
            P("dp", None, "mp"),
            P("dp", "mp"),
            P("dp", "mp"),
            P("dp", "mp"),
            P("dp", None),
            P("dp"),
            P("dp"),
        ),
        check_vma=False,
    )
```

```python
import functools
import math

import jax
import jax.numpy as jnp
from jax import lax
from jax.experimental import pallas as pl
from jax.experimental.pallas import tpu as pltpu
from jax.sharding import PartitionSpec as P

HEAD = 64
MICRO = 2
CAP_DEV = 64
LOGIT_SCALE = 40.0
SCORE_SCALE = 1.0 / math.sqrt(HEAD)
LENGTH = 16
WIDTH = 768
HEADS_HERE = 6
COLS = HEADS_HERE * HEAD
BLOCK = 32
TOKENS = BLOCK * LENGTH
STACK = HEADS_HERE * BLOCK

low = jnp.bfloat16
full = jnp.float32


def mm(a, b):
    return lax.dot_general(a, b, (((1,), (0,)), ((), ())), preferred_element_type=full)


def mm_nt(a, b):
    return lax.dot_general(a, b, (((1,), (1,)), ((), ())), preferred_element_type=full)


def mm_tn(a, b):
    return lax.dot_general(a, b, (((0,), (0,)), ((), ())), preferred_element_type=full)


def pick(flag, when_zero, when_one):
    return jnp.where(flag == 0, when_zero, when_one)


class Plane:
    def __init__(self):
        self.count = lax.axis_size("dp")
        self.index = lax.axis_index("dp")
        self.core = self.index % 2
        self.side = (self.index // 2) % 2
        self.depth = self.index // 4
        self.fast = self.count == 16

    def swap_core(self, x):
        return lax.ppermute(x, "dp", [(i, i ^ 1) for i in range(self.count)])

    def swap_side(self, x):
        return lax.ppermute(x, "dp", [(i, i ^ 2) for i in range(self.count)])

    def shift_depth(self, x, step):
        return lax.ppermute(
            x, "dp", [(i, (i + 4 * step) % self.count) for i in range(self.count)]
        )

    def join_cores(self, mine, arrived):
        rows, width = mine.shape
        block = jnp.zeros((2, rows, width), mine.dtype)
        block = lax.dynamic_update_slice(block, mine[None], (self.core, 0, 0))
        block = lax.dynamic_update_slice(block, arrived[None], (1 - self.core, 0, 0))
        return block.reshape(2 * rows, width)

    def place(self, wholes, cuts, step, here, across):
        spot = ((self.depth - step) % 4) * 2
        for block, at in ((here, spot + self.side), (across, spot + 1 - self.side)):
            wholes = [
                lax.dynamic_update_slice(whole, block[None, :, start:end], (at, 0, 0))
                for whole, start, end in zip(wholes, cuts, cuts[1:])
            ]
        return wholes

    def empty(self, rows, cuts, start_of):
        zero = after(jnp.zeros((), low), start_of)
        return [
            jnp.broadcast_to(zero, (self.count // 2, rows, end - start))
            for start, end in zip(cuts, cuts[1:])
        ]

    def gather_plain(self, mine, send):
        zero_all = lax.all_gather(pick(self.core, mine, send), "dp", axis=0, tiled=True)
        one_all = lax.all_gather(pick(self.core, send, mine), "dp", axis=0, tiled=True)
        return pick(self.core, zero_all, one_all)

    def halve(self, x, axis, bit):
        spot = (self.index // bit) % 2
        stay = lax.dynamic_index_in_dim(x, spot, axis, False)
        leave = lax.dynamic_index_in_dim(x, 1 - spot, axis, False)
        return stay, lax.ppermute(leave, "dp", [(i, i ^ bit) for i in range(self.count)])

    def scatter_plain(self, keep, send=None):
        if send is None:
            send = jnp.zeros_like(keep)
        halves = (pick(self.core, keep, send), pick(self.core, send, keep))
        return [
            lax.psum_scatter(half, "dp", scatter_dimension=0, tiled=True).astype(full)
            for half in halves
        ]

    def scatter_core(self, total):
        rows, width = total.shape[0] // 2, total.shape[1]
        total = total.reshape(2, rows, width)
        mine = lax.dynamic_index_in_dim(total, self.core, 0, False)
        arrived = self.swap_core(lax.dynamic_index_in_dim(total, 1 - self.core, 0, False))
        return pick(self.core, mine, arrived), pick(self.core, arrived, mine)

    def flip(self, x, bits):
        return lax.ppermute(x, "dp", [(i, i ^ bits) for i in range(self.count)])


def swap_near(x, flip):
    size = 2 * lax.axis_size("dp")
    return lax.ppermute(x, ("dp", "mp"), [(i, i ^ flip) for i in range(size)])


def swap_group(x):
    return swap_near(x, 1)


def after(x, *others):
    return lax.optimization_barrier((x, *others))[0]


def joint(*values):
    return lax.optimization_barrier(values)


def add_low(pair):
    return (pair[0].astype(full) + pair[1].astype(full)).astype(low)


def roll_rows(x):
    half = x.shape[0] // 2
    return jnp.concatenate([x[half:], x[:half]], 0)


def norm_rows(inputs):
    center = inputs - jnp.mean(inputs, -1, keepdims=True)
    scale = lax.rsqrt(jnp.mean(center * center, -1, keepdims=True) + 1e-05)
    return center * scale, scale


def norm_back(inner, unit, scale):
    return scale * (
        inner
        - jnp.mean(inner, -1, keepdims=True)
        - unit * jnp.mean(inner * unit, -1, keepdims=True)
    )


def gelu_parts(raised):
    cumulative = 0.5 * (1.0 + lax.erf(raised * 0.7071067811865476))
    slope = cumulative + raised * jnp.exp(-0.5 * raised * raised) * 0.3989422804014327
    return raised * cumulative, slope


LIMIT = pltpu.CompilerParams(vmem_limit_bytes=18 * 1024 * 1024)


def whole_block(shape):
    return pl.BlockSpec(shape, lambda *_: (0,) * len(shape))


def shapes(*items):
    return [jax.ShapeDtypeStruct(shape, kind) for shape, kind in items]


def pack_body(core_ref, mix_ref, back_ref, raise_ref, lower_ref, embed_ref, g1_ref, g2_ref, *outs):
    first = core_ref[0] == 0
    rows = back_ref.shape[0]
    spot = lax.broadcasted_iota(jnp.int32, (rows, rows), 0)
    diagonal = spot == lax.broadcasted_iota(jnp.int32, (rows, rows), 1)
    g1, g2 = [
        jnp.sum(jnp.where(diagonal, ref[...], 0.0), 1, keepdims=True) for ref in (g1_ref, g2_ref)
    ]

    def part(index):
        return (mix_ref[index].astype(full) * g1).astype(low)

    def put(index, columns, zero, one):
        outs[index][:, columns] = jnp.where(first, zero, one)
        outs[index + 1][:, columns] = jnp.where(first, one, zero)

    put(0, slice(0, COLS), part(1), part(0))
    put(0, slice(COLS, 2 * COLS), part(2), back_ref[...])
    hidden = raise_ref.shape[1] // 2
    raised = (raise_ref[...].astype(full) * g2).astype(low)
    put(2, slice(0, hidden), raised[:, :hidden], raised[:, hidden:])
    put(2, slice(hidden, 2 * hidden), lower_ref[:, :hidden], lower_ref[:, hidden:])
    put(4, slice(0, COLS), embed_ref[:, :COLS], embed_ref[:, COLS:])


def pack(core, w_qkv, w_out, w_up, w_down, w_proj, g1, g2):
    rows, hidden = w_up.shape
    vmem = pl.BlockSpec(memory_space=pltpu.VMEM)
    return pl.pallas_call(
        pack_body,
        out_shape=shapes(
            *[((rows, 2 * COLS), low)] * 2, *[((rows, hidden), low)] * 2, *[((rows, COLS), low)] * 2
        ),
        in_specs=[pl.BlockSpec(memory_space=pltpu.SMEM)] + [vmem] * 7,
        out_specs=[vmem] * 6,
        name="pack",
    )(core, w_qkv, w_out, w_up, w_down, w_proj, g1, g2)


def end_picks(ends, copies):
    ends = jnp.concatenate([ends] * copies, 0)
    shape = (copies * BLOCK, TOKENS)
    row = lax.broadcasted_iota(jnp.int32, shape, 0) & (BLOCK - 1)
    return lax.broadcasted_iota(jnp.int32, shape, 1) == row * LENGTH + ends


def norm_body(group_ref, x_ref, ends_ref, unit_ref, scale_ref, unit_end_ref, stream_end_ref):
    x = x_ref[...]
    stream = x.astype(full)
    center = stream - jnp.sum(stream, -1, keepdims=True) * (1.0 / WIDTH)
    scale = lax.rsqrt(jnp.sum(center * center, -1, keepdims=True) * (1.0 / WIDTH) + 1e-05)
    unit = (center * scale).astype(low)
    unit_ref[...] = unit
    scale_ref[...] = jnp.broadcast_to(scale, scale_ref.shape)
    picks = end_picks(ends_ref[...], 1).astype(low)
    unit_end_ref[...] = mm(picks, unit).astype(low)
    stream_end_ref[...] = mm(picks, x).astype(low)


def norm_first(group, x, ends):
    steps = ends.shape[0] // BLOCK
    return pl.pallas_call(
        norm_body,
        out_shape=shapes(
            (x.shape, low), ((x.shape[0], 128), full), *[((ends.shape[0], WIDTH), low)] * 2
        ),
        grid_spec=pltpu.PrefetchScalarGridSpec(
            num_scalar_prefetch=1,
            grid=(steps,),
            in_specs=[
                pl.BlockSpec((TOKENS, WIDTH), lambda i, g: ((i + g[0] * (steps // 2)) % steps, 0)),
                pl.BlockSpec((BLOCK, 1), lambda i, g: (i, 0)),
            ],
            out_specs=[
                pl.BlockSpec((TOKENS, WIDTH), lambda i, g: (i, 0)),
                pl.BlockSpec((TOKENS, 128), lambda i, g: (i, 0)),
                pl.BlockSpec((BLOCK, WIDTH), lambda i, g: (i, 0)),
                pl.BlockSpec((BLOCK, WIDTH), lambda i, g: (i, 0)),
            ],
        ),
        name="norm_first",
    )(group, x, ends)


def head_mask(head):
    return lax.broadcasted_iota(jnp.int32, (BLOCK, COLS), 1) // HEAD == head


def head_stack(x):
    zero = jnp.zeros_like(x)
    return jnp.concatenate([jnp.where(head_mask(h), x, zero) for h in range(HEADS_HERE)], 0)


def head_fold(x):
    out = jnp.zeros((BLOCK, COLS), full)
    for h in range(HEADS_HERE):
        out = jnp.where(head_mask(h), x[h * BLOCK : (h + 1) * BLOCK], out)
    return out


def stack_grid():
    row = lax.broadcasted_iota(jnp.int32, (STACK, TOKENS), 0) & (BLOCK - 1)
    token = lax.broadcasted_iota(jnp.int32, (STACK, TOKENS), 1)
    return row, token


def step_rows(i):
    return pl.ds(pl.multiple_of(i * BLOCK, BLOCK), BLOCK)


def attend_body(
    unit_ref, unit_end_ref, ends_ref, kv_ref, qo_ref, mixed_ref, p_ref, q_ref, att_ref, out_ref
):
    i = pl.program_id(0)

    @pl.when(i == 0)
    def _():
        q_ref[...] = mm(unit_end_ref[...], qo_ref[:, :COLS]).astype(low)

    mixed = mm(unit_ref[...], kv_ref[...]).astype(low)
    mixed_ref[...] = mixed
    scores = mm_nt(head_stack(q_ref[step_rows(i), :]), mixed[:, :COLS]) * SCORE_SCALE
    row, token = stack_grid()
    ends = jnp.concatenate([ends_ref[...]] * HEADS_HERE, 0)
    allowed = (token >= row * LENGTH) & (token <= row * LENGTH + ends)
    scores = jnp.where(allowed, scores, -1e30)
    weight = jnp.exp(scores - jnp.max(scores, 1, keepdims=True))
    probs = weight / jnp.sum(weight, 1, keepdims=True)
    p_ref[...] = probs
    att_ref[step_rows(i), :] = head_fold(mm(probs.astype(low), mixed[:, COLS:])).astype(low)

    @pl.when(i == pl.num_programs(0) - 1)
    def _():
        out_ref[...] = mm_nt(att_ref[...], qo_ref[:, COLS:]).astype(low)


def attend(unit, unit_end, ends, kv, qo):
    count = ends.shape[0]
    steps = count // BLOCK
    return pl.pallas_call(
        attend_body,
        grid=(steps,),
        out_shape=shapes(
            ((count * LENGTH, 2 * COLS), low),
            ((steps * STACK, TOKENS), full),
            *[((count, COLS), low)] * 2,
            ((count, WIDTH), low),
        ),
        in_specs=[
            pl.BlockSpec((TOKENS, WIDTH), lambda i: (i, 0)),
            whole_block((count, WIDTH)),
            pl.BlockSpec((BLOCK, 1), lambda i: (i, 0)),
            whole_block(kv.shape),
            whole_block(qo.shape),
        ],
        out_specs=[
            pl.BlockSpec((TOKENS, 2 * COLS), lambda i: (i, 0)),
            pl.BlockSpec((STACK, TOKENS), lambda i: (i, 0)),
            whole_block((count, COLS)),
            whole_block((count, COLS)),
            whole_block((count, WIDTH)),
        ],
        name="attend",
    )(unit, unit_end, ends, kv, qo)


def lane_group():
    return lax.broadcasted_iota(jnp.int32, (BLOCK, 128), 1) // (2 * LENGTH)


def attend_back_body(
    core_ref, d_mid_ref, d_att_ref, unit_ref, unit_end_ref, mixed_ref, p_ref, q_ref, att_ref,
    keep_ref, send_ref, d_mixed_ref, dq_ref, small_ref, sum_ref,
):
    i = pl.program_id(0)
    count = dq_ref.shape[0]

    @pl.when(i == 0)
    def _():
        sum_ref[...] = jnp.zeros_like(sum_ref)

    probs = p_ref[...]
    probs_low = probs.astype(low)
    queries = head_stack(q_ref[step_rows(i), :])
    d_att = head_stack(d_att_ref[step_rows(i), :])
    d_probs = mm_nt(d_att, mixed_ref[:, COLS:])
    d_scores = probs * (d_probs - jnp.sum(probs * d_probs, 1, keepdims=True))
    d_scores = (d_scores * SCORE_SCALE).astype(low)
    dq_ref[step_rows(i), :] = head_fold(mm(d_scores, mixed_ref[:, :COLS])).astype(low)
    d_mixed = jnp.concatenate(
        [mm_tn(d_scores, queries).astype(low), mm_tn(probs_low, d_att).astype(low)], 1
    )
    d_mixed_ref[...] = d_mixed
    spot = lax.broadcasted_iota(jnp.int32, (TOKENS, 128), 0) & (LENGTH - 1)
    lane = lax.broadcasted_iota(jnp.int32, (TOKENS, 128), 1) & (2 * LENGTH - 1)
    squeezed = mm(probs_low, (spot == lane).astype(low))
    squeezed += mm(d_scores, (spot + LENGTH == lane).astype(low))
    for first in (0, 4):
        out = jnp.zeros((BLOCK, 128), full)
        for h in range(first, min(first + 4, HEADS_HERE)):
            out = jnp.where(lane_group() == h - first, squeezed[h * BLOCK : (h + 1) * BLOCK], out)
        place = pl.multiple_of((2 * i + first // 4) * BLOCK, BLOCK)
        small_ref[pl.ds(3 * count + place, BLOCK), :] = out.astype(low)
    sum_ref[...] += mm_tn(unit_ref[...], d_mixed)

    @pl.when(i == pl.num_programs(0) - 1)
    def _():
        first = core_ref[0] == 0
        d_queries = dq_ref[...]
        for piece in range(3):
            small_ref[piece * count : (piece + 1) * count] = d_queries[
                :, piece * 128 : (piece + 1) * 128
            ]
        g_mix = sum_ref[...].astype(low)
        g_query = mm_tn(unit_end_ref[...], d_queries).astype(low)
        g_back = mm_tn(d_mid_ref[...], att_ref[...]).astype(low)
        g_rest = jnp.concatenate([g_query, g_back], 1)
        keep_ref[...] = jnp.where(first, g_mix, g_rest)
        send_ref[...] = jnp.where(first, g_rest, g_mix)


def attend_back(core, d_mid, d_att, unit, unit_end, mixed, probs, queries, attended):
    count = d_mid.shape[0]
    steps = count // BLOCK
    return pl.pallas_call(
        attend_back_body,
        grid=(steps,),
        out_shape=shapes(
            *[((WIDTH, 2 * COLS), low)] * 2,
            ((count * LENGTH, 2 * COLS), low),
            ((count, COLS), low),
            ((3 * count + steps * 2 * BLOCK, 128), low),
        ),
        in_specs=[
            pl.BlockSpec(memory_space=pltpu.SMEM),
            whole_block((count, WIDTH)),
            whole_block((count, COLS)),
            pl.BlockSpec((TOKENS, WIDTH), lambda i: (i, 0)),
            whole_block((count, WIDTH)),
            pl.BlockSpec((TOKENS, 2 * COLS), lambda i: (i, 0)),
            pl.BlockSpec((STACK, TOKENS), lambda i: (i, 0)),
            whole_block((count, COLS)),
            whole_block((count, COLS)),
        ],
        out_specs=[
            whole_block((WIDTH, 2 * COLS)),
            whole_block((WIDTH, 2 * COLS)),
            pl.BlockSpec((TOKENS, 2 * COLS), lambda i: (i, 0)),
            whole_block((count, COLS)),
            whole_block((3 * count + steps * 2 * BLOCK, 128)),
        ],
        scratch_shapes=[pltpu.VMEM((WIDTH, 2 * COLS), full)],
        name="attend_back",
        compiler_params=LIMIT,
    )(core, d_mid, d_att, unit, unit_end, mixed, probs, queries, attended)


def lower_back_body(flag_ref, d_out_ref, active_ref, pooled_ref, d_embed_ref, out_ref):
    hidden = active_ref.shape[1]
    quarter = WIDTH // 4
    out_ref[:, :hidden] = mm_tn(d_out_ref[...], active_ref[...]).astype(low)
    here = d_embed_ref[:, :quarter]
    for index in range(1, 4):
        part = d_embed_ref[:, index * quarter : (index + 1) * quarter]
        here = jnp.where(flag_ref[0] == index, part, here)
    out_ref[:, hidden:] = mm_tn(pooled_ref[...], here).astype(low)


def lower_back(flag, d_out, active, pooled, d_embed):
    vmem = pl.BlockSpec(memory_space=pltpu.VMEM)
    return pl.pallas_call(
        lower_back_body,
        out_shape=jax.ShapeDtypeStruct((WIDTH, active.shape[1] + WIDTH // 4), low),
        in_specs=[pl.BlockSpec(memory_space=pltpu.SMEM)] + [vmem] * 4,
        out_specs=vmem,
        name="lower_back",
        compiler_params=LIMIT,
    )(flag, d_out, active, pooled, d_embed)


def place_rows(picks, rows):
    high = rows.astype(low)
    rest = (rows - high.astype(full)).astype(low)
    return mm_tn(picks, jnp.concatenate([high, rest], 0))


def captions_body(
    part, group_ref, ends_ref, unit_ref, scale_ref, d_mid_ref, d_mixed_ref, dq_ref,
    q_far_ref, d_att_far_ref, small_far_ref, kv_ref, qo_ref, kv_far_ref, qo_far_ref, *refs,
):
    out_ref, inner_end_ref = refs[-2:]
    i = pl.program_id(0)
    half = dq_ref.shape[0]
    far_start = (1 - part) * half

    @pl.when(i == 0)
    def _():
        dq_far = jnp.concatenate(
            [
                small_far_ref[piece * 2 * half + far_start : piece * 2 * half + far_start + half]
                for piece in range(3)
            ],
            1,
        )
        inner_end_ref[...] = mm_nt(dq_ref[...], qo_ref[:, :COLS]) + mm_nt(
            dq_far, qo_far_ref[:, :COLS]
        )

    row, token = stack_grid()
    own_caption = token // LENGTH == row
    lane = lax.broadcasted_iota(jnp.int32, (128, TOKENS), 0) & (2 * LENGTH - 1)
    spot = lax.broadcasted_iota(jnp.int32, (128, TOKENS), 1) & (LENGTH - 1)
    zero = jnp.zeros((BLOCK, 128), low)
    place = pl.multiple_of(6 * half + 2 * far_start + 2 * BLOCK * i, 2 * BLOCK)
    packed = small_far_ref[pl.ds(place, 2 * BLOCK), :]
    pair = jnp.concatenate(
        [
            jnp.where(lane_group() == h % 4, packed[h // 4 * BLOCK : (h // 4 + 1) * BLOCK], zero)
            for h in range(HEADS_HERE)
        ],
        0,
    )
    probs = jnp.where(own_caption, mm(pair, (spot == lane).astype(low)), 0.0).astype(low)
    d_scores = jnp.where(
        own_caption, mm(pair, (spot + LENGTH == lane).astype(low)), 0.0
    ).astype(low)
    d_mixed = jnp.concatenate(
        [
            mm_tn(d_scores, head_stack(q_far_ref[step_rows(i), :])).astype(low),
            mm_tn(probs, head_stack(d_att_far_ref[step_rows(i), :])).astype(low),
        ],
        1,
    )
    inner = mm_nt(d_mixed_ref[...], kv_ref[...]) + mm_nt(d_mixed, kv_far_ref[...])
    picks = end_picks(ends_ref[...], 2).astype(low)
    inner += place_rows(picks, inner_end_ref[step_rows(i), :])
    unit = unit_ref[...].astype(full)
    flat = jnp.sum(inner, -1, keepdims=True) * (1.0 / WIDTH)
    tilt = jnp.sum(inner * unit, -1, keepdims=True) * (1.0 / WIDTH)
    out_ref[...] = place_rows(picks, d_mid_ref[...]) + scale_ref[:, :1] * (
        inner - flat - unit * tilt
    )


def captions_back(
    part, group, ends, unit, scale, d_mid, d_mixed, dq, q_far, d_att_far, small_far, kv, qo,
    kv_far, qo_far, done=None,
):
    count = ends.shape[0]
    steps = count // BLOCK
    half = steps // 2
    start = part * half
    own_half = pl.BlockSpec((count // 2, COLS), lambda i, g: (part, 0))
    far_half = pl.BlockSpec((count // 2, COLS), lambda i, g: (1 - part, 0))
    operands = [
        group, ends, unit, scale, d_mid, d_mixed, dq, q_far, d_att_far, small_far, kv, qo,
        kv_far, qo_far,
    ]
    in_specs = [
        pl.BlockSpec((BLOCK, 1), lambda i, g: (i + start, 0)),
        pl.BlockSpec((TOKENS, WIDTH), lambda i, g: (i + start, 0)),
        pl.BlockSpec((TOKENS, 128), lambda i, g: (i + start, 0)),
        pl.BlockSpec((BLOCK, WIDTH), lambda i, g: (i + start, 0)),
        pl.BlockSpec((TOKENS, 2 * COLS), lambda i, g: (i + start, 0)),
        own_half,
        far_half,
        far_half,
        whole_block(small_far.shape),
    ] + [whole_block(kv.shape)] * 4
    aliases = {}
    if done is not None:
        aliases = {len(operands): 0}
        operands.append(done)
        in_specs.append(pl.BlockSpec(memory_space=pl.ANY))
    return pl.pallas_call(
        functools.partial(captions_body, part),
        out_shape=jax.ShapeDtypeStruct(unit.shape, full),
        grid_spec=pltpu.PrefetchScalarGridSpec(
            num_scalar_prefetch=1,
            grid=(half,),
            in_specs=in_specs,
            out_specs=pl.BlockSpec(
                (TOKENS, WIDTH), lambda i, g: ((i + start + g[0] * half) % steps, 0)
            ),
            scratch_shapes=[pltpu.VMEM((count // 2, WIDTH), full)],
        ),
        input_output_aliases=aliases,
        name="captions_back",
    )(*operands)


def local(
    captions,
    image_cache,
    send_order,
    arrive_order,
    counts,
    keep_mask,
    end_pos,
    w_qkv,
    w_out,
    w_up,
    w_down,
    w_proj,
    ln1_gain,
    ln2_gain,
):
    plane = Plane()
    core = plane.core
    group = lax.axis_index("mp")
    spread = plane.count
    rows_dev, length, width = captions.shape
    rows = w_out.shape[0]
    per_peer = rows_dev // spread
    hidden = w_up.shape[1] // 2
    core_flag = core.reshape(1).astype(jnp.int32)
    group_flag = group.reshape(1).astype(jnp.int32)

    packed = pack(
        core_flag,
        w_qkv.transpose(1, 0, 2),
        w_out,
        w_up,
        w_down,
        w_proj,
        ln1_gain[None],
        ln2_gain[None],
    )
    def order_ends(end_pos):
        flipped = jnp.concatenate([end_pos, end_pos], 0)
        return lax.dynamic_slice_in_dim(flipped, group * CAP_DEV, rows_dev, 0)[:, None]

    wide = width // 2

    def pictures_of_batch(incoming):
        own_arrive = lax.dynamic_slice_in_dim(arrive_order[0], group * CAP_DEV, CAP_DEV, 0)
        take_in = (own_arrive[:, None] == places[None, :]).astype(low)
        pictures = mm(take_in, incoming.reshape(rows_dev, width)).astype(low)
        mine = pick(core, pictures[:, :wide], pictures[:, wide:])
        send = pick(core, pictures[:, wide:], pictures[:, :wide])
        return mine, send

    def prepare(image_cache):
        cached = image_cache.astype(full)
        norms = jnp.sum(cached * cached, -1, keepdims=True)
        cached = (cached * lax.rsqrt(norms + 1e-06)).astype(low)
        hand_out = (send_order[0][:, None] == places[None, :]).astype(low)
        return mm(hand_out, cached).astype(low).reshape(spread, per_peer, width)

    places = jnp.arange(rows_dev, dtype=jnp.int32)

    def deal(outgoing):
        return lax.all_to_all(outgoing, "dp", split_axis=0, concat_axis=0, tiled=True)

    def first_parts(stream, ends):
        return norm_first(group_flag, stream.reshape(rows_dev * length, width), ends)

    def attention_of(kv, qo, parts, ends):
        return attend(parts[0], parts[2], ends, kv, qo)

    main = rows if plane.fast else CAP_DEV
    spare = CAP_DEV - main
    if plane.fast:

        def join(feed, embed, half):
            parts = [half[main:, i * 128 : (i + 1) * 128] for i in range(wide // 128)]
            return jnp.concatenate([feed, embed, half[:main], jnp.concatenate(parts, 0)], 1)

        mix_cuts = (0, 2 * COLS)
        cuts = (0, 2 * hidden, 2 * hidden + 2 * wide + 128)
        arrived = plane.swap_core(packed[1])
        arrived, cache = joint(arrived, image_cache)
        block = plane.join_cores(packed[0], arrived)
        outgoing = prepare(cache)
        up = plane.shift_depth(block, 1)
        down = plane.shift_depth(block, -1)
        across = plane.swap_side(block)
        up, down, across, block, outgoing = joint(up, down, across, block, outgoing)

        incoming = deal(outgoing)
        mixes = plane.place(plane.empty(2 * rows, mix_cuts, block), mix_cuts, 0, block, across)
        far = plane.shift_depth(up, 1)
        across_up = plane.swap_side(up)
        across_down = plane.swap_side(down)
        far, across_up, across_down = joint(far, across_up, across_down)

        across = plane.swap_side(far)
        pictures = pictures_of_batch(incoming)
        mine = join(packed[2], packed[4], pictures[0])
        arrived = plane.swap_core(join(packed[3], packed[5], pictures[1]))
        mixes = plane.place(mixes, mix_cuts, 1, up, across_up)
        mixes = plane.place(mixes, mix_cuts, -1, down, across_down)
        across, arrived, mixes, counts, keep_mask, end_pos = joint(
            across, arrived, mixes, counts, keep_mask, end_pos
        )

        block = plane.join_cores(mine, arrived)
        one = plane.shift_depth(block, 1)
        across_block = plane.swap_side(block)
        mixes = plane.place(mixes, mix_cuts, 2, far, across)
        mix_own = mixes[0].reshape(width, 2 * COLS)
        mix_other = plane.swap_core(mix_own)
        far_own = swap_group(mix_own)
        kv = pick(core, mix_own, mix_other)
        qo = pick(core, mix_other, mix_own)
        ends = order_ends(end_pos)
        parts = first_parts(after(captions, block), ends)
        one, kv, qo, *parts = joint(one, kv, qo, *parts)

        two = plane.shift_depth(one, 1)
        across_one = plane.swap_side(one)
        stream_near = swap_near(parts[3], 2)
        attending = attention_of(kv, qo, parts, ends)
        two, across_block, across_one, stream_near, *attending = joint(
            two, across_block, across_one, stream_near, *attending
        )

        three = plane.shift_depth(two, 1)
        across_two = plane.swap_side(two)
        wholes = plane.place(plane.empty(2 * rows, cuts, attending[-1]), cuts, 0, block, across_block)
        wholes = plane.place(wholes, cuts, 1, one, across_one)
        attention = after(attending[-1], far_own)
        near = [swap_near(attention, flip) for flip in (1, 2, 3)]
        three, across_two, *near = joint(three, across_two, *near)

        across = plane.swap_side(three)
        queries_far = swap_group(attending[2])
        far_other = plane.swap_core(far_own)
        kv_far = pick(core, far_own, far_other)
        qo_far = pick(core, far_other, far_own)
        wholes = plane.place(wholes, cuts, 2, two, across_two)
        across, queries_far, kv_far, qo_far, wholes = joint(
            across, queries_far, kv_far, qo_far, wholes
        )
        wholes = plane.place(wholes, cuts, 3, three, across)
        feeds, third = [whole.reshape(width, -1) for whole in wholes]
        third_other = plane.swap_core(third)

        def images(x):
            extra = x[:, 2 * wide :].reshape(spread, wide // 128, spare, 128)
            extra = extra.transpose(0, 2, 1, 3).reshape(spread * spare, wide)
            return jnp.concatenate([x[:, wide : 2 * wide], extra], 0)

        image_halves = images(third), images(third_other)
        embed_halves = third[:, :wide], third_other[:, :wide]
    else:
        pictures = pictures_of_batch(deal(prepare(image_cache)))
        ends = order_ends(end_pos)
        parts = first_parts(captions, ends)
        mix_own = plane.gather_plain(packed[0], packed[1])
        mix_other = plane.swap_core(mix_own)
        far_own = swap_group(mix_own)
        kv = pick(core, mix_own, mix_other)
        qo = pick(core, mix_other, mix_own)
        attending = attention_of(kv, qo, parts, ends)
        feeds = plane.gather_plain(packed[2], packed[3])
        image_half = plane.gather_plain(*pictures)
        image_halves = image_half, plane.swap_core(image_half)
        embed_half = plane.gather_plain(packed[4], packed[5])
        embed_halves = embed_half, plane.swap_core(embed_half)
        far_other = plane.swap_core(far_own)
        kv_far = pick(core, far_own, far_other)
        qo_far = pick(core, far_other, far_own)
        stream_near = swap_near(parts[3], 2)
        attention = attending[-1]
        near = [swap_near(attention, flip) for flip in (1, 2, 3)]
        queries_far = swap_group(attending[2])
    unit, scale, unit_end, stream_end = parts
    mixed, probs, queries, attended, _ = attending

    def sides(pair):
        return jnp.concatenate([pick(core, *pair), pick(core, pair[1], pair[0])], 1)

    pictures_all = sides(image_halves)
    w_embed = sides(embed_halves)

    from_group, from_core, from_both = near
    attention = jnp.concatenate([attention, from_core], 0).astype(full)
    attention = attention + jnp.concatenate(
        [roll_rows(from_group), roll_rows(from_both)], 0
    ).astype(full)
    middle = jnp.concatenate([stream_end, stream_near], 0).astype(full) + attention
    unit_second, scale_second = norm_rows(middle)
    second_low = unit_second.astype(low)
    w_raise = feeds[:, :hidden]
    w_lower = feeds[:, hidden:]
    active, slope = gelu_parts(mm(second_low, w_raise))
    active = active.astype(low)
    lowered = mm_nt(active, w_lower).astype(low)
    feed = lowered[:CAP_DEV].astype(full)
    for flip in (1, 2, 3):
        part = swap_near(lowered[flip * CAP_DEV : (flip + 1) * CAP_DEV], flip)
        feed = feed + part.astype(full)
    pooled = (middle[:CAP_DEV] + feed).astype(low)
    embedding = mm(pooled, w_embed)
    inverse = lax.rsqrt(jnp.sum(embedding * embedding, -1, keepdims=True) + 1e-06)
    unit_text = embedding * inverse
    text_low = unit_text.astype(low)

    keep_rows = keep_mask.reshape(spread, MICRO, CAP_DEV) == 1
    filled = jnp.arange(CAP_DEV, dtype=jnp.int32)[None, None, :] < counts[:, :, None]
    valid = keep_rows & filled
    total_valid = jnp.sum(valid.astype(full))
    batch_valid = lax.dynamic_index_in_dim(valid, group, 1, False)
    own_valid = lax.dynamic_index_in_dim(batch_valid, plane.index, 0, False)
    batch_valid = jnp.concatenate(
        [batch_valid[:, :main].reshape(-1), batch_valid[:, main:].reshape(-1)]
    )
    sims = LOGIT_SCALE * mm_nt(text_low, pictures_all)
    allowed = own_valid[:, None] & batch_valid[None, :]
    weight = jnp.where(allowed, jnp.exp(sims), 0.0)
    row_sum = jnp.sum(weight, 1)
    place = jnp.arange(CAP_DEV, dtype=jnp.int32)
    slot = jnp.where(
        place < main,
        plane.index * main + place,
        spread * main + plane.index * spare + place - main,
    )
    target = (
        jnp.arange(spread * CAP_DEV, dtype=jnp.int32)[None, :] == slot[:, None]
    ) & own_valid[:, None]
    row_safe = jnp.where(own_valid, row_sum, 1.0)
    row_part = 0.5 * jnp.sum(jnp.log(row_safe)) - jnp.sum(jnp.where(target, sims, 0.0))
    col_part = jnp.sum(weight, 0)
    totals = jnp.concatenate([col_part, jnp.full((128,), 1.0 / 128, full) * row_part])
    totals = totals.reshape(-1, 128)
    if plane.fast:
        pooled_group = swap_near(pooled, 1)
        for bits in ((1, 4), (2, 8)):
            sent = [plane.flip(totals, bits[0]), plane.flip(totals, bits[1])]
            sent.append(plane.flip(totals, sum(bits)))
            if bits[0] == 1:
                sent.append(pooled_group)
            sent = joint(*sent)
            totals = (totals + sent[0]) + (sent[1] + sent[2])
            pooled_group = sent[3] if bits[0] == 1 else pooled_group
    else:
        totals = lax.psum(totals, "dp")
    totals = totals.reshape(-1)
    col_sum = totals[: spread * CAP_DEV]
    col_safe = jnp.where(batch_valid, col_sum, 1.0)
    objective = jnp.sum(totals[spread * CAP_DEV :]) + 0.5 * jnp.sum(jnp.log(col_safe))
    d_sims = (
        weight * (0.5 / row_safe[:, None] + 0.5 / col_safe[None, :]) - target.astype(full)
    ).astype(low)
    d_unit = LOGIT_SCALE * mm(d_sims, pictures_all)
    d_embed = (
        (d_unit - unit_text * jnp.sum(unit_text * d_unit, -1, keepdims=True)) * inverse
    ).astype(low)

    d_embed_near = [swap_near(d_embed, flip) for flip in (1, 2, 3)]
    if plane.fast:
        pooled_pair = jnp.concatenate([pooled, pooled_group], 0)
        *d_embed_near, objective, pooled_near = joint(
            *d_embed_near, objective, plane.swap_core(pooled_pair)
        )
        pooled_all = jnp.concatenate([pooled_pair, pooled_near], 0)
    else:
        pooled_all = jnp.concatenate([pooled] + [swap_near(pooled, flip) for flip in (1, 2, 3)], 0)
    d_embed_all = jnp.concatenate([d_embed, *d_embed_near], 0)
    d_pooled = mm_nt(d_embed_all, w_embed)
    d_out_low = d_pooled.astype(low)
    d_raised = (mm(d_out_low, w_lower) * slope).astype(low)
    d_second = mm_nt(d_raised, w_raise).astype(low)
    g_raise = mm_tn(second_low, d_raised).astype(low)
    d_out_late = after(d_out_low, g_raise, d_second)
    g_lower = lower_back(2 * group_flag + core_flag, d_out_late, active, pooled_all, d_embed_all)
    if plane.fast:
        raise_stay, raise_in = plane.halve(g_raise.reshape(2, 2, 2, 2 * rows, -1), 1, 4)
        lower_stay, lower_in = plane.halve(g_lower.reshape(2, 2, 2, 2 * rows, -1), 2, 2)
    inner = d_second[:rows_dev].astype(full)
    inner = inner + roll_rows(swap_near(d_second[:rows_dev], 1)).astype(full)
    inner = inner + swap_near(d_second[rows_dev:], 2).astype(full)
    inner = inner + roll_rows(swap_near(d_second[rows_dev:], 3)).astype(full)
    d_middle = d_pooled[:rows_dev] + norm_back(
        inner, unit_second[:rows_dev], scale_second[:rows_dev]
    )

    d_middle_low = d_middle.astype(low)
    d_attended = mm(d_middle_low, qo[:, COLS:]).astype(low)
    d_attended_far = swap_group(d_attended)
    g_keep, g_send, d_mixed, d_queries, small = attend_back(
        core_flag, d_middle_low, d_attended, unit, unit_end, mixed, probs, queries, attended
    )

    def captions_part(part, d_queries_here, far_parts, done=None):
        return captions_back(
            part, group_flag, ends, unit, scale, d_middle, d_mixed, d_queries_here, queries_far,
            *far_parts, kv, qo, kv_far, qo_far, done=done,
        )

    if plane.fast:
        raise_stay, raise_in, lower_stay, lower_in, small, d_queries, g_send = joint(
            raise_stay, raise_in, lower_stay, lower_in, small, d_queries, g_send
        )
        small_far = swap_group(small)
        mix_in = plane.swap_core(g_send)
        raise_pair = add_low((raise_stay, raise_in))
        lower_pair = add_low((lower_stay, lower_in))
        raise_side = plane.halve(raise_pair, 1, 2)
        small_far, mix_in, d_attended_far, *raise_side, lower_pair = joint(
            small_far, mix_in, d_attended_far, *raise_side, lower_pair
        )
        raise_last = plane.halve(add_low(raise_side), 0, 8)
        lower_depth = plane.halve(lower_pair, 1, 4)
        mix_pair = add_low((g_keep, mix_in)).reshape(2, 2, 2, 2 * rows, 2 * COLS)
        mix_side = plane.halve(mix_pair, 2, 2)
        first_half = captions_part(0, after(d_queries, mix_side[0]), (d_attended_far, small_far))
        raise_last, lower_depth, mix_side, first_half = joint(
            raise_last, lower_depth, mix_side, first_half
        )
        mix_depth = plane.halve(add_low(mix_side), 1, 4)
        lower_last = plane.halve(add_low(lower_depth), 0, 8)
        starts = after(d_queries, mix_depth[0], lower_last[0])
        grad_captions = captions_part(1, starts, (d_attended_far, small_far), first_half)
        mix_depth, lower_last, grad_captions = joint(mix_depth, lower_last, grad_captions)
        mix_last = plane.halve(add_low(mix_depth), 0, 8)
        raise_sum, lower_sum = [
            plane.scatter_core(pair[0].astype(full) + pair[1].astype(full))
            for pair in (raise_last, lower_last)
        ]
        mix_last, raise_sum, lower_sum = joint(mix_last, raise_sum, lower_sum)
        mix_sum = plane.scatter_core(mix_last[0].astype(full) + mix_last[1].astype(full))
    else:
        far_parts = d_attended_far, swap_group(small)
        grad_captions = captions_part(1, d_queries, far_parts, captions_part(0, d_queries, far_parts))
        raise_sum = plane.scatter_plain(g_raise)
        lower_sum = plane.scatter_plain(g_lower)
        mix_sum = plane.scatter_plain(g_keep, g_send)
    grad_captions = grad_captions.reshape(rows_dev, length, width)

    grad_down = jnp.concatenate([part[:, :hidden] for part in lower_sum], 1)
    proj_own = jnp.concatenate([part[:, hidden:] for part in lower_sum], 1)
    proj_far = swap_group(proj_own)
    grad_proj = pick(
        group,
        jnp.concatenate([proj_own, proj_far], 1),
        jnp.concatenate([proj_far, proj_own], 1),
    )
    grad_out = mix_sum[1][:, COLS:]
    unit_mix = jnp.stack([mix_sum[1][:, :COLS], mix_sum[0][:, :COLS], mix_sum[0][:, COLS:]], 1)
    grad_qkv = unit_mix * ln1_gain[:, None, None]
    raised_sum = jnp.concatenate(raise_sum, 1)
    grad_up = raised_sum * ln2_gain[:, None]
    gains = jnp.stack(
        [
            jnp.sum(unit_mix * w_qkv.astype(full), (1, 2)),
            jnp.sum(raised_sum * w_up.astype(full), 1),
            jnp.broadcast_to(objective, (rows,)),
        ]
    )
    gains = gains + swap_group(gains)
    loss = gains[2, 0] / total_valid
    return (
        loss,
        grad_captions,
        grad_qkv,
        grad_out,
        grad_up,
        grad_down,
        grad_proj,
        gains[0],
        gains[1],
    )


def solution(mesh):
    return jax.shard_map(
        local,
        mesh=mesh,
        in_specs=(
            P("dp", None, None),
            P("dp", None),
            P("dp", None),
            P("dp", None),
            P(),
            P(),
            P("dp"),
            P("dp", None, "mp"),
            P("dp", "mp"),
            P("dp", "mp"),
            P("dp", "mp"),
            P("dp", None),
            P("dp"),
            P("dp"),
        ),
        out_specs=(
            P(),
            P("dp", None, None),
            P("dp", None, "mp"),
            P("dp", "mp"),
            P("dp", "mp"),
            P("dp", "mp"),
            P("dp", None),
            P("dp"),
            P("dp"),
        ),
        check_vma=False,
    )
```

```python
import functools
import math

import jax
import jax.numpy as jnp
from jax import lax
from jax.experimental import pallas as pl
from jax.experimental.pallas import tpu as pltpu
from jax.sharding import PartitionSpec as P

HEAD = 64
MICRO = 2
CAP_DEV = 64
LOGIT_SCALE = 40.0
SCORE_SCALE = 1.0 / math.sqrt(HEAD)
LENGTH = 16
WIDTH = 768
HEADS_HERE = 6
COLS = HEADS_HERE * HEAD
BLOCK = 32
TOKENS = BLOCK * LENGTH
STACK = HEADS_HERE * BLOCK

low = jnp.bfloat16
full = jnp.float32


def mm(a, b):
    return lax.dot_general(a, b, (((1,), (0,)), ((), ())), preferred_element_type=full)


def mm_nt(a, b):
    return lax.dot_general(a, b, (((1,), (1,)), ((), ())), preferred_element_type=full)


def mm_tn(a, b):
    return lax.dot_general(a, b, (((0,), (0,)), ((), ())), preferred_element_type=full)


def pick(flag, when_zero, when_one):
    return jnp.where(flag == 0, when_zero, when_one)


class Plane:
    def __init__(self):
        self.count = lax.axis_size("dp")
        self.index = lax.axis_index("dp")
        self.core = self.index % 2
        self.side = (self.index // 2) % 2
        self.depth = self.index // 4
        self.fast = self.count == 16

    def swap_core(self, x):
        return lax.ppermute(x, "dp", [(i, i ^ 1) for i in range(self.count)])

    def swap_side(self, x):
        return lax.ppermute(x, "dp", [(i, i ^ 2) for i in range(self.count)])

    def shift_depth(self, x, step):
        return lax.ppermute(
            x, "dp", [(i, (i + 4 * step) % self.count) for i in range(self.count)]
        )

    def join_cores(self, mine, arrived):
        rows, width = mine.shape
        block = jnp.zeros((2, rows, width), mine.dtype)
        block = lax.dynamic_update_slice(block, mine[None], (self.core, 0, 0))
        block = lax.dynamic_update_slice(block, arrived[None], (1 - self.core, 0, 0))
        return block.reshape(2 * rows, width)

    def place(self, wholes, cuts, step, here, across):
        spot = ((self.depth - step) % 4) * 2
        for block, at in ((here, spot + self.side), (across, spot + 1 - self.side)):
            wholes = [
                lax.dynamic_update_slice(whole, block[None, :, start:end], (at, 0, 0))
                for whole, start, end in zip(wholes, cuts, cuts[1:])
            ]
        return wholes

    def empty(self, rows, cuts, start_of):
        zero = after(jnp.zeros((), low), start_of)
        return [
            jnp.broadcast_to(zero, (self.count // 2, rows, end - start))
            for start, end in zip(cuts, cuts[1:])
        ]

    def gather_plain(self, mine, send):
        zero_all = lax.all_gather(pick(self.core, mine, send), "dp", axis=0, tiled=True)
        one_all = lax.all_gather(pick(self.core, send, mine), "dp", axis=0, tiled=True)
        return pick(self.core, zero_all, one_all)

    def halve(self, x, axis, bit):
        spot = (self.index // bit) % 2
        stay = lax.dynamic_index_in_dim(x, spot, axis, False)
        leave = lax.dynamic_index_in_dim(x, 1 - spot, axis, False)
        return stay, lax.ppermute(leave, "dp", [(i, i ^ bit) for i in range(self.count)])

    def scatter_plain(self, keep, send=None):
        if send is None:
            send = jnp.zeros_like(keep)
        halves = (pick(self.core, keep, send), pick(self.core, send, keep))
        return [
            lax.psum_scatter(half, "dp", scatter_dimension=0, tiled=True).astype(full)
            for half in halves
        ]

    def scatter_core(self, total):
        rows, width = total.shape[0] // 2, total.shape[1]
        total = total.reshape(2, rows, width)
        mine = lax.dynamic_index_in_dim(total, self.core, 0, False)
        arrived = self.swap_core(lax.dynamic_index_in_dim(total, 1 - self.core, 0, False))
        return pick(self.core, mine, arrived), pick(self.core, arrived, mine)

    def flip(self, x, bits):
        return lax.ppermute(x, "dp", [(i, i ^ bits) for i in range(self.count)])


def swap_near(x, flip):
    size = 2 * lax.axis_size("dp")
    return lax.ppermute(x, ("dp", "mp"), [(i, i ^ flip) for i in range(size)])


def swap_group(x):
    return swap_near(x, 1)


def after(x, *others):
    return lax.optimization_barrier((x, *others))[0]


def joint(*values):
    return lax.optimization_barrier(values)


def add_low(pair):
    return (pair[0].astype(full) + pair[1].astype(full)).astype(low)


def roll_rows(x):
    half = x.shape[0] // 2
    return jnp.concatenate([x[half:], x[:half]], 0)


def norm_rows(inputs):
    center = inputs - jnp.mean(inputs, -1, keepdims=True)
    scale = lax.rsqrt(jnp.mean(center * center, -1, keepdims=True) + 1e-05)
    return center * scale, scale


def norm_back(inner, unit, scale):
    return scale * (
        inner
        - jnp.mean(inner, -1, keepdims=True)
        - unit * jnp.mean(inner * unit, -1, keepdims=True)
    )


def gelu_parts(raised):
    cumulative = 0.5 * (1.0 + lax.erf(raised * 0.7071067811865476))
    slope = cumulative + raised * jnp.exp(-0.5 * raised * raised) * 0.3989422804014327
    return raised * cumulative, slope


LIMIT = pltpu.CompilerParams(vmem_limit_bytes=18 * 1024 * 1024)


def whole_block(shape):
    return pl.BlockSpec(shape, lambda *_: (0,) * len(shape))


def shapes(*items):
    return [jax.ShapeDtypeStruct(shape, kind) for shape, kind in items]


def pack_body(core_ref, mix_ref, back_ref, raise_ref, lower_ref, embed_ref, g1_ref, g2_ref, *outs):
    first = core_ref[0] == 0
    rows = back_ref.shape[0]
    spot = lax.broadcasted_iota(jnp.int32, (rows, rows), 0)
    diagonal = spot == lax.broadcasted_iota(jnp.int32, (rows, rows), 1)
    g1, g2 = [
        jnp.sum(jnp.where(diagonal, ref[...], 0.0), 1, keepdims=True) for ref in (g1_ref, g2_ref)
    ]

    def part(index):
        return (mix_ref[index].astype(full) * g1).astype(low)

    def put(index, columns, zero, one):
        outs[index][:, columns] = jnp.where(first, zero, one)
        outs[index + 1][:, columns] = jnp.where(first, one, zero)

    put(0, slice(0, COLS), part(1), part(0))
    put(0, slice(COLS, 2 * COLS), part(2), back_ref[...])
    hidden = raise_ref.shape[1] // 2
    raised = (raise_ref[...].astype(full) * g2).astype(low)
    put(2, slice(0, hidden), raised[:, :hidden], raised[:, hidden:])
    put(2, slice(hidden, 2 * hidden), lower_ref[:, :hidden], lower_ref[:, hidden:])
    put(4, slice(0, COLS), embed_ref[:, :COLS], embed_ref[:, COLS:])


def pack(core, w_qkv, w_out, w_up, w_down, w_proj, g1, g2):
    rows, hidden = w_up.shape
    vmem = pl.BlockSpec(memory_space=pltpu.VMEM)
    return pl.pallas_call(
        pack_body,
        out_shape=shapes(
            *[((rows, 2 * COLS), low)] * 2, *[((rows, hidden), low)] * 2, *[((rows, COLS), low)] * 2
        ),
        in_specs=[pl.BlockSpec(memory_space=pltpu.SMEM)] + [vmem] * 7,
        out_specs=[vmem] * 6,
        name="pack",
    )(core, w_qkv, w_out, w_up, w_down, w_proj, g1, g2)


def end_picks(ends, copies):
    ends = jnp.concatenate([ends] * copies, 0)
    shape = (copies * BLOCK, TOKENS)
    row = lax.broadcasted_iota(jnp.int32, shape, 0) & (BLOCK - 1)
    return lax.broadcasted_iota(jnp.int32, shape, 1) == row * LENGTH + ends


def norm_body(group_ref, x_ref, ends_ref, unit_ref, scale_ref, unit_end_ref, stream_end_ref):
    x = x_ref[...]
    stream = x.astype(full)
    center = stream - jnp.sum(stream, -1, keepdims=True) * (1.0 / WIDTH)
    scale = lax.rsqrt(jnp.sum(center * center, -1, keepdims=True) * (1.0 / WIDTH) + 1e-05)
    unit = (center * scale).astype(low)
    unit_ref[...] = unit
    scale_ref[...] = jnp.broadcast_to(scale, scale_ref.shape)
    picks = end_picks(ends_ref[...], 1).astype(low)
    unit_end_ref[...] = mm(picks, unit).astype(low)
    stream_end_ref[...] = mm(picks, x).astype(low)


def norm_first(group, x, ends):
    steps = ends.shape[0] // BLOCK
    return pl.pallas_call(
        norm_body,
        out_shape=shapes(
            (x.shape, low), ((x.shape[0], 128), full), *[((ends.shape[0], WIDTH), low)] * 2
        ),
        grid_spec=pltpu.PrefetchScalarGridSpec(
            num_scalar_prefetch=1,
            grid=(steps,),
            in_specs=[
                pl.BlockSpec((TOKENS, WIDTH), lambda i, g: ((i + g[0] * (steps // 2)) % steps, 0)),
                pl.BlockSpec((BLOCK, 1), lambda i, g: (i, 0)),
            ],
            out_specs=[
                pl.BlockSpec((TOKENS, WIDTH), lambda i, g: (i, 0)),
                pl.BlockSpec((TOKENS, 128), lambda i, g: (i, 0)),
                pl.BlockSpec((BLOCK, WIDTH), lambda i, g: (i, 0)),
                pl.BlockSpec((BLOCK, WIDTH), lambda i, g: (i, 0)),
            ],
        ),
        name="norm_first",
    )(group, x, ends)


def head_mask(head):
    return lax.broadcasted_iota(jnp.int32, (BLOCK, COLS), 1) // HEAD == head


def head_stack(x):
    zero = jnp.zeros_like(x)
    return jnp.concatenate([jnp.where(head_mask(h), x, zero) for h in range(HEADS_HERE)], 0)


def head_fold(x):
    out = jnp.zeros((BLOCK, COLS), full)
    for h in range(HEADS_HERE):
        out = jnp.where(head_mask(h), x[h * BLOCK : (h + 1) * BLOCK], out)
    return out


def stack_grid():
    row = lax.broadcasted_iota(jnp.int32, (STACK, TOKENS), 0) & (BLOCK - 1)
    token = lax.broadcasted_iota(jnp.int32, (STACK, TOKENS), 1)
    return row, token


def step_rows(i):
    return pl.ds(pl.multiple_of(i * BLOCK, BLOCK), BLOCK)


def attend_body(
    unit_ref, unit_end_ref, ends_ref, kv_ref, qo_ref, mixed_ref, p_ref, q_ref, att_ref, out_ref
):
    i = pl.program_id(0)

    @pl.when(i == 0)
    def _():
        q_ref[...] = mm(unit_end_ref[...], qo_ref[:, :COLS]).astype(low)

    mixed = mm(unit_ref[...], kv_ref[...]).astype(low)
    mixed_ref[...] = mixed
    scores = mm_nt(head_stack(q_ref[step_rows(i), :]), mixed[:, :COLS]) * SCORE_SCALE
    row, token = stack_grid()
    ends = jnp.concatenate([ends_ref[...]] * HEADS_HERE, 0)
    allowed = (token >= row * LENGTH) & (token <= row * LENGTH + ends)
    scores = jnp.where(allowed, scores, -1e30)
    weight = jnp.exp(scores - jnp.max(scores, 1, keepdims=True))
    probs = weight / jnp.sum(weight, 1, keepdims=True)
    p_ref[...] = probs
    att_ref[step_rows(i), :] = head_fold(mm(probs.astype(low), mixed[:, COLS:])).astype(low)

    @pl.when(i == pl.num_programs(0) - 1)
    def _():
        out_ref[...] = mm_nt(att_ref[...], qo_ref[:, COLS:]).astype(low)


def attend(unit, unit_end, ends, kv, qo):
    count = ends.shape[0]
    steps = count // BLOCK
    return pl.pallas_call(
        attend_body,
        grid=(steps,),
        out_shape=shapes(
            ((count * LENGTH, 2 * COLS), low),
            ((steps * STACK, TOKENS), full),
            *[((count, COLS), low)] * 2,
            ((count, WIDTH), low),
        ),
        in_specs=[
            pl.BlockSpec((TOKENS, WIDTH), lambda i: (i, 0)),
            whole_block((count, WIDTH)),
            pl.BlockSpec((BLOCK, 1), lambda i: (i, 0)),
            whole_block(kv.shape),
            whole_block(qo.shape),
        ],
        out_specs=[
            pl.BlockSpec((TOKENS, 2 * COLS), lambda i: (i, 0)),
            pl.BlockSpec((STACK, TOKENS), lambda i: (i, 0)),
            whole_block((count, COLS)),
            whole_block((count, COLS)),
            whole_block((count, WIDTH)),
        ],
        name="attend",
    )(unit, unit_end, ends, kv, qo)


def lane_group():
    return lax.broadcasted_iota(jnp.int32, (BLOCK, 128), 1) // (2 * LENGTH)


def attend_back_body(
    core_ref, d_mid_ref, d_att_ref, unit_ref, unit_end_ref, mixed_ref, p_ref, q_ref, att_ref,
    keep_ref, send_ref, d_mixed_ref, dq_ref, small_ref, sum_ref,
):
    i = pl.program_id(0)
    count = dq_ref.shape[0]

    @pl.when(i == 0)
    def _():
        sum_ref[...] = jnp.zeros_like(sum_ref)

    probs = p_ref[...]
    probs_low = probs.astype(low)
    queries = head_stack(q_ref[step_rows(i), :])
    d_att = head_stack(d_att_ref[step_rows(i), :])
    d_probs = mm_nt(d_att, mixed_ref[:, COLS:])
    d_scores = probs * (d_probs - jnp.sum(probs * d_probs, 1, keepdims=True))
    d_scores = (d_scores * SCORE_SCALE).astype(low)
    dq_ref[step_rows(i), :] = head_fold(mm(d_scores, mixed_ref[:, :COLS])).astype(low)
    d_mixed = jnp.concatenate(
        [mm_tn(d_scores, queries).astype(low), mm_tn(probs_low, d_att).astype(low)], 1
    )
    d_mixed_ref[...] = d_mixed
    spot = lax.broadcasted_iota(jnp.int32, (TOKENS, 128), 0) & (LENGTH - 1)
    lane = lax.broadcasted_iota(jnp.int32, (TOKENS, 128), 1) & (2 * LENGTH - 1)
    squeezed = mm(probs_low, (spot == lane).astype(low))
    squeezed += mm(d_scores, (spot + LENGTH == lane).astype(low))
    for first in (0, 4):
        out = jnp.zeros((BLOCK, 128), full)
        for h in range(first, min(first + 4, HEADS_HERE)):
            out = jnp.where(lane_group() == h - first, squeezed[h * BLOCK : (h + 1) * BLOCK], out)
        place = pl.multiple_of((2 * i + first // 4) * BLOCK, BLOCK)
        small_ref[pl.ds(3 * count + place, BLOCK), :] = out.astype(low)
    sum_ref[...] += mm_tn(unit_ref[...], d_mixed)

    @pl.when(i == pl.num_programs(0) - 1)
    def _():
        first = core_ref[0] == 0
        d_queries = dq_ref[...]
        for piece in range(3):
            small_ref[piece * count : (piece + 1) * count] = d_queries[
                :, piece * 128 : (piece + 1) * 128
            ]
        g_mix = sum_ref[...].astype(low)
        g_query = mm_tn(unit_end_ref[...], d_queries).astype(low)
        g_back = mm_tn(d_mid_ref[...], att_ref[...]).astype(low)
        g_rest = jnp.concatenate([g_query, g_back], 1)
        keep_ref[...] = jnp.where(first, g_mix, g_rest)
        send_ref[...] = jnp.where(first, g_rest, g_mix)


def attend_back(core, d_mid, d_att, unit, unit_end, mixed, probs, queries, attended):
    count = d_mid.shape[0]
    steps = count // BLOCK
    return pl.pallas_call(
        attend_back_body,
        grid=(steps,),
        out_shape=shapes(
            *[((WIDTH, 2 * COLS), low)] * 2,
            ((count * LENGTH, 2 * COLS), low),
            ((count, COLS), low),
            ((3 * count + steps * 2 * BLOCK, 128), low),
        ),
        in_specs=[
            pl.BlockSpec(memory_space=pltpu.SMEM),
            whole_block((count, WIDTH)),
            whole_block((count, COLS)),
            pl.BlockSpec((TOKENS, WIDTH), lambda i: (i, 0)),
            whole_block((count, WIDTH)),
            pl.BlockSpec((TOKENS, 2 * COLS), lambda i: (i, 0)),
            pl.BlockSpec((STACK, TOKENS), lambda i: (i, 0)),
            whole_block((count, COLS)),
            whole_block((count, COLS)),
        ],
        out_specs=[
            whole_block((WIDTH, 2 * COLS)),
            whole_block((WIDTH, 2 * COLS)),
            pl.BlockSpec((TOKENS, 2 * COLS), lambda i: (i, 0)),
            whole_block((count, COLS)),
            whole_block((3 * count + steps * 2 * BLOCK, 128)),
        ],
        scratch_shapes=[pltpu.VMEM((WIDTH, 2 * COLS), full)],
        name="attend_back",
        compiler_params=LIMIT,
    )(core, d_mid, d_att, unit, unit_end, mixed, probs, queries, attended)


def lower_back_body(flag_ref, d_out_ref, active_ref, pooled_ref, d_embed_ref, out_ref):
    hidden = active_ref.shape[1]
    quarter = WIDTH // 4
    out_ref[:, :hidden] = mm_tn(d_out_ref[...], active_ref[...]).astype(low)
    here = d_embed_ref[:, :quarter]
    for index in range(1, 4):
        part = d_embed_ref[:, index * quarter : (index + 1) * quarter]
        here = jnp.where(flag_ref[0] == index, part, here)
    out_ref[:, hidden:] = mm_tn(pooled_ref[...], here).astype(low)


def lower_back(flag, d_out, active, pooled, d_embed):
    vmem = pl.BlockSpec(memory_space=pltpu.VMEM)
    return pl.pallas_call(
        lower_back_body,
        out_shape=jax.ShapeDtypeStruct((WIDTH, active.shape[1] + WIDTH // 4), low),
        in_specs=[pl.BlockSpec(memory_space=pltpu.SMEM)] + [vmem] * 4,
        out_specs=vmem,
        name="lower_back",
        compiler_params=LIMIT,
    )(flag, d_out, active, pooled, d_embed)


def place_rows(picks, rows):
    high = rows.astype(low)
    rest = (rows - high.astype(full)).astype(low)
    return mm_tn(picks, jnp.concatenate([high, rest], 0))


def captions_body(
    start, blocks, group_ref, ends_ref, unit_ref, scale_ref, d_mid_ref, d_mixed_ref, dq_ref,
    q_far_ref, d_att_far_ref, small_far_ref, kv_ref, qo_ref, kv_far_ref, qo_far_ref, *refs,
):
    out_ref, inner_end_ref = refs[-2:]
    i = pl.program_id(0)
    count = dq_ref.shape[0]
    steps = count // BLOCK
    far = (start + steps // 2) % steps
    rows = blocks * BLOCK

    @pl.when(i == 0)
    def _():
        dq_far = jnp.concatenate(
            [
                small_far_ref[piece * count + far * BLOCK : piece * count + far * BLOCK + rows]
                for piece in range(3)
            ],
            1,
        )
        inner_end_ref[...] = mm_nt(
            dq_ref[start * BLOCK : start * BLOCK + rows], qo_ref[:, :COLS]
        ) + mm_nt(dq_far, qo_far_ref[:, :COLS])

    row, token = stack_grid()
    own_caption = token // LENGTH == row
    lane = lax.broadcasted_iota(jnp.int32, (128, TOKENS), 0) & (2 * LENGTH - 1)
    spot = lax.broadcasted_iota(jnp.int32, (128, TOKENS), 1) & (LENGTH - 1)
    zero = jnp.zeros((BLOCK, 128), low)
    place = pl.multiple_of(3 * count + 2 * BLOCK * (far + i), 2 * BLOCK)
    packed = small_far_ref[pl.ds(place, 2 * BLOCK), :]
    pair = jnp.concatenate(
        [
            jnp.where(lane_group() == h % 4, packed[h // 4 * BLOCK : (h // 4 + 1) * BLOCK], zero)
            for h in range(HEADS_HERE)
        ],
        0,
    )
    probs = jnp.where(own_caption, mm(pair, (spot == lane).astype(low)), 0.0).astype(low)
    d_scores = jnp.where(
        own_caption, mm(pair, (spot + LENGTH == lane).astype(low)), 0.0
    ).astype(low)
    d_mixed = jnp.concatenate(
        [
            mm_tn(d_scores, head_stack(q_far_ref[step_rows(far + i), :])).astype(low),
            mm_tn(probs, head_stack(d_att_far_ref[step_rows(far + i), :])).astype(low),
        ],
        1,
    )
    inner = mm_nt(d_mixed_ref[...], kv_ref[...]) + mm_nt(d_mixed, kv_far_ref[...])
    picks = end_picks(ends_ref[...], 2).astype(low)
    inner += place_rows(picks, inner_end_ref[step_rows(i), :])
    unit = unit_ref[...].astype(full)
    flat = jnp.sum(inner, -1, keepdims=True) * (1.0 / WIDTH)
    tilt = jnp.sum(inner * unit, -1, keepdims=True) * (1.0 / WIDTH)
    out_ref[...] = place_rows(picks, d_mid_ref[...]) + scale_ref[:, :1] * (
        inner - flat - unit * tilt
    )


def captions_back(
    start, blocks, group, ends, unit, scale, d_mid, d_mixed, dq, q_far, d_att_far, small_far, kv, qo,
    kv_far, qo_far, done=None,
):
    count = ends.shape[0]
    steps = count // BLOCK
    half = steps // 2
    operands = [
        group, ends, unit, scale, d_mid, d_mixed, dq, q_far, d_att_far, small_far, kv, qo,
        kv_far, qo_far,
    ]
    in_specs = [
        pl.BlockSpec((BLOCK, 1), lambda i, g: (i + start, 0)),
        pl.BlockSpec((TOKENS, WIDTH), lambda i, g: (i + start, 0)),
        pl.BlockSpec((TOKENS, 128), lambda i, g: (i + start, 0)),
        pl.BlockSpec((BLOCK, WIDTH), lambda i, g: (i + start, 0)),
        pl.BlockSpec((TOKENS, 2 * COLS), lambda i, g: (i + start, 0)),
        *[whole_block((count, COLS))] * 3,
        whole_block(small_far.shape),
    ] + [whole_block(kv.shape)] * 4
    aliases = {}
    if done is not None:
        aliases = {len(operands): 0}
        operands.append(done)
        in_specs.append(pl.BlockSpec(memory_space=pl.ANY))
    return pl.pallas_call(
        functools.partial(captions_body, start, blocks),
        out_shape=jax.ShapeDtypeStruct(unit.shape, full),
        grid_spec=pltpu.PrefetchScalarGridSpec(
            num_scalar_prefetch=1,
            grid=(blocks,),
            in_specs=in_specs,
            out_specs=pl.BlockSpec(
                (TOKENS, WIDTH), lambda i, g: ((i + start + g[0] * half) % steps, 0)
            ),
            scratch_shapes=[pltpu.VMEM((blocks * BLOCK, WIDTH), full)],
        ),
        input_output_aliases=aliases,
        name="captions_back",
    )(*operands)


def local(
    captions,
    image_cache,
    send_order,
    arrive_order,
    counts,
    keep_mask,
    end_pos,
    w_qkv,
    w_out,
    w_up,
    w_down,
    w_proj,
    ln1_gain,
    ln2_gain,
):
    plane = Plane()
    core = plane.core
    group = lax.axis_index("mp")
    spread = plane.count
    rows_dev, length, width = captions.shape
    rows = w_out.shape[0]
    per_peer = rows_dev // spread
    hidden = w_up.shape[1] // 2
    core_flag = core.reshape(1).astype(jnp.int32)
    group_flag = group.reshape(1).astype(jnp.int32)

    packed = pack(
        core_flag,
        w_qkv.transpose(1, 0, 2),
        w_out,
        w_up,
        w_down,
        w_proj,
        ln1_gain[None],
        ln2_gain[None],
    )
    def order_ends(end_pos):
        flipped = jnp.concatenate([end_pos, end_pos], 0)
        return lax.dynamic_slice_in_dim(flipped, group * CAP_DEV, rows_dev, 0)[:, None]

    wide = width // 2

    def pictures_of_batch(incoming):
        own_arrive = lax.dynamic_slice_in_dim(arrive_order[0], group * CAP_DEV, CAP_DEV, 0)
        take_in = (own_arrive[:, None] == places[None, :]).astype(low)
        pictures = mm(take_in, incoming.reshape(rows_dev, width)).astype(low)
        mine = pick(core, pictures[:, :wide], pictures[:, wide:])
        send = pick(core, pictures[:, wide:], pictures[:, :wide])
        return mine, send

    def prepare(image_cache):
        cached = image_cache.astype(full)
        norms = jnp.sum(cached * cached, -1, keepdims=True)
        cached = (cached * lax.rsqrt(norms + 1e-06)).astype(low)
        hand_out = (send_order[0][:, None] == places[None, :]).astype(low)
        return mm(hand_out, cached).astype(low).reshape(spread, per_peer, width)

    places = jnp.arange(rows_dev, dtype=jnp.int32)

    def deal(outgoing):
        return lax.all_to_all(outgoing, "dp", split_axis=0, concat_axis=0, tiled=True)

    def first_parts(stream, ends):
        return norm_first(group_flag, stream.reshape(rows_dev * length, width), ends)

    def attention_of(kv, qo, parts, ends):
        return attend(parts[0], parts[2], ends, kv, qo)

    main = rows if plane.fast else CAP_DEV
    spare = CAP_DEV - main
    if plane.fast:

        def join(feed, embed, half):
            parts = [half[main:, i * 128 : (i + 1) * 128] for i in range(wide // 128)]
            return jnp.concatenate([feed, embed, half[:main], jnp.concatenate(parts, 0)], 1)

        mix_cuts = (0, 2 * COLS)
        cuts = (0, 2 * hidden, 2 * hidden + 2 * wide + 128)
        arrived = plane.swap_core(packed[1])
        arrived, cache = joint(arrived, image_cache)
        block = plane.join_cores(packed[0], arrived)
        incoming = deal(prepare(cache))
        up = plane.shift_depth(block, 1)
        down = plane.shift_depth(block, -1)
        across = plane.swap_side(block)
        up, down, across, block = joint(up, down, across, block)

        mixes = plane.place(plane.empty(2 * rows, mix_cuts, block), mix_cuts, 0, block, across)
        far = plane.shift_depth(up, 1)
        across_up = plane.swap_side(up)
        across_down = plane.swap_side(down)
        far, across_up, across_down, incoming = joint(far, across_up, across_down, incoming)

        across = plane.swap_side(far)
        pictures = pictures_of_batch(incoming)
        mine = join(packed[2], packed[4], pictures[0])
        arrived = plane.swap_core(join(packed[3], packed[5], pictures[1]))
        mixes = plane.place(mixes, mix_cuts, 1, up, across_up)
        mixes = plane.place(mixes, mix_cuts, -1, down, across_down)
        across, arrived, mixes, counts, keep_mask, end_pos = joint(
            across, arrived, mixes, counts, keep_mask, end_pos
        )

        block = plane.join_cores(mine, arrived)
        one = plane.shift_depth(block, 1)
        across_block = plane.swap_side(block)
        mixes = plane.place(mixes, mix_cuts, 2, far, across)
        mix_own = mixes[0].reshape(width, 2 * COLS)
        mix_other = plane.swap_core(mix_own)
        far_own = swap_group(mix_own)
        kv = pick(core, mix_own, mix_other)
        qo = pick(core, mix_other, mix_own)
        ends = order_ends(end_pos)
        parts = first_parts(after(captions, block), ends)
        one, kv, qo, *parts = joint(one, kv, qo, *parts)

        two = plane.shift_depth(one, 1)
        across_one = plane.swap_side(one)
        stream_near = swap_near(parts[3], 2)
        attending = attention_of(kv, qo, parts, ends)
        two, across_block, across_one, stream_near, *attending = joint(
            two, across_block, across_one, stream_near, *attending
        )

        three = plane.shift_depth(two, 1)
        across_two = plane.swap_side(two)
        wholes = plane.place(plane.empty(2 * rows, cuts, attending[-1]), cuts, 0, block, across_block)
        wholes = plane.place(wholes, cuts, 1, one, across_one)
        attention = after(attending[-1], far_own)
        near = [swap_near(attention, flip) for flip in (1, 2, 3)]
        three, across_two, *near = joint(three, across_two, *near)

        across = plane.swap_side(three)
        queries_far = swap_group(attending[2])
        far_other = plane.swap_core(far_own)
        kv_far = pick(core, far_own, far_other)
        qo_far = pick(core, far_other, far_own)
        wholes = plane.place(wholes, cuts, 2, two, across_two)
        across, queries_far, kv_far, qo_far, wholes = joint(
            across, queries_far, kv_far, qo_far, wholes
        )
        wholes = plane.place(wholes, cuts, 3, three, across)
        feeds, third = [whole.reshape(width, -1) for whole in wholes]
        third_other = plane.swap_core(third)

        def images(x):
            extra = x[:, 2 * wide :].reshape(spread, wide // 128, spare, 128)
            extra = extra.transpose(0, 2, 1, 3).reshape(spread * spare, wide)
            return jnp.concatenate([x[:, wide : 2 * wide], extra], 0)

        image_halves = images(third), images(third_other)
        embed_halves = third[:, :wide], third_other[:, :wide]
    else:
        pictures = pictures_of_batch(deal(prepare(image_cache)))
        ends = order_ends(end_pos)
        parts = first_parts(captions, ends)
        mix_own = plane.gather_plain(packed[0], packed[1])
        mix_other = plane.swap_core(mix_own)
        far_own = swap_group(mix_own)
        kv = pick(core, mix_own, mix_other)
        qo = pick(core, mix_other, mix_own)
        attending = attention_of(kv, qo, parts, ends)
        feeds = plane.gather_plain(packed[2], packed[3])
        image_half = plane.gather_plain(*pictures)
        image_halves = image_half, plane.swap_core(image_half)
        embed_half = plane.gather_plain(packed[4], packed[5])
        embed_halves = embed_half, plane.swap_core(embed_half)
        far_other = plane.swap_core(far_own)
        kv_far = pick(core, far_own, far_other)
        qo_far = pick(core, far_other, far_own)
        stream_near = swap_near(parts[3], 2)
        attention = attending[-1]
        near = [swap_near(attention, flip) for flip in (1, 2, 3)]
        queries_far = swap_group(attending[2])
    unit, scale, unit_end, stream_end = parts
    mixed, probs, queries, attended, _ = attending

    def sides(pair):
        return jnp.concatenate([pick(core, *pair), pick(core, pair[1], pair[0])], 1)

    pictures_all = sides(image_halves)
    w_embed = sides(embed_halves)

    from_group, from_core, from_both = near
    attention = jnp.concatenate([attention, from_core], 0).astype(full)
    attention = attention + jnp.concatenate(
        [roll_rows(from_group), roll_rows(from_both)], 0
    ).astype(full)
    middle = jnp.concatenate([stream_end, stream_near], 0).astype(full) + attention
    unit_second, scale_second = norm_rows(middle)
    second_low = unit_second.astype(low)
    w_raise = feeds[:, :hidden]
    w_lower = feeds[:, hidden:]
    active, slope = gelu_parts(mm(second_low, w_raise))
    active = active.astype(low)
    lowered = mm_nt(active, w_lower).astype(low)
    feed = lowered[:CAP_DEV].astype(full)
    for flip in (1, 2, 3):
        part = swap_near(lowered[flip * CAP_DEV : (flip + 1) * CAP_DEV], flip)
        feed = feed + part.astype(full)
    pooled = (middle[:CAP_DEV] + feed).astype(low)
    embedding = mm(pooled, w_embed)
    inverse = lax.rsqrt(jnp.sum(embedding * embedding, -1, keepdims=True) + 1e-06)
    unit_text = embedding * inverse
    text_low = unit_text.astype(low)

    keep_rows = keep_mask.reshape(spread, MICRO, CAP_DEV) == 1
    filled = jnp.arange(CAP_DEV, dtype=jnp.int32)[None, None, :] < counts[:, :, None]
    valid = keep_rows & filled
    total_valid = jnp.sum(valid.astype(full))
    batch_valid = lax.dynamic_index_in_dim(valid, group, 1, False)
    own_valid = lax.dynamic_index_in_dim(batch_valid, plane.index, 0, False)
    batch_valid = jnp.concatenate(
        [batch_valid[:, :main].reshape(-1), batch_valid[:, main:].reshape(-1)]
    )
    sims = LOGIT_SCALE * mm_nt(text_low, pictures_all)
    allowed = own_valid[:, None] & batch_valid[None, :]
    weight = jnp.where(allowed, jnp.exp(sims), 0.0)
    row_sum = jnp.sum(weight, 1)
    place = jnp.arange(CAP_DEV, dtype=jnp.int32)
    slot = jnp.where(
        place < main,
        plane.index * main + place,
        spread * main + plane.index * spare + place - main,
    )
    target = (
        jnp.arange(spread * CAP_DEV, dtype=jnp.int32)[None, :] == slot[:, None]
    ) & own_valid[:, None]
    row_safe = jnp.where(own_valid, row_sum, 1.0)
    row_part = 0.5 * jnp.sum(jnp.log(row_safe)) - jnp.sum(jnp.where(target, sims, 0.0))
    col_part = jnp.sum(weight, 0)
    totals = jnp.concatenate([col_part, jnp.full((128,), 1.0 / 128, full) * row_part])
    totals = totals.reshape(-1, 128)
    if plane.fast:
        pooled_group = swap_near(pooled, 1)
        for bits in ((1, 4), (2, 8)):
            sent = [plane.flip(totals, bits[0]), plane.flip(totals, bits[1])]
            sent.append(plane.flip(totals, sum(bits)))
            if bits[0] == 1:
                sent.append(pooled_group)
            sent = joint(*sent)
            totals = (totals + sent[0]) + (sent[1] + sent[2])
            pooled_group = sent[3] if bits[0] == 1 else pooled_group
    else:
        totals = lax.psum(totals, "dp")
    totals = totals.reshape(-1)
    col_sum = totals[: spread * CAP_DEV]
    col_safe = jnp.where(batch_valid, col_sum, 1.0)
    objective = jnp.sum(totals[spread * CAP_DEV :]) + 0.5 * jnp.sum(jnp.log(col_safe))
    d_sims = (
        weight * (0.5 / row_safe[:, None] + 0.5 / col_safe[None, :]) - target.astype(full)
    ).astype(low)
    d_unit = LOGIT_SCALE * mm(d_sims, pictures_all)
    d_embed = (
        (d_unit - unit_text * jnp.sum(unit_text * d_unit, -1, keepdims=True)) * inverse
    ).astype(low)

    d_embed_near = [swap_near(d_embed, flip) for flip in (1, 2, 3)]
    if plane.fast:
        pooled_pair = jnp.concatenate([pooled, pooled_group], 0)
        *d_embed_near, objective, pooled_near = joint(
            *d_embed_near, objective, plane.swap_core(pooled_pair)
        )
        pooled_all = jnp.concatenate([pooled_pair, pooled_near], 0)
    else:
        pooled_all = jnp.concatenate([pooled] + [swap_near(pooled, flip) for flip in (1, 2, 3)], 0)
    d_embed_all = jnp.concatenate([d_embed, *d_embed_near], 0)
    d_pooled = mm_nt(d_embed_all, w_embed)
    d_out_low = d_pooled.astype(low)
    d_raised = (mm(d_out_low, w_lower) * slope).astype(low)
    d_second = mm_nt(d_raised, w_raise).astype(low)
    g_raise = mm_tn(second_low, d_raised).astype(low)
    d_out_late = after(d_out_low, g_raise, d_second)
    g_lower = lower_back(2 * group_flag + core_flag, d_out_late, active, pooled_all, d_embed_all)
    if plane.fast:
        raise_stay, raise_in = plane.halve(g_raise.reshape(2, 2, 2, 2 * rows, -1), 1, 4)
        lower_stay, lower_in = plane.halve(g_lower.reshape(2, 2, 2, 2 * rows, -1), 2, 2)
    d_second = add_low((d_second[:rows_dev], swap_near(d_second[rows_dev:], 2)))
    inner = d_second.astype(full) + roll_rows(swap_near(d_second, 1)).astype(full)
    d_middle = d_pooled[:rows_dev] + norm_back(
        inner, unit_second[:rows_dev], scale_second[:rows_dev]
    )

    d_middle_low = d_middle.astype(low)
    d_attended = mm(d_middle_low, qo[:, COLS:]).astype(low)
    d_attended_far = swap_group(d_attended)
    g_keep, g_send, d_mixed, d_queries, small = attend_back(
        core_flag, d_middle_low, d_attended, unit, unit_end, mixed, probs, queries, attended
    )

    def early_parts(raise_sum, lower_sum):
        grad_down = jnp.concatenate([part[:, :hidden] for part in lower_sum], 1)
        proj_own = jnp.concatenate([part[:, hidden:] for part in lower_sum], 1)
        raised_sum = jnp.concatenate(raise_sum, 1)
        gain_second = jnp.sum(raised_sum * w_up.astype(full), 1)
        early = jnp.stack([gain_second, jnp.broadcast_to(objective, (rows,))])
        return proj_own, grad_down, raised_sum, early

    def captions_part(start, blocks, d_queries_here, far_parts, done=None):
        return captions_back(
            start, blocks, group_flag, ends, unit, scale, d_middle, d_mixed, d_queries_here, queries_far,
            *far_parts, kv, qo, kv_far, qo_far, done=done,
        )

    if plane.fast:
        raise_stay, raise_in, lower_stay, lower_in, small, d_queries, g_send, d_attended_far = joint(
            raise_stay, raise_in, lower_stay, lower_in, small, d_queries, g_send, d_attended_far
        )
        small_far = swap_group(small)
        mix_in = plane.swap_core(g_send)
        raise_pair = add_low((raise_stay, raise_in))
        lower_pair = add_low((lower_stay, lower_in))
        raise_side = plane.halve(raise_pair, 1, 2)
        small_far, mix_in, *raise_side, lower_pair = joint(
            small_far, mix_in, *raise_side, lower_pair
        )
        raise_last = plane.halve(add_low(raise_side), 0, 8)
        lower_depth = plane.halve(lower_pair, 1, 4)
        mix_pair = add_low((g_keep, mix_in)).reshape(2, 2, 2, 2 * rows, 2 * COLS)
        mix_side = plane.halve(mix_pair, 2, 2)
        far_parts = d_attended_far, small_far
        half = rows_dev // BLOCK // 2
        first_half = captions_part(0, half, after(d_queries, mix_side[0]), far_parts)
        raise_last, lower_depth, mix_side, first_half = joint(
            raise_last, lower_depth, mix_side, first_half
        )
        mix_depth = plane.halve(add_low(mix_side), 1, 4)
        lower_last = plane.halve(add_low(lower_depth), 0, 8)
        starts = after(d_queries, mix_depth[0], lower_last[0])
        third_part = captions_part(half, half // 2, starts, far_parts, first_half)
        mix_depth, lower_last, third_part = joint(mix_depth, lower_last, third_part)
        mix_last = plane.halve(add_low(mix_depth), 0, 8)
        starts = after(d_queries, mix_last[0])
        grad_captions = captions_part(half + half // 2, half - half // 2, starts, far_parts, third_part)
        raise_sum, lower_sum = [
            plane.scatter_core(pair[0].astype(full) + pair[1].astype(full))
            for pair in (raise_last, lower_last)
        ]
        proj_own, grad_down, raised_sum, early = early_parts(raise_sum, lower_sum)
        proj_far, early_far = swap_group(proj_own), swap_group(early)
        mix_last, proj_far, early_far, grad_down, raised_sum, grad_captions = joint(
            mix_last, proj_far, early_far, grad_down, raised_sum, grad_captions
        )
        mix_sum = plane.scatter_core(mix_last[0].astype(full) + mix_last[1].astype(full))
    else:
        far_parts = d_attended_far, swap_group(small)
        grad_captions = captions_part(0, rows_dev // BLOCK, d_queries, far_parts)
        raise_sum = plane.scatter_plain(g_raise)
        lower_sum = plane.scatter_plain(g_lower)
        proj_own, grad_down, raised_sum, early = early_parts(raise_sum, lower_sum)
        proj_far, early_far = swap_group(proj_own), swap_group(early)
        mix_sum = plane.scatter_plain(g_keep, g_send)
    grad_captions = grad_captions.reshape(rows_dev, length, width)

    grad_proj = pick(
        group,
        jnp.concatenate([proj_own, proj_far], 1),
        jnp.concatenate([proj_far, proj_own], 1),
    )
    grad_out = mix_sum[1][:, COLS:]
    unit_mix = jnp.stack([mix_sum[1][:, :COLS], mix_sum[0][:, :COLS], mix_sum[0][:, COLS:]], 1)
    grad_qkv = unit_mix * ln1_gain[:, None, None]
    grad_up = raised_sum * ln2_gain[:, None]
    early = early + early_far
    loss = early[1, 0] / total_valid
    gain_first = jnp.sum(unit_mix * w_qkv.astype(full), (1, 2))[None]
    gain_first = gain_first + swap_group(gain_first)
    return (
        loss,
        grad_captions,
        grad_qkv,
        grad_out,
        grad_up,
        grad_down,
        grad_proj,
        gain_first[0],
        early[0],
    )


def solution(mesh):
    return jax.shard_map(
        local,
        mesh=mesh,
        in_specs=(
            P("dp", None, None),
            P("dp", None),
            P("dp", None),
            P("dp", None),
            P(),
            P(),
            P("dp"),
            P("dp", None, "mp"),
            P("dp", "mp"),
            P("dp", "mp"),
            P("dp", "mp"),
            P("dp", None),
            P("dp"),
            P("dp"),
        ),
        out_specs=(
            P(),
            P("dp", None, None),
            P("dp", None, "mp"),
            P("dp", "mp"),
            P("dp", "mp"),
            P("dp", "mp"),
            P("dp", None),
            P("dp"),
            P("dp"),
        ),
        check_vma=False,
    )
```

```python
import functools
import math

import jax
import jax.numpy as jnp
from jax import lax
from jax.experimental import pallas as pl
from jax.experimental.pallas import tpu as pltpu
from jax.sharding import PartitionSpec as P

HEAD = 64
MICRO = 2
CAP_DEV = 64
LOGIT_SCALE = 40.0
SCORE_SCALE = 1.0 / math.sqrt(HEAD)
LENGTH = 16
WIDTH = 768
HEADS_HERE = 6
COLS = HEADS_HERE * HEAD
BLOCK = 32
TOKENS = BLOCK * LENGTH
STACK = HEADS_HERE * BLOCK

low = jnp.bfloat16
full = jnp.float32


def mm(a, b):
    return lax.dot_general(a, b, (((1,), (0,)), ((), ())), preferred_element_type=full)


def mm_nt(a, b):
    return lax.dot_general(a, b, (((1,), (1,)), ((), ())), preferred_element_type=full)


def mm_tn(a, b):
    return lax.dot_general(a, b, (((0,), (0,)), ((), ())), preferred_element_type=full)


def pick(flag, when_zero, when_one):
    return jnp.where(flag == 0, when_zero, when_one)


class Plane:
    def __init__(self):
        self.count = lax.axis_size("dp")
        self.index = lax.axis_index("dp")
        self.core = self.index % 2
        self.side = (self.index // 2) % 2
        self.depth = self.index // 4
        self.fast = self.count == 16

    def swap_core(self, x):
        return lax.ppermute(x, "dp", [(i, i ^ 1) for i in range(self.count)])

    def swap_side(self, x):
        return lax.ppermute(x, "dp", [(i, i ^ 2) for i in range(self.count)])

    def shift_depth(self, x, step):
        return lax.ppermute(
            x, "dp", [(i, (i + 4 * step) % self.count) for i in range(self.count)]
        )

    def join_cores(self, mine, arrived):
        rows, width = mine.shape
        block = jnp.zeros((2, rows, width), mine.dtype)
        block = lax.dynamic_update_slice(block, mine[None], (self.core, 0, 0))
        block = lax.dynamic_update_slice(block, arrived[None], (1 - self.core, 0, 0))
        return block.reshape(2 * rows, width)

    def place(self, wholes, cuts, step, here, across):
        spot = ((self.depth - step) % 4) * 2
        for block, at in ((here, spot + self.side), (across, spot + 1 - self.side)):
            wholes = [
                lax.dynamic_update_slice(whole, block[None, :, start:end], (at, 0, 0))
                for whole, start, end in zip(wholes, cuts, cuts[1:])
            ]
        return wholes

    def empty(self, rows, cuts, start_of):
        zero = after(jnp.zeros((), low), start_of)
        return [
            jnp.broadcast_to(zero, (self.count // 2, rows, end - start))
            for start, end in zip(cuts, cuts[1:])
        ]

    def gather_plain(self, mine, send):
        zero_all = lax.all_gather(pick(self.core, mine, send), "dp", axis=0, tiled=True)
        one_all = lax.all_gather(pick(self.core, send, mine), "dp", axis=0, tiled=True)
        return pick(self.core, zero_all, one_all)

    def halve(self, x, axis, bit):
        spot = (self.index // bit) % 2
        stay = lax.dynamic_index_in_dim(x, spot, axis, False)
        leave = lax.dynamic_index_in_dim(x, 1 - spot, axis, False)
        return stay, lax.ppermute(leave, "dp", [(i, i ^ bit) for i in range(self.count)])

    def scatter_plain(self, keep, send=None):
        if send is None:
            send = jnp.zeros_like(keep)
        halves = (pick(self.core, keep, send), pick(self.core, send, keep))
        return [
            lax.psum_scatter(half, "dp", scatter_dimension=0, tiled=True).astype(full)
            for half in halves
        ]

    def scatter_core(self, total):
        rows, width = total.shape[0] // 2, total.shape[1]
        total = total.reshape(2, rows, width)
        mine = lax.dynamic_index_in_dim(total, self.core, 0, False)
        arrived = self.swap_core(lax.dynamic_index_in_dim(total, 1 - self.core, 0, False))
        return pick(self.core, mine, arrived), pick(self.core, arrived, mine)

    def flip(self, x, bits):
        return lax.ppermute(x, "dp", [(i, i ^ bits) for i in range(self.count)])


def swap_near(x, flip):
    size = 2 * lax.axis_size("dp")
    return lax.ppermute(x, ("dp", "mp"), [(i, i ^ flip) for i in range(size)])


def swap_group(x):
    return swap_near(x, 1)


def after(x, *others):
    return lax.optimization_barrier((x, *others))[0]


def joint(*values):
    return lax.optimization_barrier(values)


def add_low(pair):
    return (pair[0].astype(full) + pair[1].astype(full)).astype(low)


def roll_rows(x):
    half = x.shape[0] // 2
    return jnp.concatenate([x[half:], x[:half]], 0)


def norm_rows(inputs):
    center = inputs - jnp.mean(inputs, -1, keepdims=True)
    scale = lax.rsqrt(jnp.mean(center * center, -1, keepdims=True) + 1e-05)
    return center * scale, scale


def norm_back(inner, unit, scale):
    return scale * (
        inner
        - jnp.mean(inner, -1, keepdims=True)
        - unit * jnp.mean(inner * unit, -1, keepdims=True)
    )


def gelu_parts(raised):
    cumulative = 0.5 * (1.0 + lax.erf(raised * 0.7071067811865476))
    slope = cumulative + raised * jnp.exp(-0.5 * raised * raised) * 0.3989422804014327
    return raised * cumulative, slope


LIMIT = pltpu.CompilerParams(vmem_limit_bytes=18 * 1024 * 1024)


def whole_block(shape):
    return pl.BlockSpec(shape, lambda *_: (0,) * len(shape))


def shapes(*items):
    return [jax.ShapeDtypeStruct(shape, kind) for shape, kind in items]


def pack_body(core_ref, mix_ref, back_ref, raise_ref, lower_ref, embed_ref, g1_ref, g2_ref, *outs):
    first = core_ref[0] == 0
    rows = back_ref.shape[0]
    spot = lax.broadcasted_iota(jnp.int32, (rows, rows), 0)
    diagonal = spot == lax.broadcasted_iota(jnp.int32, (rows, rows), 1)
    g1, g2 = [
        jnp.sum(jnp.where(diagonal, ref[...], 0.0), 1, keepdims=True) for ref in (g1_ref, g2_ref)
    ]

    def part(index):
        return (mix_ref[index].astype(full) * g1).astype(low)

    def put(index, columns, zero, one):
        outs[index][:, columns] = jnp.where(first, zero, one)
        outs[index + 1][:, columns] = jnp.where(first, one, zero)

    put(0, slice(0, COLS), part(1), part(0))
    put(0, slice(COLS, 2 * COLS), part(2), back_ref[...])
    hidden = raise_ref.shape[1] // 2
    raised = (raise_ref[...].astype(full) * g2).astype(low)
    put(2, slice(0, hidden), raised[:, :hidden], raised[:, hidden:])
    put(2, slice(hidden, 2 * hidden), lower_ref[:, :hidden], lower_ref[:, hidden:])
    put(4, slice(0, COLS), embed_ref[:, :COLS], embed_ref[:, COLS:])


def pack(core, w_qkv, w_out, w_up, w_down, w_proj, g1, g2):
    rows, hidden = w_up.shape
    vmem = pl.BlockSpec(memory_space=pltpu.VMEM)
    return pl.pallas_call(
        pack_body,
        out_shape=shapes(
            *[((rows, 2 * COLS), low)] * 2, *[((rows, hidden), low)] * 2, *[((rows, COLS), low)] * 2
        ),
        in_specs=[pl.BlockSpec(memory_space=pltpu.SMEM)] + [vmem] * 7,
        out_specs=[vmem] * 6,
        name="pack",
    )(core, w_qkv, w_out, w_up, w_down, w_proj, g1, g2)


def end_picks(ends, copies):
    ends = jnp.concatenate([ends] * copies, 0)
    shape = (copies * BLOCK, TOKENS)
    row = lax.broadcasted_iota(jnp.int32, shape, 0) & (BLOCK - 1)
    return lax.broadcasted_iota(jnp.int32, shape, 1) == row * LENGTH + ends


def norm_body(group_ref, x_ref, ends_ref, unit_ref, scale_ref, unit_end_ref, stream_end_ref):
    x = x_ref[...]
    stream = x.astype(full)
    center = stream - jnp.sum(stream, -1, keepdims=True) * (1.0 / WIDTH)
    scale = lax.rsqrt(jnp.sum(center * center, -1, keepdims=True) * (1.0 / WIDTH) + 1e-05)
    unit = (center * scale).astype(low)
    unit_ref[...] = unit
    scale_ref[...] = jnp.broadcast_to(scale, scale_ref.shape)
    picks = end_picks(ends_ref[...], 1).astype(low)
    unit_end_ref[...] = mm(picks, unit).astype(low)
    stream_end_ref[...] = mm(picks, x).astype(low)


def norm_first(group, x, ends):
    steps = ends.shape[0] // BLOCK
    return pl.pallas_call(
        norm_body,
        out_shape=shapes(
            (x.shape, low), ((x.shape[0], 128), full), *[((ends.shape[0], WIDTH), low)] * 2
        ),
        grid_spec=pltpu.PrefetchScalarGridSpec(
            num_scalar_prefetch=1,
            grid=(steps,),
            in_specs=[
                pl.BlockSpec((TOKENS, WIDTH), lambda i, g: ((i + g[0] * (steps // 2)) % steps, 0)),
                pl.BlockSpec((BLOCK, 1), lambda i, g: (i, 0)),
            ],
            out_specs=[
                pl.BlockSpec((TOKENS, WIDTH), lambda i, g: (i, 0)),
                pl.BlockSpec((TOKENS, 128), lambda i, g: (i, 0)),
                pl.BlockSpec((BLOCK, WIDTH), lambda i, g: (i, 0)),
                pl.BlockSpec((BLOCK, WIDTH), lambda i, g: (i, 0)),
            ],
        ),
        name="norm_first",
    )(group, x, ends)


def head_mask(head):
    return lax.broadcasted_iota(jnp.int32, (BLOCK, COLS), 1) // HEAD == head


def head_stack(x):
    zero = jnp.zeros_like(x)
    return jnp.concatenate([jnp.where(head_mask(h), x, zero) for h in range(HEADS_HERE)], 0)


def head_fold(x):
    out = jnp.zeros((BLOCK, COLS), full)
    for h in range(HEADS_HERE):
        out = jnp.where(head_mask(h), x[h * BLOCK : (h + 1) * BLOCK], out)
    return out


def stack_grid():
    row = lax.broadcasted_iota(jnp.int32, (STACK, TOKENS), 0) & (BLOCK - 1)
    token = lax.broadcasted_iota(jnp.int32, (STACK, TOKENS), 1)
    return row, token


def step_rows(i):
    return pl.ds(pl.multiple_of(i * BLOCK, BLOCK), BLOCK)


def attend_body(
    unit_ref, unit_end_ref, ends_ref, kv_ref, qo_ref, mixed_ref, p_ref, q_ref, att_ref, out_ref
):
    i = pl.program_id(0)

    @pl.when(i == 0)
    def _():
        q_ref[...] = mm(unit_end_ref[...], qo_ref[:, :COLS]).astype(low)

    mixed = mm(unit_ref[...], kv_ref[...]).astype(low)
    mixed_ref[...] = mixed
    scores = mm_nt(head_stack(q_ref[step_rows(i), :]), mixed[:, :COLS]) * SCORE_SCALE
    row, token = stack_grid()
    ends = jnp.concatenate([ends_ref[...]] * HEADS_HERE, 0)
    allowed = (token >= row * LENGTH) & (token <= row * LENGTH + ends)
    scores = jnp.where(allowed, scores, -1e30)
    weight = jnp.exp(scores - jnp.max(scores, 1, keepdims=True))
    probs = weight / jnp.sum(weight, 1, keepdims=True)
    p_ref[...] = probs
    att_ref[step_rows(i), :] = head_fold(mm(probs.astype(low), mixed[:, COLS:])).astype(low)

    @pl.when(i == pl.num_programs(0) - 1)
    def _():
        out_ref[...] = mm_nt(att_ref[...], qo_ref[:, COLS:]).astype(low)


def attend(unit, unit_end, ends, kv, qo):
    count = ends.shape[0]
    steps = count // BLOCK
    return pl.pallas_call(
        attend_body,
        grid=(steps,),
        out_shape=shapes(
            ((count * LENGTH, 2 * COLS), low),
            ((steps * STACK, TOKENS), full),
            *[((count, COLS), low)] * 2,
            ((count, WIDTH), low),
        ),
        in_specs=[
            pl.BlockSpec((TOKENS, WIDTH), lambda i: (i, 0)),
            whole_block((count, WIDTH)),
            pl.BlockSpec((BLOCK, 1), lambda i: (i, 0)),
            whole_block(kv.shape),
            whole_block(qo.shape),
        ],
        out_specs=[
            pl.BlockSpec((TOKENS, 2 * COLS), lambda i: (i, 0)),
            pl.BlockSpec((STACK, TOKENS), lambda i: (i, 0)),
            whole_block((count, COLS)),
            whole_block((count, COLS)),
            whole_block((count, WIDTH)),
        ],
        name="attend",
    )(unit, unit_end, ends, kv, qo)


def lane_group():
    return lax.broadcasted_iota(jnp.int32, (BLOCK, 128), 1) // (2 * LENGTH)


def attend_back_body(
    core_ref, d_mid_ref, d_att_ref, unit_ref, unit_end_ref, mixed_ref, p_ref, q_ref, att_ref,
    keep_ref, send_ref, d_mixed_ref, dq_ref, small_ref, sum_ref,
):
    i = pl.program_id(0)
    count = dq_ref.shape[0]

    @pl.when(i == 0)
    def _():
        sum_ref[...] = jnp.zeros_like(sum_ref)

    probs = p_ref[...]
    probs_low = probs.astype(low)
    queries = head_stack(q_ref[step_rows(i), :])
    d_att = head_stack(d_att_ref[step_rows(i), :])
    d_probs = mm_nt(d_att, mixed_ref[:, COLS:])
    d_scores = probs * (d_probs - jnp.sum(probs * d_probs, 1, keepdims=True))
    d_scores = (d_scores * SCORE_SCALE).astype(low)
    dq_ref[step_rows(i), :] = head_fold(mm(d_scores, mixed_ref[:, :COLS])).astype(low)
    d_mixed = jnp.concatenate(
        [mm_tn(d_scores, queries).astype(low), mm_tn(probs_low, d_att).astype(low)], 1
    )
    d_mixed_ref[...] = d_mixed
    spot = lax.broadcasted_iota(jnp.int32, (TOKENS, 128), 0) & (LENGTH - 1)
    lane = lax.broadcasted_iota(jnp.int32, (TOKENS, 128), 1) & (2 * LENGTH - 1)
    squeezed = mm(probs_low, (spot == lane).astype(low))
    squeezed += mm(d_scores, (spot + LENGTH == lane).astype(low))
    for first in (0, 4):
        out = jnp.zeros((BLOCK, 128), full)
        for h in range(first, min(first + 4, HEADS_HERE)):
            out = jnp.where(lane_group() == h - first, squeezed[h * BLOCK : (h + 1) * BLOCK], out)
        place = pl.multiple_of((2 * i + first // 4) * BLOCK, BLOCK)
        small_ref[pl.ds(3 * count + place, BLOCK), :] = out.astype(low)
    sum_ref[...] += mm_tn(unit_ref[...], d_mixed)

    @pl.when(i == pl.num_programs(0) - 1)
    def _():
        first = core_ref[0] == 0
        d_queries = dq_ref[...]
        for piece in range(3):
            small_ref[piece * count : (piece + 1) * count] = d_queries[
                :, piece * 128 : (piece + 1) * 128
            ]
        g_mix = sum_ref[...].astype(low)
        g_query = mm_tn(unit_end_ref[...], d_queries).astype(low)
        g_back = mm_tn(d_mid_ref[...], att_ref[...]).astype(low)
        g_rest = jnp.concatenate([g_query, g_back], 1)
        keep_ref[...] = jnp.where(first, g_mix, g_rest)
        send_ref[...] = jnp.where(first, g_rest, g_mix)


def attend_back(core, d_mid, d_att, unit, unit_end, mixed, probs, queries, attended):
    count = d_mid.shape[0]
    steps = count // BLOCK
    return pl.pallas_call(
        attend_back_body,
        grid=(steps,),
        out_shape=shapes(
            *[((WIDTH, 2 * COLS), low)] * 2,
            ((count * LENGTH, 2 * COLS), low),
            ((count, COLS), low),
            ((3 * count + steps * 2 * BLOCK, 128), low),
        ),
        in_specs=[
            pl.BlockSpec(memory_space=pltpu.SMEM),
            whole_block((count, WIDTH)),
            whole_block((count, COLS)),
            pl.BlockSpec((TOKENS, WIDTH), lambda i: (i, 0)),
            whole_block((count, WIDTH)),
            pl.BlockSpec((TOKENS, 2 * COLS), lambda i: (i, 0)),
            pl.BlockSpec((STACK, TOKENS), lambda i: (i, 0)),
            whole_block((count, COLS)),
            whole_block((count, COLS)),
        ],
        out_specs=[
            whole_block((WIDTH, 2 * COLS)),
            whole_block((WIDTH, 2 * COLS)),
            pl.BlockSpec((TOKENS, 2 * COLS), lambda i: (i, 0)),
            whole_block((count, COLS)),
            whole_block((3 * count + steps * 2 * BLOCK, 128)),
        ],
        scratch_shapes=[pltpu.VMEM((WIDTH, 2 * COLS), full)],
        name="attend_back",
        compiler_params=LIMIT,
    )(core, d_mid, d_att, unit, unit_end, mixed, probs, queries, attended)


def lower_back_body(flag_ref, d_out_ref, active_ref, pooled_ref, d_embed_ref, out_ref):
    hidden = active_ref.shape[1]
    quarter = WIDTH // 4
    out_ref[:, :hidden] = mm_tn(d_out_ref[...], active_ref[...]).astype(low)
    here = d_embed_ref[:, :quarter]
    for index in range(1, 4):
        part = d_embed_ref[:, index * quarter : (index + 1) * quarter]
        here = jnp.where(flag_ref[0] == index, part, here)
    out_ref[:, hidden:] = mm_tn(pooled_ref[...], here).astype(low)


def lower_back(flag, d_out, active, pooled, d_embed):
    vmem = pl.BlockSpec(memory_space=pltpu.VMEM)
    return pl.pallas_call(
        lower_back_body,
        out_shape=jax.ShapeDtypeStruct((WIDTH, active.shape[1] + WIDTH // 4), low),
        in_specs=[pl.BlockSpec(memory_space=pltpu.SMEM)] + [vmem] * 4,
        out_specs=vmem,
        name="lower_back",
        compiler_params=LIMIT,
    )(flag, d_out, active, pooled, d_embed)


def own_slots(index_ref, valid, main):
    count = valid.shape[1]
    row = lax.broadcasted_iota(jnp.int32, (CAP_DEV, count), 0)
    spare = CAP_DEV - main
    first = index_ref[0] * main + row
    second = count // CAP_DEV * main + index_ref[0] * spare + row - main
    slot = jnp.where(row < main, first, second)
    spot = lax.broadcasted_iota(jnp.int32, (CAP_DEV, count), 1) == slot
    own = jnp.sum(jnp.where(spot, valid, 0.0), 1, keepdims=True)
    return jnp.where(spot, valid, 0.0), own


def loss_front_body(
    main, index_ref, middle_ref, *refs
):
    feeds = refs[:4]
    valid_ref, embed_ref, picture_ref = refs[4:7]
    pooled_ref, text_ref, inverse_ref, weight_ref, row_ref, total_ref = refs[7:]
    total = middle_ref[...]
    for ref in feeds:
        total = total + ref[...].astype(full)
    pooled = total.astype(low)
    pooled_ref[...] = pooled
    embedding = mm(pooled, embed_ref[...])
    inverse = lax.rsqrt(jnp.sum(embedding * embedding, -1, keepdims=True) + 1e-06)
    text = embedding * inverse
    text_ref[...] = text
    inverse_ref[...] = jnp.broadcast_to(inverse, inverse_ref.shape)
    sims = LOGIT_SCALE * mm_nt(text.astype(low), picture_ref[...])
    valid = valid_ref[...]
    target, own = own_slots(index_ref, valid, main)
    weight = jnp.where((own > 0.5) & (valid > 0.5), jnp.exp(sims), 0.0)
    weight_ref[...] = weight
    row_safe = jnp.where(own > 0.5, jnp.sum(weight, 1, keepdims=True), 1.0)
    row_ref[...] = jnp.broadcast_to(0.5 / row_safe, row_ref.shape)
    part = 0.5 * jnp.log(row_safe) - jnp.sum(target * sims, 1, keepdims=True)
    part = jnp.sum(part, 0, keepdims=True)
    columns = jnp.sum(weight, 0, keepdims=True)
    blocks = columns.shape[1] // 128
    for block in range(blocks):
        total_ref[block : block + 1] = columns[:, block * 128 : (block + 1) * 128]
    total_ref[blocks:] = jnp.broadcast_to(part * (1.0 / 128), (1, 128))


def loss_front(main, index, middle, feeds, valid, w_embed, pictures):
    vmem = pl.BlockSpec(memory_space=pltpu.VMEM)
    count = pictures.shape[0]
    return pl.pallas_call(
        functools.partial(loss_front_body, main),
        out_shape=shapes(
            ((CAP_DEV, WIDTH), low),
            ((CAP_DEV, WIDTH), full),
            ((CAP_DEV, 128), full),
            ((CAP_DEV, count), full),
            ((CAP_DEV, 128), full),
            ((count // 128 + 1, 128), full),
        ),
        in_specs=[pl.BlockSpec(memory_space=pltpu.SMEM)] + [vmem] * 8,
        out_specs=[vmem] * 6,
        name="loss_front",
        compiler_params=LIMIT,
    )(index, middle, *feeds, valid, w_embed, pictures)


def loss_back_body(main, parts, index_ref, *refs):
    totals = refs[:parts]
    valid_ref, text_ref, inverse_ref, weight_ref, row_ref, picture_ref = refs[parts:-2]
    d_embed_ref, objective_ref = refs[-2:]
    total = totals[0][...]
    for ref in totals[1:]:
        total = total + ref[...]
    valid = valid_ref[...]
    blocks = valid.shape[1] // 128
    columns = jnp.concatenate([total[block : block + 1] for block in range(blocks)], 1)
    col_safe = jnp.where(valid > 0.5, columns, 1.0)
    logs = 0.5 * jnp.sum(jnp.log(col_safe), 1, keepdims=True)
    rows_part = jnp.sum(total[blocks:], 1, keepdims=True)
    objective_ref[...] = jnp.broadcast_to(logs + rows_part, objective_ref.shape)
    target, _ = own_slots(index_ref, valid, main)
    d_sims = weight_ref[...] * (row_ref[:, :1] + 0.5 / col_safe) - target
    d_unit = LOGIT_SCALE * mm(d_sims.astype(low), picture_ref[...])
    text = text_ref[...]
    along = jnp.sum(text * d_unit, -1, keepdims=True)
    d_embed_ref[...] = ((d_unit - text * along) * inverse_ref[:, :1]).astype(low)


def loss_back(main, index, totals, valid, text, inverse, weight, row, pictures):
    vmem = pl.BlockSpec(memory_space=pltpu.VMEM)
    return pl.pallas_call(
        functools.partial(loss_back_body, main, len(totals)),
        out_shape=shapes(((CAP_DEV, WIDTH), low), ((1, 128), full)),
        in_specs=[pl.BlockSpec(memory_space=pltpu.SMEM)] + [vmem] * (6 + len(totals)),
        out_specs=[vmem] * 2,
        name="loss_back",
        compiler_params=LIMIT,
    )(index, *totals, valid, text, inverse, weight, row, pictures)


def place_rows(picks, rows):
    high = rows.astype(low)
    rest = (rows - high.astype(full)).astype(low)
    return mm_tn(picks, jnp.concatenate([high, rest], 0))


def captions_body(
    start, blocks, group_ref, ends_ref, unit_ref, scale_ref, d_mid_ref, d_mixed_ref, dq_ref,
    q_far_ref, d_att_far_ref, small_far_ref, kv_ref, qo_ref, kv_far_ref, qo_far_ref, *refs,
):
    out_ref, inner_end_ref = refs[-2:]
    i = pl.program_id(0)
    count = dq_ref.shape[0]
    steps = count // BLOCK
    far = (start + steps // 2) % steps
    rows = blocks * BLOCK

    @pl.when(i == 0)
    def _():
        dq_far = jnp.concatenate(
            [
                small_far_ref[piece * count + far * BLOCK : piece * count + far * BLOCK + rows]
                for piece in range(3)
            ],
            1,
        )
        inner_end_ref[...] = mm_nt(
            dq_ref[start * BLOCK : start * BLOCK + rows], qo_ref[:, :COLS]
        ) + mm_nt(dq_far, qo_far_ref[:, :COLS])

    row, token = stack_grid()
    own_caption = token // LENGTH == row
    lane = lax.broadcasted_iota(jnp.int32, (128, TOKENS), 0) & (2 * LENGTH - 1)
    spot = lax.broadcasted_iota(jnp.int32, (128, TOKENS), 1) & (LENGTH - 1)
    zero = jnp.zeros((BLOCK, 128), low)
    place = pl.multiple_of(3 * count + 2 * BLOCK * (far + i), 2 * BLOCK)
    packed = small_far_ref[pl.ds(place, 2 * BLOCK), :]
    pair = jnp.concatenate(
        [
            jnp.where(lane_group() == h % 4, packed[h // 4 * BLOCK : (h // 4 + 1) * BLOCK], zero)
            for h in range(HEADS_HERE)
        ],
        0,
    )
    probs = jnp.where(own_caption, mm(pair, (spot == lane).astype(low)), 0.0).astype(low)
    d_scores = jnp.where(
        own_caption, mm(pair, (spot + LENGTH == lane).astype(low)), 0.0
    ).astype(low)
    d_mixed = jnp.concatenate(
        [
            mm_tn(d_scores, head_stack(q_far_ref[step_rows(far + i), :])).astype(low),
            mm_tn(probs, head_stack(d_att_far_ref[step_rows(far + i), :])).astype(low),
        ],
        1,
    )
    inner = mm_nt(d_mixed_ref[...], kv_ref[...]) + mm_nt(d_mixed, kv_far_ref[...])
    picks = end_picks(ends_ref[...], 2).astype(low)
    inner += place_rows(picks, inner_end_ref[step_rows(i), :])
    unit = unit_ref[...].astype(full)
    flat = jnp.sum(inner, -1, keepdims=True) * (1.0 / WIDTH)
    tilt = jnp.sum(inner * unit, -1, keepdims=True) * (1.0 / WIDTH)
    out_ref[...] = place_rows(picks, d_mid_ref[...]) + scale_ref[:, :1] * (
        inner - flat - unit * tilt
    )


def captions_back(
    start, blocks, group, ends, unit, scale, d_mid, d_mixed, dq, q_far, d_att_far, small_far, kv, qo,
    kv_far, qo_far, done=None,
):
    count = ends.shape[0]
    steps = count // BLOCK
    half = steps // 2
    operands = [
        group, ends, unit, scale, d_mid, d_mixed, dq, q_far, d_att_far, small_far, kv, qo,
        kv_far, qo_far,
    ]
    in_specs = [
        pl.BlockSpec((BLOCK, 1), lambda i, g: (i + start, 0)),
        pl.BlockSpec((TOKENS, WIDTH), lambda i, g: (i + start, 0)),
        pl.BlockSpec((TOKENS, 128), lambda i, g: (i + start, 0)),
        pl.BlockSpec((BLOCK, WIDTH), lambda i, g: (i + start, 0)),
        pl.BlockSpec((TOKENS, 2 * COLS), lambda i, g: (i + start, 0)),
        *[whole_block((count, COLS))] * 3,
        whole_block(small_far.shape),
    ] + [whole_block(kv.shape)] * 4
    aliases = {}
    if done is not None:
        aliases = {len(operands): 0}
        operands.append(done)
        in_specs.append(pl.BlockSpec(memory_space=pl.ANY))
    return pl.pallas_call(
        functools.partial(captions_body, start, blocks),
        out_shape=jax.ShapeDtypeStruct(unit.shape, full),
        grid_spec=pltpu.PrefetchScalarGridSpec(
            num_scalar_prefetch=1,
            grid=(blocks,),
            in_specs=in_specs,
            out_specs=pl.BlockSpec(
                (TOKENS, WIDTH), lambda i, g: ((i + start + g[0] * half) % steps, 0)
            ),
            scratch_shapes=[pltpu.VMEM((blocks * BLOCK, WIDTH), full)],
        ),
        input_output_aliases=aliases,
        name="captions_back",
    )(*operands)


def local(
    captions,
    image_cache,
    send_order,
    arrive_order,
    counts,
    keep_mask,
    end_pos,
    w_qkv,
    w_out,
    w_up,
    w_down,
    w_proj,
    ln1_gain,
    ln2_gain,
):
    plane = Plane()
    core = plane.core
    group = lax.axis_index("mp")
    spread = plane.count
    rows_dev, length, width = captions.shape
    rows = w_out.shape[0]
    per_peer = rows_dev // spread
    hidden = w_up.shape[1] // 2
    core_flag = core.reshape(1).astype(jnp.int32)
    group_flag = group.reshape(1).astype(jnp.int32)

    packed = pack(
        core_flag,
        w_qkv.transpose(1, 0, 2),
        w_out,
        w_up,
        w_down,
        w_proj,
        ln1_gain[None],
        ln2_gain[None],
    )
    def order_ends(end_pos):
        flipped = jnp.concatenate([end_pos, end_pos], 0)
        return lax.dynamic_slice_in_dim(flipped, group * CAP_DEV, rows_dev, 0)[:, None]

    wide = width // 2

    def pictures_of_batch(incoming):
        own_arrive = lax.dynamic_slice_in_dim(arrive_order[0], group * CAP_DEV, CAP_DEV, 0)
        take_in = (own_arrive[:, None] == places[None, :]).astype(low)
        pictures = mm(take_in, incoming.reshape(rows_dev, width)).astype(low)
        mine = pick(core, pictures[:, :wide], pictures[:, wide:])
        send = pick(core, pictures[:, wide:], pictures[:, :wide])
        return mine, send

    def prepare(image_cache):
        cached = image_cache.astype(full)
        norms = jnp.sum(cached * cached, -1, keepdims=True)
        cached = (cached * lax.rsqrt(norms + 1e-06)).astype(low)
        hand_out = (send_order[0][:, None] == places[None, :]).astype(low)
        return mm(hand_out, cached).astype(low).reshape(spread, per_peer, width)

    places = jnp.arange(rows_dev, dtype=jnp.int32)

    def deal(outgoing):
        return lax.all_to_all(outgoing, "dp", split_axis=0, concat_axis=0, tiled=True)

    def first_parts(stream, ends):
        return norm_first(group_flag, stream.reshape(rows_dev * length, width), ends)

    def attention_of(kv, qo, parts, ends):
        return attend(parts[0], parts[2], ends, kv, qo)

    main = rows if plane.fast else CAP_DEV
    spare = CAP_DEV - main
    if plane.fast:

        def join(feed, embed, half):
            parts = [half[main:, i * 128 : (i + 1) * 128] for i in range(wide // 128)]
            return jnp.concatenate([feed, embed, half[:main], jnp.concatenate(parts, 0)], 1)

        mix_cuts = (0, 2 * COLS)
        cuts = (0, 2 * hidden, 2 * hidden + 2 * wide + 128)
        arrived = plane.swap_core(packed[1])
        arrived, cache = joint(arrived, image_cache)
        block = plane.join_cores(packed[0], arrived)
        incoming = deal(prepare(cache))
        up = plane.shift_depth(block, 1)
        down = plane.shift_depth(block, -1)
        across = plane.swap_side(block)
        up, down, across, block = joint(up, down, across, block)

        mixes = plane.place(plane.empty(2 * rows, mix_cuts, block), mix_cuts, 0, block, across)
        far = plane.shift_depth(up, 1)
        across_up = plane.swap_side(up)
        across_down = plane.swap_side(down)
        far, across_up, across_down, incoming = joint(far, across_up, across_down, incoming)

        across = plane.swap_side(far)
        pictures = pictures_of_batch(incoming)
        mine = join(packed[2], packed[4], pictures[0])
        arrived = plane.swap_core(join(packed[3], packed[5], pictures[1]))
        mixes = plane.place(mixes, mix_cuts, 1, up, across_up)
        mixes = plane.place(mixes, mix_cuts, -1, down, across_down)
        across, arrived, mixes, counts, keep_mask, end_pos = joint(
            across, arrived, mixes, counts, keep_mask, end_pos
        )

        block = plane.join_cores(mine, arrived)
        one = plane.shift_depth(block, 1)
        across_block = plane.swap_side(block)
        mixes = plane.place(mixes, mix_cuts, 2, far, across)
        mix_own = mixes[0].reshape(width, 2 * COLS)
        mix_other = plane.swap_core(mix_own)
        far_own = swap_group(mix_own)
        kv = pick(core, mix_own, mix_other)
        qo = pick(core, mix_other, mix_own)
        ends = order_ends(end_pos)
        parts = first_parts(after(captions, block), ends)
        one, kv, qo, *parts = joint(one, kv, qo, *parts)

        two = plane.shift_depth(one, 1)
        across_one = plane.swap_side(one)
        stream_near = swap_near(parts[3], 2)
        attending = attention_of(kv, qo, parts, ends)
        two, across_block, across_one, stream_near, *attending = joint(
            two, across_block, across_one, stream_near, *attending
        )

        three = plane.shift_depth(two, 1)
        across_two = plane.swap_side(two)
        wholes = plane.place(plane.empty(2 * rows, cuts, attending[-1]), cuts, 0, block, across_block)
        wholes = plane.place(wholes, cuts, 1, one, across_one)
        attention = after(attending[-1], far_own)
        near = [swap_near(attention, flip) for flip in (1, 2, 3)]
        three, across_two, *near = joint(three, across_two, *near)

        across = plane.swap_side(three)
        queries_far = swap_group(attending[2])
        far_other = plane.swap_core(far_own)
        kv_far = pick(core, far_own, far_other)
        qo_far = pick(core, far_other, far_own)
        wholes = plane.place(wholes, cuts, 2, two, across_two)
        across, queries_far, kv_far, qo_far, wholes = joint(
            across, queries_far, kv_far, qo_far, wholes
        )
        wholes = plane.place(wholes, cuts, 3, three, across)
        feeds, third = [whole.reshape(width, -1) for whole in wholes]
        third_other = plane.swap_core(third)

        def images(x):
            extra = x[:, 2 * wide :].reshape(spread, wide // 128, spare, 128)
            extra = extra.transpose(0, 2, 1, 3).reshape(spread * spare, wide)
            return jnp.concatenate([x[:, wide : 2 * wide], extra], 0)

        image_halves = images(third), images(third_other)
        embed_halves = third[:, :wide], third_other[:, :wide]
    else:
        pictures = pictures_of_batch(deal(prepare(image_cache)))
        ends = order_ends(end_pos)
        parts = first_parts(captions, ends)
        mix_own = plane.gather_plain(packed[0], packed[1])
        mix_other = plane.swap_core(mix_own)
        far_own = swap_group(mix_own)
        kv = pick(core, mix_own, mix_other)
        qo = pick(core, mix_other, mix_own)
        attending = attention_of(kv, qo, parts, ends)
        feeds = plane.gather_plain(packed[2], packed[3])
        image_half = plane.gather_plain(*pictures)
        image_halves = image_half, plane.swap_core(image_half)
        embed_half = plane.gather_plain(packed[4], packed[5])
        embed_halves = embed_half, plane.swap_core(embed_half)
        far_other = plane.swap_core(far_own)
        kv_far = pick(core, far_own, far_other)
        qo_far = pick(core, far_other, far_own)
        stream_near = swap_near(parts[3], 2)
        attention = attending[-1]
        near = [swap_near(attention, flip) for flip in (1, 2, 3)]
        queries_far = swap_group(attending[2])
    unit, scale, unit_end, stream_end = parts
    mixed, probs, queries, attended, _ = attending

    def sides(pair):
        return jnp.concatenate([pick(core, *pair), pick(core, pair[1], pair[0])], 1)

    pictures_all = sides(image_halves)
    w_embed = sides(embed_halves)

    from_group, from_core, from_both = near
    attention = jnp.concatenate([attention, from_core], 0).astype(full)
    attention = attention + jnp.concatenate(
        [roll_rows(from_group), roll_rows(from_both)], 0
    ).astype(full)
    middle = jnp.concatenate([stream_end, stream_near], 0).astype(full) + attention
    unit_second, scale_second = norm_rows(middle)
    second_low = unit_second.astype(low)
    w_raise = feeds[:, :hidden]
    w_lower = feeds[:, hidden:]
    active, slope = gelu_parts(mm(second_low, w_raise))
    active = active.astype(low)
    lowered = mm_nt(active, w_lower).astype(low)
    feed_parts = [lowered[:CAP_DEV]] + [
        swap_near(lowered[flip * CAP_DEV : (flip + 1) * CAP_DEV], flip) for flip in (1, 2, 3)
    ]

    keep_rows = keep_mask.reshape(spread, MICRO, CAP_DEV) == 1
    filled = jnp.arange(CAP_DEV, dtype=jnp.int32)[None, None, :] < counts[:, :, None]
    valid = (keep_rows & filled).astype(full)
    total_valid = jnp.sum(valid)
    batch_valid = lax.dynamic_index_in_dim(valid, group, 1, False)
    batch_valid = jnp.concatenate(
        [batch_valid[:, :main].reshape(-1), batch_valid[:, main:].reshape(-1)]
    )[None]
    if plane.fast:
        batch_valid = after(batch_valid, near[0])
    place_flag = plane.index.reshape(1).astype(jnp.int32)
    pooled, unit_text, inverse, weight, row_half, totals = loss_front(
        main, place_flag, middle[:CAP_DEV], feed_parts, batch_valid, w_embed, pictures_all
    )
    if plane.fast:
        pooled_group = swap_near(pooled, 1)
        sent = [plane.flip(totals, bits) for bits in (1, 4, 5)]
        *sent, pooled_group = joint(*sent, pooled_group)
        totals = (totals + sent[0]) + (sent[1] + sent[2])
        totals = totals, *joint(*[plane.flip(totals, bits) for bits in (2, 8, 10)])
    else:
        totals = (lax.psum(totals, "dp"),)
    d_embed, objective = loss_back(
        main, place_flag, totals, batch_valid, unit_text, inverse, weight, row_half, pictures_all
    )

    d_embed_near = [swap_near(d_embed, flip) for flip in (1, 2, 3)]
    if plane.fast:
        pooled_pair = jnp.concatenate([pooled, pooled_group], 0)
        *d_embed_near, objective, pooled_near = joint(
            *d_embed_near, objective, plane.swap_core(pooled_pair)
        )
        pooled_all = jnp.concatenate([pooled_pair, pooled_near], 0)
    else:
        pooled_all = jnp.concatenate([pooled] + [swap_near(pooled, flip) for flip in (1, 2, 3)], 0)
    d_embed_all = jnp.concatenate([d_embed, *d_embed_near], 0)
    d_pooled = mm_nt(d_embed_all, w_embed)
    d_out_low = d_pooled.astype(low)
    d_raised = (mm(d_out_low, w_lower) * slope).astype(low)
    d_second = mm_nt(d_raised, w_raise).astype(low)
    g_raise = mm_tn(second_low, d_raised).astype(low)
    d_out_late = after(d_out_low, g_raise, d_second)
    g_lower = lower_back(2 * group_flag + core_flag, d_out_late, active, pooled_all, d_embed_all)
    if plane.fast:
        raise_stay, raise_in = plane.halve(g_raise.reshape(2, 2, 2, 2 * rows, -1), 1, 4)
        lower_stay, lower_in = plane.halve(g_lower.reshape(2, 2, 2, 2 * rows, -1), 2, 2)
    d_second = add_low((d_second[:rows_dev], swap_near(d_second[rows_dev:], 2)))
    inner = d_second.astype(full) + roll_rows(swap_near(d_second, 1)).astype(full)
    d_middle = d_pooled[:rows_dev] + norm_back(
        inner, unit_second[:rows_dev], scale_second[:rows_dev]
    )

    d_middle_low = d_middle.astype(low)
    d_attended = mm(d_middle_low, qo[:, COLS:]).astype(low)
    d_attended_far = swap_group(d_attended)
    g_keep, g_send, d_mixed, d_queries, small = attend_back(
        core_flag, d_middle_low, d_attended, unit, unit_end, mixed, probs, queries, attended
    )

    def early_parts(raise_sum, lower_sum):
        grad_down = jnp.concatenate([part[:, :hidden] for part in lower_sum], 1)
        proj_own = jnp.concatenate([part[:, hidden:] for part in lower_sum], 1)
        raised_sum = jnp.concatenate(raise_sum, 1)
        gain_second = jnp.sum(raised_sum * w_up.astype(full), 1)
        early = jnp.stack([gain_second, jnp.broadcast_to(objective[0, 0], (rows,))])
        return proj_own, grad_down, raised_sum, early

    def captions_part(start, blocks, d_queries_here, far_parts, done=None):
        return captions_back(
            start, blocks, group_flag, ends, unit, scale, d_middle, d_mixed, d_queries_here, queries_far,
            *far_parts, kv, qo, kv_far, qo_far, done=done,
        )

    if plane.fast:
        raise_stay, raise_in, lower_stay, lower_in, small, d_queries, g_send, d_attended_far = joint(
            raise_stay, raise_in, lower_stay, lower_in, small, d_queries, g_send, d_attended_far
        )
        small_far = swap_group(small)
        mix_in = plane.swap_core(g_send)
        raise_pair = add_low((raise_stay, raise_in))
        lower_pair = add_low((lower_stay, lower_in))
        raise_side = plane.halve(raise_pair, 1, 2)
        small_far, mix_in, *raise_side, lower_pair = joint(
            small_far, mix_in, *raise_side, lower_pair
        )
        raise_last = plane.halve(add_low(raise_side), 0, 8)
        lower_depth = plane.halve(lower_pair, 1, 4)
        mix_pair = add_low((g_keep, mix_in)).reshape(2, 2, 2, 2 * rows, 2 * COLS)
        mix_side = plane.halve(mix_pair, 2, 2)
        far_parts = d_attended_far, small_far
        half = rows_dev // BLOCK // 2
        first_half = captions_part(0, half, after(d_queries, mix_side[0]), far_parts)
        raise_last, lower_depth, mix_side, first_half = joint(
            raise_last, lower_depth, mix_side, first_half
        )
        mix_depth = plane.halve(add_low(mix_side), 1, 4)
        lower_last = plane.halve(add_low(lower_depth), 0, 8)
        starts = after(d_queries, mix_depth[0], lower_last[0])
        third_part = captions_part(half, half // 2, starts, far_parts, first_half)
        mix_depth, lower_last, third_part = joint(mix_depth, lower_last, third_part)
        mix_last = plane.halve(add_low(mix_depth), 0, 8)
        starts = after(d_queries, mix_last[0])
        grad_captions = captions_part(half + half // 2, half - half // 2, starts, far_parts, third_part)
        raise_sum, lower_sum = [
            plane.scatter_core(pair[0].astype(full) + pair[1].astype(full))
            for pair in (raise_last, lower_last)
        ]
        proj_own, grad_down, raised_sum, early = early_parts(raise_sum, lower_sum)
        proj_far, early_far = swap_group(proj_own), swap_group(early)
        mix_last, proj_far, early_far, grad_down, raised_sum, grad_captions = joint(
            mix_last, proj_far, early_far, grad_down, raised_sum, grad_captions
        )
        mix_sum = plane.scatter_core(mix_last[0].astype(full) + mix_last[1].astype(full))
    else:
        far_parts = d_attended_far, swap_group(small)
        grad_captions = captions_part(0, rows_dev // BLOCK, d_queries, far_parts)
        raise_sum = plane.scatter_plain(g_raise)
        lower_sum = plane.scatter_plain(g_lower)
        proj_own, grad_down, raised_sum, early = early_parts(raise_sum, lower_sum)
        proj_far, early_far = swap_group(proj_own), swap_group(early)
        mix_sum = plane.scatter_plain(g_keep, g_send)
    grad_captions = grad_captions.reshape(rows_dev, length, width)

    grad_proj = pick(
        group,
        jnp.concatenate([proj_own, proj_far], 1),
        jnp.concatenate([proj_far, proj_own], 1),
    )
    grad_out = mix_sum[1][:, COLS:]
    unit_mix = jnp.stack([mix_sum[1][:, :COLS], mix_sum[0][:, :COLS], mix_sum[0][:, COLS:]], 1)
    grad_qkv = unit_mix * ln1_gain[:, None, None]
    grad_up = raised_sum * ln2_gain[:, None]
    early = early + early_far
    loss = early[1, 0] / total_valid
    gain_first = jnp.sum(unit_mix * w_qkv.astype(full), (1, 2))[None]
    gain_first = gain_first + swap_group(gain_first)
    return (
        loss,
        grad_captions,
        grad_qkv,
        grad_out,
        grad_up,
        grad_down,
        grad_proj,
        gain_first[0],
        early[0],
    )


def solution(mesh):
    return jax.shard_map(
        local,
        mesh=mesh,
        in_specs=(
            P("dp", None, None),
            P("dp", None),
            P("dp", None),
            P("dp", None),
            P(),
            P(),
            P("dp"),
            P("dp", None, "mp"),
            P("dp", "mp"),
            P("dp", "mp"),
            P("dp", "mp"),
            P("dp", None),
            P("dp"),
            P("dp"),
        ),
        out_specs=(
            P(),
            P("dp", None, None),
            P("dp", None, "mp"),
            P("dp", "mp"),
            P("dp", "mp"),
            P("dp", "mp"),
            P("dp", None),
            P("dp"),
            P("dp"),
        ),
        check_vma=False,
    )
```

```python
import functools
import math

import jax
import jax.numpy as jnp
from jax import lax
from jax.experimental import pallas as pl
from jax.experimental.pallas import tpu as pltpu
from jax.sharding import PartitionSpec as P

HEAD = 64
MICRO = 2
CAP_DEV = 64
LOGIT_SCALE = 40.0
SCORE_SCALE = 1.0 / math.sqrt(HEAD)
LENGTH = 16
WIDTH = 768
HEADS_HERE = 6
COLS = HEADS_HERE * HEAD
BLOCK = 32
TOKENS = BLOCK * LENGTH
STACK = HEADS_HERE * BLOCK

low = jnp.bfloat16
full = jnp.float32


def mm(a, b):
    return lax.dot_general(a, b, (((1,), (0,)), ((), ())), preferred_element_type=full)


def mm_nt(a, b):
    return lax.dot_general(a, b, (((1,), (1,)), ((), ())), preferred_element_type=full)


def mm_tn(a, b):
    return lax.dot_general(a, b, (((0,), (0,)), ((), ())), preferred_element_type=full)


def pick(flag, when_zero, when_one):
    return jnp.where(flag == 0, when_zero, when_one)


class Plane:
    def __init__(self):
        self.count = lax.axis_size("dp")
        self.index = lax.axis_index("dp")
        self.core = self.index % 2
        self.side = (self.index // 2) % 2
        self.depth = self.index // 4
        self.fast = self.count == 16

    def swap_core(self, x):
        return lax.ppermute(x, "dp", [(i, i ^ 1) for i in range(self.count)])

    def swap_side(self, x):
        return lax.ppermute(x, "dp", [(i, i ^ 2) for i in range(self.count)])

    def shift_depth(self, x, step):
        return lax.ppermute(
            x, "dp", [(i, (i + 4 * step) % self.count) for i in range(self.count)]
        )

    def join_cores(self, mine, arrived):
        rows, width = mine.shape
        block = jnp.zeros((2, rows, width), mine.dtype)
        block = lax.dynamic_update_slice(block, mine[None], (self.core, 0, 0))
        block = lax.dynamic_update_slice(block, arrived[None], (1 - self.core, 0, 0))
        return block.reshape(2 * rows, width)

    def place(self, wholes, cuts, step, here, across):
        spot = ((self.depth - step) % 4) * 2
        for block, at in ((here, spot + self.side), (across, spot + 1 - self.side)):
            wholes = [
                lax.dynamic_update_slice(whole, block[None, :, start:end], (at, 0, 0))
                for whole, start, end in zip(wholes, cuts, cuts[1:])
            ]
        return wholes

    def empty(self, rows, cuts, start_of):
        zero = after(jnp.zeros((), low), start_of)
        return [
            jnp.broadcast_to(zero, (self.count // 2, rows, end - start))
            for start, end in zip(cuts, cuts[1:])
        ]

    def gather_plain(self, mine, send):
        zero_all = lax.all_gather(pick(self.core, mine, send), "dp", axis=0, tiled=True)
        one_all = lax.all_gather(pick(self.core, send, mine), "dp", axis=0, tiled=True)
        return pick(self.core, zero_all, one_all)

    def halve(self, x, axis, bit):
        spot = (self.index // bit) % 2
        stay = lax.dynamic_index_in_dim(x, spot, axis, False)
        leave = lax.dynamic_index_in_dim(x, 1 - spot, axis, False)
        return stay, lax.ppermute(leave, "dp", [(i, i ^ bit) for i in range(self.count)])

    def scatter_plain(self, keep, send=None):
        if send is None:
            send = jnp.zeros_like(keep)
        halves = (pick(self.core, keep, send), pick(self.core, send, keep))
        return [
            lax.psum_scatter(half, "dp", scatter_dimension=0, tiled=True).astype(full)
            for half in halves
        ]

    def scatter_core(self, total):
        rows, width = total.shape[0] // 2, total.shape[1]
        total = total.reshape(2, rows, width)
        mine = lax.dynamic_index_in_dim(total, self.core, 0, False)
        arrived = self.swap_core(lax.dynamic_index_in_dim(total, 1 - self.core, 0, False))
        return pick(self.core, mine, arrived), pick(self.core, arrived, mine)

    def flip(self, x, bits):
        return lax.ppermute(x, "dp", [(i, i ^ bits) for i in range(self.count)])


def swap_near(x, flip):
    size = 2 * lax.axis_size("dp")
    return lax.ppermute(x, ("dp", "mp"), [(i, i ^ flip) for i in range(size)])


def swap_group(x):
    return swap_near(x, 1)


def after(x, *others):
    return lax.optimization_barrier((x, *others))[0]


def joint(*values):
    return lax.optimization_barrier(values)


def add_low(pair):
    return (pair[0].astype(full) + pair[1].astype(full)).astype(low)


def roll_rows(x):
    half = x.shape[0] // 2
    return jnp.concatenate([x[half:], x[:half]], 0)


def norm_rows(inputs):
    center = inputs - jnp.mean(inputs, -1, keepdims=True)
    scale = lax.rsqrt(jnp.mean(center * center, -1, keepdims=True) + 1e-05)
    return center * scale, scale


def norm_back(inner, unit, scale):
    return scale * (
        inner
        - jnp.mean(inner, -1, keepdims=True)
        - unit * jnp.mean(inner * unit, -1, keepdims=True)
    )


def gelu_parts(raised):
    cumulative = 0.5 * (1.0 + lax.erf(raised * 0.7071067811865476))
    slope = cumulative + raised * jnp.exp(-0.5 * raised * raised) * 0.3989422804014327
    return raised * cumulative, slope


LIMIT = pltpu.CompilerParams(vmem_limit_bytes=18 * 1024 * 1024)


def whole_block(shape):
    return pl.BlockSpec(shape, lambda *_: (0,) * len(shape))


def shapes(*items):
    return [jax.ShapeDtypeStruct(shape, kind) for shape, kind in items]


def pack_body(core_ref, mix_ref, back_ref, raise_ref, lower_ref, embed_ref, g1_ref, g2_ref, *outs):
    first = core_ref[0] == 0
    rows = back_ref.shape[0]
    spot = lax.broadcasted_iota(jnp.int32, (rows, rows), 0)
    diagonal = spot == lax.broadcasted_iota(jnp.int32, (rows, rows), 1)
    g1, g2 = [
        jnp.sum(jnp.where(diagonal, ref[...], 0.0), 1, keepdims=True) for ref in (g1_ref, g2_ref)
    ]

    def part(index):
        return (mix_ref[index].astype(full) * g1).astype(low)

    def put(index, columns, zero, one):
        outs[index][:, columns] = jnp.where(first, zero, one)
        outs[index + 1][:, columns] = jnp.where(first, one, zero)

    put(0, slice(0, COLS), part(1), part(0))
    put(0, slice(COLS, 2 * COLS), part(2), back_ref[...])
    hidden = raise_ref.shape[1] // 2
    raised = (raise_ref[...].astype(full) * g2).astype(low)
    put(2, slice(0, hidden), raised[:, :hidden], raised[:, hidden:])
    put(2, slice(hidden, 2 * hidden), lower_ref[:, :hidden], lower_ref[:, hidden:])
    put(4, slice(0, COLS), embed_ref[:, :COLS], embed_ref[:, COLS:])


def pack(core, w_qkv, w_out, w_up, w_down, w_proj, g1, g2):
    rows, hidden = w_up.shape
    vmem = pl.BlockSpec(memory_space=pltpu.VMEM)
    return pl.pallas_call(
        pack_body,
        out_shape=shapes(
            *[((rows, 2 * COLS), low)] * 2, *[((rows, hidden), low)] * 2, *[((rows, COLS), low)] * 2
        ),
        in_specs=[pl.BlockSpec(memory_space=pltpu.SMEM)] + [vmem] * 7,
        out_specs=[vmem] * 6,
        name="pack",
    )(core, w_qkv, w_out, w_up, w_down, w_proj, g1, g2)


def end_picks(ends, copies):
    ends = jnp.concatenate([ends] * copies, 0)
    shape = (copies * BLOCK, TOKENS)
    row = lax.broadcasted_iota(jnp.int32, shape, 0) & (BLOCK - 1)
    return lax.broadcasted_iota(jnp.int32, shape, 1) == row * LENGTH + ends


def norm_body(group_ref, x_ref, ends_ref, unit_ref, scale_ref, unit_end_ref, stream_end_ref):
    x = x_ref[...]
    stream = x.astype(full)
    center = stream - jnp.sum(stream, -1, keepdims=True) * (1.0 / WIDTH)
    scale = lax.rsqrt(jnp.sum(center * center, -1, keepdims=True) * (1.0 / WIDTH) + 1e-05)
    unit = (center * scale).astype(low)
    unit_ref[...] = unit
    scale_ref[...] = jnp.broadcast_to(scale, scale_ref.shape)
    picks = end_picks(ends_ref[...], 1).astype(low)
    unit_end_ref[...] = mm(picks, unit).astype(low)
    stream_end_ref[...] = mm(picks, x).astype(low)


def norm_first(group, x, ends):
    steps = ends.shape[0] // BLOCK
    return pl.pallas_call(
        norm_body,
        out_shape=shapes(
            (x.shape, low), ((x.shape[0], 128), full), *[((ends.shape[0], WIDTH), low)] * 2
        ),
        grid_spec=pltpu.PrefetchScalarGridSpec(
            num_scalar_prefetch=1,
            grid=(steps,),
            in_specs=[
                pl.BlockSpec((TOKENS, WIDTH), lambda i, g: ((i + g[0] * (steps // 2)) % steps, 0)),
                pl.BlockSpec((BLOCK, 1), lambda i, g: (i, 0)),
            ],
            out_specs=[
                pl.BlockSpec((TOKENS, WIDTH), lambda i, g: (i, 0)),
                pl.BlockSpec((TOKENS, 128), lambda i, g: (i, 0)),
                pl.BlockSpec((BLOCK, WIDTH), lambda i, g: (i, 0)),
                pl.BlockSpec((BLOCK, WIDTH), lambda i, g: (i, 0)),
            ],
        ),
        name="norm_first",
    )(group, x, ends)


def head_mask(head):
    return lax.broadcasted_iota(jnp.int32, (BLOCK, COLS), 1) // HEAD == head


def head_stack(x):
    zero = jnp.zeros_like(x)
    return jnp.concatenate([jnp.where(head_mask(h), x, zero) for h in range(HEADS_HERE)], 0)


def head_fold(x):
    out = jnp.zeros((BLOCK, COLS), full)
    for h in range(HEADS_HERE):
        out = jnp.where(head_mask(h), x[h * BLOCK : (h + 1) * BLOCK], out)
    return out


def stack_grid():
    row = lax.broadcasted_iota(jnp.int32, (STACK, TOKENS), 0) & (BLOCK - 1)
    token = lax.broadcasted_iota(jnp.int32, (STACK, TOKENS), 1)
    return row, token


def step_rows(i):
    return pl.ds(pl.multiple_of(i * BLOCK, BLOCK), BLOCK)


def attend_body(
    unit_ref, unit_end_ref, ends_ref, kv_ref, qo_ref, mixed_ref, p_ref, q_ref, att_ref, out_ref
):
    i = pl.program_id(0)

    @pl.when(i == 0)
    def _():
        q_ref[...] = mm(unit_end_ref[...], qo_ref[:, :COLS]).astype(low)

    mixed = mm(unit_ref[...], kv_ref[...]).astype(low)
    mixed_ref[...] = mixed
    scores = mm_nt(head_stack(q_ref[step_rows(i), :]), mixed[:, :COLS]) * SCORE_SCALE
    row, token = stack_grid()
    ends = jnp.concatenate([ends_ref[...]] * HEADS_HERE, 0)
    allowed = (token >= row * LENGTH) & (token <= row * LENGTH + ends)
    scores = jnp.where(allowed, scores, -1e30)
    weight = jnp.exp(scores - jnp.max(scores, 1, keepdims=True))
    probs = weight / jnp.sum(weight, 1, keepdims=True)
    p_ref[...] = probs
    att_ref[step_rows(i), :] = head_fold(mm(probs.astype(low), mixed[:, COLS:])).astype(low)

    @pl.when(i == pl.num_programs(0) - 1)
    def _():
        out_ref[...] = mm_nt(att_ref[...], qo_ref[:, COLS:]).astype(low)


def attend(unit, unit_end, ends, kv, qo):
    count = ends.shape[0]
    steps = count // BLOCK
    return pl.pallas_call(
        attend_body,
        grid=(steps,),
        out_shape=shapes(
            ((count * LENGTH, 2 * COLS), low),
            ((steps * STACK, TOKENS), full),
            *[((count, COLS), low)] * 2,
            ((count, WIDTH), low),
        ),
        in_specs=[
            pl.BlockSpec((TOKENS, WIDTH), lambda i: (i, 0)),
            whole_block((count, WIDTH)),
            pl.BlockSpec((BLOCK, 1), lambda i: (i, 0)),
            whole_block(kv.shape),
            whole_block(qo.shape),
        ],
        out_specs=[
            pl.BlockSpec((TOKENS, 2 * COLS), lambda i: (i, 0)),
            pl.BlockSpec((STACK, TOKENS), lambda i: (i, 0)),
            whole_block((count, COLS)),
            whole_block((count, COLS)),
            whole_block((count, WIDTH)),
        ],
        name="attend",
    )(unit, unit_end, ends, kv, qo)


def lane_group():
    return lax.broadcasted_iota(jnp.int32, (BLOCK, 128), 1) // (2 * LENGTH)


def attend_back_body(
    core_ref, d_mid_ref, d_att_ref, unit_ref, unit_end_ref, mixed_ref, p_ref, q_ref, att_ref,
    keep_ref, send_ref, d_mixed_ref, dq_ref, small_ref, sum_ref,
):
    i = pl.program_id(0)
    count = dq_ref.shape[0]

    @pl.when(i == 0)
    def _():
        sum_ref[...] = jnp.zeros_like(sum_ref)

    probs = p_ref[...]
    probs_low = probs.astype(low)
    queries = head_stack(q_ref[step_rows(i), :])
    d_att = head_stack(d_att_ref[step_rows(i), :])
    d_probs = mm_nt(d_att, mixed_ref[:, COLS:])
    d_scores = probs * (d_probs - jnp.sum(probs * d_probs, 1, keepdims=True))
    d_scores = (d_scores * SCORE_SCALE).astype(low)
    dq_ref[step_rows(i), :] = head_fold(mm(d_scores, mixed_ref[:, :COLS])).astype(low)
    d_mixed = jnp.concatenate(
        [mm_tn(d_scores, queries).astype(low), mm_tn(probs_low, d_att).astype(low)], 1
    )
    d_mixed_ref[...] = d_mixed
    spot = lax.broadcasted_iota(jnp.int32, (TOKENS, 128), 0) & (LENGTH - 1)
    lane = lax.broadcasted_iota(jnp.int32, (TOKENS, 128), 1) & (2 * LENGTH - 1)
    squeezed = mm(probs_low, (spot == lane).astype(low))
    squeezed += mm(d_scores, (spot + LENGTH == lane).astype(low))
    for first in (0, 4):
        out = jnp.zeros((BLOCK, 128), full)
        for h in range(first, min(first + 4, HEADS_HERE)):
            out = jnp.where(lane_group() == h - first, squeezed[h * BLOCK : (h + 1) * BLOCK], out)
        place = pl.multiple_of((2 * i + first // 4) * BLOCK, BLOCK)
        small_ref[pl.ds(3 * count + place, BLOCK), :] = out.astype(low)
    sum_ref[...] += mm_tn(unit_ref[...], d_mixed)

    @pl.when(i == pl.num_programs(0) - 1)
    def _():
        first = core_ref[0] == 0
        d_queries = dq_ref[...]
        for piece in range(3):
            small_ref[piece * count : (piece + 1) * count] = d_queries[
                :, piece * 128 : (piece + 1) * 128
            ]
        g_mix = sum_ref[...].astype(low)
        g_query = mm_tn(unit_end_ref[...], d_queries).astype(low)
        g_back = mm_tn(d_mid_ref[...], att_ref[...]).astype(low)
        g_rest = jnp.concatenate([g_query, g_back], 1)
        keep_ref[...] = jnp.where(first, g_mix, g_rest)
        send_ref[...] = jnp.where(first, g_rest, g_mix)


def attend_back(core, d_mid, d_att, unit, unit_end, mixed, probs, queries, attended):
    count = d_mid.shape[0]
    steps = count // BLOCK
    return pl.pallas_call(
        attend_back_body,
        grid=(steps,),
        out_shape=shapes(
            *[((WIDTH, 2 * COLS), low)] * 2,
            ((count * LENGTH, 2 * COLS), low),
            ((count, COLS), low),
            ((3 * count + steps * 2 * BLOCK, 128), low),
        ),
        in_specs=[
            pl.BlockSpec(memory_space=pltpu.SMEM),
            whole_block((count, WIDTH)),
            whole_block((count, COLS)),
            pl.BlockSpec((TOKENS, WIDTH), lambda i: (i, 0)),
            whole_block((count, WIDTH)),
            pl.BlockSpec((TOKENS, 2 * COLS), lambda i: (i, 0)),
            pl.BlockSpec((STACK, TOKENS), lambda i: (i, 0)),
            whole_block((count, COLS)),
            whole_block((count, COLS)),
        ],
        out_specs=[
            whole_block((WIDTH, 2 * COLS)),
            whole_block((WIDTH, 2 * COLS)),
            pl.BlockSpec((TOKENS, 2 * COLS), lambda i: (i, 0)),
            whole_block((count, COLS)),
            whole_block((3 * count + steps * 2 * BLOCK, 128)),
        ],
        scratch_shapes=[pltpu.VMEM((WIDTH, 2 * COLS), full)],
        name="attend_back",
        compiler_params=LIMIT,
    )(core, d_mid, d_att, unit, unit_end, mixed, probs, queries, attended)


def raise_back_body(flag_ref, second_ref, d_raised_ref, pooled_ref, d_embed_ref, out_ref):
    hidden = d_raised_ref.shape[1]
    quarter = WIDTH // 4
    out_ref[:, :hidden] = mm_tn(second_ref[...], d_raised_ref[...]).astype(low)
    here = d_embed_ref[:, :quarter]
    for index in range(1, 4):
        part = d_embed_ref[:, index * quarter : (index + 1) * quarter]
        here = jnp.where(flag_ref[0] == index, part, here)
    out_ref[:, hidden:] = mm_tn(pooled_ref[...], here).astype(low)


def raise_back(flag, second, d_raised, pooled, d_embed):
    vmem = pl.BlockSpec(memory_space=pltpu.VMEM)
    return pl.pallas_call(
        raise_back_body,
        out_shape=jax.ShapeDtypeStruct((WIDTH, d_raised.shape[1] + WIDTH // 4), low),
        in_specs=[pl.BlockSpec(memory_space=pltpu.SMEM)] + [vmem] * 4,
        out_specs=vmem,
        name="raise_back",
        compiler_params=LIMIT,
    )(flag, second, d_raised, pooled, d_embed)


def own_slots(index_ref, valid, main):
    count = valid.shape[1]
    row = lax.broadcasted_iota(jnp.int32, (CAP_DEV, count), 0)
    spare = CAP_DEV - main
    first = index_ref[0] * main + row
    second = count // CAP_DEV * main + index_ref[0] * spare + row - main
    slot = jnp.where(row < main, first, second)
    spot = lax.broadcasted_iota(jnp.int32, (CAP_DEV, count), 1) == slot
    own = jnp.sum(jnp.where(spot, valid, 0.0), 1, keepdims=True)
    return jnp.where(spot, valid, 0.0), own


def loss_front_body(
    main, index_ref, middle_ref, *refs
):
    feeds = refs[:4]
    valid_ref, embed_ref, picture_ref = refs[4:7]
    pooled_ref, text_ref, inverse_ref, weight_ref, row_ref, total_ref = refs[7:]
    total = middle_ref[...]
    for ref in feeds:
        total = total + ref[...].astype(full)
    pooled = total.astype(low)
    pooled_ref[...] = pooled
    embedding = mm(pooled, embed_ref[...])
    inverse = lax.rsqrt(jnp.sum(embedding * embedding, -1, keepdims=True) + 1e-06)
    text = embedding * inverse
    text_ref[...] = text
    inverse_ref[...] = jnp.broadcast_to(inverse, inverse_ref.shape)
    sims = LOGIT_SCALE * mm_nt(text.astype(low), picture_ref[...])
    valid = valid_ref[...]
    target, own = own_slots(index_ref, valid, main)
    weight = jnp.where((own > 0.5) & (valid > 0.5), jnp.exp(sims), 0.0)
    weight_ref[...] = weight
    row_safe = jnp.where(own > 0.5, jnp.sum(weight, 1, keepdims=True), 1.0)
    row_ref[...] = jnp.broadcast_to(0.5 / row_safe, row_ref.shape)
    part = 0.5 * jnp.log(row_safe) - jnp.sum(target * sims, 1, keepdims=True)
    part = jnp.sum(part, 0, keepdims=True)
    columns = jnp.sum(weight, 0, keepdims=True)
    blocks = columns.shape[1] // 128
    for block in range(blocks):
        total_ref[block : block + 1] = columns[:, block * 128 : (block + 1) * 128]
    total_ref[blocks:] = jnp.broadcast_to(part * (1.0 / 128), (1, 128))


def loss_front(main, index, middle, feeds, valid, w_embed, pictures):
    vmem = pl.BlockSpec(memory_space=pltpu.VMEM)
    count = pictures.shape[0]
    return pl.pallas_call(
        functools.partial(loss_front_body, main),
        out_shape=shapes(
            ((CAP_DEV, WIDTH), low),
            ((CAP_DEV, WIDTH), full),
            ((CAP_DEV, 128), full),
            ((CAP_DEV, count), full),
            ((CAP_DEV, 128), full),
            ((count // 128 + 1, 128), full),
        ),
        in_specs=[pl.BlockSpec(memory_space=pltpu.SMEM)] + [vmem] * 8,
        out_specs=[vmem] * 6,
        name="loss_front",
        compiler_params=LIMIT,
    )(index, middle, *feeds, valid, w_embed, pictures)


def loss_back_body(main, parts, index_ref, *refs):
    totals = refs[:parts]
    valid_ref, text_ref, inverse_ref, weight_ref, row_ref, picture_ref = refs[parts:-2]
    d_embed_ref, objective_ref = refs[-2:]
    total = totals[0][...]
    for ref in totals[1:]:
        total = total + ref[...]
    valid = valid_ref[...]
    blocks = valid.shape[1] // 128
    columns = jnp.concatenate([total[block : block + 1] for block in range(blocks)], 1)
    col_safe = jnp.where(valid > 0.5, columns, 1.0)
    logs = 0.5 * jnp.sum(jnp.log(col_safe), 1, keepdims=True)
    rows_part = jnp.sum(total[blocks:], 1, keepdims=True)
    objective_ref[...] = jnp.broadcast_to(logs + rows_part, objective_ref.shape)
    target, _ = own_slots(index_ref, valid, main)
    d_sims = weight_ref[...] * (row_ref[:, :1] + 0.5 / col_safe) - target
    d_unit = LOGIT_SCALE * mm(d_sims.astype(low), picture_ref[...])
    text = text_ref[...]
    along = jnp.sum(text * d_unit, -1, keepdims=True)
    d_embed_ref[...] = ((d_unit - text * along) * inverse_ref[:, :1]).astype(low)


def loss_back(main, index, totals, valid, text, inverse, weight, row, pictures):
    vmem = pl.BlockSpec(memory_space=pltpu.VMEM)
    return pl.pallas_call(
        functools.partial(loss_back_body, main, len(totals)),
        out_shape=shapes(((CAP_DEV, WIDTH), low), ((1, 128), full)),
        in_specs=[pl.BlockSpec(memory_space=pltpu.SMEM)] + [vmem] * (6 + len(totals)),
        out_specs=[vmem] * 2,
        name="loss_back",
        compiler_params=LIMIT,
    )(index, *totals, valid, text, inverse, weight, row, pictures)


def place_rows(picks, rows):
    high = rows.astype(low)
    rest = (rows - high.astype(full)).astype(low)
    return mm_tn(picks, jnp.concatenate([high, rest], 0))


def captions_body(
    start, blocks, group_ref, ends_ref, unit_ref, scale_ref, d_mid_ref, d_mixed_ref, dq_ref,
    q_far_ref, d_att_far_ref, small_far_ref, kv_ref, qo_ref, kv_far_ref, qo_far_ref, *refs,
):
    out_ref, inner_end_ref = refs[-2:]
    i = pl.program_id(0)
    count = dq_ref.shape[0]
    steps = count // BLOCK
    far = (start + steps // 2) % steps
    rows = blocks * BLOCK

    @pl.when(i == 0)
    def _():
        dq_far = jnp.concatenate(
            [
                small_far_ref[piece * count + far * BLOCK : piece * count + far * BLOCK + rows]
                for piece in range(3)
            ],
            1,
        )
        inner_end_ref[...] = mm_nt(
            dq_ref[start * BLOCK : start * BLOCK + rows], qo_ref[:, :COLS]
        ) + mm_nt(dq_far, qo_far_ref[:, :COLS])

    row, token = stack_grid()
    own_caption = token // LENGTH == row
    lane = lax.broadcasted_iota(jnp.int32, (128, TOKENS), 0) & (2 * LENGTH - 1)
    spot = lax.broadcasted_iota(jnp.int32, (128, TOKENS), 1) & (LENGTH - 1)
    zero = jnp.zeros((BLOCK, 128), low)
    place = pl.multiple_of(3 * count + 2 * BLOCK * (far + i), 2 * BLOCK)
    packed = small_far_ref[pl.ds(place, 2 * BLOCK), :]
    pair = jnp.concatenate(
        [
            jnp.where(lane_group() == h % 4, packed[h // 4 * BLOCK : (h // 4 + 1) * BLOCK], zero)
            for h in range(HEADS_HERE)
        ],
        0,
    )
    probs = jnp.where(own_caption, mm(pair, (spot == lane).astype(low)), 0.0).astype(low)
    d_scores = jnp.where(
        own_caption, mm(pair, (spot + LENGTH == lane).astype(low)), 0.0
    ).astype(low)
    d_mixed = jnp.concatenate(
        [
            mm_tn(d_scores, head_stack(q_far_ref[step_rows(far + i), :])).astype(low),
            mm_tn(probs, head_stack(d_att_far_ref[step_rows(far + i), :])).astype(low),
        ],
        1,
    )
    inner = mm_nt(d_mixed_ref[...], kv_ref[...]) + mm_nt(d_mixed, kv_far_ref[...])
    picks = end_picks(ends_ref[...], 2).astype(low)
    inner += place_rows(picks, inner_end_ref[step_rows(i), :])
    unit = unit_ref[...].astype(full)
    flat = jnp.sum(inner, -1, keepdims=True) * (1.0 / WIDTH)
    tilt = jnp.sum(inner * unit, -1, keepdims=True) * (1.0 / WIDTH)
    out_ref[...] = place_rows(picks, d_mid_ref[...]) + scale_ref[:, :1] * (
        inner - flat - unit * tilt
    )


def captions_back(
    start, blocks, group, ends, unit, scale, d_mid, d_mixed, dq, q_far, d_att_far, small_far, kv, qo,
    kv_far, qo_far, done=None,
):
    count = ends.shape[0]
    steps = count // BLOCK
    half = steps // 2
    operands = [
        group, ends, unit, scale, d_mid, d_mixed, dq, q_far, d_att_far, small_far, kv, qo,
        kv_far, qo_far,
    ]
    in_specs = [
        pl.BlockSpec((BLOCK, 1), lambda i, g: (i + start, 0)),
        pl.BlockSpec((TOKENS, WIDTH), lambda i, g: (i + start, 0)),
        pl.BlockSpec((TOKENS, 128), lambda i, g: (i + start, 0)),
        pl.BlockSpec((BLOCK, WIDTH), lambda i, g: (i + start, 0)),
        pl.BlockSpec((TOKENS, 2 * COLS), lambda i, g: (i + start, 0)),
        *[whole_block((count, COLS))] * 3,
        whole_block(small_far.shape),
    ] + [whole_block(kv.shape)] * 4
    aliases = {}
    if done is not None:
        aliases = {len(operands): 0}
        operands.append(done)
        in_specs.append(pl.BlockSpec(memory_space=pl.ANY))
    return pl.pallas_call(
        functools.partial(captions_body, start, blocks),
        out_shape=jax.ShapeDtypeStruct(unit.shape, full),
        grid_spec=pltpu.PrefetchScalarGridSpec(
            num_scalar_prefetch=1,
            grid=(blocks,),
            in_specs=in_specs,
            out_specs=pl.BlockSpec(
                (TOKENS, WIDTH), lambda i, g: ((i + start + g[0] * half) % steps, 0)
            ),
            scratch_shapes=[pltpu.VMEM((blocks * BLOCK, WIDTH), full)],
        ),
        input_output_aliases=aliases,
        name="captions_back",
    )(*operands)


def local(
    captions,
    image_cache,
    send_order,
    arrive_order,
    counts,
    keep_mask,
    end_pos,
    w_qkv,
    w_out,
    w_up,
    w_down,
    w_proj,
    ln1_gain,
    ln2_gain,
):
    plane = Plane()
    core = plane.core
    group = lax.axis_index("mp")
    spread = plane.count
    rows_dev, length, width = captions.shape
    rows = w_out.shape[0]
    per_peer = rows_dev // spread
    hidden = w_up.shape[1] // 2
    core_flag = core.reshape(1).astype(jnp.int32)
    group_flag = group.reshape(1).astype(jnp.int32)

    packed = pack(
        core_flag,
        w_qkv.transpose(1, 0, 2),
        w_out,
        w_up,
        w_down,
        w_proj,
        ln1_gain[None],
        ln2_gain[None],
    )
    def order_ends(end_pos):
        flipped = jnp.concatenate([end_pos, end_pos], 0)
        return lax.dynamic_slice_in_dim(flipped, group * CAP_DEV, rows_dev, 0)[:, None]

    wide = width // 2

    def pictures_of_batch(incoming):
        own_arrive = lax.dynamic_slice_in_dim(arrive_order[0], group * CAP_DEV, CAP_DEV, 0)
        take_in = (own_arrive[:, None] == places[None, :]).astype(low)
        pictures = mm(take_in, incoming.reshape(rows_dev, width)).astype(low)
        mine = pick(core, pictures[:, :wide], pictures[:, wide:])
        send = pick(core, pictures[:, wide:], pictures[:, :wide])
        return mine, send

    def prepare(image_cache):
        cached = image_cache.astype(full)
        norms = jnp.sum(cached * cached, -1, keepdims=True)
        cached = (cached * lax.rsqrt(norms + 1e-06)).astype(low)
        hand_out = (send_order[0][:, None] == places[None, :]).astype(low)
        return mm(hand_out, cached).astype(low).reshape(spread, per_peer, width)

    places = jnp.arange(rows_dev, dtype=jnp.int32)

    def deal(outgoing):
        return lax.all_to_all(outgoing, "dp", split_axis=0, concat_axis=0, tiled=True)

    def first_parts(stream, ends):
        return norm_first(group_flag, stream.reshape(rows_dev * length, width), ends)

    def attention_of(kv, qo, parts, ends):
        return attend(parts[0], parts[2], ends, kv, qo)

    main = rows if plane.fast else CAP_DEV
    spare = CAP_DEV - main
    if plane.fast:

        def join(feed, embed, half):
            parts = [half[main:, i * 128 : (i + 1) * 128] for i in range(wide // 128)]
            return jnp.concatenate([feed, embed, half[:main], jnp.concatenate(parts, 0)], 1)

        mix_cuts = (0, 2 * COLS)
        cuts = (0, 2 * hidden, 2 * hidden + 2 * wide + 128)
        arrived = plane.swap_core(packed[1])
        arrived, cache = joint(arrived, image_cache)
        block = plane.join_cores(packed[0], arrived)
        incoming = deal(prepare(cache))
        up = plane.shift_depth(block, 1)
        down = plane.shift_depth(block, -1)
        across = plane.swap_side(block)
        up, down, across, block = joint(up, down, across, block)

        mixes = plane.place(plane.empty(2 * rows, mix_cuts, block), mix_cuts, 0, block, across)
        far = plane.shift_depth(up, 1)
        across_up = plane.swap_side(up)
        across_down = plane.swap_side(down)
        far, across_up, across_down, incoming = joint(far, across_up, across_down, incoming)

        across = plane.swap_side(far)
        pictures = pictures_of_batch(incoming)
        mine = join(packed[2], packed[4], pictures[0])
        arrived = plane.swap_core(join(packed[3], packed[5], pictures[1]))
        mixes = plane.place(mixes, mix_cuts, 1, up, across_up)
        mixes = plane.place(mixes, mix_cuts, -1, down, across_down)
        across, arrived, mixes, counts, keep_mask, end_pos = joint(
            across, arrived, mixes, counts, keep_mask, end_pos
        )

        block = plane.join_cores(mine, arrived)
        one = plane.shift_depth(block, 1)
        across_block = plane.swap_side(block)
        mixes = plane.place(mixes, mix_cuts, 2, far, across)
        mix_own = mixes[0].reshape(width, 2 * COLS)
        mix_other = plane.swap_core(mix_own)
        far_own = swap_group(mix_own)
        kv = pick(core, mix_own, mix_other)
        qo = pick(core, mix_other, mix_own)
        ends = order_ends(end_pos)
        parts = first_parts(after(captions, block), ends)
        one, kv, qo, *parts = joint(one, kv, qo, *parts)

        two = plane.shift_depth(one, 1)
        across_one = plane.swap_side(one)
        stream_near = swap_near(parts[3], 2)
        attending = attention_of(kv, qo, parts, ends)
        two, across_block, across_one, stream_near, *attending = joint(
            two, across_block, across_one, stream_near, *attending
        )

        three = plane.shift_depth(two, 1)
        across_two = plane.swap_side(two)
        wholes = plane.place(plane.empty(2 * rows, cuts, attending[-1]), cuts, 0, block, across_block)
        wholes = plane.place(wholes, cuts, 1, one, across_one)
        attention = after(attending[-1], far_own)
        near = [swap_near(attention, flip) for flip in (1, 2, 3)]
        three, across_two, *near = joint(three, across_two, *near)

        across = plane.swap_side(three)
        queries_far = swap_group(attending[2])
        far_other = plane.swap_core(far_own)
        kv_far = pick(core, far_own, far_other)
        qo_far = pick(core, far_other, far_own)
        wholes = plane.place(wholes, cuts, 2, two, across_two)
        across, queries_far, kv_far, qo_far, wholes = joint(
            across, queries_far, kv_far, qo_far, wholes
        )
        wholes = plane.place(wholes, cuts, 3, three, across)
        feeds, third = [whole.reshape(width, -1) for whole in wholes]
        third_other = plane.swap_core(third)

        def images(x):
            extra = x[:, 2 * wide :].reshape(spread, wide // 128, spare, 128)
            extra = extra.transpose(0, 2, 1, 3).reshape(spread * spare, wide)
            return jnp.concatenate([x[:, wide : 2 * wide], extra], 0)

        image_halves = images(third), images(third_other)
        embed_halves = third[:, :wide], third_other[:, :wide]
    else:
        pictures = pictures_of_batch(deal(prepare(image_cache)))
        ends = order_ends(end_pos)
        parts = first_parts(captions, ends)
        mix_own = plane.gather_plain(packed[0], packed[1])
        mix_other = plane.swap_core(mix_own)
        far_own = swap_group(mix_own)
        kv = pick(core, mix_own, mix_other)
        qo = pick(core, mix_other, mix_own)
        attending = attention_of(kv, qo, parts, ends)
        feeds = plane.gather_plain(packed[2], packed[3])
        image_half = plane.gather_plain(*pictures)
        image_halves = image_half, plane.swap_core(image_half)
        embed_half = plane.gather_plain(packed[4], packed[5])
        embed_halves = embed_half, plane.swap_core(embed_half)
        far_other = plane.swap_core(far_own)
        kv_far = pick(core, far_own, far_other)
        qo_far = pick(core, far_other, far_own)
        stream_near = swap_near(parts[3], 2)
        attention = attending[-1]
        near = [swap_near(attention, flip) for flip in (1, 2, 3)]
        queries_far = swap_group(attending[2])
    unit, scale, unit_end, stream_end = parts
    mixed, probs, queries, attended, _ = attending

    def sides(pair):
        return jnp.concatenate([pick(core, *pair), pick(core, pair[1], pair[0])], 1)

    pictures_all = sides(image_halves)
    w_embed = sides(embed_halves)

    from_group, from_core, from_both = near
    attention = jnp.concatenate([attention, from_core], 0).astype(full)
    attention = attention + jnp.concatenate(
        [roll_rows(from_group), roll_rows(from_both)], 0
    ).astype(full)
    middle = jnp.concatenate([stream_end, stream_near], 0).astype(full) + attention
    unit_second, scale_second = norm_rows(middle)
    second_low = unit_second.astype(low)
    w_raise = feeds[:, :hidden]
    w_lower = feeds[:, hidden:]
    active, slope = gelu_parts(mm(second_low, w_raise))
    active = active.astype(low)
    lowered = mm_nt(active, w_lower).astype(low)
    feed_parts = [lowered[:CAP_DEV]] + [
        swap_near(lowered[flip * CAP_DEV : (flip + 1) * CAP_DEV], flip) for flip in (1, 2, 3)
    ]

    keep_rows = keep_mask.reshape(spread, MICRO, CAP_DEV) == 1
    filled = jnp.arange(CAP_DEV, dtype=jnp.int32)[None, None, :] < counts[:, :, None]
    valid = (keep_rows & filled).astype(full)
    total_valid = jnp.sum(valid)
    batch_valid = lax.dynamic_index_in_dim(valid, group, 1, False)
    batch_valid = jnp.concatenate(
        [batch_valid[:, :main].reshape(-1), batch_valid[:, main:].reshape(-1)]
    )[None]
    if plane.fast:
        batch_valid = after(batch_valid, near[0])
    place_flag = plane.index.reshape(1).astype(jnp.int32)
    pooled, unit_text, inverse, weight, row_half, totals = loss_front(
        main, place_flag, middle[:CAP_DEV], feed_parts, batch_valid, w_embed, pictures_all
    )
    if plane.fast:
        pooled_group = swap_near(pooled, 1)
        sent = [plane.flip(totals, bits) for bits in (1, 4, 5)]
        *sent, pooled_group = joint(*sent, pooled_group)
        totals = (totals + sent[0]) + (sent[1] + sent[2])
        totals = totals, *joint(*[plane.flip(totals, bits) for bits in (2, 8, 10)])
    else:
        totals = (lax.psum(totals, "dp"),)
    d_embed, objective = loss_back(
        main, place_flag, totals, batch_valid, unit_text, inverse, weight, row_half, pictures_all
    )

    d_embed_near = [swap_near(d_embed, flip) for flip in (1, 2, 3)]
    if plane.fast:
        pooled_pair = jnp.concatenate([pooled, pooled_group], 0)
        *d_embed_near, objective, pooled_near = joint(
            *d_embed_near, objective, plane.swap_core(pooled_pair)
        )
        pooled_all = jnp.concatenate([pooled_pair, pooled_near], 0)
    else:
        pooled_all = jnp.concatenate([pooled] + [swap_near(pooled, flip) for flip in (1, 2, 3)], 0)
    d_embed_all = jnp.concatenate([d_embed, *d_embed_near], 0)
    d_pooled = mm_nt(d_embed_all, w_embed)
    d_out_low = d_pooled.astype(low)
    d_raised = (mm(d_out_low, w_lower) * slope).astype(low)
    d_second = mm_nt(d_raised, w_raise).astype(low)
    second_late = after(second_low, d_second)
    g_raise = raise_back(2 * group_flag + core_flag, second_late, d_raised, pooled_all, d_embed_all)
    g_lower = mm_tn(after(d_out_low, d_second), active).astype(low)
    if plane.fast:
        raise_stay, raise_in = plane.halve(g_raise.reshape(2, 2, 2, 2 * rows, -1), 1, 4)
        lower_stay, lower_in = plane.halve(g_lower.reshape(2, 2, 2, 2 * rows, -1), 2, 2)
    d_second = add_low((d_second[:rows_dev], swap_near(d_second[rows_dev:], 2)))
    inner = d_second.astype(full) + roll_rows(swap_near(d_second, 1)).astype(full)
    d_middle = d_pooled[:rows_dev] + norm_back(
        inner, unit_second[:rows_dev], scale_second[:rows_dev]
    )

    d_middle_low = d_middle.astype(low)
    d_attended = mm(d_middle_low, qo[:, COLS:]).astype(low)
    d_attended_far = swap_group(d_attended)
    g_keep, g_send, d_mixed, d_queries, small = attend_back(
        core_flag, d_middle_low, d_attended, unit, unit_end, mixed, probs, queries, attended
    )

    def early_parts(raise_sum, lower_sum):
        grad_down = jnp.concatenate(lower_sum, 1)
        proj_own = jnp.concatenate([part[:, hidden:] for part in raise_sum], 1)
        raised_sum = jnp.concatenate([part[:, :hidden] for part in raise_sum], 1)
        gain_second = jnp.sum(raised_sum * w_up.astype(full), 1)
        early = jnp.stack([gain_second, jnp.broadcast_to(objective[0, 0], (rows,))])
        return proj_own, grad_down, raised_sum, early

    def captions_part(start, blocks, d_queries_here, far_parts, done=None):
        return captions_back(
            start, blocks, group_flag, ends, unit, scale, d_middle, d_mixed, d_queries_here, queries_far,
            *far_parts, kv, qo, kv_far, qo_far, done=done,
        )

    if plane.fast:
        raise_stay, raise_in, lower_stay, lower_in, d_queries, g_send, d_attended_far = joint(
            raise_stay, raise_in, lower_stay, lower_in, d_queries, g_send, d_attended_far
        )
        small_far = swap_group(small)
        mix_in = plane.swap_core(g_send)
        raise_pair = add_low((raise_stay, raise_in))
        lower_pair = add_low((lower_stay, lower_in))
        raise_side = plane.halve(raise_pair, 1, 2)
        small_far, mix_in, *raise_side, lower_pair = joint(
            small_far, mix_in, *raise_side, lower_pair
        )
        raise_last = plane.halve(add_low(raise_side), 0, 8)
        lower_depth = plane.halve(lower_pair, 1, 4)
        mix_pair = add_low((g_keep, mix_in)).reshape(2, 2, 2, 2 * rows, 2 * COLS)
        mix_side = plane.halve(mix_pair, 2, 2)
        far_parts = d_attended_far, small_far
        half = rows_dev // BLOCK // 2
        first_half = captions_part(0, half, after(d_queries, mix_side[0]), far_parts)
        raise_last, lower_depth, mix_side, first_half = joint(
            raise_last, lower_depth, mix_side, first_half
        )
        mix_depth = plane.halve(add_low(mix_side), 1, 4)
        lower_last = plane.halve(add_low(lower_depth), 0, 8)
        starts = after(d_queries, mix_depth[0], lower_last[0])
        third_part = captions_part(half, half // 2, starts, far_parts, first_half)
        mix_depth, lower_last, third_part = joint(mix_depth, lower_last, third_part)
        mix_last = plane.halve(add_low(mix_depth), 0, 8)
        starts = after(d_queries, mix_last[0])
        grad_captions = captions_part(half + half // 2, half - half // 2, starts, far_parts, third_part)
        raise_sum, lower_sum = [
            plane.scatter_core(pair[0].astype(full) + pair[1].astype(full))
            for pair in (raise_last, lower_last)
        ]
        proj_own, grad_down, raised_sum, early = early_parts(raise_sum, lower_sum)
        proj_far, early_far = swap_group(proj_own), swap_group(early)
        mix_last, proj_far, early_far, grad_down, raised_sum, grad_captions = joint(
            mix_last, proj_far, early_far, grad_down, raised_sum, grad_captions
        )
        mix_sum = plane.scatter_core(mix_last[0].astype(full) + mix_last[1].astype(full))
    else:
        far_parts = d_attended_far, swap_group(small)
        grad_captions = captions_part(0, rows_dev // BLOCK, d_queries, far_parts)
        raise_sum = plane.scatter_plain(g_raise)
        lower_sum = plane.scatter_plain(g_lower)
        proj_own, grad_down, raised_sum, early = early_parts(raise_sum, lower_sum)
        proj_far, early_far = swap_group(proj_own), swap_group(early)
        mix_sum = plane.scatter_plain(g_keep, g_send)
    grad_captions = grad_captions.reshape(rows_dev, length, width)

    grad_proj = pick(
        group,
        jnp.concatenate([proj_own, proj_far], 1),
        jnp.concatenate([proj_far, proj_own], 1),
    )
    grad_out = mix_sum[1][:, COLS:]
    unit_mix = jnp.stack([mix_sum[1][:, :COLS], mix_sum[0][:, :COLS], mix_sum[0][:, COLS:]], 1)
    grad_qkv = unit_mix * ln1_gain[:, None, None]
    grad_up = raised_sum * ln2_gain[:, None]
    early = early + early_far
    loss = early[1, 0] / total_valid
    gain_first = jnp.sum(unit_mix * w_qkv.astype(full), (1, 2))[None]
    gain_first = gain_first + swap_group(gain_first)
    return (
        loss,
        grad_captions,
        grad_qkv,
        grad_out,
        grad_up,
        grad_down,
        grad_proj,
        gain_first[0],
        early[0],
    )


def solution(mesh):
    return jax.shard_map(
        local,
        mesh=mesh,
        in_specs=(
            P("dp", None, None),
            P("dp", None),
            P("dp", None),
            P("dp", None),
            P(),
            P(),
            P("dp"),
            P("dp", None, "mp"),
            P("dp", "mp"),
            P("dp", "mp"),
            P("dp", "mp"),
            P("dp", None),
            P("dp"),
            P("dp"),
        ),
        out_specs=(
            P(),
            P("dp", None, None),
            P("dp", None, "mp"),
            P("dp", "mp"),
            P("dp", "mp"),
            P("dp", "mp"),
            P("dp", None),
            P("dp"),
            P("dp"),
        ),
        check_vma=False,
    )
```

```python
import functools
import math

import jax
import jax.numpy as jnp
from jax import lax
from jax.experimental import pallas as pl
from jax.experimental.pallas import tpu as pltpu
from jax.sharding import PartitionSpec as P

HEAD = 64
MICRO = 2
CAP_DEV = 64
LOGIT_SCALE = 40.0
SCORE_SCALE = 1.0 / math.sqrt(HEAD)
LENGTH = 16
WIDTH = 768
HEADS_HERE = 6
COLS = HEADS_HERE * HEAD
BLOCK = 32
TOKENS = BLOCK * LENGTH
STACK = HEADS_HERE * BLOCK

low = jnp.bfloat16
full = jnp.float32


def mm(a, b):
    return lax.dot_general(a, b, (((1,), (0,)), ((), ())), preferred_element_type=full)


def mm_nt(a, b):
    return lax.dot_general(a, b, (((1,), (1,)), ((), ())), preferred_element_type=full)


def mm_tn(a, b):
    return lax.dot_general(a, b, (((0,), (0,)), ((), ())), preferred_element_type=full)


def pick(flag, when_zero, when_one):
    return jnp.where(flag == 0, when_zero, when_one)


class Plane:
    def __init__(self):
        self.count = lax.axis_size("dp")
        self.index = lax.axis_index("dp")
        self.core = self.index % 2
        self.side = (self.index // 2) % 2
        self.depth = self.index // 4
        self.fast = self.count == 16

    def swap_core(self, x):
        return lax.ppermute(x, "dp", [(i, i ^ 1) for i in range(self.count)])

    def swap_side(self, x):
        return lax.ppermute(x, "dp", [(i, i ^ 2) for i in range(self.count)])

    def shift_depth(self, x, step):
        return lax.ppermute(
            x, "dp", [(i, (i + 4 * step) % self.count) for i in range(self.count)]
        )

    def join_cores(self, mine, arrived):
        rows, width = mine.shape
        block = jnp.zeros((2, rows, width), mine.dtype)
        block = lax.dynamic_update_slice(block, mine[None], (self.core, 0, 0))
        block = lax.dynamic_update_slice(block, arrived[None], (1 - self.core, 0, 0))
        return block.reshape(2 * rows, width)

    def place(self, wholes, cuts, step, here, across):
        spot = ((self.depth - step) % 4) * 2
        for block, at in ((here, spot + self.side), (across, spot + 1 - self.side)):
            wholes = [
                lax.dynamic_update_slice(whole, block[None, :, start:end], (at, 0, 0))
                for whole, start, end in zip(wholes, cuts, cuts[1:])
            ]
        return wholes

    def empty(self, rows, cuts, start_of):
        zero = after(jnp.zeros((), low), start_of)
        return [
            jnp.broadcast_to(zero, (self.count // 2, rows, end - start))
            for start, end in zip(cuts, cuts[1:])
        ]

    def gather_plain(self, mine, send):
        zero_all = lax.all_gather(pick(self.core, mine, send), "dp", axis=0, tiled=True)
        one_all = lax.all_gather(pick(self.core, send, mine), "dp", axis=0, tiled=True)
        return pick(self.core, zero_all, one_all)

    def halve(self, x, axis, bit):
        spot = (self.index // bit) % 2
        stay = lax.dynamic_index_in_dim(x, spot, axis, False)
        leave = lax.dynamic_index_in_dim(x, 1 - spot, axis, False)
        return stay, lax.ppermute(leave, "dp", [(i, i ^ bit) for i in range(self.count)])

    def scatter_plain(self, keep, send=None):
        if send is None:
            send = jnp.zeros_like(keep)
        halves = (pick(self.core, keep, send), pick(self.core, send, keep))
        return [
            lax.psum_scatter(half, "dp", scatter_dimension=0, tiled=True).astype(full)
            for half in halves
        ]

    def scatter_core(self, total):
        rows, width = total.shape[0] // 2, total.shape[1]
        total = total.reshape(2, rows, width)
        mine = lax.dynamic_index_in_dim(total, self.core, 0, False)
        arrived = self.swap_core(lax.dynamic_index_in_dim(total, 1 - self.core, 0, False))
        return pick(self.core, mine, arrived), pick(self.core, arrived, mine)

    def flip(self, x, bits):
        return lax.ppermute(x, "dp", [(i, i ^ bits) for i in range(self.count)])


def swap_near(x, flip):
    size = 2 * lax.axis_size("dp")
    return lax.ppermute(x, ("dp", "mp"), [(i, i ^ flip) for i in range(size)])


def swap_group(x):
    return swap_near(x, 1)


def after(x, *others):
    return lax.optimization_barrier((x, *others))[0]


def joint(*values):
    return lax.optimization_barrier(values)


def add_low(pair):
    return (pair[0].astype(full) + pair[1].astype(full)).astype(low)


def roll_rows(x):
    half = x.shape[0] // 2
    return jnp.concatenate([x[half:], x[:half]], 0)


def norm_rows(inputs):
    center = inputs - jnp.mean(inputs, -1, keepdims=True)
    scale = lax.rsqrt(jnp.mean(center * center, -1, keepdims=True) + 1e-05)
    return center * scale, scale


def norm_back(inner, unit, scale):
    return scale * (
        inner
        - jnp.mean(inner, -1, keepdims=True)
        - unit * jnp.mean(inner * unit, -1, keepdims=True)
    )


def gelu_parts(raised):
    cumulative = 0.5 * (1.0 + lax.erf(raised * 0.7071067811865476))
    slope = cumulative + raised * jnp.exp(-0.5 * raised * raised) * 0.3989422804014327
    return raised * cumulative, slope


LIMIT = pltpu.CompilerParams(vmem_limit_bytes=14 * 1024 * 1024)


def whole_block(shape):
    return pl.BlockSpec(shape, lambda *_: (0,) * len(shape))


def shapes(*items):
    return [jax.ShapeDtypeStruct(shape, kind) for shape, kind in items]


def pack_body(core_ref, mix_ref, back_ref, raise_ref, lower_ref, embed_ref, g1_ref, g2_ref, *outs):
    first = core_ref[0] == 0
    rows = back_ref.shape[0]
    spot = lax.broadcasted_iota(jnp.int32, (rows, rows), 0)
    diagonal = spot == lax.broadcasted_iota(jnp.int32, (rows, rows), 1)
    g1, g2 = [
        jnp.sum(jnp.where(diagonal, ref[...], 0.0), 1, keepdims=True) for ref in (g1_ref, g2_ref)
    ]

    def part(index):
        return (mix_ref[index].astype(full) * g1).astype(low)

    def put(index, columns, zero, one):
        outs[index][:, columns] = jnp.where(first, zero, one)
        outs[index + 1][:, columns] = jnp.where(first, one, zero)

    put(0, slice(0, COLS), part(1), part(0))
    put(0, slice(COLS, 2 * COLS), part(2), back_ref[...])
    hidden = raise_ref.shape[1] // 2
    raised = (raise_ref[...].astype(full) * g2).astype(low)
    put(2, slice(0, hidden), raised[:, :hidden], raised[:, hidden:])
    put(2, slice(hidden, 2 * hidden), lower_ref[:, :hidden], lower_ref[:, hidden:])
    put(4, slice(0, COLS), embed_ref[:, :COLS], embed_ref[:, COLS:])


def pack(core, w_qkv, w_out, w_up, w_down, w_proj, g1, g2):
    rows, hidden = w_up.shape
    vmem = pl.BlockSpec(memory_space=pltpu.VMEM)
    return pl.pallas_call(
        pack_body,
        out_shape=shapes(
            *[((rows, 2 * COLS), low)] * 2, *[((rows, hidden), low)] * 2, *[((rows, COLS), low)] * 2
        ),
        in_specs=[pl.BlockSpec(memory_space=pltpu.SMEM)] + [vmem] * 7,
        out_specs=[vmem] * 6,
        name="pack",
    )(core, w_qkv, w_out, w_up, w_down, w_proj, g1, g2)


def end_picks(ends, copies):
    ends = jnp.concatenate([ends] * copies, 0)
    shape = (copies * BLOCK, TOKENS)
    row = lax.broadcasted_iota(jnp.int32, shape, 0) & (BLOCK - 1)
    return lax.broadcasted_iota(jnp.int32, shape, 1) == row * LENGTH + ends


def norm_body(group_ref, x_ref, ends_ref, unit_ref, scale_ref, unit_end_ref, stream_end_ref):
    x = x_ref[...]
    stream = x.astype(full)
    center = stream - jnp.sum(stream, -1, keepdims=True) * (1.0 / WIDTH)
    scale = lax.rsqrt(jnp.sum(center * center, -1, keepdims=True) * (1.0 / WIDTH) + 1e-05)
    unit = (center * scale).astype(low)
    unit_ref[...] = unit
    scale_ref[...] = jnp.broadcast_to(scale, scale_ref.shape)
    picks = end_picks(ends_ref[...], 1).astype(low)
    unit_end_ref[...] = mm(picks, unit).astype(low)
    stream_end_ref[...] = mm(picks, x).astype(low)


def norm_first(group, x, ends):
    steps = ends.shape[0] // BLOCK
    return pl.pallas_call(
        norm_body,
        out_shape=shapes(
            (x.shape, low), ((x.shape[0], 128), full), *[((ends.shape[0], WIDTH), low)] * 2
        ),
        grid_spec=pltpu.PrefetchScalarGridSpec(
            num_scalar_prefetch=1,
            grid=(steps,),
            in_specs=[
                pl.BlockSpec((TOKENS, WIDTH), lambda i, g: ((i + g[0] * (steps // 2)) % steps, 0)),
                pl.BlockSpec((BLOCK, 1), lambda i, g: (i, 0)),
            ],
            out_specs=[
                pl.BlockSpec((TOKENS, WIDTH), lambda i, g: (i, 0)),
                pl.BlockSpec((TOKENS, 128), lambda i, g: (i, 0)),
                pl.BlockSpec((BLOCK, WIDTH), lambda i, g: (i, 0)),
                pl.BlockSpec((BLOCK, WIDTH), lambda i, g: (i, 0)),
            ],
        ),
        name="norm_first",
    )(group, x, ends)


def head_mask(head):
    return lax.broadcasted_iota(jnp.int32, (BLOCK, COLS), 1) // HEAD == head


def head_stack(x):
    zero = jnp.zeros_like(x)
    return jnp.concatenate([jnp.where(head_mask(h), x, zero) for h in range(HEADS_HERE)], 0)


def head_fold(x):
    out = jnp.zeros((BLOCK, COLS), full)
    for h in range(HEADS_HERE):
        out = jnp.where(head_mask(h), x[h * BLOCK : (h + 1) * BLOCK], out)
    return out


def stack_grid():
    row = lax.broadcasted_iota(jnp.int32, (STACK, TOKENS), 0) & (BLOCK - 1)
    token = lax.broadcasted_iota(jnp.int32, (STACK, TOKENS), 1)
    return row, token


def step_rows(i):
    return pl.ds(pl.multiple_of(i * BLOCK, BLOCK), BLOCK)


def attend_body(
    unit_ref, unit_end_ref, ends_ref, kv_ref, qo_ref, mixed_ref, p_ref, q_ref, att_ref, out_ref
):
    i = pl.program_id(0)

    @pl.when(i == 0)
    def _():
        q_ref[...] = mm(unit_end_ref[...], qo_ref[:, :COLS]).astype(low)

    mixed = mm(unit_ref[...], kv_ref[...]).astype(low)
    mixed_ref[...] = mixed
    scores = mm_nt(head_stack(q_ref[step_rows(i), :]), mixed[:, :COLS]) * SCORE_SCALE
    row, token = stack_grid()
    ends = jnp.concatenate([ends_ref[...]] * HEADS_HERE, 0)
    allowed = (token >= row * LENGTH) & (token <= row * LENGTH + ends)
    scores = jnp.where(allowed, scores, -1e30)
    weight = jnp.exp(scores - jnp.max(scores, 1, keepdims=True))
    probs = weight / jnp.sum(weight, 1, keepdims=True)
    p_ref[...] = probs
    att_ref[step_rows(i), :] = head_fold(mm(probs.astype(low), mixed[:, COLS:])).astype(low)

    @pl.when(i == pl.num_programs(0) - 1)
    def _():
        out_ref[...] = mm_nt(att_ref[...], qo_ref[:, COLS:]).astype(low)


def attend(unit, unit_end, ends, kv, qo):
    count = ends.shape[0]
    steps = count // BLOCK
    return pl.pallas_call(
        attend_body,
        grid=(steps,),
        out_shape=shapes(
            ((count * LENGTH, 2 * COLS), low),
            ((steps * STACK, TOKENS), full),
            *[((count, COLS), low)] * 2,
            ((count, WIDTH), low),
        ),
        in_specs=[
            pl.BlockSpec((TOKENS, WIDTH), lambda i: (i, 0)),
            whole_block((count, WIDTH)),
            pl.BlockSpec((BLOCK, 1), lambda i: (i, 0)),
            whole_block(kv.shape),
            whole_block(qo.shape),
        ],
        out_specs=[
            pl.BlockSpec((TOKENS, 2 * COLS), lambda i: (i, 0)),
            pl.BlockSpec((STACK, TOKENS), lambda i: (i, 0)),
            whole_block((count, COLS)),
            whole_block((count, COLS)),
            whole_block((count, WIDTH)),
        ],
        name="attend",
    )(unit, unit_end, ends, kv, qo)


def lane_group():
    return lax.broadcasted_iota(jnp.int32, (BLOCK, 128), 1) // (2 * LENGTH)


def attend_back_body(
    core_ref, d_mid_ref, d_att_ref, unit_ref, unit_end_ref, mixed_ref, p_ref, q_ref, att_ref,
    keep_ref, send_ref, d_mixed_ref, dq_ref, small_ref, sum_ref,
):
    i = pl.program_id(0)
    count = dq_ref.shape[0]

    @pl.when(i == 0)
    def _():
        sum_ref[...] = jnp.zeros_like(sum_ref)

    probs = p_ref[...]
    probs_low = probs.astype(low)
    queries = head_stack(q_ref[step_rows(i), :])
    d_att = head_stack(d_att_ref[step_rows(i), :])
    d_probs = mm_nt(d_att, mixed_ref[:, COLS:])
    d_scores = probs * (d_probs - jnp.sum(probs * d_probs, 1, keepdims=True))
    d_scores = (d_scores * SCORE_SCALE).astype(low)
    dq_ref[step_rows(i), :] = head_fold(mm(d_scores, mixed_ref[:, :COLS])).astype(low)
    d_mixed = jnp.concatenate(
        [mm_tn(d_scores, queries).astype(low), mm_tn(probs_low, d_att).astype(low)], 1
    )
    d_mixed_ref[...] = d_mixed
    spot = lax.broadcasted_iota(jnp.int32, (TOKENS, 128), 0) & (LENGTH - 1)
    lane = lax.broadcasted_iota(jnp.int32, (TOKENS, 128), 1) & (2 * LENGTH - 1)
    squeezed = mm(probs_low, (spot == lane).astype(low))
    squeezed += mm(d_scores, (spot + LENGTH == lane).astype(low))
    for first in (0, 4):
        out = jnp.zeros((BLOCK, 128), full)
        for h in range(first, min(first + 4, HEADS_HERE)):
            out = jnp.where(lane_group() == h - first, squeezed[h * BLOCK : (h + 1) * BLOCK], out)
        place = pl.multiple_of((2 * i + first // 4) * BLOCK, BLOCK)
        small_ref[pl.ds(3 * count + place, BLOCK), :] = out.astype(low)
    sum_ref[...] += mm_tn(unit_ref[...], d_mixed)

    @pl.when(i == pl.num_programs(0) - 1)
    def _():
        first = core_ref[0] == 0
        d_queries = dq_ref[...]
        for piece in range(3):
            small_ref[piece * count : (piece + 1) * count] = d_queries[
                :, piece * 128 : (piece + 1) * 128
            ]
        g_mix = sum_ref[...].astype(low)
        g_query = mm_tn(unit_end_ref[...], d_queries).astype(low)
        g_back = mm_tn(d_mid_ref[...], att_ref[...]).astype(low)
        g_rest = jnp.concatenate([g_query, g_back], 1)
        keep_ref[...] = jnp.where(first, g_mix, g_rest)
        send_ref[...] = jnp.where(first, g_rest, g_mix)


def attend_back(core, d_mid, d_att, unit, unit_end, mixed, probs, queries, attended):
    count = d_mid.shape[0]
    steps = count // BLOCK
    return pl.pallas_call(
        attend_back_body,
        grid=(steps,),
        out_shape=shapes(
            *[((WIDTH, 2 * COLS), low)] * 2,
            ((count * LENGTH, 2 * COLS), low),
            ((count, COLS), low),
            ((3 * count + steps * 2 * BLOCK, 128), low),
        ),
        in_specs=[
            pl.BlockSpec(memory_space=pltpu.SMEM),
            whole_block((count, WIDTH)),
            whole_block((count, COLS)),
            pl.BlockSpec((TOKENS, WIDTH), lambda i: (i, 0)),
            whole_block((count, WIDTH)),
            pl.BlockSpec((TOKENS, 2 * COLS), lambda i: (i, 0)),
            pl.BlockSpec((STACK, TOKENS), lambda i: (i, 0)),
            whole_block((count, COLS)),
            whole_block((count, COLS)),
        ],
        out_specs=[
            whole_block((WIDTH, 2 * COLS)),
            whole_block((WIDTH, 2 * COLS)),
            pl.BlockSpec((TOKENS, 2 * COLS), lambda i: (i, 0)),
            whole_block((count, COLS)),
            whole_block((3 * count + steps * 2 * BLOCK, 128)),
        ],
        scratch_shapes=[pltpu.VMEM((WIDTH, 2 * COLS), full)],
        name="attend_back",
        compiler_params=LIMIT,
    )(core, d_mid, d_att, unit, unit_end, mixed, probs, queries, attended)


def raise_back_body(flag_ref, second_ref, d_raised_ref, pooled_ref, d_embed_ref, out_ref):
    hidden = d_raised_ref.shape[1]
    quarter = WIDTH // 4
    out_ref[:, :hidden] = mm_tn(second_ref[...], d_raised_ref[...]).astype(low)
    here = d_embed_ref[:, :quarter]
    for index in range(1, 4):
        part = d_embed_ref[:, index * quarter : (index + 1) * quarter]
        here = jnp.where(flag_ref[0] == index, part, here)
    out_ref[:, hidden:] = mm_tn(pooled_ref[...], here).astype(low)


def raise_back(flag, second, d_raised, pooled, d_embed):
    vmem = pl.BlockSpec(memory_space=pltpu.VMEM)
    return pl.pallas_call(
        raise_back_body,
        out_shape=jax.ShapeDtypeStruct((WIDTH, d_raised.shape[1] + WIDTH // 4), low),
        in_specs=[pl.BlockSpec(memory_space=pltpu.SMEM)] + [vmem] * 4,
        out_specs=vmem,
        name="raise_back",
        compiler_params=LIMIT,
    )(flag, second, d_raised, pooled, d_embed)


def own_slots(index_ref, valid, main):
    count = valid.shape[1]
    row = lax.broadcasted_iota(jnp.int32, (CAP_DEV, count), 0)
    spare = CAP_DEV - main
    first = index_ref[0] * main + row
    second = count // CAP_DEV * main + index_ref[0] * spare + row - main
    slot = jnp.where(row < main, first, second)
    spot = lax.broadcasted_iota(jnp.int32, (CAP_DEV, count), 1) == slot
    own = jnp.sum(jnp.where(spot, valid, 0.0), 1, keepdims=True)
    return jnp.where(spot, valid, 0.0), own


def loss_front_body(
    main, index_ref, middle_ref, *refs
):
    feeds = refs[:4]
    valid_ref, embed_ref, picture_ref = refs[4:7]
    pooled_ref, text_ref, inverse_ref, weight_ref, row_ref, total_ref = refs[7:]
    total = middle_ref[...]
    for ref in feeds:
        total = total + ref[...].astype(full)
    pooled = total.astype(low)
    pooled_ref[...] = pooled
    embedding = mm(pooled, embed_ref[...])
    inverse = lax.rsqrt(jnp.sum(embedding * embedding, -1, keepdims=True) + 1e-06)
    text = embedding * inverse
    text_ref[...] = text
    inverse_ref[...] = jnp.broadcast_to(inverse, inverse_ref.shape)
    sims = LOGIT_SCALE * mm_nt(text.astype(low), picture_ref[...])
    valid = valid_ref[...]
    target, own = own_slots(index_ref, valid, main)
    weight = jnp.where((own > 0.5) & (valid > 0.5), jnp.exp(sims), 0.0)
    weight_ref[...] = weight
    row_safe = jnp.where(own > 0.5, jnp.sum(weight, 1, keepdims=True), 1.0)
    row_ref[...] = jnp.broadcast_to(0.5 / row_safe, row_ref.shape)
    part = 0.5 * jnp.log(row_safe) - jnp.sum(target * sims, 1, keepdims=True)
    part = jnp.sum(part, 0, keepdims=True)
    columns = jnp.sum(weight, 0, keepdims=True)
    blocks = columns.shape[1] // 128
    for block in range(blocks):
        total_ref[block : block + 1] = columns[:, block * 128 : (block + 1) * 128]
    total_ref[blocks:] = jnp.broadcast_to(part * (1.0 / 128), (1, 128))


def loss_front(main, index, middle, feeds, valid, w_embed, pictures):
    vmem = pl.BlockSpec(memory_space=pltpu.VMEM)
    count = pictures.shape[0]
    return pl.pallas_call(
        functools.partial(loss_front_body, main),
        out_shape=shapes(
            ((CAP_DEV, WIDTH), low),
            ((CAP_DEV, WIDTH), full),
            ((CAP_DEV, 128), full),
            ((CAP_DEV, count), full),
            ((CAP_DEV, 128), full),
            ((count // 128 + 1, 128), full),
        ),
        in_specs=[pl.BlockSpec(memory_space=pltpu.SMEM)] + [vmem] * 8,
        out_specs=[vmem] * 6,
        name="loss_front",
        compiler_params=LIMIT,
    )(index, middle, *feeds, valid, w_embed, pictures)


def loss_back_body(main, parts, index_ref, *refs):
    totals = refs[:parts]
    valid_ref, text_ref, inverse_ref, weight_ref, row_ref, picture_ref = refs[parts:-2]
    d_embed_ref, objective_ref = refs[-2:]
    total = totals[0][...]
    for ref in totals[1:]:
        total = total + ref[...]
    valid = valid_ref[...]
    blocks = valid.shape[1] // 128
    columns = jnp.concatenate([total[block : block + 1] for block in range(blocks)], 1)
    col_safe = jnp.where(valid > 0.5, columns, 1.0)
    logs = 0.5 * jnp.sum(jnp.log(col_safe), 1, keepdims=True)
    rows_part = jnp.sum(total[blocks:], 1, keepdims=True)
    objective_ref[...] = jnp.broadcast_to(logs + rows_part, objective_ref.shape)
    target, _ = own_slots(index_ref, valid, main)
    d_sims = weight_ref[...] * (row_ref[:, :1] + 0.5 / col_safe) - target
    d_unit = LOGIT_SCALE * mm(d_sims.astype(low), picture_ref[...])
    text = text_ref[...]
    along = jnp.sum(text * d_unit, -1, keepdims=True)
    d_embed_ref[...] = ((d_unit - text * along) * inverse_ref[:, :1]).astype(low)


def loss_back(main, index, totals, valid, text, inverse, weight, row, pictures):
    vmem = pl.BlockSpec(memory_space=pltpu.VMEM)
    return pl.pallas_call(
        functools.partial(loss_back_body, main, len(totals)),
        out_shape=shapes(((CAP_DEV, WIDTH), low), ((1, 128), full)),
        in_specs=[pl.BlockSpec(memory_space=pltpu.SMEM)] + [vmem] * (6 + len(totals)),
        out_specs=[vmem] * 2,
        name="loss_back",
        compiler_params=LIMIT,
    )(index, *totals, valid, text, inverse, weight, row, pictures)


def place_rows(picks, rows):
    high = rows.astype(low)
    rest = (rows - high.astype(full)).astype(low)
    return mm_tn(picks, jnp.concatenate([high, rest], 0))


def captions_body(
    start, blocks, group_ref, ends_ref, unit_ref, scale_ref, d_mid_ref, d_mixed_ref, dq_ref,
    q_far_ref, d_att_far_ref, small_far_ref, kv_ref, qo_ref, kv_far_ref, qo_far_ref, *refs,
):
    out_ref, inner_end_ref = refs[-2:]
    i = pl.program_id(0)
    count = dq_ref.shape[0]
    steps = count // BLOCK
    far = (start + steps // 2) % steps
    rows = blocks * BLOCK

    @pl.when(i == 0)
    def _():
        dq_far = jnp.concatenate(
            [
                small_far_ref[piece * count + far * BLOCK : piece * count + far * BLOCK + rows]
                for piece in range(3)
            ],
            1,
        )
        inner_end_ref[...] = mm_nt(
            dq_ref[start * BLOCK : start * BLOCK + rows], qo_ref[:, :COLS]
        ) + mm_nt(dq_far, qo_far_ref[:, :COLS])

    row, token = stack_grid()
    own_caption = token // LENGTH == row
    lane = lax.broadcasted_iota(jnp.int32, (128, TOKENS), 0) & (2 * LENGTH - 1)
    spot = lax.broadcasted_iota(jnp.int32, (128, TOKENS), 1) & (LENGTH - 1)
    zero = jnp.zeros((BLOCK, 128), low)
    place = pl.multiple_of(3 * count + 2 * BLOCK * (far + i), 2 * BLOCK)
    packed = small_far_ref[pl.ds(place, 2 * BLOCK), :]
    pair = jnp.concatenate(
        [
            jnp.where(lane_group() == h % 4, packed[h // 4 * BLOCK : (h // 4 + 1) * BLOCK], zero)
            for h in range(HEADS_HERE)
        ],
        0,
    )
    probs = jnp.where(own_caption, mm(pair, (spot == lane).astype(low)), 0.0).astype(low)
    d_scores = jnp.where(
        own_caption, mm(pair, (spot + LENGTH == lane).astype(low)), 0.0
    ).astype(low)
    d_mixed = jnp.concatenate(
        [
            mm_tn(d_scores, head_stack(q_far_ref[step_rows(far + i), :])).astype(low),
            mm_tn(probs, head_stack(d_att_far_ref[step_rows(far + i), :])).astype(low),
        ],
        1,
    )
    inner = mm_nt(d_mixed_ref[...], kv_ref[...]) + mm_nt(d_mixed, kv_far_ref[...])
    picks = end_picks(ends_ref[...], 2).astype(low)
    inner += place_rows(picks, inner_end_ref[step_rows(i), :])
    unit = unit_ref[...].astype(full)
    flat = jnp.sum(inner, -1, keepdims=True) * (1.0 / WIDTH)
    tilt = jnp.sum(inner * unit, -1, keepdims=True) * (1.0 / WIDTH)
    out_ref[...] = place_rows(picks, d_mid_ref[...]) + scale_ref[:, :1] * (
        inner - flat - unit * tilt
    )


def captions_back(
    start, blocks, group, ends, unit, scale, d_mid, d_mixed, dq, q_far, d_att_far, small_far, kv, qo,
    kv_far, qo_far, done=None,
):
    count = ends.shape[0]
    steps = count // BLOCK
    half = steps // 2
    operands = [
        group, ends, unit, scale, d_mid, d_mixed, dq, q_far, d_att_far, small_far, kv, qo,
        kv_far, qo_far,
    ]
    in_specs = [
        pl.BlockSpec((BLOCK, 1), lambda i, g: (i + start, 0)),
        pl.BlockSpec((TOKENS, WIDTH), lambda i, g: (i + start, 0)),
        pl.BlockSpec((TOKENS, 128), lambda i, g: (i + start, 0)),
        pl.BlockSpec((BLOCK, WIDTH), lambda i, g: (i + start, 0)),
        pl.BlockSpec((TOKENS, 2 * COLS), lambda i, g: (i + start, 0)),
        *[whole_block((count, COLS))] * 3,
        whole_block(small_far.shape),
    ] + [whole_block(kv.shape)] * 4
    aliases = {}
    if done is not None:
        aliases = {len(operands): 0}
        operands.append(done)
        in_specs.append(pl.BlockSpec(memory_space=pl.ANY))
    return pl.pallas_call(
        functools.partial(captions_body, start, blocks),
        out_shape=jax.ShapeDtypeStruct(unit.shape, full),
        grid_spec=pltpu.PrefetchScalarGridSpec(
            num_scalar_prefetch=1,
            grid=(blocks,),
            in_specs=in_specs,
            out_specs=pl.BlockSpec(
                (TOKENS, WIDTH), lambda i, g: ((i + start + g[0] * half) % steps, 0)
            ),
            scratch_shapes=[pltpu.VMEM((blocks * BLOCK, WIDTH), full)],
        ),
        input_output_aliases=aliases,
        name="captions_back",
    )(*operands)


def local(
    captions,
    image_cache,
    send_order,
    arrive_order,
    counts,
    keep_mask,
    end_pos,
    w_qkv,
    w_out,
    w_up,
    w_down,
    w_proj,
    ln1_gain,
    ln2_gain,
):
    plane = Plane()
    core = plane.core
    group = lax.axis_index("mp")
    spread = plane.count
    rows_dev, length, width = captions.shape
    rows = w_out.shape[0]
    per_peer = rows_dev // spread
    hidden = w_up.shape[1] // 2
    core_flag = core.reshape(1).astype(jnp.int32)
    group_flag = group.reshape(1).astype(jnp.int32)

    packed = pack(
        core_flag,
        w_qkv.transpose(1, 0, 2),
        w_out,
        w_up,
        w_down,
        w_proj,
        ln1_gain[None],
        ln2_gain[None],
    )
    def order_ends(end_pos):
        flipped = jnp.concatenate([end_pos, end_pos], 0)
        return lax.dynamic_slice_in_dim(flipped, group * CAP_DEV, rows_dev, 0)[:, None]

    wide = width // 2

    def pictures_of_batch(incoming):
        own_arrive = lax.dynamic_slice_in_dim(arrive_order[0], group * CAP_DEV, CAP_DEV, 0)
        take_in = (own_arrive[:, None] == places[None, :]).astype(low)
        pictures = mm(take_in, incoming.reshape(rows_dev, width)).astype(low)
        mine = pick(core, pictures[:, :wide], pictures[:, wide:])
        send = pick(core, pictures[:, wide:], pictures[:, :wide])
        return mine, send

    def prepare(image_cache):
        cached = image_cache.astype(full)
        norms = jnp.sum(cached * cached, -1, keepdims=True)
        cached = (cached * lax.rsqrt(norms + 1e-06)).astype(low)
        hand_out = (send_order[0][:, None] == places[None, :]).astype(low)
        return mm(hand_out, cached).astype(low).reshape(spread, per_peer, width)

    places = jnp.arange(rows_dev, dtype=jnp.int32)

    def deal(outgoing):
        return lax.all_to_all(outgoing, "dp", split_axis=0, concat_axis=0, tiled=True)

    def first_parts(stream, ends):
        return norm_first(group_flag, stream.reshape(rows_dev * length, width), ends)

    def attention_of(kv, qo, parts, ends):
        return attend(parts[0], parts[2], ends, kv, qo)

    main = rows if plane.fast else CAP_DEV
    spare = CAP_DEV - main
    if plane.fast:

        def join(feed, embed, half):
            parts = [half[main:, i * 128 : (i + 1) * 128] for i in range(wide // 128)]
            return jnp.concatenate([feed, embed, half[:main], jnp.concatenate(parts, 0)], 1)

        mix_cuts = (0, 2 * COLS)
        cuts = (0, 2 * hidden, 2 * hidden + 2 * wide + 128)
        arrived = plane.swap_core(packed[1])
        arrived, cache = joint(arrived, image_cache)
        block = plane.join_cores(packed[0], arrived)
        incoming = deal(prepare(cache))
        up = plane.shift_depth(block, 1)
        down = plane.shift_depth(block, -1)
        across = plane.swap_side(block)
        up, down, across, block = joint(up, down, across, block)

        mixes = plane.place(plane.empty(2 * rows, mix_cuts, block), mix_cuts, 0, block, across)
        far = plane.shift_depth(up, 1)
        across_up = plane.swap_side(up)
        across_down = plane.swap_side(down)
        far, across_up, across_down, incoming = joint(far, across_up, across_down, incoming)

        across = plane.swap_side(far)
        pictures = pictures_of_batch(incoming)
        mine = join(packed[2], packed[4], pictures[0])
        arrived = plane.swap_core(join(packed[3], packed[5], pictures[1]))
        mixes = plane.place(mixes, mix_cuts, 1, up, across_up)
        mixes = plane.place(mixes, mix_cuts, -1, down, across_down)
        across, arrived, mixes, counts, keep_mask, end_pos = joint(
            across, arrived, mixes, counts, keep_mask, end_pos
        )

        block = plane.join_cores(mine, arrived)
        one = plane.shift_depth(block, 1)
        across_block = plane.swap_side(block)
        mixes = plane.place(mixes, mix_cuts, 2, far, across)
        mix_own = mixes[0].reshape(width, 2 * COLS)
        mix_other = plane.swap_core(mix_own)
        far_own = swap_group(mix_own)
        kv = pick(core, mix_own, mix_other)
        qo = pick(core, mix_other, mix_own)
        ends = order_ends(end_pos)
        parts = first_parts(after(captions, block), ends)
        one, kv, qo, *parts = joint(one, kv, qo, *parts)

        two = plane.shift_depth(one, 1)
        across_one = plane.swap_side(one)
        stream_near = swap_near(parts[3], 2)
        attending = attention_of(kv, qo, parts, ends)
        two, across_block, across_one, stream_near, *attending = joint(
            two, across_block, across_one, stream_near, *attending
        )

        three = plane.shift_depth(two, 1)
        across_two = plane.swap_side(two)
        wholes = plane.place(plane.empty(2 * rows, cuts, attending[-1]), cuts, 0, block, across_block)
        wholes = plane.place(wholes, cuts, 1, one, across_one)
        attention = after(attending[-1], far_own)
        near = [swap_near(attention, flip) for flip in (1, 2, 3)]
        three, across_two, *near = joint(three, across_two, *near)

        across = plane.swap_side(three)
        queries_far = swap_group(attending[2])
        far_other = plane.swap_core(far_own)
        kv_far = pick(core, far_own, far_other)
        qo_far = pick(core, far_other, far_own)
        wholes = plane.place(wholes, cuts, 2, two, across_two)
        across, queries_far, kv_far, qo_far, wholes = joint(
            across, queries_far, kv_far, qo_far, wholes
        )
        wholes = plane.place(wholes, cuts, 3, three, across)
        feeds, third = [whole.reshape(width, -1) for whole in wholes]
        third_other = plane.swap_core(third)

        def images(x):
            extra = x[:, 2 * wide :].reshape(spread, wide // 128, spare, 128)
            extra = extra.transpose(0, 2, 1, 3).reshape(spread * spare, wide)
            return jnp.concatenate([x[:, wide : 2 * wide], extra], 0)

        image_halves = images(third), images(third_other)
        embed_halves = third[:, :wide], third_other[:, :wide]
    else:
        pictures = pictures_of_batch(deal(prepare(image_cache)))
        ends = order_ends(end_pos)
        parts = first_parts(captions, ends)
        mix_own = plane.gather_plain(packed[0], packed[1])
        mix_other = plane.swap_core(mix_own)
        far_own = swap_group(mix_own)
        kv = pick(core, mix_own, mix_other)
        qo = pick(core, mix_other, mix_own)
        attending = attention_of(kv, qo, parts, ends)
        feeds = plane.gather_plain(packed[2], packed[3])
        image_half = plane.gather_plain(*pictures)
        image_halves = image_half, plane.swap_core(image_half)
        embed_half = plane.gather_plain(packed[4], packed[5])
        embed_halves = embed_half, plane.swap_core(embed_half)
        far_other = plane.swap_core(far_own)
        kv_far = pick(core, far_own, far_other)
        qo_far = pick(core, far_other, far_own)
        stream_near = swap_near(parts[3], 2)
        attention = attending[-1]
        near = [swap_near(attention, flip) for flip in (1, 2, 3)]
        queries_far = swap_group(attending[2])
    unit, scale, unit_end, stream_end = parts
    mixed, probs, queries, attended, _ = attending

    def sides(pair):
        return jnp.concatenate([pick(core, *pair), pick(core, pair[1], pair[0])], 1)

    pictures_all = sides(image_halves)
    w_embed = sides(embed_halves)

    from_group, from_core, from_both = near
    attention = jnp.concatenate([attention, from_core], 0).astype(full)
    attention = attention + jnp.concatenate(
        [roll_rows(from_group), roll_rows(from_both)], 0
    ).astype(full)
    middle = jnp.concatenate([stream_end, stream_near], 0).astype(full) + attention
    unit_second, scale_second = norm_rows(middle)
    second_low = unit_second.astype(low)
    w_raise = feeds[:, :hidden]
    w_lower = feeds[:, hidden:]
    active, slope = gelu_parts(mm(second_low, w_raise))
    active = active.astype(low)
    lowered = mm_nt(active, w_lower).astype(low)
    feed_parts = [lowered[:CAP_DEV]] + [
        swap_near(lowered[flip * CAP_DEV : (flip + 1) * CAP_DEV], flip) for flip in (1, 2, 3)
    ]

    keep_rows = keep_mask.reshape(spread, MICRO, CAP_DEV) == 1
    filled = jnp.arange(CAP_DEV, dtype=jnp.int32)[None, None, :] < counts[:, :, None]
    valid = (keep_rows & filled).astype(full)
    total_valid = jnp.sum(valid)
    batch_valid = lax.dynamic_index_in_dim(valid, group, 1, False)
    batch_valid = jnp.concatenate(
        [batch_valid[:, :main].reshape(-1), batch_valid[:, main:].reshape(-1)]
    )[None]
    if plane.fast:
        batch_valid = after(batch_valid, near[0])
    place_flag = plane.index.reshape(1).astype(jnp.int32)
    pooled, unit_text, inverse, weight, row_half, totals = loss_front(
        main, place_flag, middle[:CAP_DEV], feed_parts, batch_valid, w_embed, pictures_all
    )
    if plane.fast:
        pooled_group = swap_near(pooled, 1)
        sent = [plane.flip(totals, bits) for bits in (1, 4, 5)]
        *sent, pooled_group = joint(*sent, pooled_group)
        totals = (totals + sent[0]) + (sent[1] + sent[2])
        totals = totals, *joint(*[plane.flip(totals, bits) for bits in (2, 8, 10)])
    else:
        totals = (lax.psum(totals, "dp"),)
    d_embed, objective = loss_back(
        main, place_flag, totals, batch_valid, unit_text, inverse, weight, row_half, pictures_all
    )

    d_embed_near = [swap_near(d_embed, flip) for flip in (1, 2, 3)]
    if plane.fast:
        pooled_pair = jnp.concatenate([pooled, pooled_group], 0)
        *d_embed_near, objective, pooled_near = joint(
            *d_embed_near, objective, plane.swap_core(pooled_pair)
        )
        pooled_all = jnp.concatenate([pooled_pair, pooled_near], 0)
    else:
        pooled_all = jnp.concatenate([pooled] + [swap_near(pooled, flip) for flip in (1, 2, 3)], 0)
    d_embed_all = jnp.concatenate([d_embed, *d_embed_near], 0)
    d_pooled = mm_nt(d_embed_all, w_embed)
    d_out_low = d_pooled.astype(low)
    d_raised = (mm(d_out_low, w_lower) * slope).astype(low)
    d_second = mm_nt(d_raised, w_raise).astype(low)
    second_late = after(second_low, d_second)
    g_raise = raise_back(2 * group_flag + core_flag, second_late, d_raised, pooled_all, d_embed_all)
    g_lower = mm_tn(after(d_out_low, d_second), active).astype(low)
    if plane.fast:
        raise_stay, raise_in = plane.halve(g_raise.reshape(2, 2, 2, 2 * rows, -1), 1, 4)
        lower_stay, lower_in = plane.halve(g_lower.reshape(2, 2, 2, 2 * rows, -1), 2, 2)
    d_second = add_low((d_second[:rows_dev], swap_near(d_second[rows_dev:], 2)))
    inner = d_second.astype(full) + roll_rows(swap_near(d_second, 1)).astype(full)
    d_middle = d_pooled[:rows_dev] + norm_back(
        inner, unit_second[:rows_dev], scale_second[:rows_dev]
    )

    d_middle_low = d_middle.astype(low)
    d_attended = mm(d_middle_low, qo[:, COLS:]).astype(low)
    d_attended_far = swap_group(d_attended)
    g_keep, g_send, d_mixed, d_queries, small = attend_back(
        core_flag, d_middle_low, d_attended, unit, unit_end, mixed, probs, queries, attended
    )

    def early_parts(raise_sum, lower_sum):
        grad_down = jnp.concatenate(lower_sum, 1)
        proj_own = jnp.concatenate([part[:, hidden:] for part in raise_sum], 1)
        raised_sum = jnp.concatenate([part[:, :hidden] for part in raise_sum], 1)
        gain_second = jnp.sum(raised_sum * w_up.astype(full), 1)
        early = jnp.stack([gain_second, jnp.broadcast_to(objective[0, 0], (rows,))])
        return proj_own, grad_down, raised_sum, early

    def captions_part(start, blocks, d_queries_here, far_parts, done=None):
        return captions_back(
            start, blocks, group_flag, ends, unit, scale, d_middle, d_mixed, d_queries_here, queries_far,
            *far_parts, kv, qo, kv_far, qo_far, done=done,
        )

    if plane.fast:
        raise_stay, raise_in, lower_stay, lower_in, d_queries, g_send, d_attended_far = joint(
            raise_stay, raise_in, lower_stay, lower_in, d_queries, g_send, d_attended_far
        )
        small_far = swap_group(small)
        mix_in = plane.swap_core(g_send)
        raise_pair = add_low((raise_stay, raise_in))
        lower_pair = add_low((lower_stay, lower_in))
        raise_side = plane.halve(raise_pair, 1, 2)
        small_far, mix_in, *raise_side, lower_pair = joint(
            small_far, mix_in, *raise_side, lower_pair
        )
        raise_last = plane.halve(add_low(raise_side), 0, 8)
        lower_depth = plane.halve(lower_pair, 1, 4)
        mix_pair = add_low((g_keep, mix_in)).reshape(2, 2, 2, 2 * rows, 2 * COLS)
        mix_side = plane.halve(mix_pair, 2, 2)
        far_parts = d_attended_far, small_far
        half = rows_dev // BLOCK // 2
        first_half = captions_part(0, half, after(d_queries, mix_side[0]), far_parts)
        raise_last, lower_depth, mix_side, first_half = joint(
            raise_last, lower_depth, mix_side, first_half
        )
        mix_depth = plane.halve(add_low(mix_side), 1, 4)
        lower_last = plane.halve(add_low(lower_depth), 0, 8)
        starts = after(d_queries, mix_depth[0], lower_last[0])
        third_part = captions_part(half, half // 2, starts, far_parts, first_half)
        mix_depth, lower_last, third_part = joint(mix_depth, lower_last, third_part)
        mix_last = plane.halve(add_low(mix_depth), 0, 8)
        starts = after(d_queries, mix_last[0])
        grad_captions = captions_part(half + half // 2, half - half // 2, starts, far_parts, third_part)
        raise_sum, lower_sum = [
            plane.scatter_core(pair[0].astype(full) + pair[1].astype(full))
            for pair in (raise_last, lower_last)
        ]
        proj_own, grad_down, raised_sum, early = early_parts(raise_sum, lower_sum)
        proj_far, early_far = swap_group(proj_own), swap_group(early)
        mix_last, proj_far, early_far, grad_down, raised_sum, grad_captions = joint(
            mix_last, proj_far, early_far, grad_down, raised_sum, grad_captions
        )
        mix_sum = plane.scatter_core(mix_last[0].astype(full) + mix_last[1].astype(full))
    else:
        far_parts = d_attended_far, swap_group(small)
        grad_captions = captions_part(0, rows_dev // BLOCK, d_queries, far_parts)
        raise_sum = plane.scatter_plain(g_raise)
        lower_sum = plane.scatter_plain(g_lower)
        proj_own, grad_down, raised_sum, early = early_parts(raise_sum, lower_sum)
        proj_far, early_far = swap_group(proj_own), swap_group(early)
        mix_sum = plane.scatter_plain(g_keep, g_send)
    grad_captions = grad_captions.reshape(rows_dev, length, width)

    grad_proj = pick(
        group,
        jnp.concatenate([proj_own, proj_far], 1),
        jnp.concatenate([proj_far, proj_own], 1),
    )
    grad_out = mix_sum[1][:, COLS:]
    unit_mix = jnp.stack([mix_sum[1][:, :COLS], mix_sum[0][:, :COLS], mix_sum[0][:, COLS:]], 1)
    grad_qkv = unit_mix * ln1_gain[:, None, None]
    grad_up = raised_sum * ln2_gain[:, None]
    early = early + early_far
    loss = early[1, 0] / total_valid
    gain_first = jnp.sum(unit_mix * w_qkv.astype(full), (1, 2))[None]
    gain_first = gain_first + swap_group(gain_first)
    return (
        loss,
        grad_captions,
        grad_qkv,
        grad_out,
        grad_up,
        grad_down,
        grad_proj,
        gain_first[0],
        early[0],
    )


def solution(mesh):
    return jax.shard_map(
        local,
        mesh=mesh,
        in_specs=(
            P("dp", None, None),
            P("dp", None),
            P("dp", None),
            P("dp", None),
            P(),
            P(),
            P("dp"),
            P("dp", None, "mp"),
            P("dp", "mp"),
            P("dp", "mp"),
            P("dp", "mp"),
            P("dp", None),
            P("dp"),
            P("dp"),
        ),
        out_specs=(
            P(),
            P("dp", None, None),
            P("dp", None, "mp"),
            P("dp", "mp"),
            P("dp", "mp"),
            P("dp", "mp"),
            P("dp", None),
            P("dp"),
            P("dp"),
        ),
        check_vma=False,
    )
```
